32 devices in a mesh: dp: 2 (over y), seq: 4 (over x, core), shard: 4 (over z).
Axes of the slice: x: 2, y: 2, z: 4, core: 2. Of those that a mesh axis runs over, the one named last changes fastest.
Arguments:
- tokens: int32 [8, 1024], P(('dp', 'shard'), 'seq'), may hold values from 0 to 50277
- block_ids: int32 [8, 1024], P(('dp', 'shard')), may hold values from 0 to 7, never falling along the last dimension, each value on 1 to 256 neighbouring positions
- completion: int32 [8, 1024], P(('dp', 'seq')), may hold values from 0 to 1, as said below
- regroup: int32 [8, 256], P(('dp', 'seq')), may hold values from 0 to 255, each once within a row
- targets: int32 [2048], replicated, may hold values from 0 to 50277
- step_count: int32 [1], replicated, may hold values from 1 to 20
- layer_mats: float32 [2, 3, 4352, 1088], P(None, None, ('dp', 'seq', 'shard'))
- mats_moment: float32 [2, 3, 4352, 1088], P(None, None, ('dp', 'seq', 'shard')), may hold values from -3.8146973e-06 to 3.8146973e-06
- mats_square: float32 [2, 3, 4352, 1088], P(None, None, ('dp', 'seq', 'shard')), may hold values from 1.2343522e-13 to 1.9939536e-12
- embed_table: float32 [51328, 1088], P(('dp', 'seq', 'shard'))
- table_moment: float32 [51328, 1088], P(('dp', 'seq', 'shard')), may hold values from -3.8146973e-06 to 3.8146973e-06
- table_square: float32 [51328, 1088], P(('dp', 'seq', 'shard')), may hold values from 1.2343522e-13 to 1.9939536e-12
Outputs:
- loss_value: float32 [1], replicated
- grad_norm: float32 [1], replicated
- updated_mats: float32 [2, 3, 4352, 1088], P(None, None, ('dp', 'seq', 'shard'))
- moment_mats: float32 [2, 3, 4352, 1088], P(None, None, ('dp', 'seq', 'shard'))
- square_mats: float32 [2, 3, 4352, 1088], P(None, None, ('dp', 'seq', 'shard'))
- updated_table: float32 [51328, 1088], P(('dp', 'seq', 'shard'))
- moment_table: float32 [51328, 1088], P(('dp', 'seq', 'shard'))
- square_table: float32 [51328, 1088], P(('dp', 'seq', 'shard'))
The draws below stay inside these ranges and needn't reach their ends.
Inputs may be any that keep to these rules, and one draw needn't show every extreme that they name: `completion`: each row holds exactly 256 ones; their split among the 4 column blocks of 256 varies. `regroup`: each row is a permutation. `block_ids`: along a sequence the numbers never fall; a block has at most 256 positions.
All inputs are finite; a program needn't handle non-finite values.
Results may differ from the reference program's by a relative error of at most 0.007.
The reference program's roundings to bfloat16 on the way count: a program that leaves them out, or rounds other values in their place, can miss the bound.
Values may be sent and summed in bfloat16 or wider, within the bound.
A program may use at most 896 MiB of HBM per device.

```python
import functools
import math
import jax
import jax.numpy as jnp
import numpy as np
from jax import lax

D = 1088
HEADS = 17
FF = 4352
HEAD = 64
VOCAB = 50278
LAYERS = 2
LEN = 1024
BLOCK = 256
SEQ_DEV = 1
TOK = 256
TOKR = 256
SEQS = 8
GROUPS = 8
GROUP_ROWS = 1024
GROUP_COMP = 256
ROWS_ALL = 2048
TABLE = 51328
SEGS = 8
N_SEQ = 4
N_SHARD = 4


def draw_completion(key, part):
    key_lean, key_noise = jax.random.split(key)
    shards = GROUP_ROWS // TOKR
    lean = jax.random.randint(key_lean, (GROUPS, shards, 1), 0, 4)
    noise = jax.random.randint(key_noise, (GROUPS, shards, TOKR), 0, 64)
    score = (noise + 48 * lean).reshape(GROUPS, GROUP_ROWS)
    score = score * GROUP_ROWS + jnp.arange(GROUP_ROWS, dtype=jnp.int32)[None, :]
    unused, picked = lax.top_k(score, GROUP_COMP)
    group = jnp.arange(GROUPS, dtype=jnp.int32)[:, None]
    return jnp.zeros((GROUPS, GROUP_ROWS), jnp.int32).at[group, picked].set(1)


def draw_layer_mats(key, part):
    shape = (LAYERS, 3, FF, D)
    base = jax.random.normal(key, shape, jnp.float32)
    row = jnp.arange(FF)[:, None]
    first = jnp.where(row < 3 * D, D ** (-0.5), 0.3)
    second = jnp.full((FF, 1), D ** (-0.5))
    third = jnp.full((FF, 1), FF ** (-0.5))
    scale = jnp.stack([first, second, third]).astype(jnp.float32)
    return base * scale[None]


def draw_embed_table(key, part):
    key_base, key_flat = jax.random.split(key)
    shape = (TABLE, D)
    base = jax.random.normal(key_base, shape, jnp.float32)
    flat = jax.random.uniform(key_flat, shape, jnp.float32, -1.0, 1.0)
    row = jnp.arange(TABLE)[:, None]
    kind = (row - VOCAB - LEN) % 12
    small = row >= VOCAB + LEN
    gain = small & ((kind == 0) | (kind == 5))
    bias_scale = jnp.where(kind == 3, 0.02, jnp.where((kind == 4) | (kind == 7), 0.05, 0.1))
    scale = jnp.where(row < VOCAB, 2.0 * D ** (-0.5), jnp.where(small, bias_scale, 0.1))
    return jnp.where(gain, 1.0 + 0.3 * flat, base * scale)


def place_ends(values, key, low, high):
    index_at = [jax.random.randint(jax.random.fold_in(key, axis), (), 0, length) for axis, length in enumerate(values.shape)]
    longest = values.shape.index(max(values.shape))
    next_to = index_at[:longest] + [(index_at[longest] + 1) % values.shape[longest]] + index_at[longest + 1:]
    return values.at[tuple(index_at)].set(low).at[tuple(next_to)].set(high)


def shard_levels(stream_key, extent, cuts, smallest, high):
    factor_of = 1.0
    for axis_at, parts in cuts:
        draws = jax.random.uniform(jax.random.fold_in(jax.random.fold_in(stream_key, 6), axis_at), (parts,), jnp.float32, smallest / len(cuts), high / len(cuts))
        factor_of = factor_of * jnp.repeat(jnp.exp(draws), extent[axis_at] // parts).reshape((-1,) + (1,) * (len(extent) - 1 - axis_at))
    return factor_of


def rank_bounds(number_of, skew):
    portions = [(1 << 20) // math.isqrt(grade ** skew) + 1 for grade in range(1, number_of + 1)]
    width = 1 + sum(portions) // (1 << 30)
    return np.cumsum(np.array([max(1, weight // width) for weight in portions]))


def ranked_ids(rng, dims, number_of, skew):
    table = rank_bounds(number_of, skew)
    pick = jax.random.randint(jax.random.fold_in(rng, 1), dims, 0, int(table[number_of - 1]))
    grade = jnp.searchsorted(jnp.asarray(table, jnp.int32), pick, side="right")
    return jax.random.permutation(jax.random.fold_in(rng, 2), number_of)[grade].astype(jnp.int32)


def split_up(amount, total, reach, skew):
    loads = [(1 << 20) // math.isqrt(standing ** skew) + 1 for standing in range(2, amount + 1)]
    spare, holding = total - reach - (amount - 1), [1] * (amount - 1)
    while spare > 0:
        free = [i for i in range(amount - 1) if holding[i] < reach]
        pool, remaining = sum([loads[i] for i in free]), spare
        for i in free:
            extra = min(reach - holding[i], max(1, remaining * loads[i] // pool), spare)
            holding[i] = holding[i] + extra
            spare = spare - extra
    return np.array([reach] + holding)


def ragged(key, number_of, total, most, skew):
    if number_of == 2:
        one = jax.random.randint(key, (), max(1, total - most), min(most, total - 1) + 1)
        return jnp.stack([one, total - one])
    lengths = jnp.asarray(split_up(number_of, total, most, skew), jnp.int32)
    pairs = (number_of - 1) // 2
    donor, taker = lengths[1:1 + 2 * pairs:2], lengths[2:2 + 2 * pairs:2]
    slack = jnp.minimum(donor - 1, most - taker)
    moved = jax.random.randint(jax.random.fold_in(key, 1), (pairs,), 0, 1 << 20) % (slack + 1)
    lengths = lengths.at[1:1 + 2 * pairs:2].set(donor - moved).at[2:2 + 2 * pairs:2].set(taker + moved)
    return lengths[jax.random.permutation(jax.random.fold_in(key, 2), number_of)]


def centred(rng, shape, scale, reach, pieces=(), kind=jnp.bfloat16):
    result = jax.random.normal(rng, shape, jnp.float32) * scale
    if len(pieces) > 0:
        result = shard_levels(rng, shape, pieces, -0.22, 0.18) * result
    return jnp.clip(result, min=-reach, max=reach).astype(kind)


def setup_inputs(seed: int = 0) -> dict:
    key_list = jax.random.split(jax.random.key(seed), 13)
    return {
        "tokens": place_ends(ranked_ids(key_list[0], (SEQS, LEN), VOCAB, 0), jax.random.fold_in(key_list[0], 3), 0, VOCAB - 1).astype(jnp.int32),
        "block_ids": jax.vmap(lambda own: jnp.searchsorted(jnp.cumsum(ragged(own, SEGS, LEN, BLOCK, 0)), jnp.arange(LEN), side="right"))(jax.random.split(key_list[1], SEQS)).reshape((SEQS, LEN)).astype(jnp.int32),
        "completion": draw_completion(jax.random.fold_in(key_list[12], 71), 0),
        "regroup": jax.vmap(lambda own: jax.random.permutation(own, GROUP_COMP))(jax.random.split(key_list[3], GROUPS)).reshape((GROUPS, GROUP_COMP)).astype(jnp.int32),
        "targets": place_ends(ranked_ids(key_list[4], (ROWS_ALL,), VOCAB, 0), jax.random.fold_in(key_list[4], 3), 0, VOCAB - 1).astype(jnp.int32),
        "step_count": jax.random.randint(key_list[5], (1,), 1, 21).astype(jnp.int32),
        "layer_mats": draw_layer_mats(jax.random.fold_in(key_list[12], 71), 0),
        "mats_moment": centred(key_list[7], (LAYERS, 3, FF, D), (0.0022 * (3 * LAYERS * FF * D + TABLE * D) ** -0.5), 3.814697265625e-06, ((2, 32),), jnp.float32),
        "mats_square": jnp.clip(jnp.exp(math.log(1.9939536133328772e-12) - 2.7821582 * jax.random.uniform(key_list[8], (LAYERS, 3, FF, D), jnp.float32) ** shard_levels(key_list[8], (LAYERS, 3, FF, D), ((2, 32),), -0.2, 0.2)), 1.2343522471508495e-13, 1.9939536133328772e-12),
        "embed_table": draw_embed_table(jax.random.fold_in(key_list[12], 71), 0),
        "table_moment": centred(key_list[10], (TABLE, D), (0.0022 * (3 * LAYERS * FF * D + TABLE * D) ** -0.5), 3.814697265625e-06, ((0, 32),), jnp.float32),
        "table_square": jnp.clip(jnp.exp(math.log(1.9939536133328772e-12) - 2.7821582 * jax.random.uniform(key_list[11], (TABLE, D), jnp.float32) ** shard_levels(key_list[11], (TABLE, D), ((0, 32),), -0.2, 0.2)), 1.2343522471508495e-13, 1.9939536133328772e-12),
    }


@jax.custom_vjp
def low(v):
    return lax.optimization_barrier(v.astype(jnp.bfloat16)).astype(jnp.float32)

@jax.custom_vjp
def low_back(v):
    return v

def low_keep(v):
    return (low(v), None)

def low_pass(kept, grad):
    return (grad,)

def back_keep(v):
    return (v, None)

def back_low(kept, grad):
    return (low(grad),)
low.defvjp(low_keep, low_pass)
low_back.defvjp(back_keep, back_low)
HIGHEST = lax.Precision.HIGHEST
NORM_EPS = 1e-05
CLIP_NORM = 0.02
BETA_ONE = 0.9
BETA_TWO = 0.95
ADAM_EPS = 1e-08
DECAY_RATE = 0.1
RATE_MATS = 0.05
RATE_TABLE = 0.1
RATE_SMALL = 0.5
MASK_FILL = -1e+30

def dot_rows(left_op, right_op):
    return lax.dot_general(left_op, right_op, (((1,), (1,)), ((), ())), precision=HIGHEST)

def layer_norm(values, gain, shift):
    center = values - lax.optimization_barrier(jnp.mean(values, -1, keepdims=True))
    spread = lax.optimization_barrier(jnp.mean(center * center, -1, keepdims=True))
    return center * lax.rsqrt(spread + NORM_EPS) * gain + shift

def seq_layer(pair, weights, params):
    state, block_of = pair
    scale = HEAD ** (-0.5)
    hidden = low(layer_norm(state, params[0], params[1]))
    joined = dot_rows(hidden, weights[0, :3 * D])
    queries = low(low_back(joined[:, :D] + params[2])).reshape(LEN, HEADS, HEAD)
    key_rows = low(low_back(joined[:, D:2 * D])).reshape(LEN, HEADS, HEAD)
    val_rows = low(low_back(joined[:, 2 * D:] + params[3])).reshape(LEN, HEADS, HEAD)
    scores = low_back(jnp.einsum('qhd,khd->hqk', queries, key_rows, precision=HIGHEST) * scale)
    allowed = block_of[None, :] <= block_of[:, None]
    scores = jnp.where(allowed[None], scores, MASK_FILL)
    probs = low(jax.nn.softmax(scores, axis=-1))
    attended = jnp.einsum('hqk,khd->qhd', probs, val_rows, precision=HIGHEST).reshape(LEN, D)
    attended = low(low_back(attended))
    mid_state = state + low_back(jnp.dot(attended, weights[0, 3 * D:], precision=HIGHEST) + params[4])
    normed = low(layer_norm(mid_state, params[5], params[6]))
    upward = low_back(dot_rows(normed, weights[1]) + params[8:12].reshape(-1))
    active = low(jax.nn.gelu(upward, approximate=True))
    return mid_state + low_back(jnp.dot(active, weights[2], precision=HIGHEST) + params[7])

def head_block(pair, vocab_rows):
    rows_in, wanted = pair
    logits = low_back(dot_rows(rows_in, vocab_rows))
    highest = lax.optimization_barrier(jnp.max(logits, -1, keepdims=True))
    totals = highest[:, 0] + jnp.log(lax.optimization_barrier(jnp.sum(jnp.exp(logits - highest), -1)))
    chosen = jnp.take_along_axis(logits, wanted[:, None], 1)[:, 0]
    return jnp.sum(totals - chosen)

def completion_rows(completion, regroup):
    order = jnp.argsort(1 - completion, axis=1, stable=True)[:, :GROUP_COMP].astype(jnp.int32)
    shard_of = order // TOKR
    within = order % TOKR
    group = jnp.arange(GROUPS, dtype=jnp.int32)[:, None]
    sequence = (group // N_SEQ * N_SHARD + shard_of) * SEQ_DEV + within // TOK
    flat = sequence * LEN + group % N_SEQ * TOK + within % TOK
    slots = group * GROUP_COMP + regroup
    return jnp.zeros((ROWS_ALL,), jnp.int32).at[slots.reshape(-1)].set(flat.reshape(-1).astype(jnp.int32))

def forward(layer_mats, embed_table, tokens, block_ids, row_index, targets):
    table_low = low(embed_table)
    weights_low = low(layer_mats)
    places = jnp.arange(LEN, dtype=jnp.int32)
    state = table_low[tokens] + table_low[VOCAB + places][None]
    small = table_low[VOCAB + LEN:]
    for layer_at in range(LAYERS):
        step_fn = jax.checkpoint(functools.partial(seq_layer, weights=weights_low[layer_at], params=small[12 * layer_at:12 * layer_at + 12]))
        state = lax.map(step_fn, (state, block_ids))
    final = low(low_back(layer_norm(state, small[12 * LAYERS], small[12 * LAYERS + 1])))
    block_rows = math.gcd(512, ROWS_ALL)
    picked_rows = final.reshape(-1, D)[row_index].reshape(-1, block_rows, D)
    picked_targets = targets.reshape(-1, block_rows)
    head_fn = jax.checkpoint(functools.partial(head_block, vocab_rows=table_low[:VOCAB]))
    losses = lax.map(head_fn, (picked_rows, picked_targets))
    return jnp.sum(losses) / ROWS_ALL

def adam_step(weights, moment, square, grad, rate, decay, step):
    moment = BETA_ONE * moment + (1 - BETA_ONE) * grad
    square = BETA_TWO * square + (1 - BETA_TWO) * grad * grad
    moment_hat = moment / (1 - BETA_ONE ** step)
    square_hat = square / (1 - BETA_TWO ** step)
    weights = weights - rate * (moment_hat / (jnp.sqrt(square_hat) + ADAM_EPS) + decay * weights)
    return (weights, moment, square)

def reference(tokens, block_ids, completion, regroup, targets, step_count, layer_mats, mats_moment, mats_square, embed_table, table_moment, table_square):
    row_index = completion_rows(completion, regroup)
    loss_value, pull = jax.vjp(lambda mats_in, table_in: forward(mats_in, table_in, tokens, block_ids, row_index, targets), layer_mats, embed_table)
    grad_mats, grad_table = pull(jnp.ones_like(loss_value))
    grad_norm = jnp.sqrt(jnp.sum(grad_mats * grad_mats) + jnp.sum(grad_table * grad_table))
    factor = CLIP_NORM / grad_norm
    step = step_count[0].astype(jnp.float32)
    new_mats = adam_step(layer_mats, mats_moment, mats_square, factor * grad_mats, RATE_MATS, DECAY_RATE, step)
    plain_rows = (jnp.arange(TABLE) < VOCAB + LEN)[:, None]
    rate = jnp.where(plain_rows, RATE_TABLE, RATE_SMALL)
    decay = jnp.where(plain_rows, DECAY_RATE, 0.0)
    new_table = adam_step(embed_table, table_moment, table_square, factor * grad_table, rate, decay, step)
    return (loss_value.reshape(1), grad_norm.reshape(1), new_mats[0], new_mats[1], new_mats[2], new_table[0], new_table[1], new_table[2])
```

```python
import itertools
from functools import partial

import jax
import jax.numpy as jnp
from jax import lax
from jax.experimental import pallas as pl
from jax.experimental.layout import Layout, with_layout_constraint
from jax.experimental.pallas import tpu as pltpu
from jax.sharding import PartitionSpec as P

HEADS = 17
HEAD = 64
VOCAB = 50278

NORM_EPS = 1e-05
CLIP_NORM = 0.02
BETA_ONE = 0.9
BETA_TWO = 0.95
ADAM_EPS = 1e-08
DECAY_RATE = 0.1
RATE_MATS = 0.05
RATE_TABLE = 0.1
RATE_SMALL = 0.5
MASK_FILL = -1e30

AXES = ("dp", "seq", "shard")
MESH = pl.DeviceIdType.MESH
SLOTS = 24


def bits_of(axis):
    return [(axis, b) for b in range(lax.axis_size(axis).bit_length() - 1)]


def bit_here(bit):
    return lax.rem(lax.axis_index(bit[0]) // 2 ** bit[1], 2)


def partner(bit):
    at = lax.axis_index(bit[0])
    return {bit[0]: at + (1 - 2 * bit_here(bit)) * 2 ** bit[1]}


def greet(bits):
    barrier = pltpu.get_barrier_semaphore()
    for bit in bits:
        pl.semaphore_signal(barrier, inc=1, device_id=partner(bit), device_id_type=MESH)
    pl.semaphore_wait(barrier, len(bits))


def block_weight(axes, bit):
    weight = 2 ** bit[1]
    for axis in axes[axes.index(bit[0]) + 1 :]:
        weight *= lax.axis_size(axis)
    return weight


def block_runs(weights):
    weights = sorted(weights)
    joined = 0
    while joined < len(weights) and weights[joined] == 2**joined:
        joined += 1
    rest = [(0, w) for w in weights[joined:]]
    return 2**joined, [sum(c) for c in itertools.product(*rest)]


def exchange_kernel(sum_axes, sum_orders, join_axes, join_orders, rows, *refs):
    it = iter(refs)
    x_ref, o_ref = next(it), next(it)
    work, parcel, recv = (next(it), next(it), next(it)) if sum_axes else (None, None, None)
    send_sems, recv_sems = next(it), next(it)
    streams = max(len(sum_orders), len(join_orders))
    share = rows // streams
    spans = [pl.ds(s * share, share) for s in range(streams)]
    greet(sorted(set(sum(sum_orders, []) + sum(join_orders, []))))
    count = itertools.count()
    if sum_axes:
        slot = [0] * streams
        for step in range(len(sum_orders[0])):
            started = []
            source = x_ref if step == 0 else work
            for s, order in enumerate(sum_orders):
                bit = order[step]
                base = sum(bit_here(b) * block_weight(sum_axes, b) for b in order[:step])
                weight = block_weight(sum_axes, bit)
                mine = bit_here(bit)
                size, offsets = block_runs([block_weight(sum_axes, b) for b in order[step + 1 :]])
                for offset in offsets:
                    k = next(count)
                    leave = base + (1 - mine) * weight + offset
                    if source.dtype == parcel.dtype:
                        packed = source.at[pl.ds(leave, size), spans[s]]
                    else:

                        def pack(i, carry, s=s, leave=leave, at=slot[s], source=source):
                            parcel[at + i, spans[s]] = source[leave + i, spans[s]].astype(parcel.dtype)
                            return carry

                        lax.fori_loop(0, size, pack, 0)
                        packed = parcel.at[pl.ds(slot[s], size), spans[s]]
                    copy = pltpu.make_async_remote_copy(
                        packed,
                        recv.at[pl.ds(slot[s], size), spans[s]],
                        send_sems.at[k],
                        recv_sems.at[k],
                        device_id=partner(bit),
                        device_id_type=MESH,
                    )
                    copy.start()
                    started.append((copy, s, base + mine * weight + offset, slot[s], size))
                    slot[s] += size
            for copy, s, keep, at, size in started:
                copy.wait()

                def add(i, carry, s=s, keep=keep, at=at, source=source):
                    total = source[keep + i, spans[s]].astype(jnp.float32)
                    total = total + recv[at + i, spans[s]].astype(jnp.float32)
                    work[keep + i, spans[s]] = total.astype(work.dtype)
                    return carry

                lax.fori_loop(0, size, add, 0)
        result = work[sum(bit_here(b) * block_weight(sum_axes, b) for b in sum_orders[0])]
    else:
        result = x_ref[0]
    result = result.astype(o_ref.dtype)
    if not join_axes:
        o_ref[...] = result
        return
    o_ref[sum(bit_here(b) * block_weight(join_axes, b) for b in join_orders[0])] = result
    for step in range(len(join_orders[0])):
        started = []
        for s, order in enumerate(join_orders):
            bit = order[step]
            base = sum(bit_here(b) * block_weight(join_axes, b) for b in order[step:])
            size, offsets = block_runs([block_weight(join_axes, b) for b in order[:step]])
            for offset in offsets:
                k = next(count)
                here = o_ref.at[pl.ds(base + offset, size), spans[s]]
                copy = pltpu.make_async_remote_copy(
                    here,
                    here,
                    send_sems.at[k],
                    recv_sems.at[k],
                    device_id=partner(bit),
                    device_id_type=MESH,
                )
                copy.start()
                started.append(copy)
        for copy in started:
            copy.wait()


def exchange(x, name, number, sum_axes=(), sum_orders=(), join_axes=(), join_orders=()):
    rows, width = x.shape[-2:]
    blocks = 1
    for axis in join_axes:
        blocks *= lax.axis_size(axis)
    out = (blocks, rows, width) if join_axes else (rows, width)
    kind = jnp.bfloat16 if sum_axes else x.dtype
    sends = 0
    for step in range(len(sum_orders[0]) if sum_orders else 0):
        for order in sum_orders:
            sends += len(block_runs([block_weight(sum_axes, b) for b in order[step + 1 :]])[1])
    for step in range(len(join_orders[0]) if join_orders else 0):
        for order in join_orders:
            sends += len(block_runs([block_weight(join_axes, b) for b in order[:step]])[1])
    scratch = []
    if sum_axes:
        if x.size * 14 > 56 * 2**20:
            x = x.astype(jnp.bfloat16)
        scratch = [
            pltpu.VMEM(x.shape, jnp.float32 if x.dtype == jnp.float32 or x.size < 2**22 else kind),
            pltpu.VMEM(x.shape, kind),
            pltpu.VMEM(x.shape, kind),
        ]
    scratch += [pltpu.SemaphoreType.DMA((sends,)), pltpu.SemaphoreType.DMA((sends,))]
    return pl.pallas_call(
        partial(exchange_kernel, sum_axes, sum_orders, join_axes, join_orders, rows),
        out_shape=jax.ShapeDtypeStruct(out, kind),
        in_specs=[pl.BlockSpec(memory_space=pltpu.VMEM)],
        out_specs=pl.BlockSpec(memory_space=pltpu.VMEM),
        scratch_shapes=scratch,
        compiler_params=pltpu.CompilerParams(
            collective_id=number, has_side_effects=True, vmem_limit_bytes=60 * 2**20
        ),
        name=name,
    )(x)


def combine_kernel(bits, combine, x_ref, o_ref, out_buf, in_buf, send_sems, recv_sems):
    greet(bits)
    current = x_ref[...]
    for i, bit in enumerate(bits):
        out_buf[i] = current
        copy = pltpu.make_async_remote_copy(
            out_buf.at[i],
            in_buf.at[i],
            send_sems.at[i],
            recv_sems.at[i],
            device_id=partner(bit),
            device_id_type=MESH,
        )
        copy.start()
        copy.wait()
        other = in_buf[i]
        low = bit_here(bit) == 0
        current = combine(jnp.where(low, current, other), jnp.where(low, other, current))
    o_ref[...] = current


def combine_all(x, combine, name, number):
    bits = [bit for axis in reversed(AXES) for bit in bits_of(axis)]
    slots = (len(bits),) + x.shape
    return pl.pallas_call(
        partial(combine_kernel, bits, combine),
        out_shape=jax.ShapeDtypeStruct(x.shape, x.dtype),
        in_specs=[pl.BlockSpec(memory_space=pltpu.VMEM)],
        out_specs=pl.BlockSpec(memory_space=pltpu.VMEM),
        scratch_shapes=[
            pltpu.VMEM(slots, x.dtype),
            pltpu.VMEM(slots, x.dtype),
            pltpu.SemaphoreType.DMA((len(bits),)),
            pltpu.SemaphoreType.DMA((len(bits),)),
        ],
        compiler_params=pltpu.CompilerParams(collective_id=number, has_side_effects=True),
        name=name,
    )(x)


def swap_kernel(x_ref, o_ref, send_sems, recv_sems, own_sem):
    seq_size, shard_size = lax.axis_size("seq"), lax.axis_size("shard")
    total = lax.axis_size("dp") * seq_size * shard_size
    me = (lax.axis_index("dp") * seq_size + lax.axis_index("seq")) * shard_size + lax.axis_index("shard")

    def place(at):
        return {
            "dp": at // (seq_size * shard_size),
            "seq": lax.rem(at // shard_size, seq_size),
            "shard": lax.rem(at, shard_size),
        }

    barrier = pltpu.get_barrier_semaphore()

    def hello(k, carry):
        pl.semaphore_signal(
            barrier, inc=1, device_id=place(lax.rem(me + k, total)), device_id_type=MESH
        )
        return carry

    lax.fori_loop(1, total, hello, 0)
    pl.semaphore_wait(barrier, total - 1)
    keep = pltpu.make_async_copy(x_ref.at[me], o_ref.at[me], own_sem)
    keep.start()

    def send(k, carry):
        to = lax.rem(me + k, total)
        pltpu.make_async_remote_copy(
            x_ref.at[to],
            o_ref.at[me],
            send_sems.at[to],
            recv_sems.at[me],
            device_id=place(to),
            device_id_type=MESH,
        ).start()
        return carry

    lax.fori_loop(1, total, send, 0)

    def finish(k, carry):
        other = lax.rem(me + k, total)
        pltpu.make_async_remote_copy(
            x_ref.at[other],
            o_ref.at[other],
            send_sems.at[other],
            recv_sems.at[other],
            device_id=place(other),
            device_id_type=MESH,
        ).wait()
        return carry

    lax.fori_loop(1, total, finish, 0)
    keep.wait()


def swap(x, name, number):
    total = x.shape[0]
    return pl.pallas_call(
        swap_kernel,
        out_shape=jax.ShapeDtypeStruct(x.shape, x.dtype),
        in_specs=[pl.BlockSpec(memory_space=pl.ANY)],
        out_specs=pl.BlockSpec(memory_space=pl.ANY),
        scratch_shapes=[
            pltpu.SemaphoreType.DMA((total,)),
            pltpu.SemaphoreType.DMA((total,)),
            pltpu.SemaphoreType.DMA,
        ],
        compiler_params=pltpu.CompilerParams(collective_id=number, has_side_effects=True),
        name=name,
    )(x)


def add_pair(first, second):
    return first + second


def merge_soft(first, second):
    highest = jnp.maximum(first[0], second[0])
    total = first[1] * jnp.exp(first[0] - highest) + second[1] * jnp.exp(second[0] - highest)
    return jnp.stack([highest, total, first[2] + second[2]])


def dot_rows(left_op, right_op):
    return lax.dot_general(
        left_op, right_op, (((1,), (1,)), ((), ())), preferred_element_type=jnp.float32
    )


def dot_cols(left_op, right_op):
    return lax.dot_general(
        left_op, right_op, (((0,), (0,)), ((), ())), preferred_element_type=jnp.float32
    )


def dot_plain(left_op, right_op):
    return jnp.dot(left_op, right_op, preferred_element_type=jnp.float32)


def column_sums(values):
    return jnp.sum(values.astype(jnp.float32), 0)


def layer_norm(values, gain, shift):
    center = values - jnp.mean(values, -1, keepdims=True)
    spread = jnp.mean(center * center, -1, keepdims=True)
    return center * lax.rsqrt(spread + NORM_EPS) * gain + shift


def norm_back(values, gain, shift, grad):
    unused, pull = jax.vjp(layer_norm, values, gain, shift)
    return pull(grad)


def one_hot(wanted, length, axis):
    shape = list(wanted.shape)
    shape.insert(axis, length)
    at = lax.broadcasted_iota(jnp.int32, shape, axis)
    return (at == jnp.expand_dims(wanted, axis)).astype(jnp.bfloat16)


def counts_before(flags):
    length = flags.shape[-1]
    earlier = (
        lax.broadcasted_iota(jnp.int32, (length, length), 0)
        < lax.broadcasted_iota(jnp.int32, (length, length), 1)
    ).astype(jnp.bfloat16)
    return dot_plain(flags.astype(jnp.bfloat16), earlier).astype(jnp.int32)


def seq_orders():
    return [bits_of("seq")]


def share_keys(key_rows, val_rows):
    rows, width = key_rows.shape
    pair = jnp.concatenate([key_rows, val_rows], 0)[None]
    both = exchange(
        pair, "share_keys", 4, join_axes=("seq",), join_orders=[bits_of("seq")[::-1]]
    )
    groups = both.shape[0]
    return (
        both[:, :rows].reshape(groups * rows, HEADS, HEAD),
        both[:, rows:].reshape(groups * rows, HEADS, HEAD),
    )


def return_grads(key_part, val_part):
    groups = lax.axis_size("seq")
    rows = key_part.shape[0] // groups
    width = HEADS * HEAD
    pair = jnp.concatenate(
        [key_part.reshape(groups, rows, width), val_part.reshape(groups, rows, width)], 1
    )
    own = exchange(pair, "return_grads", 8, sum_axes=("seq",), sum_orders=[bits_of("seq")])
    return own[:rows], own[rows:]


def layer_forward(state, weights, params, query_ids, key_ids):
    width = state.shape[1]
    scale = HEAD ** (-0.5)
    hidden = layer_norm(state, params[0], params[1]).astype(jnp.bfloat16)
    joined = dot_rows(hidden, weights[0, : 3 * width])
    queries = (joined[:, :width] + params[2]).astype(jnp.bfloat16)
    key_rows = joined[:, width : 2 * width].astype(jnp.bfloat16)
    val_rows = (joined[:, 2 * width :] + params[3]).astype(jnp.bfloat16)
    key_seq, val_seq = share_keys(key_rows, val_rows)
    query_seq = queries.reshape(-1, HEADS, HEAD)
    scores = (
        jnp.einsum("qhd,khd->hqk", query_seq, key_seq, preferred_element_type=jnp.float32) * scale
    )
    allowed = key_ids[None, None, :] <= query_ids[None, :, None]
    scores = jnp.where(allowed, scores, MASK_FILL)
    raised = jnp.exp(scores - jnp.max(scores, -1, keepdims=True))
    probs = raised / jnp.sum(raised, -1, keepdims=True)
    attended = jnp.einsum(
        "hqk,khd->qhd", probs.astype(jnp.bfloat16), val_seq, preferred_element_type=jnp.float32
    )
    attended = attended.reshape(-1, width).astype(jnp.bfloat16)
    mid_state = state + dot_plain(attended, weights[0, 3 * width :]) + params[4]
    normed = layer_norm(mid_state, params[5], params[6]).astype(jnp.bfloat16)
    upward = dot_rows(normed, weights[1]) + params[8:12].reshape(-1)
    active = jax.nn.gelu(upward, approximate=True).astype(jnp.bfloat16)
    output = mid_state + dot_plain(active, weights[2]) + params[7]
    return (
        output,
        (hidden, query_seq, key_seq, val_seq, probs, attended, mid_state, normed, upward, active),
    )


def rows_major(x):
    return with_layout_constraint(x, Layout(major_to_minor=tuple(range(x.ndim))))


def scatter_rows(grad):
    total = lax.axis_size(AXES)
    blocks = rows_major(grad.astype(jnp.bfloat16)).reshape(total, -1, grad.shape[1])
    return lax.psum_scatter(blocks, AXES, scatter_dimension=0, tiled=True)[0]


def layer_backward(state, weights, params, saved, grad_in):
    width = state.shape[1]
    scale = HEAD ** (-0.5)
    hidden, query_seq, key_seq, val_seq, probs, attended, mid_state, normed, upward, active = saved
    down_grad = grad_in.astype(jnp.bfloat16)
    grad_down = scatter_rows(dot_cols(active, down_grad))
    act_grad = dot_rows(down_grad, weights[2])
    unused_gelu, gelu_pull = jax.vjp(partial(jax.nn.gelu, approximate=True), upward)
    up_grad = gelu_pull(act_grad)[0].astype(jnp.bfloat16)
    grad_up = scatter_rows(dot_cols(up_grad, normed))
    mid_back, gain_two, shift_two = norm_back(
        mid_state, params[5], params[6], dot_plain(up_grad, weights[1])
    )
    mid_grad = grad_in + mid_back
    out_grad = mid_grad.astype(jnp.bfloat16)
    grad_proj = dot_cols(attended, out_grad)
    att_grad = dot_rows(out_grad, weights[0, 3 * width :]).astype(jnp.bfloat16)
    att_seq = att_grad.reshape(query_seq.shape)
    prob_grad = jnp.einsum("qhd,khd->hqk", att_seq, val_seq, preferred_element_type=jnp.float32)
    val_part = jnp.einsum(
        "hqk,qhd->khd", probs.astype(jnp.bfloat16), att_seq, preferred_element_type=jnp.float32
    )
    score_grad = (probs * (prob_grad - jnp.sum(probs * prob_grad, -1, keepdims=True))).astype(
        jnp.bfloat16
    )
    query_grad = (
        jnp.einsum("hqk,khd->qhd", score_grad, key_seq, preferred_element_type=jnp.float32) * scale
    )
    query_grad = query_grad.reshape(-1, width).astype(jnp.bfloat16)
    key_part = (
        jnp.einsum("hqk,qhd->khd", score_grad, query_seq, preferred_element_type=jnp.float32)
        * scale
    )
    key_grad, val_grad = return_grads(key_part, val_part)
    joined_grad = jnp.concatenate([query_grad, key_grad, val_grad], 1)
    grad_joined = dot_cols(joined_grad, hidden)
    state_back, gain_one, shift_one = norm_back(
        state, params[0], params[1], dot_plain(joined_grad, weights[0, : 3 * width])
    )
    small_grad = jnp.concatenate(
        [
            jnp.stack(
                [
                    gain_one,
                    shift_one,
                    column_sums(query_grad),
                    column_sums(val_grad),
                    column_sums(out_grad),
                    gain_two,
                    shift_two,
                    column_sums(down_grad),
                ]
            ),
            column_sums(up_grad).reshape(4, width),
        ],
        0,
    )
    grad_first = scatter_rows(jnp.concatenate([grad_joined, grad_proj], 0))
    mats_grad = jnp.stack([grad_first, grad_up, grad_down]).astype(jnp.float32)
    return (mid_grad + state_back, mats_grad, small_grad)


def adam_step(weights, moment, square, grad, rate, decay, step):
    moment = BETA_ONE * moment + (1 - BETA_ONE) * grad
    square = BETA_TWO * square + (1 - BETA_TWO) * grad * grad
    moment_hat = moment / (1 - BETA_ONE**step)
    square_hat = square / (1 - BETA_TWO**step)
    weights = weights - rate * (moment_hat / (jnp.sqrt(square_hat) + ADAM_EPS) + decay * weights)
    return (weights, moment, square)


def pad_rows(x, rows):
    return jnp.pad(x, ((0, rows - x.shape[0]), (0, 0)))


def on_device(
    tokens,
    block_ids,
    completion,
    regroup,
    targets,
    step_count,
    layer_mats,
    mats_moment,
    mats_square,
    embed_table,
    table_moment,
    table_square,
):
    seqs, tok_count = tokens.shape
    seq_length = block_ids.shape[1]
    width = embed_table.shape[1]
    table_local = embed_table.shape[0]
    layers = layer_mats.shape[0]
    replicas, groups, shards = (lax.axis_size(axis) for axis in AXES)
    total = replicas * groups * shards
    seq_at = lax.axis_index("seq")
    shard_at = lax.axis_index("shard")
    device_at = lax.axis_index(AXES)
    seq_bits, dp_bits, shard_bits = bits_of("seq"), bits_of("dp"), bits_of("shard")
    first_row = device_at * table_local
    table_own = embed_table.astype(jnp.bfloat16)
    mats_low = layer_mats.astype(jnp.bfloat16)
    token_ids = tokens.reshape(-1)
    local_rows = token_ids.shape[0]
    small_count = 12 * layers + 2
    small_rows = -(-small_count // 16) * 16

    ids_all = exchange(
        jnp.pad(token_ids, (0, -local_rows % 1024)).reshape(1, -1, 128),
        "share_ids",
        0,
        join_axes=AXES,
        join_orders=[shard_bits[::-1] + dp_bits[::-1] + seq_bits[::-1]],
    )
    ids_all = ids_all.reshape(total, -1)[:, :local_rows]
    owner_all = ids_all // table_local
    loads = jnp.sum(
        (owner_all[:, :, None] == jnp.arange(total)[None, None, :]).astype(jnp.int32), 1
    )
    rounds = (jnp.max(loads) + SLOTS - 1) // SLOTS
    asked = owner_all == device_at
    asked_rank = counts_before(asked)
    asked_row = ids_all - first_row
    own_owner = token_ids // table_local
    same = own_owner[:, None] == own_owner[None, :]
    before = jnp.arange(local_rows)[None, :] < jnp.arange(local_rows)[:, None]
    own_rank = jnp.sum((same & before).astype(jnp.int32), 1)

    def asked_rows(at):
        chosen = asked[:, None, :] & (
            asked_rank[:, None, :] == at * SLOTS + jnp.arange(SLOTS)[None, :, None]
        )
        return (jnp.sum(jnp.where(chosen, asked_row[:, None, :] + 1, 0), 2) - 1).reshape(-1)

    def own_slots(at):
        slot = own_rank - at * SLOTS
        return jnp.where((slot >= 0) & (slot < SLOTS), own_owner * SLOTS + slot, -1)

    def fetch(at, rows):
        given = swap(rows.astype(jnp.bfloat16).reshape(total, SLOTS, width), "swap_rows", 1)
        return dot_plain(
            one_hot(own_slots(at), total * SLOTS, 1), given.reshape(total * SLOTS, width)
        )

    fixed = jnp.arange(seq_length + small_rows, dtype=jnp.int32)
    fixed_row = jnp.where(fixed < seq_length + small_count, VOCAB + fixed - first_row, -1)
    wanted = jnp.concatenate([asked_rows(0), fixed_row])
    rows_out = dot_plain(one_hot(wanted, table_local, 1), table_own).astype(jnp.bfloat16)
    exchanged = total * SLOTS
    piece = seq_length // total
    place_rows = exchange(
        rows_out[exchanged : exchanged + seq_length].reshape(total, piece, width),
        "share_places",
        2,
        sum_axes=("seq", "dp", "shard"),
        sum_orders=[seq_bits + dp_bits + shard_bits],
        join_axes=("dp", "shard"),
        join_orders=[shard_bits[::-1] + dp_bits[::-1]],
    ).reshape(tok_count, width)
    small = combine_all(
        rows_out[exchanged + seq_length :], add_pair, "share_small", 3
    )[:small_count].astype(jnp.float32)
    place_state = jnp.broadcast_to(place_rows.astype(jnp.float32), (seqs, tok_count, width))
    state = fetch(0, rows_out[:exchanged]) + place_state.reshape(local_rows, width)
    state = lax.fori_loop(
        1,
        rounds,
        lambda at, held: held
        + fetch(at, dot_plain(one_hot(asked_rows(at), table_local, 1), table_own)),
        state,
    )

    query_ids = lax.dynamic_slice_in_dim(block_ids[0], seq_at * tok_count, tok_count, 0)
    inputs, kept, saved = [], [], []
    for layer_at in range(layers):
        weights = lax.all_gather(mats_low[layer_at], AXES, axis=1, tiled=True)
        inputs.append(state)
        kept.append(weights)
        state, held = layer_forward(
            state,
            weights,
            small[12 * layer_at : 12 * layer_at + 12],
            query_ids,
            block_ids[0],
        )
        saved.append(held)
    final_gain = small[12 * layers]
    final_shift = small[12 * layers + 1]
    final = layer_norm(state, final_gain, final_shift).astype(jnp.bfloat16)

    group_mask = completion[0]
    slot_of = regroup[0]
    slots = slot_of.shape[0]
    comp_rows = slots // shards
    rank_all = counts_before(group_mask[None])[0]
    mine = lax.dynamic_slice_in_dim(group_mask, shard_at * local_rows, local_rows)
    my_rank = lax.dynamic_slice_in_dim(rank_all, shard_at * local_rows, local_rows)
    my_slot = jnp.sum(
        jnp.where(my_rank[:, None] == jnp.arange(slots)[None, :], slot_of[None, :], 0), 1
    )
    to_slot = one_hot(jnp.where(mine == 1, my_slot, -1), slots, 0)
    outgoing = dot_plain(to_slot, final).astype(jnp.bfloat16).reshape(shards, comp_rows, width)
    two_ways = [seq_bits[1:] + dp_bits, dp_bits + seq_bits[1:]]
    head_in = exchange(
        outgoing,
        "share_final",
        5,
        sum_axes=("shard",),
        sum_orders=[shard_bits, shard_bits],
        join_axes=AXES,
        join_orders=[shard_bits[::-1] + way[::-1] + seq_bits[:1] for way in two_ways],
    ).reshape(-1, width)

    rows_all = targets.shape[0]
    columns = first_row + jnp.arange(table_local, dtype=jnp.int32)
    live = (columns < VOCAB)[None, :]
    logits = dot_rows(head_in, table_own)
    masked = jnp.where(live, logits, MASK_FILL)
    top_local = jnp.max(masked, 1)
    total_local = jnp.sum(jnp.where(live, jnp.exp(masked - top_local[:, None]), 0.0), 1)
    target_hit = columns[None, :] == targets[:, None]
    pick_local = jnp.sum(jnp.where(target_hit, logits, 0.0), 1)
    stats = combine_all(
        jnp.stack([top_local, total_local, pick_local]).reshape(3, -1, 128),
        merge_soft,
        "share_stats",
        6,
    ).reshape(3, rows_all)
    log_total = stats[0] + jnp.log(stats[1])
    loss_value = jnp.sum(log_total - stats[2]) / rows_all
    probs = jnp.where(live, jnp.exp(masked - log_total[:, None]), 0.0)
    logit_grad = ((probs - target_hit.astype(jnp.float32)) / rows_all).astype(jnp.bfloat16)
    head_grad = dot_cols(logit_grad, head_in)
    returned = exchange(
        dot_plain(logit_grad, table_own).reshape(total, comp_rows, width),
        "return_final",
        7,
        sum_axes=AXES,
        sum_orders=[seq_bits[:1] + way + shard_bits for way in two_ways],
        join_axes=("shard",),
        join_orders=[shard_bits[::-1], shard_bits[::-1]],
    ).reshape(slots, width)
    final_grad = dot_cols(to_slot, returned)
    state_grad, gain_final, shift_final = norm_back(state, final_gain, final_shift, final_grad)

    mats_grads = [None] * layers
    small_grads = [None] * layers
    for layer_at in reversed(range(layers)):
        state_grad, mats_grads[layer_at], small_grads[layer_at] = layer_backward(
            inputs[layer_at],
            kept[layer_at],
            small[12 * layer_at : 12 * layer_at + 12],
            saved[layer_at],
            state_grad,
        )

    low_grad = state_grad.astype(jnp.bfloat16)
    place_grad = jnp.sum(state_grad.reshape(seqs, tok_count, width), 0)
    place_grad = exchange(
        place_grad.reshape(replicas * shards, piece, width),
        "return_places",
        10,
        sum_axes=("dp", "shard"),
        sum_orders=[dp_bits + shard_bits],
        join_axes=("seq", "dp", "shard"),
        join_orders=[shard_bits[::-1] + dp_bits[::-1] + seq_bits[::-1]],
    ).reshape(seq_length, width)
    small_grad = combine_all(
        pad_rows(
            jnp.concatenate(small_grads + [jnp.stack([gain_final, shift_final])], 0), small_rows
        ),
        add_pair,
        "return_small",
        9,
    )
    small_high = small_grad.astype(jnp.bfloat16)
    small_low = (small_grad - small_high.astype(jnp.float32)).astype(jnp.bfloat16)

    def send_back(at):
        rows = dot_cols(one_hot(own_slots(at), total * SLOTS, 1), low_grad).astype(jnp.bfloat16)
        return swap(rows.reshape(total, SLOTS, width), "swap_rows", 1).reshape(-1, width)

    values = jnp.concatenate([send_back(0), place_grad, small_high, small_low], 0)
    value_row = jnp.concatenate([wanted, fixed_row[seq_length:]])
    table_grad = dot_plain(one_hot(value_row, table_local, 0), values) + head_grad
    table_grad = lax.fori_loop(
        1,
        rounds,
        lambda at, held: held + dot_plain(one_hot(asked_rows(at), table_local, 0), send_back(at)),
        table_grad,
    )
    mats_grad = jnp.stack(mats_grads)
    local_squares = jnp.sum(mats_grad * mats_grad) + jnp.sum(table_grad * table_grad)
    squares = combine_all(jnp.full((8, 128), local_squares), add_pair, "share_norm", 11)
    grad_norm = jnp.sqrt(squares[0, 0])
    factor = CLIP_NORM / grad_norm
    step = step_count[0].astype(jnp.float32)
    new_mats = adam_step(
        layer_mats, mats_moment, mats_square, factor * mats_grad, RATE_MATS, DECAY_RATE, step
    )
    plain_rows = (columns < VOCAB + seq_length)[:, None]
    rate = jnp.where(plain_rows, RATE_TABLE, RATE_SMALL)
    decay = jnp.where(plain_rows, DECAY_RATE, 0.0)
    new_table = adam_step(
        embed_table, table_moment, table_square, factor * table_grad, rate, decay, step
    )
    return (
        loss_value.reshape(1),
        grad_norm.reshape(1),
        new_mats[0],
        new_mats[1],
        new_mats[2],
        new_table[0],
        new_table[1],
        new_table[2],
    )


def solution(mesh):
    in_specs = (
        P(("dp", "shard"), "seq"),
        P(("dp", "shard"), None),
        P(("dp", "seq"), None),
        P(("dp", "seq"), None),
        P(),
        P(),
        P(None, None, ("dp", "seq", "shard"), None),
        P(None, None, ("dp", "seq", "shard"), None),
        P(None, None, ("dp", "seq", "shard"), None),
        P(("dp", "seq", "shard"), None),
        P(("dp", "seq", "shard"), None),
        P(("dp", "seq", "shard"), None),
    )
    out_specs = (
        P(),
        P(),
        P(None, None, ("dp", "seq", "shard"), None),
        P(None, None, ("dp", "seq", "shard"), None),
        P(None, None, ("dp", "seq", "shard"), None),
        P(("dp", "seq", "shard"), None),
        P(("dp", "seq", "shard"), None),
        P(("dp", "seq", "shard"), None),
    )
    return jax.shard_map(
        on_device, mesh=mesh, in_specs=in_specs, out_specs=out_specs, check_vma=False
    )
```

```python
import itertools
from functools import partial

import jax
import jax.numpy as jnp
from jax import lax
from jax.experimental import pallas as pl
from jax.experimental.layout import Layout, with_layout_constraint
from jax.experimental.pallas import tpu as pltpu
from jax.sharding import PartitionSpec as P

HEADS = 17
HEAD = 64
VOCAB = 50278

NORM_EPS = 1e-05
CLIP_NORM = 0.02
BETA_ONE = 0.9
BETA_TWO = 0.95
ADAM_EPS = 1e-08
DECAY_RATE = 0.1
RATE_MATS = 0.05
RATE_TABLE = 0.1
RATE_SMALL = 0.5
MASK_FILL = -1e30

AXES = ("dp", "seq", "shard")
MESH = pl.DeviceIdType.MESH
SLOTS = 24


def bits_of(axis):
    return [(axis, b) for b in range(lax.axis_size(axis).bit_length() - 1)]


def bit_here(bit):
    return lax.rem(lax.axis_index(bit[0]) // 2 ** bit[1], 2)


def partner(bit):
    at = lax.axis_index(bit[0])
    return {bit[0]: at + (1 - 2 * bit_here(bit)) * 2 ** bit[1]}


def greet(bits):
    barrier = pltpu.get_barrier_semaphore()
    for bit in bits:
        pl.semaphore_signal(barrier, inc=1, device_id=partner(bit), device_id_type=MESH)
    pl.semaphore_wait(barrier, len(bits))


def block_weight(axes, bit):
    weight = 2 ** bit[1]
    for axis in axes[axes.index(bit[0]) + 1 :]:
        weight *= lax.axis_size(axis)
    return weight


def block_runs(weights):
    weights = sorted(weights)
    joined = 0
    while joined < len(weights) and weights[joined] == 2**joined:
        joined += 1
    rest = [(0, w) for w in weights[joined:]]
    return 2**joined, [sum(c) for c in itertools.product(*rest)]


class Job:
    def __init__(
        self, inputs, outputs, scratch, sends, keeps, bits, steps, spaces=(pltpu.VMEM, pltpu.VMEM)
    ):
        self.inputs, self.outputs, self.scratch = inputs, outputs, scratch
        self.sends, self.keeps, self.bits, self.steps, self.spaces = sends, keeps, bits, steps, spaces


def me_and_total():
    seq_size, shard_size = lax.axis_size("seq"), lax.axis_size("shard")
    at = (lax.axis_index("dp") * seq_size + lax.axis_index("seq")) * shard_size
    return at + lax.axis_index("shard"), lax.axis_size("dp") * seq_size * shard_size


def place_of(at):
    seq_size, shard_size = lax.axis_size("seq"), lax.axis_size("shard")
    return {
        "dp": at // (seq_size * shard_size),
        "seq": lax.rem(at // shard_size, seq_size),
        "shard": lax.rem(at, shard_size),
    }


def greet_all():
    me, total = me_and_total()
    barrier = pltpu.get_barrier_semaphore()

    def hello(k, carry):
        pl.semaphore_signal(
            barrier, inc=1, device_id=place_of(lax.rem(me + k, total)), device_id_type=MESH
        )
        return carry

    lax.fori_loop(1, total, hello, 0)
    pl.semaphore_wait(barrier, total - 1)


class Sems:
    def __init__(self, send, recv, keep):
        self.send, self.recv, self.keep = send, recv, keep
        self.used = self.kept = 0

    def copy(self, source, target, device):
        k = self.used
        self.used += 1
        copy = pltpu.make_async_remote_copy(
            source, target, self.send.at[k], self.recv.at[k], device_id=device, device_id_type=MESH
        )
        copy.start()
        return copy

    def local(self, source, target):
        k = self.kept
        self.kept += 1
        copy = pltpu.make_async_copy(source, target, self.keep.at[k])
        copy.start()
        return copy

    def span(self, count):
        first = self.used
        self.used += count
        return first


def jobs_kernel(jobs, *refs):
    refs = list(refs)

    def take(count):
        out = refs[:count]
        del refs[:count]
        return out

    held = [take(len(job.inputs)) for job in jobs]
    made = [take(len(job.outputs)) for job in jobs]
    used = [take(len(job.scratch)) for job in jobs]
    sems = Sems(*refs)
    if any(job.bits is None for job in jobs):
        greet_all()
    else:
        greet(sorted(set(bit for job in jobs for bit in job.bits)))
    active = []
    for job, x, o, w in zip(jobs, held, made, used):
        active += job.steps(x, o, w, sems)
    tick = 0
    while active:
        left = []
        for delay, gen in active:
            if delay > tick or next(gen, "end") != "end":
                left.append((delay, gen))
        active = left
        tick += 1


def run_jobs(jobs, name, number, vmem=60):
    inputs = [x for job in jobs for x in job.inputs]
    outputs = [o for job in jobs for o in job.outputs]
    in_specs = [pl.BlockSpec(memory_space=job.spaces[0]) for job in jobs for unused in job.inputs]
    out_specs = [pl.BlockSpec(memory_space=job.spaces[1]) for job in jobs for unused in job.outputs]
    sends = sum(job.sends for job in jobs)
    keeps = max(1, sum(job.keeps for job in jobs))
    flat = pl.pallas_call(
        partial(jobs_kernel, jobs),
        out_shape=outputs,
        in_specs=in_specs,
        out_specs=out_specs,
        scratch_shapes=[w for job in jobs for w in job.scratch]
        + [
            pltpu.SemaphoreType.DMA((sends,)),
            pltpu.SemaphoreType.DMA((sends,)),
            pltpu.SemaphoreType.DMA((keeps,)),
        ],
        compiler_params=pltpu.CompilerParams(
            collective_id=number, has_side_effects=True, vmem_limit_bytes=vmem * 2**20
        ),
        name=name,
    )(*inputs)
    out = []
    for job in jobs:
        out.append(flat[: len(job.outputs)])
        flat = flat[len(job.outputs) :]
    return out


def sum_stream(x_ref, o_ref, scratch, sems, rows, first_slot, sum_axes, sums, join_axes, joins):
    source = x_ref
    slot = first_slot
    if sums:
        work, parcel, recv = scratch
    for step, bit in enumerate(sums):
        base = sum(bit_here(b) * block_weight(sum_axes, b) for b in sums[:step])
        weight = block_weight(sum_axes, bit)
        mine = bit_here(bit)
        size, offsets = block_runs([block_weight(sum_axes, b) for b in sums[step + 1 :]])
        started = []
        for offset in offsets:
            leave = base + (1 - mine) * weight + offset
            if source.dtype == parcel.dtype:
                packed = source.at[pl.ds(leave, size), rows]
            else:

                def pack(i, carry, leave=leave, at=slot, source=source):
                    parcel[at + i, rows] = source[leave + i, rows].astype(parcel.dtype)
                    return carry

                lax.fori_loop(0, size, pack, 0)
                packed = parcel.at[pl.ds(slot, size), rows]
            copy = sems.copy(packed, recv.at[pl.ds(slot, size), rows], partner(bit))
            started.append((copy, base + mine * weight + offset, slot, size))
            slot += size
        yield
        for copy, keep, at, size in started:
            copy.wait()

            def add(i, carry, keep=keep, at=at, source=source):
                total = source[keep + i, rows].astype(jnp.float32)
                total = total + recv[at + i, rows].astype(jnp.float32)
                work[keep + i, rows] = total.astype(work.dtype)
                return carry

            lax.fori_loop(0, size, add, 0)
        source = work
    own = sum(bit_here(b) * block_weight(sum_axes, b) for b in sums) if sums else 0
    result = source[own, rows].astype(o_ref.dtype)
    if not joins:
        o_ref[rows] = result
        return
    o_ref[sum(bit_here(b) * block_weight(join_axes, b) for b in joins), rows] = result
    for step, bit in enumerate(joins):
        base = sum(bit_here(b) * block_weight(join_axes, b) for b in joins[step:])
        size, offsets = block_runs([block_weight(join_axes, b) for b in joins[:step]])
        started = []
        for offset in offsets:
            here = o_ref.at[pl.ds(base + offset, size), rows]
            started.append(sems.copy(here, here, partner(bit)))
        yield
        for copy in started:
            copy.wait()


def sum_job(x, sum_axes=(), sum_orders=(), join_axes=(), join_orders=(), chunks=1):
    rows, width = x.shape[-2:]
    blocks = 1
    for axis in join_axes:
        blocks *= lax.axis_size(axis)
    kind = jnp.bfloat16 if sum_axes else x.dtype
    streams = max(len(sum_orders), len(join_orders))
    if rows % (streams * chunks * 16):
        chunks = 1
    share = rows // (streams * chunks)
    sends = 0
    for order in sum_orders:
        for step in range(len(order)):
            sends += len(block_runs([block_weight(sum_axes, b) for b in order[step + 1 :]])[1])
    for order in join_orders:
        for step in range(len(order)):
            sends += len(block_runs([block_weight(join_axes, b) for b in order[:step]])[1])
    scratch = []
    if sum_axes:
        if x.size * 14 > 56 * 2**20:
            x = x.astype(jnp.bfloat16)
        exact = x.dtype == jnp.float32 or x.size < 2**22
        scratch = [
            pltpu.VMEM(x.shape, jnp.float32 if exact else kind),
            pltpu.VMEM(x.shape, kind),
            pltpu.VMEM(x.shape, kind),
        ]

    def steps(x_refs, o_refs, scratch_refs, sems):
        gens = []
        for c in range(chunks):
            for k in range(streams):
                rows_here = pl.ds((k * chunks + c) * share, share)
                sums = sum_orders[k] if sum_orders else []
                joins = join_orders[k] if join_orders else []
                gens.append(
                    (
                        c,
                        sum_stream(
                            x_refs[0], o_refs[0], scratch_refs, sems, rows_here, 0,
                            sum_axes, sums, join_axes, joins,
                        ),
                    )
                )
        return gens

    bits = set(bit for order in list(sum_orders) + list(join_orders) for bit in order)
    shape = (blocks, rows, width) if join_axes else (rows, width)
    return Job(
        [x], [jax.ShapeDtypeStruct(shape, kind)], scratch, sends * chunks, 0, bits, steps
    )


def exchange(x, name, number, **how):
    return run_jobs([sum_job(x, **how)], name, number)[0][0]


def combine_job(x, combine):
    bits = [bit for axis in reversed(AXES) for bit in bits_of(axis)]
    slots = (len(bits),) + x.shape

    def steps(x_refs, o_refs, scratch, sems):
        out_buf, in_buf = scratch

        def gen():
            current = x_refs[0][...]
            for i, bit in enumerate(bits):
                out_buf[i] = current
                copy = sems.copy(out_buf.at[i], in_buf.at[i], partner(bit))
                yield
                copy.wait()
                current, other = out_buf[i], in_buf[i]
                low = bit_here(bit) == 0
                current = combine(jnp.where(low, current, other), jnp.where(low, other, current))
            o_refs[0][...] = current

        return [(0, gen())]

    return Job(
        [x],
        [jax.ShapeDtypeStruct(x.shape, x.dtype)],
        [pltpu.VMEM(slots, x.dtype), pltpu.VMEM(slots, x.dtype)],
        len(bits),
        0,
        bits,
        steps,
    )


def combine_all(x, combine, name, number):
    return run_jobs([combine_job(x, combine)], name, number, 16)[0][0]


def swap_job(x, late=0):
    total = x.shape[0]

    def steps(x_refs, o_refs, scratch, sems):
        x_ref, o_ref = x_refs[0], o_refs[0]

        def gen():
            me, unused = me_and_total()
            first = sems.span(total)
            keep = sems.local(x_ref.at[me], o_ref.at[me])

            def copy_to(other, here):
                return pltpu.make_async_remote_copy(
                    x_ref.at[other],
                    o_ref.at[here],
                    sems.send.at[first + other],
                    sems.recv.at[first + here],
                    device_id=place_of(other),
                    device_id_type=MESH,
                )

            def send(k, carry):
                copy_to(lax.rem(me + k, total), me).start()
                return carry

            lax.fori_loop(1, total, send, 0)
            for unused in range(late + 1):
                yield

            def finish(k, carry):
                other = lax.rem(me + k, total)
                copy_to(other, other).wait()
                return carry

            lax.fori_loop(1, total, finish, 0)
            keep.wait()

        return [(0, gen())]

    return Job(
        [x],
        [jax.ShapeDtypeStruct(x.shape, x.dtype)],
        [],
        total,
        1,
        None,
        steps,
        spaces=(pl.ANY, pl.ANY),
    )


def swap(x, name, number):
    return run_jobs([swap_job(x)], name, number, 16)[0][0]


def sum_orders_for(rows):
    across, along, deep = bits_of("seq")[1:], bits_of("dp"), bits_of("shard")
    if rows < 64 or rows % 8:
        return [(0, rows)], [across + along + deep]
    one = rows * 6 // 17 // 16 * 16
    spans = [(0, one), (one, one), (2 * one, rows - 2 * one)]
    return spans, [across + along + deep, along + across + deep, deep + across + along]


def mats_stream(x_ref, o_ref, scratch, sems, m, span, order, weights):
    kept, work, parcel, recv = scratch
    steps = len(order)
    rows = pl.ds(*span)
    slot = 0
    rest = sorted((b for b in weights if b != order[0]), key=lambda b: weights[b])
    small = {b: 2**k for k, b in enumerate(rest)}
    for step, bit in enumerate(order):
        mine = bit_here(bit)
        base = sum(bit_here(b) * small[b] for b in order[1:step])
        runs, keeps = [], []
        if step == 0:
            size, offsets = block_runs([weights[b] for b in order[1:]])
            for offset in offsets:
                left, place = offset, 0
                for b in reversed(rest):
                    if left >= weights[b]:
                        left -= weights[b]
                        place += small[b]
                keeps.append(
                    sems.local(
                        x_ref.at[pl.ds(mine * weights[bit] + offset, size), rows],
                        kept.at[m % 2, pl.ds(place, size), rows],
                    )
                )
                runs.append(((1 - mine) * weights[bit] + offset, place))
        else:
            size, offsets = block_runs([small[b] for b in order[step + 1 :]])
            for offset in offsets:
                here = base + offset
                runs.append((here + (1 - mine) * small[bit], here + mine * small[bit]))
        started = []
        for leave, keep_at in runs:
            at = slot
            slot += size
            if step == 0:
                packed = x_ref.at[pl.ds(leave, size), rows]
            else:
                spot = at - 2 ** (steps - 1)

                def pack(i, carry, leave=leave, spot=spot):
                    parcel[m, spot + i, rows] = work[m, leave + i, rows].astype(parcel.dtype)
                    return carry

                lax.fori_loop(0, size, pack, 0)
                packed = parcel.at[m, pl.ds(spot, size), rows]
            copy = sems.copy(packed, recv.at[m, pl.ds(at, size), rows], partner(bit))
            started.append((copy, at, keep_at, size))
        yield
        for keep in keeps:
            keep.wait()
        for copy, at, keep_at, size in started:
            copy.wait()

            def add(i, carry, at=at, keep_at=keep_at, step=step):
                if step == 0:
                    total = kept[m % 2, keep_at + i, rows].astype(jnp.float32)
                else:
                    total = work[m, keep_at + i, rows]
                work[m, keep_at + i, rows] = total + recv[m, at + i, rows].astype(jnp.float32)
                return carry

            lax.fori_loop(0, size, add, 0)
    o_ref[rows] = work[m, sum(bit_here(b) * small[b] for b in order[1:]), rows]


def mats_job(mats):
    blocks, rows, width = mats[0].shape
    spans, orders = sum_orders_for(rows)
    weights = {}
    for bit in orders[0]:
        weight = block_weight(AXES, bit)
        weights[bit] = weight if bit[0] == "shard" else weight // 2
    keeps = sends = 0
    for order in orders:
        keeps += len(block_runs([weights[b] for b in order[1:]])[1])
        sends += len(block_runs([weights[b] for b in order[1:]])[1])
        rest = sorted((b for b in weights if b != order[0]), key=lambda b: weights[b])
        small = {b: 2**k for k, b in enumerate(rest)}
        for step in range(1, len(order)):
            sends += len(block_runs([small[b] for b in order[step + 1 :]])[1])
    count = len(mats)

    def steps(x_refs, o_refs, scratch, sems):
        return [
            (m, mats_stream(x_refs[m], o_refs[m], scratch, sems, m, spans[k], orders[k], weights))
            for m in range(count)
            for k in range(len(orders))
        ]

    return Job(
        mats,
        [jax.ShapeDtypeStruct((rows, width), jnp.float32)] * count,
        [
            pltpu.VMEM((min(2, count), blocks // 2, rows, width), jnp.bfloat16),
            pltpu.VMEM((count, blocks // 2, rows, width), jnp.float32),
            pltpu.VMEM((count, blocks // 2 - 1, rows, width), jnp.bfloat16),
            pltpu.VMEM((count, blocks - 1, rows, width), jnp.bfloat16),
        ],
        count * sends,
        count * keeps,
        set(orders[0]),
        steps,
        spaces=(pl.ANY, pltpu.VMEM),
    )


def trade_kernel(count, *refs):
    x_refs, o_refs = refs[:count], refs[count : 2 * count]
    send_sems, recv_sems = refs[2 * count :]
    bit = ("seq", 0)
    greet([bit])
    copies = []
    for k in range(count):
        copy = pltpu.make_async_remote_copy(
            x_refs[k],
            o_refs[k],
            send_sems.at[k],
            recv_sems.at[k],
            device_id=partner(bit),
            device_id_type=MESH,
        )
        copy.start()
        copies.append(copy)
    for copy in copies:
        copy.wait()


def trade(arrays, name, number):
    count = len(arrays)
    return pl.pallas_call(
        partial(trade_kernel, count),
        out_shape=[jax.ShapeDtypeStruct(x.shape, x.dtype) for x in arrays],
        in_specs=[pl.BlockSpec(memory_space=pl.ANY)] * count,
        out_specs=[pl.BlockSpec(memory_space=pl.ANY)] * count,
        scratch_shapes=[pltpu.SemaphoreType.DMA((count,)), pltpu.SemaphoreType.DMA((count,))],
        compiler_params=pltpu.CompilerParams(collective_id=number, has_side_effects=True),
        name=name,
    )(*arrays)


def my_rows(features, own):
    rows = features.shape[0]
    parts = features.reshape(rows, -1, 2, own)
    at = lax.rem(lax.axis_index("seq"), 2)
    mine = lax.dynamic_index_in_dim(parts, at, 2, keepdims=False)
    other = lax.dynamic_index_in_dim(parts, 1 - at, 2, keepdims=False)
    return mine.reshape(rows, -1), other.reshape(rows, -1)


def late_mats(first, up, down, number):
    joined_grad, hidden, attended, out_grad = first
    own = up[0].shape[1] // lax.axis_size(AXES) * lax.axis_size("shard")
    halves = [my_rows(x, own) for x in (joined_grad, attended, up[0], down[0])]
    tails = [hidden, out_grad, up[1], down[1]]
    got = trade([other for unused, other in halves] + tails, "trade_rows", number)
    parts = []
    for k, (mine, unused) in enumerate(halves):
        grad = dot_cols(
            jnp.concatenate([mine, got[k]], 0),
            jnp.concatenate([tails[k], got[len(halves) + k]], 0),
        )
        parts.append(rows_major(grad.astype(jnp.bfloat16)))
    mats = [jnp.concatenate(parts[:2], 0), parts[2], parts[3]]
    blocks = lax.axis_size(AXES) // 2
    return [grad.reshape(blocks, -1, grad.shape[1]) for grad in mats]


def mats_fit(mats):
    blocks, rows, width = mats[0].shape
    tile = -(-rows // 16) * 16 * -(-width // 128) * 128
    return min(len(mats), max(1, (50 * 2**20 - tile * blocks * 2) // (tile * blocks * 5)))


def head_lanes(half, shape):
    lane = lax.broadcasted_iota(jnp.int32, shape, 1)
    return (lane < HEAD) if half == 0 else (lane >= HEAD)


def attend_kernel(q_ref, kv_ref, key_ids_ref, query_ids_ref, o_ref, lse_ref, blocked):
    groups, twice, unused = kv_ref.shape
    rows = twice // 2
    keys = groups * rows
    blocked[...] = jnp.where(key_ids_ref[...] <= query_ids_ref[...], 0.0, MASK_FILL)

    def pair(p, carry):
        lanes = pl.ds(pl.multiple_of(p * 2 * HEAD, 2 * HEAD), 2 * HEAD)
        key_pair = kv_ref[:, :rows, lanes].reshape(keys, 2 * HEAD)
        val_turned = kv_ref[:, rows:, lanes].reshape(keys, 2 * HEAD).T
        query_pair = q_ref[:, lanes]
        outs = []
        for half in range(2):
            query = jnp.where(head_lanes(half, query_pair.shape), query_pair, 0)
            scores = dot_rows(key_pair, query.astype(jnp.bfloat16)) * HEAD ** (-0.5) + blocked[...]
            top = jnp.max(scores, 0, keepdims=True)
            raised = jnp.exp(scores - top)
            total = jnp.sum(raised, 0, keepdims=True)
            probs = (raised * (1.0 / total)).astype(jnp.bfloat16)
            outs.append(dot_plain(val_turned[half * HEAD : (half + 1) * HEAD], probs))
            lse_ref[p, half] = (top + jnp.log(total))[0]
        o_ref[:, lanes] = jnp.concatenate(outs, 0).T.astype(o_ref.dtype)
        return carry

    lax.fori_loop(0, q_ref.shape[1] // (2 * HEAD), pair, 0)


def attend(queries, key_vals, key_ids, query_ids):
    rows, width = queries.shape
    keys = key_ids.shape[0]
    pairs = width // (2 * HEAD)
    return pl.pallas_call(
        attend_kernel,
        out_shape=(
            jax.ShapeDtypeStruct((rows, width), jnp.bfloat16),
            jax.ShapeDtypeStruct((pairs, 2, rows), jnp.float32),
        ),
        in_specs=[pl.BlockSpec(memory_space=pltpu.VMEM)] * 4,
        out_specs=(pl.BlockSpec(memory_space=pltpu.VMEM),) * 2,
        scratch_shapes=[pltpu.VMEM((keys, rows), jnp.float32)],
        compiler_params=pltpu.CompilerParams(vmem_limit_bytes=48 * 2**20),
        cost_estimate=pl.CostEstimate(
            flops=4 * rows * keys * width,
            transcendentals=rows * keys * HEADS,
            bytes_accessed=4 * keys * width,
        ),
        name="attend",
    )(queries, key_vals, key_ids[:, None], query_ids[None, :])


def attend_back_kernel(
    q_ref, kv_ref, grad_ref, lse_ref, key_ids_ref, query_ids_ref, dq_ref, dkv_ref, blocked
):
    groups, twice, unused = kv_ref.shape
    rows = twice // 2
    keys = groups * rows
    scale = HEAD ** (-0.5)
    blocked[...] = jnp.where(key_ids_ref[...] <= query_ids_ref[...], 0.0, MASK_FILL)

    def pair(p, carry):
        lanes = pl.ds(pl.multiple_of(p * 2 * HEAD, 2 * HEAD), 2 * HEAD)
        key_pair = kv_ref[:, :rows, lanes].reshape(keys, 2 * HEAD)
        val_pair = kv_ref[:, rows:, lanes].reshape(keys, 2 * HEAD)
        key_turned = key_pair.T
        query_pair = q_ref[:, lanes]
        grad_pair = grad_ref[:, lanes]
        key_grad = jnp.zeros((keys, 2 * HEAD), jnp.float32)
        val_grad = jnp.zeros((keys, 2 * HEAD), jnp.float32)
        outs = []
        for half in range(2):
            here = head_lanes(half, query_pair.shape)
            query = jnp.where(here, query_pair, 0).astype(jnp.bfloat16)
            grad = jnp.where(here, grad_pair, 0).astype(jnp.bfloat16)
            scores = dot_rows(key_pair, query) * scale + blocked[...]
            probs = jnp.exp(scores - lse_ref[p, half][None, :])
            prob_grad = dot_rows(val_pair, grad)
            inner = jnp.sum(probs * prob_grad, 0, keepdims=True)
            score_grad = (probs * (prob_grad - inner)).astype(jnp.bfloat16)
            key_grad = key_grad + dot_plain(score_grad, query)
            val_grad = val_grad + dot_plain(probs.astype(jnp.bfloat16), grad)
            outs.append(dot_plain(key_turned[half * HEAD : (half + 1) * HEAD], score_grad))
        dq_ref[:, lanes] = (jnp.concatenate(outs, 0).T * scale).astype(dq_ref.dtype)
        dkv_ref[:, :rows, lanes] = (key_grad * scale).reshape(groups, rows, 2 * HEAD)
        dkv_ref[:, rows:, lanes] = val_grad.reshape(groups, rows, 2 * HEAD)
        return carry

    lax.fori_loop(0, q_ref.shape[1] // (2 * HEAD), pair, 0)


def attend_back(queries, key_vals, grad, lse, key_ids, query_ids):
    rows, width = queries.shape
    keys = key_ids.shape[0]
    return pl.pallas_call(
        attend_back_kernel,
        out_shape=(
            jax.ShapeDtypeStruct((rows, width), jnp.bfloat16),
            jax.ShapeDtypeStruct(key_vals.shape, jnp.float32),
        ),
        in_specs=[pl.BlockSpec(memory_space=pltpu.VMEM)] * 6,
        out_specs=(pl.BlockSpec(memory_space=pltpu.VMEM),) * 2,
        scratch_shapes=[pltpu.VMEM((keys, rows), jnp.float32)],
        compiler_params=pltpu.CompilerParams(vmem_limit_bytes=56 * 2**20),
        cost_estimate=pl.CostEstimate(
            flops=10 * rows * keys * width,
            transcendentals=rows * keys * HEADS,
            bytes_accessed=12 * keys * width,
        ),
        name="attend_back",
    )(queries, key_vals, grad, lse, key_ids[:, None], query_ids[None, :])


def add_pair(first, second):
    return first + second


def merge_soft(first, second):
    highest = jnp.maximum(first[0], second[0])
    total = first[1] * jnp.exp(first[0] - highest) + second[1] * jnp.exp(second[0] - highest)
    return jnp.stack([highest, total, first[2] + second[2]])


def dot_rows(left_op, right_op):
    return lax.dot_general(
        left_op, right_op, (((1,), (1,)), ((), ())), preferred_element_type=jnp.float32
    )


def dot_cols(left_op, right_op):
    return lax.dot_general(
        left_op, right_op, (((0,), (0,)), ((), ())), preferred_element_type=jnp.float32
    )


def dot_plain(left_op, right_op):
    return jnp.dot(left_op, right_op, preferred_element_type=jnp.float32)


def column_sums(values):
    return jnp.sum(values.astype(jnp.float32), 0)


def layer_norm(values, gain, shift):
    center = values - jnp.mean(values, -1, keepdims=True)
    spread = jnp.mean(center * center, -1, keepdims=True)
    return center * lax.rsqrt(spread + NORM_EPS) * gain + shift


def norm_back(values, gain, shift, grad):
    unused, pull = jax.vjp(layer_norm, values, gain, shift)
    return pull(grad)


def one_hot(wanted, length, axis):
    shape = list(wanted.shape)
    shape.insert(axis, length)
    at = lax.broadcasted_iota(jnp.int32, shape, axis)
    return (at == jnp.expand_dims(wanted, axis)).astype(jnp.bfloat16)


def counts_before(flags):
    length = flags.shape[-1]
    earlier = (
        lax.broadcasted_iota(jnp.int32, (length, length), 0)
        < lax.broadcasted_iota(jnp.int32, (length, length), 1)
    ).astype(jnp.bfloat16)
    return dot_plain(flags.astype(jnp.bfloat16), earlier).astype(jnp.int32)


def wide(rows_in):
    return jnp.pad(rows_in, ((0, 0), (0, -rows_in.shape[1] % (2 * HEAD))))


def share_keys(key_rows, val_rows):
    pair = jnp.concatenate([wide(key_rows), wide(val_rows)], 0)[None]
    return exchange(
        pair, "share_keys", 4, join_axes=("seq",), join_orders=[bits_of("seq")[::-1]]
    )


def rows_major(x):
    return with_layout_constraint(x, Layout(major_to_minor=tuple(range(x.ndim))))


def scatter_rows(features, cotangents):
    total = lax.axis_size(AXES)
    grad = dot_cols(features, cotangents)
    blocks = rows_major(grad.astype(jnp.bfloat16)).reshape(total, -1, grad.shape[1])
    return lax.psum_scatter(blocks, AXES, scatter_dimension=0, tiled=True)[0]


def layer_forward(state, weights, params, query_ids, key_ids):
    width = state.shape[1]
    hidden = layer_norm(state, params[0], params[1]).astype(jnp.bfloat16)
    joined = dot_rows(hidden, weights[0][: 3 * width])
    queries = wide((joined[:, :width] + params[2]).astype(jnp.bfloat16))
    key_rows = joined[:, width : 2 * width].astype(jnp.bfloat16)
    val_rows = (joined[:, 2 * width :] + params[3]).astype(jnp.bfloat16)
    key_vals = share_keys(key_rows, val_rows)
    attended, lse = attend(queries, key_vals, key_ids, query_ids)
    attended = attended[:, :width]
    mid_state = state + dot_plain(attended, weights[0][3 * width :]) + params[4]
    normed = layer_norm(mid_state, params[5], params[6]).astype(jnp.bfloat16)
    upward = dot_rows(normed, weights[1]) + params[8:12].reshape(-1)
    active = jax.nn.gelu(upward, approximate=True).astype(jnp.bfloat16)
    output = mid_state + dot_plain(active, weights[2]) + params[7]
    return (
        output,
        (hidden, queries, key_vals, lse, attended, mid_state, normed, upward, active),
    )


def layer_backward(state, weights, params, saved, query_ids, key_ids, grad_in):
    width = state.shape[1]
    hidden, queries, key_vals, lse, attended, mid_state, normed, upward, active = saved
    down_grad = grad_in.astype(jnp.bfloat16)
    act_grad = dot_rows(down_grad, weights[2])
    unused_gelu, gelu_pull = jax.vjp(partial(jax.nn.gelu, approximate=True), upward)
    up_grad = gelu_pull(act_grad)[0].astype(jnp.bfloat16)
    mid_back, gain_two, shift_two = norm_back(
        mid_state, params[5], params[6], dot_plain(up_grad, weights[1])
    )
    mid_grad = grad_in + mid_back
    out_grad = mid_grad.astype(jnp.bfloat16)
    att_grad = wide(dot_rows(out_grad, weights[0][3 * width :]).astype(jnp.bfloat16))
    query_grad, pair_grad = attend_back(queries, key_vals, att_grad, lse, key_ids, query_ids)
    own = exchange(
        pair_grad, "return_grads", 8, sum_axes=("seq",), sum_orders=[bits_of("seq")]
    )
    query_grad = query_grad[:, :width]
    key_grad, val_grad = own[: own.shape[0] // 2, :width], own[own.shape[0] // 2 :, :width]
    joined_grad = jnp.concatenate([query_grad, key_grad, val_grad], 1)
    state_back, gain_one, shift_one = norm_back(
        state, params[0], params[1], dot_plain(joined_grad, weights[0][: 3 * width])
    )
    small_grad = jnp.concatenate(
        [
            jnp.stack(
                [
                    gain_one,
                    shift_one,
                    column_sums(query_grad),
                    column_sums(val_grad),
                    column_sums(out_grad),
                    gain_two,
                    shift_two,
                    column_sums(down_grad),
                ]
            ),
            column_sums(up_grad).reshape(4, width),
        ],
        0,
    )
    factors = [(joined_grad, hidden, attended, out_grad), (up_grad, normed), (active, down_grad)]
    return (mid_grad + state_back, factors, small_grad)


def adam_step(weights, moment, square, grad, rate, decay, step):
    moment = BETA_ONE * moment + (1 - BETA_ONE) * grad
    square = BETA_TWO * square + (1 - BETA_TWO) * grad * grad
    moment_hat = moment / (1 - BETA_ONE**step)
    square_hat = square / (1 - BETA_TWO**step)
    weights = weights - rate * (moment_hat / (jnp.sqrt(square_hat) + ADAM_EPS) + decay * weights)
    return (weights, moment, square)


def pad_rows(x, rows):
    return jnp.pad(x, ((0, rows - x.shape[0]), (0, 0)))


def on_device(
    tokens,
    block_ids,
    completion,
    regroup,
    targets,
    step_count,
    layer_mats,
    mats_moment,
    mats_square,
    embed_table,
    table_moment,
    table_square,
):
    seqs, tok_count = tokens.shape
    seq_length = block_ids.shape[1]
    width = embed_table.shape[1]
    table_local = embed_table.shape[0]
    layers = layer_mats.shape[0]
    replicas, groups, shards = (lax.axis_size(axis) for axis in AXES)
    total = replicas * groups * shards
    seq_at = lax.axis_index("seq")
    shard_at = lax.axis_index("shard")
    device_at = lax.axis_index(AXES)
    seq_bits, dp_bits, shard_bits = bits_of("seq"), bits_of("dp"), bits_of("shard")
    first_row = device_at * table_local
    table_own = embed_table.astype(jnp.bfloat16)
    mats_low = layer_mats.astype(jnp.bfloat16)
    token_ids = tokens.reshape(-1)
    local_rows = token_ids.shape[0]
    small_count = 12 * layers + 2
    small_rows = -(-small_count // 16) * 16

    ids_all = exchange(
        jnp.pad(token_ids, (0, -local_rows % 1024)).reshape(1, -1, 128),
        "share_ids",
        0,
        join_axes=AXES,
        join_orders=[shard_bits[::-1] + dp_bits[::-1] + seq_bits[::-1]],
    )
    ids_all = ids_all.reshape(total, -1)[:, :local_rows]
    owner_all = ids_all // table_local
    loads = jnp.sum(
        (owner_all[:, :, None] == jnp.arange(total)[None, None, :]).astype(jnp.int32), 1
    )
    rounds = (jnp.max(loads) + SLOTS - 1) // SLOTS
    asked = owner_all == device_at
    asked_rank = counts_before(asked)
    asked_row = ids_all - first_row
    own_owner = token_ids // table_local
    same = own_owner[:, None] == own_owner[None, :]
    before = jnp.arange(local_rows)[None, :] < jnp.arange(local_rows)[:, None]
    own_rank = jnp.sum((same & before).astype(jnp.int32), 1)

    def asked_rows(at):
        chosen = asked[:, None, :] & (
            asked_rank[:, None, :] == at * SLOTS + jnp.arange(SLOTS)[None, :, None]
        )
        return (jnp.sum(jnp.where(chosen, asked_row[:, None, :] + 1, 0), 2) - 1).reshape(-1)

    def own_slots(at):
        slot = own_rank - at * SLOTS
        return jnp.where((slot >= 0) & (slot < SLOTS), own_owner * SLOTS + slot, -1)

    def fetch(at, given):
        return dot_plain(
            one_hot(own_slots(at), total * SLOTS, 1), given.reshape(total * SLOTS, width)
        )

    fixed = jnp.arange(seq_length + small_rows, dtype=jnp.int32)
    fixed_row = jnp.where(fixed < seq_length + small_count, VOCAB + fixed - first_row, -1)
    wanted = jnp.concatenate([asked_rows(0), fixed_row])
    rows_out = dot_plain(one_hot(wanted, table_local, 1), table_own).astype(jnp.bfloat16)
    exchanged = total * SLOTS
    piece = seq_length // total
    (place_rows,), (small,), (given,) = run_jobs(
        [
            sum_job(
                rows_out[exchanged : exchanged + seq_length].reshape(total, piece, width),
                sum_axes=("seq", "dp", "shard"),
                sum_orders=[seq_bits + dp_bits + shard_bits],
                join_axes=("dp", "shard"),
                join_orders=[shard_bits[::-1] + dp_bits[::-1]],
            ),
            combine_job(rows_out[exchanged + seq_length :], add_pair),
            swap_job(rows_out[:exchanged].reshape(total, SLOTS, width), late=7),
        ],
        "open_rows",
        2,
        32,
    )
    place_rows = place_rows.reshape(tok_count, width)
    small = small[:small_count].astype(jnp.float32)
    place_state = jnp.broadcast_to(place_rows.astype(jnp.float32), (seqs, tok_count, width))
    state = fetch(0, given) + place_state.reshape(local_rows, width)

    def fetch_more(at, held):
        rows = dot_plain(one_hot(asked_rows(at), table_local, 1), table_own).astype(jnp.bfloat16)
        return held + fetch(at, swap(rows.reshape(total, SLOTS, width), "swap_rows", 1))

    state = lax.fori_loop(1, rounds, fetch_more, state)

    query_ids = lax.dynamic_slice_in_dim(block_ids[0], seq_at * tok_count, tok_count, 0)
    inputs, kept, saved = [], [], []
    for layer_at in range(layers):
        weights = [
            lax.all_gather(mats_low[layer_at, k], AXES, axis=0, tiled=True)
            for k in range(layer_mats.shape[1])
        ]
        inputs.append(state)
        kept.append(weights)
        state, held = layer_forward(
            state,
            weights,
            small[12 * layer_at : 12 * layer_at + 12],
            query_ids,
            block_ids[0],
        )
        saved.append(held)
    final_gain = small[12 * layers]
    final_shift = small[12 * layers + 1]
    final = layer_norm(state, final_gain, final_shift).astype(jnp.bfloat16)

    group_mask = completion[0]
    slot_of = regroup[0]
    slots = slot_of.shape[0]
    comp_rows = slots // shards
    rank_all = counts_before(group_mask[None])[0]
    mine = lax.dynamic_slice_in_dim(group_mask, shard_at * local_rows, local_rows)
    my_rank = lax.dynamic_slice_in_dim(rank_all, shard_at * local_rows, local_rows)
    my_slot = jnp.sum(
        jnp.where(my_rank[:, None] == jnp.arange(slots)[None, :], slot_of[None, :], 0), 1
    )
    to_slot = one_hot(jnp.where(mine == 1, my_slot, -1), slots, 0)
    outgoing = dot_plain(to_slot, final).astype(jnp.bfloat16).reshape(shards, comp_rows, width)
    two_ways = [seq_bits[1:] + dp_bits, dp_bits + seq_bits[1:]]
    head_in = exchange(
        outgoing,
        "share_final",
        5,
        sum_axes=("shard",),
        sum_orders=[shard_bits, shard_bits],
        join_axes=AXES,
        join_orders=[shard_bits[::-1] + way[::-1] + seq_bits[:1] for way in two_ways],
        chunks=2,
    ).reshape(-1, width)

    rows_all = targets.shape[0]
    columns = first_row + jnp.arange(table_local, dtype=jnp.int32)
    live = (columns < VOCAB)[None, :]
    logits = dot_rows(head_in, table_own)
    masked = jnp.where(live, logits, MASK_FILL)
    top_local = jnp.max(masked, 1)
    total_local = jnp.sum(jnp.where(live, jnp.exp(masked - top_local[:, None]), 0.0), 1)
    target_hit = columns[None, :] == targets[:, None]
    pick_local = jnp.sum(jnp.where(target_hit, logits, 0.0), 1)
    stats = combine_all(
        jnp.stack([top_local, total_local, pick_local]).reshape(3, -1, 128),
        merge_soft,
        "share_stats",
        6,
    ).reshape(3, rows_all)
    log_total = stats[0] + jnp.log(stats[1])
    loss_value = jnp.sum(log_total - stats[2]) / rows_all
    probs = jnp.where(live, jnp.exp(masked - log_total[:, None]), 0.0)
    logit_grad = ((probs - target_hit.astype(jnp.float32)) / rows_all).astype(jnp.bfloat16)
    head_grad = dot_cols(logit_grad, head_in)
    returned = exchange(
        dot_plain(logit_grad, table_own).reshape(total, comp_rows, width),
        "return_final",
        7,
        sum_axes=AXES,
        sum_orders=[seq_bits[:1] + way + shard_bits for way in two_ways],
        join_axes=("shard",),
        join_orders=[shard_bits[::-1], shard_bits[::-1]],
        chunks=2,
    ).reshape(slots, width)
    final_grad = dot_cols(to_slot, returned)
    state_grad, gain_final, shift_final = norm_back(state, final_gain, final_shift, final_grad)

    mats_grads = [None] * layers
    small_grads = [None] * layers
    for layer_at in reversed(range(layers)):
        state_grad, factors, small_grads[layer_at] = layer_backward(
            inputs[layer_at],
            kept[layer_at],
            small[12 * layer_at : 12 * layer_at + 12],
            saved[layer_at],
            query_ids,
            block_ids[0],
            state_grad,
        )
        first, up, down = factors
        if layer_at > 0:
            joined_grad, hidden, attended, out_grad = first
            total_rows = lax.axis_size(AXES)
            parts = [dot_cols(joined_grad, hidden), dot_cols(attended, out_grad)]
            grad = jnp.concatenate([rows_major(part.astype(jnp.bfloat16)) for part in parts], 0)
            blocks = grad.reshape(total_rows, -1, width)
            state_grad, blocks = lax.optimization_barrier((state_grad, blocks))
            mats_grads[layer_at] = jnp.stack(
                [
                    lax.psum_scatter(blocks, AXES, scatter_dimension=0, tiled=True)[0],
                    scatter_rows(*up),
                    scatter_rows(*down),
                ]
            ).astype(jnp.float32)
        else:
            late = late_mats(first, up, down, 12)

    low_grad = state_grad.astype(jnp.bfloat16)
    place_grad = jnp.sum(state_grad.reshape(seqs, tok_count, width), 0)
    small_grad = pad_rows(
        jnp.concatenate(small_grads + [jnp.stack([gain_final, shift_final])], 0), small_rows
    )

    def leaving(at):
        rows = dot_cols(one_hot(own_slots(at), total * SLOTS, 1), low_grad).astype(jnp.bfloat16)
        return rows.reshape(total, SLOTS, width)

    fits = mats_fit(late)
    own_mats, (place_grad,), (small_grad,), (came,) = run_jobs(
        [
            mats_job(late[:fits]),
            sum_job(
                place_grad.reshape(replicas * shards, piece, width),
                sum_axes=("dp", "shard"),
                sum_orders=[dp_bits + shard_bits],
                join_axes=("seq", "dp", "shard"),
                join_orders=[shard_bits[::-1] + dp_bits[::-1] + seq_bits[::-1]],
            ),
            combine_job(small_grad, add_pair),
            swap_job(leaving(0), late=5),
        ],
        "close_rows",
        10,
        61,
    )
    for k in range(fits, len(late), fits):
        own_mats = own_mats + run_jobs([mats_job(late[k : k + fits])], "sum_mats", 14 + k, 61)[0]
    mats_grads[0] = jnp.stack(own_mats)
    place_grad = place_grad.reshape(seq_length, width)
    small_high = small_grad.astype(jnp.bfloat16)
    small_low = (small_grad - small_high.astype(jnp.float32)).astype(jnp.bfloat16)
    values = jnp.concatenate([came.reshape(-1, width), place_grad, small_high, small_low], 0)
    value_row = jnp.concatenate([wanted, fixed_row[seq_length:]])
    table_grad = dot_plain(one_hot(value_row, table_local, 0), values) + head_grad

    def return_more(at, held):
        rows = swap(leaving(at), "swap_rows", 1).reshape(-1, width)
        return held + dot_plain(one_hot(asked_rows(at), table_local, 0), rows)

    table_grad = lax.fori_loop(1, rounds, return_more, table_grad)
    mats_grad = jnp.stack(mats_grads)
    local_squares = jnp.sum(mats_grad * mats_grad) + jnp.sum(table_grad * table_grad)
    squares = combine_all(jnp.full((8, 128), local_squares), add_pair, "share_norm", 11)
    grad_norm = jnp.sqrt(squares[0, 0])
    factor = CLIP_NORM / grad_norm
    step = step_count[0].astype(jnp.float32)
    new_mats = adam_step(
        layer_mats, mats_moment, mats_square, factor * mats_grad, RATE_MATS, DECAY_RATE, step
    )
    plain_rows = (columns < VOCAB + seq_length)[:, None]
    rate = jnp.where(plain_rows, RATE_TABLE, RATE_SMALL)
    decay = jnp.where(plain_rows, DECAY_RATE, 0.0)
    new_table = adam_step(
        embed_table, table_moment, table_square, factor * table_grad, rate, decay, step
    )
    return (
        loss_value.reshape(1),
        grad_norm.reshape(1),
        new_mats[0],
        new_mats[1],
        new_mats[2],
        new_table[0],
        new_table[1],
        new_table[2],
    )


def solution(mesh):
    in_specs = (
        P(("dp", "shard"), "seq"),
        P(("dp", "shard"), None),
        P(("dp", "seq"), None),
        P(("dp", "seq"), None),
        P(),
        P(),
        P(None, None, ("dp", "seq", "shard"), None),
        P(None, None, ("dp", "seq", "shard"), None),
        P(None, None, ("dp", "seq", "shard"), None),
        P(("dp", "seq", "shard"), None),
        P(("dp", "seq", "shard"), None),
        P(("dp", "seq", "shard"), None),
    )
    out_specs = (
        P(),
        P(),
        P(None, None, ("dp", "seq", "shard"), None),
        P(None, None, ("dp", "seq", "shard"), None),
        P(None, None, ("dp", "seq", "shard"), None),
        P(("dp", "seq", "shard"), None),
        P(("dp", "seq", "shard"), None),
        P(("dp", "seq", "shard"), None),
    )
    return jax.shard_map(
        on_device, mesh=mesh, in_specs=in_specs, out_specs=out_specs, check_vma=False
    )
```

```python
import itertools
from functools import partial

import jax
import jax.numpy as jnp
from jax import lax
from jax.experimental import pallas as pl
from jax.experimental.layout import Layout, with_layout_constraint
from jax.experimental.pallas import tpu as pltpu
from jax.sharding import PartitionSpec as P

HEADS = 17
HEAD = 64
VOCAB = 50278

NORM_EPS = 1e-05
CLIP_NORM = 0.02
BETA_ONE = 0.9
BETA_TWO = 0.95
ADAM_EPS = 1e-08
DECAY_RATE = 0.1
RATE_MATS = 0.05
RATE_TABLE = 0.1
RATE_SMALL = 0.5
MASK_FILL = -1e30

AXES = ("dp", "seq", "shard")
MESH = pl.DeviceIdType.MESH
SLOTS = 24


def bits_of(axis):
    return [(axis, b) for b in range(lax.axis_size(axis).bit_length() - 1)]


def bit_here(bit):
    return lax.rem(lax.axis_index(bit[0]) // 2 ** bit[1], 2)


def partner(bit):
    at = lax.axis_index(bit[0])
    return {bit[0]: at + (1 - 2 * bit_here(bit)) * 2 ** bit[1]}


def greet(bits):
    barrier = pltpu.get_barrier_semaphore()
    for bit in bits:
        pl.semaphore_signal(barrier, inc=1, device_id=partner(bit), device_id_type=MESH)
    pl.semaphore_wait(barrier, len(bits))


def block_weight(axes, bit):
    weight = 2 ** bit[1]
    for axis in axes[axes.index(bit[0]) + 1 :]:
        weight *= lax.axis_size(axis)
    return weight


def block_runs(weights):
    weights = sorted(weights)
    joined = 0
    while joined < len(weights) and weights[joined] == 2**joined:
        joined += 1
    rest = [(0, w) for w in weights[joined:]]
    return 2**joined, [sum(c) for c in itertools.product(*rest)]


class Job:
    def __init__(
        self, inputs, outputs, scratch, sends, keeps, bits, steps, spaces=(pltpu.VMEM, pltpu.VMEM)
    ):
        self.inputs, self.outputs, self.scratch = inputs, outputs, scratch
        self.sends, self.keeps, self.bits, self.steps, self.spaces = sends, keeps, bits, steps, spaces


def me_and_total():
    seq_size, shard_size = lax.axis_size("seq"), lax.axis_size("shard")
    at = (lax.axis_index("dp") * seq_size + lax.axis_index("seq")) * shard_size
    return at + lax.axis_index("shard"), lax.axis_size("dp") * seq_size * shard_size


def place_of(at):
    seq_size, shard_size = lax.axis_size("seq"), lax.axis_size("shard")
    return {
        "dp": at // (seq_size * shard_size),
        "seq": lax.rem(at // shard_size, seq_size),
        "shard": lax.rem(at, shard_size),
    }


def greet_all():
    me, total = me_and_total()
    barrier = pltpu.get_barrier_semaphore()

    def hello(k, carry):
        pl.semaphore_signal(
            barrier, inc=1, device_id=place_of(lax.rem(me + k, total)), device_id_type=MESH
        )
        return carry

    lax.fori_loop(1, total, hello, 0)
    pl.semaphore_wait(barrier, total - 1)


class Sems:
    def __init__(self, send, recv, keep):
        self.send, self.recv, self.keep = send, recv, keep
        self.used = self.kept = 0

    def copy(self, source, target, device):
        k = self.used
        self.used += 1
        copy = pltpu.make_async_remote_copy(
            source, target, self.send.at[k], self.recv.at[k], device_id=device, device_id_type=MESH
        )
        copy.start()
        return copy

    def local(self, source, target):
        k = self.kept
        self.kept += 1
        copy = pltpu.make_async_copy(source, target, self.keep.at[k])
        copy.start()
        return copy

    def span(self, count):
        first = self.used
        self.used += count
        return first


def jobs_kernel(jobs, *refs):
    refs = list(refs)

    def take(count):
        out = refs[:count]
        del refs[:count]
        return out

    held = [take(len(job.inputs)) for job in jobs]
    made = [take(len(job.outputs)) for job in jobs]
    used = [take(len(job.scratch)) for job in jobs]
    sems = Sems(*refs)
    if any(job.bits is None for job in jobs):
        greet_all()
    else:
        greet(sorted(set(bit for job in jobs for bit in job.bits)))
    active = []
    for job, x, o, w in zip(jobs, held, made, used):
        active += job.steps(x, o, w, sems)
    tick = 0
    while active:
        left = []
        for delay, gen in active:
            if delay > tick or next(gen, "end") != "end":
                left.append((delay, gen))
        active = left
        tick += 1


def run_jobs(jobs, name, number, vmem=60):
    inputs = [x for job in jobs for x in job.inputs]
    outputs = [o for job in jobs for o in job.outputs]
    in_specs = [pl.BlockSpec(memory_space=job.spaces[0]) for job in jobs for unused in job.inputs]
    out_specs = [pl.BlockSpec(memory_space=job.spaces[1]) for job in jobs for unused in job.outputs]
    sends = sum(job.sends for job in jobs)
    keeps = max(1, sum(job.keeps for job in jobs))
    flat = pl.pallas_call(
        partial(jobs_kernel, jobs),
        out_shape=outputs,
        in_specs=in_specs,
        out_specs=out_specs,
        scratch_shapes=[w for job in jobs for w in job.scratch]
        + [
            pltpu.SemaphoreType.DMA((sends,)),
            pltpu.SemaphoreType.DMA((sends,)),
            pltpu.SemaphoreType.DMA((keeps,)),
        ],
        compiler_params=pltpu.CompilerParams(
            collective_id=number, has_side_effects=True, vmem_limit_bytes=vmem * 2**20
        ),
        name=name,
    )(*inputs)
    out = []
    for job in jobs:
        out.append(flat[: len(job.outputs)])
        flat = flat[len(job.outputs) :]
    return out


def sum_stream(x_ref, o_ref, scratch, sems, rows, first_slot, sum_axes, sums, join_axes, joins):
    source = x_ref
    slot = first_slot
    if sums:
        work, parcel, recv = scratch
    for step, bit in enumerate(sums):
        base = sum(bit_here(b) * block_weight(sum_axes, b) for b in sums[:step])
        weight = block_weight(sum_axes, bit)
        mine = bit_here(bit)
        size, offsets = block_runs([block_weight(sum_axes, b) for b in sums[step + 1 :]])
        started = []
        for offset in offsets:
            leave = base + (1 - mine) * weight + offset
            if source.dtype == parcel.dtype:
                packed = source.at[pl.ds(leave, size), rows]
            else:

                def pack(i, carry, leave=leave, at=slot, source=source):
                    parcel[at + i, rows] = source[leave + i, rows].astype(parcel.dtype)
                    return carry

                lax.fori_loop(0, size, pack, 0)
                packed = parcel.at[pl.ds(slot, size), rows]
            copy = sems.copy(packed, recv.at[pl.ds(slot, size), rows], partner(bit))
            started.append((copy, base + mine * weight + offset, slot, size))
            slot += size
        yield
        for copy, keep, at, size in started:
            copy.wait()

            def add(i, carry, keep=keep, at=at, source=source):
                total = source[keep + i, rows].astype(jnp.float32)
                total = total + recv[at + i, rows].astype(jnp.float32)
                work[keep + i, rows] = total.astype(work.dtype)
                return carry

            lax.fori_loop(0, size, add, 0)
        source = work
    own = sum(bit_here(b) * block_weight(sum_axes, b) for b in sums) if sums else 0
    result = source[own, rows].astype(o_ref.dtype)
    if not joins:
        o_ref[rows] = result
        return
    o_ref[sum(bit_here(b) * block_weight(join_axes, b) for b in joins), rows] = result
    for step, bit in enumerate(joins):
        base = sum(bit_here(b) * block_weight(join_axes, b) for b in joins[step:])
        size, offsets = block_runs([block_weight(join_axes, b) for b in joins[:step]])
        started = []
        for offset in offsets:
            here = o_ref.at[pl.ds(base + offset, size), rows]
            started.append(sems.copy(here, here, partner(bit)))
        yield
        for copy in started:
            copy.wait()


def sum_job(x, sum_axes=(), sum_orders=(), join_axes=(), join_orders=(), chunks=1):
    rows, width = x.shape[-2:]
    blocks = 1
    for axis in join_axes:
        blocks *= lax.axis_size(axis)
    kind = jnp.bfloat16 if sum_axes else x.dtype
    streams = max(len(sum_orders), len(join_orders))
    if rows % (streams * chunks * 16):
        chunks = 1
    share = rows // (streams * chunks)
    sends = 0
    for order in sum_orders:
        for step in range(len(order)):
            sends += len(block_runs([block_weight(sum_axes, b) for b in order[step + 1 :]])[1])
    for order in join_orders:
        for step in range(len(order)):
            sends += len(block_runs([block_weight(join_axes, b) for b in order[:step]])[1])
    scratch = []
    if sum_axes:
        if x.size * 14 > 56 * 2**20:
            x = x.astype(jnp.bfloat16)
        exact = x.dtype == jnp.float32 or x.size < 2**22
        scratch = [
            pltpu.VMEM(x.shape, jnp.float32 if exact else kind),
            pltpu.VMEM(x.shape, kind),
            pltpu.VMEM(x.shape, kind),
        ]

    def steps(x_refs, o_refs, scratch_refs, sems):
        gens = []
        for c in range(chunks):
            for k in range(streams):
                rows_here = pl.ds((k * chunks + c) * share, share)
                sums = sum_orders[k] if sum_orders else []
                joins = join_orders[k] if join_orders else []
                gens.append(
                    (
                        c,
                        sum_stream(
                            x_refs[0], o_refs[0], scratch_refs, sems, rows_here, 0,
                            sum_axes, sums, join_axes, joins,
                        ),
                    )
                )
        return gens

    bits = set(bit for order in list(sum_orders) + list(join_orders) for bit in order)
    shape = (blocks, rows, width) if join_axes else (rows, width)
    return Job(
        [x], [jax.ShapeDtypeStruct(shape, kind)], scratch, sends * chunks, 0, bits, steps
    )


def exchange(x, name, number, **how):
    return run_jobs([sum_job(x, **how)], name, number)[0][0]


def combine_job(x, combine):
    bits = [bit for axis in reversed(AXES) for bit in bits_of(axis)]
    slots = (len(bits),) + x.shape

    def steps(x_refs, o_refs, scratch, sems):
        out_buf, in_buf = scratch

        def gen():
            current = x_refs[0][...]
            for i, bit in enumerate(bits):
                out_buf[i] = current
                copy = sems.copy(out_buf.at[i], in_buf.at[i], partner(bit))
                yield
                copy.wait()
                current, other = out_buf[i], in_buf[i]
                low = bit_here(bit) == 0
                current = combine(jnp.where(low, current, other), jnp.where(low, other, current))
            o_refs[0][...] = current

        return [(0, gen())]

    return Job(
        [x],
        [jax.ShapeDtypeStruct(x.shape, x.dtype)],
        [pltpu.VMEM(slots, x.dtype), pltpu.VMEM(slots, x.dtype)],
        len(bits),
        0,
        bits,
        steps,
    )


def combine_all(x, combine, name, number):
    return run_jobs([combine_job(x, combine)], name, number, 16)[0][0]


def swap_job(x, late=0):
    total = x.shape[0]

    def steps(x_refs, o_refs, scratch, sems):
        x_ref, o_ref = x_refs[0], o_refs[0]

        def gen():
            me, unused = me_and_total()
            first = sems.span(total)
            keep = sems.local(x_ref.at[me], o_ref.at[me])

            def copy_to(other, here):
                return pltpu.make_async_remote_copy(
                    x_ref.at[other],
                    o_ref.at[here],
                    sems.send.at[first + other],
                    sems.recv.at[first + here],
                    device_id=place_of(other),
                    device_id_type=MESH,
                )

            def send(k, carry):
                copy_to(lax.rem(me + k, total), me).start()
                return carry

            lax.fori_loop(1, total, send, 0)
            for unused in range(late + 1):
                yield

            def finish(k, carry):
                other = lax.rem(me + k, total)
                copy_to(other, other).wait()
                return carry

            lax.fori_loop(1, total, finish, 0)
            keep.wait()

        return [(0, gen())]

    return Job(
        [x],
        [jax.ShapeDtypeStruct(x.shape, x.dtype)],
        [],
        total,
        1,
        None,
        steps,
        spaces=(pl.ANY, pl.ANY),
    )


def swap(x, name, number):
    return run_jobs([swap_job(x)], name, number, 16)[0][0]


def sum_orders_for(rows):
    across, along, deep = bits_of("seq")[1:], bits_of("dp"), bits_of("shard")
    if rows < 64 or rows % 8:
        return [(0, rows)], [across + along + deep]
    one = rows * 6 // 17 // 16 * 16
    spans = [(0, one), (one, one), (2 * one, rows - 2 * one)]
    return spans, [across + along + deep, along + across + deep, deep + across + along]


def mats_stream(x_ref, o_ref, scratch, sems, m, span, order, weights):
    kept, work, parcel, recv = scratch
    turn, m = m % 2, m % work.shape[0]
    steps = len(order)
    rows = pl.ds(*span)
    slot = 0
    rest = sorted((b for b in weights if b != order[0]), key=lambda b: weights[b])
    small = {b: 2**k for k, b in enumerate(rest)}
    for step, bit in enumerate(order):
        mine = bit_here(bit)
        base = sum(bit_here(b) * small[b] for b in order[1:step])
        runs, keeps = [], []
        if step == 0:
            size, offsets = block_runs([weights[b] for b in order[1:]])
            for offset in offsets:
                left, place = offset, 0
                for b in reversed(rest):
                    if left >= weights[b]:
                        left -= weights[b]
                        place += small[b]
                keeps.append(
                    sems.local(
                        x_ref.at[pl.ds(mine * weights[bit] + offset, size), rows],
                        kept.at[turn, pl.ds(place, size), rows],
                    )
                )
                runs.append(((1 - mine) * weights[bit] + offset, place))
        else:
            size, offsets = block_runs([small[b] for b in order[step + 1 :]])
            for offset in offsets:
                here = base + offset
                runs.append((here + (1 - mine) * small[bit], here + mine * small[bit]))
        started = []
        for leave, keep_at in runs:
            at = slot
            slot += size
            if step == 0:
                packed = x_ref.at[pl.ds(leave, size), rows]
            else:
                spot = at - 2 ** (steps - 1)

                def pack(i, carry, leave=leave, spot=spot):
                    parcel[m, spot + i, rows] = work[m, leave + i, rows].astype(parcel.dtype)
                    return carry

                lax.fori_loop(0, size, pack, 0)
                packed = parcel.at[m, pl.ds(spot, size), rows]
            copy = sems.copy(packed, recv.at[m, pl.ds(at, size), rows], partner(bit))
            started.append((copy, at, keep_at, size))
        yield
        for keep in keeps:
            keep.wait()
        for copy, at, keep_at, size in started:
            copy.wait()

            def add(i, carry, at=at, keep_at=keep_at, step=step):
                if step == 0:
                    total = kept[turn, keep_at + i, rows].astype(jnp.float32)
                else:
                    total = work[m, keep_at + i, rows]
                work[m, keep_at + i, rows] = total + recv[m, at + i, rows].astype(jnp.float32)
                return carry

            lax.fori_loop(0, size, add, 0)
    o_ref[rows] = work[m, sum(bit_here(b) * small[b] for b in order[1:]), rows]


def mats_job(mats):
    blocks, rows, width = mats[0].shape
    spans, orders = sum_orders_for(rows)
    weights = {}
    for bit in orders[0]:
        weight = block_weight(AXES, bit)
        weights[bit] = weight if bit[0] == "shard" else weight // 2
    keeps = sends = 0
    for order in orders:
        keeps += len(block_runs([weights[b] for b in order[1:]])[1])
        sends += len(block_runs([weights[b] for b in order[1:]])[1])
        rest = sorted((b for b in weights if b != order[0]), key=lambda b: weights[b])
        small = {b: 2**k for k, b in enumerate(rest)}
        for step in range(1, len(order)):
            sends += len(block_runs([small[b] for b in order[step + 1 :]])[1])
    count = len(mats)

    def steps(x_refs, o_refs, scratch, sems):
        return [
            (m, mats_stream(x_refs[m], o_refs[m], scratch, sems, m, spans[k], orders[k], weights))
            for m in range(count)
            for k in range(len(orders))
        ]

    return Job(
        mats,
        [jax.ShapeDtypeStruct((rows, width), jnp.float32)] * count,
        [
            pltpu.VMEM((min(2, count), blocks // 2, rows, width), jnp.bfloat16),
            pltpu.VMEM((min(3, count), blocks // 2, rows, width), jnp.float32),
            pltpu.VMEM((min(3, count), blocks // 2 - 1, rows, width), jnp.bfloat16),
            pltpu.VMEM((min(3, count), blocks - 1, rows, width), jnp.bfloat16),
        ],
        count * sends,
        count * keeps,
        set(orders[0]),
        steps,
        spaces=(pl.ANY, pltpu.VMEM),
    )


def gather_job(parts):
    rows, width = parts[0].shape
    spans, orders = sum_orders_for(rows)
    orders = [order[::-1] + bits_of("seq")[:1] for order in orders]
    total = lax.axis_size(AXES)
    sends = 0
    for order in orders:
        for step in range(len(order)):
            sends += len(block_runs([block_weight(AXES, b) for b in order[:step]])[1])

    def gen(x_ref, o_ref, sems, span, order):
        here = pl.ds(*span)
        own = me_and_total()[0]
        keep = sems.local(x_ref.at[here], o_ref.at[own, here])
        for step, bit in enumerate(order):
            base = sum(bit_here(b) * block_weight(AXES, b) for b in order[step:])
            size, offsets = block_runs([block_weight(AXES, b) for b in order[:step]])
            started = []
            for offset in offsets:
                target = o_ref.at[pl.ds(base + offset, size), here]
                source = x_ref.at[here] if step == 0 else target
                target = o_ref.at[own, here] if step == 0 else target
                started.append(sems.copy(source, target, partner(bit)))
            yield
            if step == 0:
                keep.wait()
            for copy in started:
                copy.wait()

    def steps(x_refs, o_refs, scratch, sems):
        return [
            (m, gen(x_refs[m], o_refs[m], sems, spans[k], orders[k]))
            for m in range(len(parts))
            for k in range(len(orders))
        ]

    return Job(
        parts,
        [jax.ShapeDtypeStruct((total, rows, width), parts[0].dtype)] * len(parts),
        [],
        sends * len(parts),
        len(orders) * len(parts),
        set(orders[0]),
        steps,
        spaces=(pl.ANY, pl.ANY),
    )


def trade_kernel(count, *refs):
    x_refs, o_refs = refs[:count], refs[count : 2 * count]
    send_sems, recv_sems = refs[2 * count :]
    bit = ("seq", 0)
    greet([bit])
    copies = []
    for k in range(count):
        copy = pltpu.make_async_remote_copy(
            x_refs[k],
            o_refs[k],
            send_sems.at[k],
            recv_sems.at[k],
            device_id=partner(bit),
            device_id_type=MESH,
        )
        copy.start()
        copies.append(copy)
    for copy in copies:
        copy.wait()


def trade(arrays, name, number):
    count = len(arrays)
    return pl.pallas_call(
        partial(trade_kernel, count),
        out_shape=[jax.ShapeDtypeStruct(x.shape, x.dtype) for x in arrays],
        in_specs=[pl.BlockSpec(memory_space=pl.ANY)] * count,
        out_specs=[pl.BlockSpec(memory_space=pl.ANY)] * count,
        scratch_shapes=[pltpu.SemaphoreType.DMA((count,)), pltpu.SemaphoreType.DMA((count,))],
        compiler_params=pltpu.CompilerParams(collective_id=number, has_side_effects=True),
        name=name,
    )(*arrays)


def my_rows(features, own):
    rows = features.shape[0]
    parts = features.reshape(rows, -1, 2, own)
    at = lax.rem(lax.axis_index("seq"), 2)
    mine = lax.dynamic_index_in_dim(parts, at, 2, keepdims=False)
    other = lax.dynamic_index_in_dim(parts, 1 - at, 2, keepdims=False)
    return mine.reshape(rows, -1), other.reshape(rows, -1)


def late_mats(groups, number):
    pairs = [pair for group in groups for pair in group]
    total = lax.axis_size(AXES)
    height = sum(features.shape[1] for features, unused in groups[0])
    own = height // total * lax.axis_size("shard")
    halves = [my_rows(features, own) for features, unused in pairs]
    tails = [tail for unused, tail in pairs]
    got = trade([other for unused, other in halves] + tails, "trade_rows", number)
    parts = []
    for k, (mine, unused) in enumerate(halves):
        grad = dot_cols(
            jnp.concatenate([mine, got[k]], 0),
            jnp.concatenate([tails[k], got[len(halves) + k]], 0),
        )
        parts.append(rows_major(grad.astype(jnp.bfloat16)))
    mats = []
    for group in groups:
        grad = jnp.concatenate(parts[: len(group)], 0) if len(group) > 1 else parts[0]
        parts = parts[len(group) :]
        mats.append(grad.reshape(total // 2, -1, grad.shape[1]))
    return mats


def mats_fit(mats):
    blocks, rows, width = mats[0].shape
    tile = -(-rows // 16) * 16 * -(-width // 128) * 128
    fits = (50 * 2**20 - tile * blocks * 2) // (tile * blocks * 5)
    return len(mats) if fits >= 3 else max(1, fits)


def head_lanes(half, shape):
    lane = lax.broadcasted_iota(jnp.int32, shape, 1)
    return (lane < HEAD) if half == 0 else (lane >= HEAD)


def attend_kernel(q_ref, kv_ref, key_ids_ref, query_ids_ref, o_ref, lse_ref, blocked):
    groups, twice, unused = kv_ref.shape
    rows = twice // 2
    keys = groups * rows
    blocked[...] = jnp.where(key_ids_ref[...] <= query_ids_ref[...], 0.0, MASK_FILL)

    def pair(p, carry):
        lanes = pl.ds(pl.multiple_of(p * 2 * HEAD, 2 * HEAD), 2 * HEAD)
        key_pair = kv_ref[:, :rows, lanes].reshape(keys, 2 * HEAD)
        val_turned = kv_ref[:, rows:, lanes].reshape(keys, 2 * HEAD).T
        query_pair = q_ref[:, lanes]
        outs = []
        for half in range(2):
            query = jnp.where(head_lanes(half, query_pair.shape), query_pair, 0)
            scores = dot_rows(key_pair, query.astype(jnp.bfloat16)) * HEAD ** (-0.5) + blocked[...]
            top = jnp.max(scores, 0, keepdims=True)
            raised = jnp.exp(scores - top)
            total = jnp.sum(raised, 0, keepdims=True)
            probs = (raised * (1.0 / total)).astype(jnp.bfloat16)
            outs.append(dot_plain(val_turned[half * HEAD : (half + 1) * HEAD], probs))
            lse_ref[p, half] = (top + jnp.log(total))[0]
        o_ref[:, lanes] = jnp.concatenate(outs, 0).T.astype(o_ref.dtype)
        return carry

    lax.fori_loop(0, q_ref.shape[1] // (2 * HEAD), pair, 0)


def attend(queries, key_vals, key_ids, query_ids):
    rows, width = queries.shape
    keys = key_ids.shape[0]
    pairs = width // (2 * HEAD)
    return pl.pallas_call(
        attend_kernel,
        out_shape=(
            jax.ShapeDtypeStruct((rows, width), jnp.bfloat16),
            jax.ShapeDtypeStruct((pairs, 2, rows), jnp.float32),
        ),
        in_specs=[pl.BlockSpec(memory_space=pltpu.VMEM)] * 4,
        out_specs=(pl.BlockSpec(memory_space=pltpu.VMEM),) * 2,
        scratch_shapes=[pltpu.VMEM((keys, rows), jnp.float32)],
        compiler_params=pltpu.CompilerParams(vmem_limit_bytes=48 * 2**20),
        cost_estimate=pl.CostEstimate(
            flops=4 * rows * keys * width,
            transcendentals=rows * keys * HEADS,
            bytes_accessed=4 * keys * width,
        ),
        name="attend",
    )(queries, key_vals, key_ids[:, None], query_ids[None, :])


def attend_back_kernel(
    q_ref, kv_ref, grad_ref, lse_ref, key_ids_ref, query_ids_ref, dq_ref, dkv_ref, blocked
):
    groups, twice, unused = kv_ref.shape
    rows = twice // 2
    keys = groups * rows
    scale = HEAD ** (-0.5)
    blocked[...] = jnp.where(key_ids_ref[...] <= query_ids_ref[...], 0.0, MASK_FILL)

    def pair(p, carry):
        lanes = pl.ds(pl.multiple_of(p * 2 * HEAD, 2 * HEAD), 2 * HEAD)
        key_pair = kv_ref[:, :rows, lanes].reshape(keys, 2 * HEAD)
        val_pair = kv_ref[:, rows:, lanes].reshape(keys, 2 * HEAD)
        key_turned = key_pair.T
        query_pair = q_ref[:, lanes]
        grad_pair = grad_ref[:, lanes]
        key_grad = jnp.zeros((keys, 2 * HEAD), jnp.float32)
        val_grad = jnp.zeros((keys, 2 * HEAD), jnp.float32)
        outs = []
        for half in range(2):
            here = head_lanes(half, query_pair.shape)
            query = jnp.where(here, query_pair, 0).astype(jnp.bfloat16)
            grad = jnp.where(here, grad_pair, 0).astype(jnp.bfloat16)
            scores = dot_rows(key_pair, query) * scale + blocked[...]
            probs = jnp.exp(scores - lse_ref[p, half][None, :])
            prob_grad = dot_rows(val_pair, grad)
            inner = jnp.sum(probs * prob_grad, 0, keepdims=True)
            score_grad = (probs * (prob_grad - inner)).astype(jnp.bfloat16)
            key_grad = key_grad + dot_plain(score_grad, query)
            val_grad = val_grad + dot_plain(probs.astype(jnp.bfloat16), grad)
            outs.append(dot_plain(key_turned[half * HEAD : (half + 1) * HEAD], score_grad))
        dq_ref[:, lanes] = (jnp.concatenate(outs, 0).T * scale).astype(dq_ref.dtype)
        dkv_ref[:, :rows, lanes] = (key_grad * scale).reshape(groups, rows, 2 * HEAD)
        dkv_ref[:, rows:, lanes] = val_grad.reshape(groups, rows, 2 * HEAD)
        return carry

    lax.fori_loop(0, q_ref.shape[1] // (2 * HEAD), pair, 0)


def attend_back(queries, key_vals, grad, lse, key_ids, query_ids):
    rows, width = queries.shape
    keys = key_ids.shape[0]
    return pl.pallas_call(
        attend_back_kernel,
        out_shape=(
            jax.ShapeDtypeStruct((rows, width), jnp.bfloat16),
            jax.ShapeDtypeStruct(key_vals.shape, jnp.float32),
        ),
        in_specs=[pl.BlockSpec(memory_space=pltpu.VMEM)] * 6,
        out_specs=(pl.BlockSpec(memory_space=pltpu.VMEM),) * 2,
        scratch_shapes=[pltpu.VMEM((keys, rows), jnp.float32)],
        compiler_params=pltpu.CompilerParams(vmem_limit_bytes=56 * 2**20),
        cost_estimate=pl.CostEstimate(
            flops=10 * rows * keys * width,
            transcendentals=rows * keys * HEADS,
            bytes_accessed=12 * keys * width,
        ),
        name="attend_back",
    )(queries, key_vals, grad, lse, key_ids[:, None], query_ids[None, :])


def add_pair(first, second):
    return first + second


def merge_soft(first, second):
    highest = jnp.maximum(first[0], second[0])
    total = first[1] * jnp.exp(first[0] - highest) + second[1] * jnp.exp(second[0] - highest)
    return jnp.stack([highest, total, first[2] + second[2]])


def dot_rows(left_op, right_op):
    return lax.dot_general(
        left_op, right_op, (((1,), (1,)), ((), ())), preferred_element_type=jnp.float32
    )


def dot_cols(left_op, right_op):
    return lax.dot_general(
        left_op, right_op, (((0,), (0,)), ((), ())), preferred_element_type=jnp.float32
    )


def dot_plain(left_op, right_op):
    return jnp.dot(left_op, right_op, preferred_element_type=jnp.float32)


def column_sums(values):
    return jnp.sum(values.astype(jnp.float32), 0)


def layer_norm(values, gain, shift):
    center = values - jnp.mean(values, -1, keepdims=True)
    spread = jnp.mean(center * center, -1, keepdims=True)
    return center * lax.rsqrt(spread + NORM_EPS) * gain + shift


def norm_back(values, gain, shift, grad):
    unused, pull = jax.vjp(layer_norm, values, gain, shift)
    return pull(grad)


def one_hot(wanted, length, axis):
    shape = list(wanted.shape)
    shape.insert(axis, length)
    at = lax.broadcasted_iota(jnp.int32, shape, axis)
    return (at == jnp.expand_dims(wanted, axis)).astype(jnp.bfloat16)


def counts_before(flags):
    length = flags.shape[-1]
    earlier = (
        lax.broadcasted_iota(jnp.int32, (length, length), 0)
        < lax.broadcasted_iota(jnp.int32, (length, length), 1)
    ).astype(jnp.bfloat16)
    return dot_plain(flags.astype(jnp.bfloat16), earlier).astype(jnp.int32)


def wide(rows_in):
    return jnp.pad(rows_in, ((0, 0), (0, -rows_in.shape[1] % (2 * HEAD))))


def share_keys(key_rows, val_rows):
    pair = jnp.concatenate([wide(key_rows), wide(val_rows)], 0)[None]
    return exchange(
        pair, "share_keys", 4, join_axes=("seq",), join_orders=[bits_of("seq")[::-1]]
    )


def rows_major(x):
    return with_layout_constraint(x, Layout(major_to_minor=tuple(range(x.ndim))))


def scatter_rows(features, cotangents):
    total = lax.axis_size(AXES)
    grad = dot_cols(features, cotangents)
    blocks = rows_major(grad.astype(jnp.bfloat16)).reshape(total, -1, grad.shape[1])
    return lax.psum_scatter(blocks, AXES, scatter_dimension=0, tiled=True)[0]


def layer_forward(state, weights, params, query_ids, key_ids):
    width = state.shape[1]
    hidden = layer_norm(state, params[0], params[1]).astype(jnp.bfloat16)
    joined = dot_rows(hidden, weights[0][: 3 * width])
    queries = wide((joined[:, :width] + params[2]).astype(jnp.bfloat16))
    key_rows = joined[:, width : 2 * width].astype(jnp.bfloat16)
    val_rows = (joined[:, 2 * width :] + params[3]).astype(jnp.bfloat16)
    key_vals = share_keys(key_rows, val_rows)
    attended, lse = attend(queries, key_vals, key_ids, query_ids)
    attended = attended[:, :width]
    mid_state = state + dot_plain(attended, weights[0][3 * width :]) + params[4]
    normed = layer_norm(mid_state, params[5], params[6]).astype(jnp.bfloat16)
    upward = dot_rows(normed, weights[1]) + params[8:12].reshape(-1)
    active = jax.nn.gelu(upward, approximate=True).astype(jnp.bfloat16)
    output = mid_state + dot_plain(active, weights[2]) + params[7]
    return (
        output,
        (hidden, queries, key_vals, lse, attended, mid_state, normed, upward, active),
    )


def layer_backward(state, weights, params, saved, query_ids, key_ids, grad_in, arrived):
    width = state.shape[1]
    hidden, queries, key_vals, lse, attended, mid_state, normed, upward, active = saved
    down_grad = grad_in.astype(jnp.bfloat16)
    act_grad = dot_rows(down_grad, weights[2])
    unused_gelu, gelu_pull = jax.vjp(partial(jax.nn.gelu, approximate=True), upward)
    up_grad = gelu_pull(act_grad)[0].astype(jnp.bfloat16)
    mid_back, gain_two, shift_two = norm_back(
        mid_state, params[5], params[6], dot_plain(up_grad, weights[1])
    )
    mid_grad = grad_in + mid_back
    out_grad = mid_grad.astype(jnp.bfloat16)
    att_grad = wide(dot_rows(out_grad, weights[0][3 * width :]).astype(jnp.bfloat16))
    if arrived:
        att_grad, arrived[0] = lax.optimization_barrier((att_grad, arrived[0]))
    query_grad, pair_grad = attend_back(queries, key_vals, att_grad, lse, key_ids, query_ids)
    own = exchange(
        pair_grad, "return_grads", 8, sum_axes=("seq",), sum_orders=[bits_of("seq")]
    )
    query_grad = query_grad[:, :width]
    key_grad, val_grad = own[: own.shape[0] // 2, :width], own[own.shape[0] // 2 :, :width]
    joined_grad = jnp.concatenate([query_grad, key_grad, val_grad], 1)
    state_back, gain_one, shift_one = norm_back(
        state, params[0], params[1], dot_plain(joined_grad, weights[0][: 3 * width])
    )
    small_grad = jnp.concatenate(
        [
            jnp.stack(
                [
                    gain_one,
                    shift_one,
                    column_sums(query_grad),
                    column_sums(val_grad),
                    column_sums(out_grad),
                    gain_two,
                    shift_two,
                    column_sums(down_grad),
                ]
            ),
            column_sums(up_grad).reshape(4, width),
        ],
        0,
    )
    factors = [
        [(joined_grad, hidden), (attended, out_grad)],
        [(up_grad, normed)],
        [(active, down_grad)],
    ]
    return (mid_grad + state_back, factors, small_grad)


def adam_step(weights, moment, square, grad, rate, decay, step):
    moment = BETA_ONE * moment + (1 - BETA_ONE) * grad
    square = BETA_TWO * square + (1 - BETA_TWO) * grad * grad
    moment_hat = moment / (1 - BETA_ONE**step)
    square_hat = square / (1 - BETA_TWO**step)
    weights = weights - rate * (moment_hat / (jnp.sqrt(square_hat) + ADAM_EPS) + decay * weights)
    return (weights, moment, square)


def pad_rows(x, rows):
    return jnp.pad(x, ((0, rows - x.shape[0]), (0, 0)))


def on_device(
    tokens,
    block_ids,
    completion,
    regroup,
    targets,
    step_count,
    layer_mats,
    mats_moment,
    mats_square,
    embed_table,
    table_moment,
    table_square,
):
    seqs, tok_count = tokens.shape
    seq_length = block_ids.shape[1]
    width = embed_table.shape[1]
    table_local = embed_table.shape[0]
    layers = layer_mats.shape[0]
    replicas, groups, shards = (lax.axis_size(axis) for axis in AXES)
    total = replicas * groups * shards
    seq_at = lax.axis_index("seq")
    shard_at = lax.axis_index("shard")
    device_at = lax.axis_index(AXES)
    seq_bits, dp_bits, shard_bits = bits_of("seq"), bits_of("dp"), bits_of("shard")
    first_row = device_at * table_local
    table_own = embed_table.astype(jnp.bfloat16)
    mats_low = layer_mats.astype(jnp.bfloat16)
    token_ids = tokens.reshape(-1)
    local_rows = token_ids.shape[0]
    small_count = 12 * layers + 2
    small_rows = -(-small_count // 16) * 16

    ids_all = exchange(
        jnp.pad(token_ids, (0, -local_rows % 1024)).reshape(1, -1, 128),
        "share_ids",
        0,
        join_axes=AXES,
        join_orders=[shard_bits[::-1] + dp_bits[::-1] + seq_bits[::-1]],
    )
    ids_all = ids_all.reshape(total, -1)[:, :local_rows]
    owner_all = ids_all // table_local
    loads = jnp.sum(
        (owner_all[:, :, None] == jnp.arange(total)[None, None, :]).astype(jnp.int32), 1
    )
    rounds = (jnp.max(loads) + SLOTS - 1) // SLOTS
    asked = owner_all == device_at
    asked_rank = counts_before(asked)
    asked_row = ids_all - first_row
    own_owner = token_ids // table_local
    same = own_owner[:, None] == own_owner[None, :]
    before = jnp.arange(local_rows)[None, :] < jnp.arange(local_rows)[:, None]
    own_rank = jnp.sum((same & before).astype(jnp.int32), 1)

    def asked_rows(at):
        chosen = asked[:, None, :] & (
            asked_rank[:, None, :] == at * SLOTS + jnp.arange(SLOTS)[None, :, None]
        )
        return (jnp.sum(jnp.where(chosen, asked_row[:, None, :] + 1, 0), 2) - 1).reshape(-1)

    def own_slots(at):
        slot = own_rank - at * SLOTS
        return jnp.where((slot >= 0) & (slot < SLOTS), own_owner * SLOTS + slot, -1)

    def fetch(at, given):
        return dot_plain(
            one_hot(own_slots(at), total * SLOTS, 1), given.reshape(total * SLOTS, width)
        )

    fixed = jnp.arange(seq_length + small_rows, dtype=jnp.int32)
    fixed_row = jnp.where(fixed < seq_length + small_count, VOCAB + fixed - first_row, -1)
    wanted = jnp.concatenate([asked_rows(0), fixed_row])
    rows_out = dot_plain(one_hot(wanted, table_local, 1), table_own).astype(jnp.bfloat16)
    exchanged = total * SLOTS
    piece = seq_length // total
    gathered = []
    for layer_at in range(layers):
        first = lax.all_gather(mats_low[layer_at, 0], AXES, axis=0, tiled=True)
        rest = [None, None]
        if layer_at > 0:
            rest = lax.all_gather(mats_low[layer_at, 1:], AXES, axis=1, tiled=True)
        gathered.append([first, rest[0], rest[1]])
    rest, (place_rows,), (small,), (given,) = run_jobs(
        [
            gather_job([mats_low[0, 1], mats_low[0, 2]]),
            sum_job(
                rows_out[exchanged : exchanged + seq_length].reshape(total, piece, width),
                sum_axes=("seq", "dp", "shard"),
                sum_orders=[seq_bits + dp_bits + shard_bits],
                join_axes=("dp", "shard"),
                join_orders=[shard_bits[::-1] + dp_bits[::-1]],
            ),
            combine_job(rows_out[exchanged + seq_length :], add_pair),
            swap_job(rows_out[:exchanged].reshape(total, SLOTS, width), late=7),
        ],
        "open_rows",
        2,
        32,
    )
    gathered[0][1:] = [x.reshape(-1, width) for x in rest]
    place_rows = place_rows.reshape(tok_count, width)
    small = small[:small_count].astype(jnp.float32)
    place_state = jnp.broadcast_to(place_rows.astype(jnp.float32), (seqs, tok_count, width))
    state = fetch(0, given) + place_state.reshape(local_rows, width)

    def fetch_more(at, held):
        rows = dot_plain(one_hot(asked_rows(at), table_local, 1), table_own).astype(jnp.bfloat16)
        return held + fetch(at, swap(rows.reshape(total, SLOTS, width), "swap_rows", 1))

    state = lax.fori_loop(1, rounds, fetch_more, state)

    query_ids = lax.dynamic_slice_in_dim(block_ids[0], seq_at * tok_count, tok_count, 0)
    inputs, kept, saved = [], [], []
    for layer_at in range(layers):
        weights = gathered[layer_at]
        inputs.append(state)
        kept.append(weights)
        state, held = layer_forward(
            state,
            weights,
            small[12 * layer_at : 12 * layer_at + 12],
            query_ids,
            block_ids[0],
        )
        saved.append(held)
    final_gain = small[12 * layers]
    final_shift = small[12 * layers + 1]
    final = layer_norm(state, final_gain, final_shift).astype(jnp.bfloat16)

    group_mask = completion[0]
    slot_of = regroup[0]
    slots = slot_of.shape[0]
    comp_rows = slots // shards
    rank_all = counts_before(group_mask[None])[0]
    mine = lax.dynamic_slice_in_dim(group_mask, shard_at * local_rows, local_rows)
    my_rank = lax.dynamic_slice_in_dim(rank_all, shard_at * local_rows, local_rows)
    my_slot = jnp.sum(
        jnp.where(my_rank[:, None] == jnp.arange(slots)[None, :], slot_of[None, :], 0), 1
    )
    to_slot = one_hot(jnp.where(mine == 1, my_slot, -1), slots, 0)
    outgoing = dot_plain(to_slot, final).astype(jnp.bfloat16).reshape(shards, comp_rows, width)
    two_ways = [seq_bits[1:] + dp_bits, dp_bits + seq_bits[1:]]
    head_in = exchange(
        outgoing,
        "share_final",
        5,
        sum_axes=("shard",),
        sum_orders=[shard_bits, shard_bits],
        join_axes=AXES,
        join_orders=[shard_bits[::-1] + way[::-1] + seq_bits[:1] for way in two_ways],
        chunks=2,
    ).reshape(-1, width)

    rows_all = targets.shape[0]
    columns = first_row + jnp.arange(table_local, dtype=jnp.int32)
    live = (columns < VOCAB)[None, :]
    logits = dot_rows(head_in, table_own)
    masked = jnp.where(live, logits, MASK_FILL)
    top_local = jnp.max(masked, 1)
    total_local = jnp.sum(jnp.where(live, jnp.exp(masked - top_local[:, None]), 0.0), 1)
    target_hit = columns[None, :] == targets[:, None]
    pick_local = jnp.sum(jnp.where(target_hit, logits, 0.0), 1)
    stats = combine_all(
        jnp.stack([top_local, total_local, pick_local]).reshape(3, -1, 128),
        merge_soft,
        "share_stats",
        6,
    ).reshape(3, rows_all)
    log_total = stats[0] + jnp.log(stats[1])
    loss_value = jnp.sum(log_total - stats[2]) / rows_all
    probs = jnp.where(live, jnp.exp(masked - log_total[:, None]), 0.0)
    logit_grad = ((probs - target_hit.astype(jnp.float32)) / rows_all).astype(jnp.bfloat16)
    head_grad = dot_cols(logit_grad, head_in)
    returned = exchange(
        dot_plain(logit_grad, table_own).reshape(total, comp_rows, width),
        "return_final",
        7,
        sum_axes=AXES,
        sum_orders=[seq_bits[:1] + way + shard_bits for way in two_ways],
        join_axes=("shard",),
        join_orders=[shard_bits[::-1], shard_bits[::-1]],
        chunks=2,
    ).reshape(slots, width)
    final_grad = dot_cols(to_slot, returned)
    state_grad, gain_final, shift_final = norm_back(state, final_gain, final_shift, final_grad)

    mats_grads = {}
    late = []
    arrived = []
    small_grads = [None] * layers
    for layer_at in reversed(range(layers)):
        state_grad, factors, small_grads[layer_at] = layer_backward(
            inputs[layer_at],
            kept[layer_at],
            small[12 * layer_at : 12 * layer_at + 12],
            saved[layer_at],
            query_ids,
            block_ids[0],
            state_grad,
            arrived,
        )
        late.append(factors[0])
        if layer_at > 0:
            arrived = [scatter_rows(*factors[k][0]) for k in (2, 1)]
        else:
            late += factors[1:]

    low_grad = state_grad.astype(jnp.bfloat16)
    place_grad = jnp.sum(state_grad.reshape(seqs, tok_count, width), 0)
    small_grad = pad_rows(
        jnp.concatenate(small_grads + [jnp.stack([gain_final, shift_final])], 0), small_rows
    )

    def leaving(at):
        rows = dot_cols(one_hot(own_slots(at), total * SLOTS, 1), low_grad).astype(jnp.bfloat16)
        return rows.reshape(total, SLOTS, width)

    (low_grad, arrived[1]) = lax.optimization_barrier((low_grad, arrived[1]))
    mats_grads[1, 2], mats_grads[1, 1] = (x.astype(jnp.float32) for x in arrived)
    late = late_mats(late, 12)
    fits = mats_fit(late)
    own_mats, (place_grad,), (small_grad,), (came,) = run_jobs(
        [
            mats_job(late[:fits]),
            sum_job(
                place_grad.reshape(replicas * shards, piece, width),
                sum_axes=("dp", "shard"),
                sum_orders=[dp_bits + shard_bits],
                join_axes=("seq", "dp", "shard"),
                join_orders=[shard_bits[::-1] + dp_bits[::-1] + seq_bits[::-1]],
            ),
            combine_job(small_grad, add_pair),
            swap_job(leaving(0), late=5),
        ],
        "close_rows",
        10,
        61,
    )
    for k in range(fits, len(late), fits):
        own_mats = own_mats + run_jobs([mats_job(late[k : k + fits])], "sum_mats", 14 + k, 61)[0]
    own_mats = list(own_mats)
    for layer_at in reversed(range(layers)):
        mats_grads[layer_at, 0] = own_mats.pop(0)
    mats_grads[0, 1], mats_grads[0, 2] = own_mats
    place_grad = place_grad.reshape(seq_length, width)
    small_high = small_grad.astype(jnp.bfloat16)
    small_low = (small_grad - small_high.astype(jnp.float32)).astype(jnp.bfloat16)
    values = jnp.concatenate([came.reshape(-1, width), place_grad, small_high, small_low], 0)
    value_row = jnp.concatenate([wanted, fixed_row[seq_length:]])
    table_grad = dot_plain(one_hot(value_row, table_local, 0), values) + head_grad

    def return_more(at, held):
        rows = swap(leaving(at), "swap_rows", 1).reshape(-1, width)
        return held + dot_plain(one_hot(asked_rows(at), table_local, 0), rows)

    table_grad = lax.fori_loop(1, rounds, return_more, table_grad)
    mats_grad = jnp.stack(
        [jnp.stack([mats_grads[layer_at, k] for k in range(3)]) for layer_at in range(layers)]
    )
    local_squares = jnp.sum(mats_grad * mats_grad) + jnp.sum(table_grad * table_grad)
    squares = combine_all(jnp.full((8, 128), local_squares), add_pair, "share_norm", 11)
    grad_norm = jnp.sqrt(squares[0, 0])
    factor = CLIP_NORM / grad_norm
    step = step_count[0].astype(jnp.float32)
    new_mats = adam_step(
        layer_mats, mats_moment, mats_square, factor * mats_grad, RATE_MATS, DECAY_RATE, step
    )
    plain_rows = (columns < VOCAB + seq_length)[:, None]
    rate = jnp.where(plain_rows, RATE_TABLE, RATE_SMALL)
    decay = jnp.where(plain_rows, DECAY_RATE, 0.0)
    new_table = adam_step(
        embed_table, table_moment, table_square, factor * table_grad, rate, decay, step
    )
    return (
        loss_value.reshape(1),
        grad_norm.reshape(1),
        new_mats[0],
        new_mats[1],
        new_mats[2],
        new_table[0],
        new_table[1],
        new_table[2],
    )


def solution(mesh):
    in_specs = (
        P(("dp", "shard"), "seq"),
        P(("dp", "shard"), None),
        P(("dp", "seq"), None),
        P(("dp", "seq"), None),
        P(),
        P(),
        P(None, None, ("dp", "seq", "shard"), None),
        P(None, None, ("dp", "seq", "shard"), None),
        P(None, None, ("dp", "seq", "shard"), None),
        P(("dp", "seq", "shard"), None),
        P(("dp", "seq", "shard"), None),
        P(("dp", "seq", "shard"), None),
    )
    out_specs = (
        P(),
        P(),
        P(None, None, ("dp", "seq", "shard"), None),
        P(None, None, ("dp", "seq", "shard"), None),
        P(None, None, ("dp", "seq", "shard"), None),
        P(("dp", "seq", "shard"), None),
        P(("dp", "seq", "shard"), None),
        P(("dp", "seq", "shard"), None),
    )
    return jax.shard_map(
        on_device, mesh=mesh, in_specs=in_specs, out_specs=out_specs, check_vma=False
    )
```

```python
import itertools
from functools import partial

import jax
import jax.numpy as jnp
from jax import lax
from jax.experimental import pallas as pl
from jax.experimental.layout import Layout, with_layout_constraint
from jax.experimental.pallas import tpu as pltpu
from jax.sharding import PartitionSpec as P

HEADS = 17
HEAD = 64
VOCAB = 50278

NORM_EPS = 1e-05
CLIP_NORM = 0.02
BETA_ONE = 0.9
BETA_TWO = 0.95
ADAM_EPS = 1e-08
DECAY_RATE = 0.1
RATE_MATS = 0.05
RATE_TABLE = 0.1
RATE_SMALL = 0.5
MASK_FILL = -1e30

AXES = ("dp", "seq", "shard")
MESH = pl.DeviceIdType.MESH
SLOTS = 24


def bits_of(axis):
    return [(axis, b) for b in range(lax.axis_size(axis).bit_length() - 1)]


def bit_here(bit):
    return lax.rem(lax.axis_index(bit[0]) // 2 ** bit[1], 2)


def partner(bit):
    at = lax.axis_index(bit[0])
    return {bit[0]: at + (1 - 2 * bit_here(bit)) * 2 ** bit[1]}


def greet(bits):
    barrier = pltpu.get_barrier_semaphore()
    for bit in bits:
        pl.semaphore_signal(barrier, inc=1, device_id=partner(bit), device_id_type=MESH)
    pl.semaphore_wait(barrier, len(bits))


def block_weight(axes, bit):
    weight = 2 ** bit[1]
    for axis in axes[axes.index(bit[0]) + 1 :]:
        weight *= lax.axis_size(axis)
    return weight


def block_runs(weights):
    weights = sorted(weights)
    joined = 0
    while joined < len(weights) and weights[joined] == 2**joined:
        joined += 1
    rest = [(0, w) for w in weights[joined:]]
    return 2**joined, [sum(c) for c in itertools.product(*rest)]


class Job:
    def __init__(
        self, inputs, outputs, scratch, sends, keeps, bits, steps, spaces=(pltpu.VMEM, pltpu.VMEM)
    ):
        self.inputs, self.outputs, self.scratch = inputs, outputs, scratch
        self.sends, self.keeps, self.bits, self.steps, self.spaces = sends, keeps, bits, steps, spaces


def me_and_total():
    seq_size, shard_size = lax.axis_size("seq"), lax.axis_size("shard")
    at = (lax.axis_index("dp") * seq_size + lax.axis_index("seq")) * shard_size
    return at + lax.axis_index("shard"), lax.axis_size("dp") * seq_size * shard_size


def place_of(at):
    seq_size, shard_size = lax.axis_size("seq"), lax.axis_size("shard")
    return {
        "dp": at // (seq_size * shard_size),
        "seq": lax.rem(at // shard_size, seq_size),
        "shard": lax.rem(at, shard_size),
    }


def greet_all():
    me, total = me_and_total()
    barrier = pltpu.get_barrier_semaphore()

    def hello(k, carry):
        pl.semaphore_signal(
            barrier, inc=1, device_id=place_of(lax.rem(me + k, total)), device_id_type=MESH
        )
        return carry

    lax.fori_loop(1, total, hello, 0)
    pl.semaphore_wait(barrier, total - 1)


class Sems:
    def __init__(self, send, recv, keep):
        self.send, self.recv, self.keep = send, recv, keep
        self.used = self.kept = 0

    def copy(self, source, target, device):
        k = self.used
        self.used += 1
        copy = pltpu.make_async_remote_copy(
            source, target, self.send.at[k], self.recv.at[k], device_id=device, device_id_type=MESH
        )
        copy.start()
        return copy

    def local(self, source, target):
        k = self.kept
        self.kept += 1
        copy = pltpu.make_async_copy(source, target, self.keep.at[k])
        copy.start()
        return copy

    def span(self, count):
        first = self.used
        self.used += count
        return first


def jobs_kernel(jobs, *refs):
    refs = list(refs)

    def take(count):
        out = refs[:count]
        del refs[:count]
        return out

    held = [take(len(job.inputs)) for job in jobs]
    made = [take(len(job.outputs)) for job in jobs]
    used = [take(len(job.scratch)) for job in jobs]
    sems = Sems(*refs)
    if any(job.bits is None for job in jobs):
        greet_all()
    else:
        greet(sorted(set(bit for job in jobs for bit in job.bits)))
    active = []
    for job, x, o, w in zip(jobs, held, made, used):
        active += job.steps(x, o, w, sems)
    tick = 0
    while active:
        left = []
        for delay, gen in active:
            if delay > tick or next(gen, "end") != "end":
                left.append((delay, gen))
        active = left
        tick += 1


def run_jobs(jobs, name, number, vmem=60):
    inputs = [x for job in jobs for x in job.inputs]
    outputs = [o for job in jobs for o in job.outputs]
    in_specs = [pl.BlockSpec(memory_space=job.spaces[0]) for job in jobs for unused in job.inputs]
    out_specs = [pl.BlockSpec(memory_space=job.spaces[1]) for job in jobs for unused in job.outputs]
    sends = sum(job.sends for job in jobs)
    keeps = max(1, sum(job.keeps for job in jobs))
    flat = pl.pallas_call(
        partial(jobs_kernel, jobs),
        out_shape=outputs,
        in_specs=in_specs,
        out_specs=out_specs,
        scratch_shapes=[w for job in jobs for w in job.scratch]
        + [
            pltpu.SemaphoreType.DMA((sends,)),
            pltpu.SemaphoreType.DMA((sends,)),
            pltpu.SemaphoreType.DMA((keeps,)),
        ],
        compiler_params=pltpu.CompilerParams(
            collective_id=number, has_side_effects=True, vmem_limit_bytes=vmem * 2**20
        ),
        name=name,
    )(*inputs)
    out = []
    for job in jobs:
        out.append(flat[: len(job.outputs)])
        flat = flat[len(job.outputs) :]
    return out


def sum_stream(x_ref, o_ref, scratch, sems, rows, first_slot, sum_axes, sums, join_axes, joins):
    source = x_ref
    slot = first_slot
    if sums:
        work, parcel, recv = scratch
    for step, bit in enumerate(sums):
        base = sum(bit_here(b) * block_weight(sum_axes, b) for b in sums[:step])
        weight = block_weight(sum_axes, bit)
        mine = bit_here(bit)
        size, offsets = block_runs([block_weight(sum_axes, b) for b in sums[step + 1 :]])
        started = []
        for offset in offsets:
            leave = base + (1 - mine) * weight + offset
            if source.dtype == parcel.dtype:
                packed = source.at[pl.ds(leave, size), rows]
            else:

                def pack(i, carry, leave=leave, at=slot, source=source):
                    parcel[at + i, rows] = source[leave + i, rows].astype(parcel.dtype)
                    return carry

                lax.fori_loop(0, size, pack, 0)
                packed = parcel.at[pl.ds(slot, size), rows]
            copy = sems.copy(packed, recv.at[pl.ds(slot, size), rows], partner(bit))
            started.append((copy, base + mine * weight + offset, slot, size))
            slot += size
        yield
        for copy, keep, at, size in started:
            copy.wait()

            def add(i, carry, keep=keep, at=at, source=source):
                total = source[keep + i, rows].astype(jnp.float32)
                total = total + recv[at + i, rows].astype(jnp.float32)
                work[keep + i, rows] = total.astype(work.dtype)
                return carry

            lax.fori_loop(0, size, add, 0)
        source = work
    own = sum(bit_here(b) * block_weight(sum_axes, b) for b in sums) if sums else 0
    result = source[own, rows].astype(o_ref.dtype)
    if not joins:
        o_ref[rows] = result
        return
    o_ref[sum(bit_here(b) * block_weight(join_axes, b) for b in joins), rows] = result
    for step, bit in enumerate(joins):
        base = sum(bit_here(b) * block_weight(join_axes, b) for b in joins[step:])
        size, offsets = block_runs([block_weight(join_axes, b) for b in joins[:step]])
        started = []
        for offset in offsets:
            here = o_ref.at[pl.ds(base + offset, size), rows]
            started.append(sems.copy(here, here, partner(bit)))
        yield
        for copy in started:
            copy.wait()


def sum_job(x, sum_axes=(), sum_orders=(), join_axes=(), join_orders=(), chunks=1):
    rows, width = x.shape[-2:]
    blocks = 1
    for axis in join_axes:
        blocks *= lax.axis_size(axis)
    kind = jnp.bfloat16 if sum_axes else x.dtype
    streams = max(len(sum_orders), len(join_orders))
    if rows % (streams * chunks * 16):
        chunks = 1
    share = rows // (streams * chunks)
    sends = 0
    for order in sum_orders:
        for step in range(len(order)):
            sends += len(block_runs([block_weight(sum_axes, b) for b in order[step + 1 :]])[1])
    for order in join_orders:
        for step in range(len(order)):
            sends += len(block_runs([block_weight(join_axes, b) for b in order[:step]])[1])
    scratch = []
    if sum_axes:
        if x.size * 14 > 56 * 2**20:
            x = x.astype(jnp.bfloat16)
        exact = x.dtype == jnp.float32 or x.size < 2**22
        scratch = [
            pltpu.VMEM(x.shape, jnp.float32 if exact else kind),
            pltpu.VMEM(x.shape, kind),
            pltpu.VMEM(x.shape, kind),
        ]

    def steps(x_refs, o_refs, scratch_refs, sems):
        gens = []
        for c in range(chunks):
            for k in range(streams):
                rows_here = pl.ds((k * chunks + c) * share, share)
                sums = sum_orders[k] if sum_orders else []
                joins = join_orders[k] if join_orders else []
                gens.append(
                    (
                        c,
                        sum_stream(
                            x_refs[0], o_refs[0], scratch_refs, sems, rows_here, 0,
                            sum_axes, sums, join_axes, joins,
                        ),
                    )
                )
        return gens

    bits = set(bit for order in list(sum_orders) + list(join_orders) for bit in order)
    shape = (blocks, rows, width) if join_axes else (rows, width)
    return Job(
        [x], [jax.ShapeDtypeStruct(shape, kind)], scratch, sends * chunks, 0, bits, steps
    )


def exchange(x, name, number, **how):
    return run_jobs([sum_job(x, **how)], name, number)[0][0]


def combine_job(x, combine):
    bits = [bit for axis in reversed(AXES) for bit in bits_of(axis)]
    slots = (len(bits),) + x.shape

    def steps(x_refs, o_refs, scratch, sems):
        out_buf, in_buf = scratch

        def gen():
            current = x_refs[0][...]
            for i, bit in enumerate(bits):
                out_buf[i] = current
                copy = sems.copy(out_buf.at[i], in_buf.at[i], partner(bit))
                yield
                copy.wait()
                current, other = out_buf[i], in_buf[i]
                low = bit_here(bit) == 0
                current = combine(jnp.where(low, current, other), jnp.where(low, other, current))
            o_refs[0][...] = current

        return [(0, gen())]

    return Job(
        [x],
        [jax.ShapeDtypeStruct(x.shape, x.dtype)],
        [pltpu.VMEM(slots, x.dtype), pltpu.VMEM(slots, x.dtype)],
        len(bits),
        0,
        bits,
        steps,
    )


def combine_all(x, combine, name, number):
    return run_jobs([combine_job(x, combine)], name, number, 16)[0][0]


def swap_job(x, late=0):
    total = x.shape[0]

    def steps(x_refs, o_refs, scratch, sems):
        x_ref, o_ref = x_refs[0], o_refs[0]

        def gen():
            me, unused = me_and_total()
            first = sems.span(total)
            keep = sems.local(x_ref.at[me], o_ref.at[me])

            def copy_to(other, here):
                return pltpu.make_async_remote_copy(
                    x_ref.at[other],
                    o_ref.at[here],
                    sems.send.at[first + other],
                    sems.recv.at[first + here],
                    device_id=place_of(other),
                    device_id_type=MESH,
                )

            def send(k, carry):
                copy_to(lax.rem(me + k, total), me).start()
                return carry

            lax.fori_loop(1, total, send, 0)
            for unused in range(late + 1):
                yield

            def finish(k, carry):
                other = lax.rem(me + k, total)
                copy_to(other, other).wait()
                return carry

            lax.fori_loop(1, total, finish, 0)
            keep.wait()

        return [(0, gen())]

    return Job(
        [x],
        [jax.ShapeDtypeStruct(x.shape, x.dtype)],
        [],
        total,
        1,
        None,
        steps,
        spaces=(pl.ANY, pl.ANY),
    )


def swap(x, name, number):
    return run_jobs([swap_job(x)], name, number, 16)[0][0]


def sum_orders_for(rows):
    across, along, deep = bits_of("seq")[1:], bits_of("dp"), bits_of("shard")
    if rows < 64 or rows % 8:
        return [(0, rows)], [across + along + deep]
    one, two = rows * 8 // 17 // 16 * 16, rows * 6 // 17 // 16 * 16
    spans = [(0, one), (one, two), (one + two, rows - one - two)]
    return spans, [across + along + deep, along + across + deep, deep + along + across]


def mats_stream(x_ref, o_ref, scratch, sems, m, span, order, weights):
    kept, work, parcel, recv = scratch
    turn, m = m % 2, m % work.shape[0]
    steps = len(order)
    rows = pl.ds(*span)
    slot = 0
    rest = sorted((b for b in weights if b != order[0]), key=lambda b: weights[b])
    small = {b: 2**k for k, b in enumerate(rest)}
    for step, bit in enumerate(order):
        mine = bit_here(bit)
        base = sum(bit_here(b) * small[b] for b in order[1:step])
        runs, keeps = [], []
        if step == 0:
            size, offsets = block_runs([weights[b] for b in order[1:]])
            for offset in offsets:
                left, place = offset, 0
                for b in reversed(rest):
                    if left >= weights[b]:
                        left -= weights[b]
                        place += small[b]
                keeps.append(
                    sems.local(
                        x_ref.at[pl.ds(mine * weights[bit] + offset, size), rows],
                        kept.at[turn, pl.ds(place, size), rows],
                    )
                )
                runs.append(((1 - mine) * weights[bit] + offset, place))
        else:
            size, offsets = block_runs([small[b] for b in order[step + 1 :]])
            for offset in offsets:
                here = base + offset
                runs.append((here + (1 - mine) * small[bit], here + mine * small[bit]))
        started = []
        for leave, keep_at in runs:
            at = slot
            slot += size
            if step == 0:
                packed = x_ref.at[pl.ds(leave, size), rows]
            else:
                spot = at - 2 ** (steps - 1)

                def pack(i, carry, leave=leave, spot=spot):
                    parcel[m, spot + i, rows] = work[m, leave + i, rows].astype(parcel.dtype)
                    return carry

                lax.fori_loop(0, size, pack, 0)
                packed = parcel.at[m, pl.ds(spot, size), rows]
            copy = sems.copy(packed, recv.at[m, pl.ds(at, size), rows], partner(bit))
            started.append((copy, at, keep_at, size))
        yield
        for keep in keeps:
            keep.wait()
        for copy, at, keep_at, size in started:
            copy.wait()

            def add(i, carry, at=at, keep_at=keep_at, step=step):
                if step == 0:
                    total = kept[turn, keep_at + i, rows].astype(jnp.float32)
                else:
                    total = work[m, keep_at + i, rows]
                work[m, keep_at + i, rows] = total + recv[m, at + i, rows].astype(jnp.float32)
                return carry

            lax.fori_loop(0, size, add, 0)
    o_ref[rows] = work[m, sum(bit_here(b) * small[b] for b in order[1:]), rows]


def mats_job(mats):
    blocks, rows, width = mats[0].shape
    spans, orders = sum_orders_for(rows)
    weights = {}
    for bit in orders[0]:
        weight = block_weight(AXES, bit)
        weights[bit] = weight if bit[0] == "shard" else weight // 2
    keeps = sends = 0
    for order in orders:
        keeps += len(block_runs([weights[b] for b in order[1:]])[1])
        sends += len(block_runs([weights[b] for b in order[1:]])[1])
        rest = sorted((b for b in weights if b != order[0]), key=lambda b: weights[b])
        small = {b: 2**k for k, b in enumerate(rest)}
        for step in range(1, len(order)):
            sends += len(block_runs([small[b] for b in order[step + 1 :]])[1])
    count = len(mats)

    def steps(x_refs, o_refs, scratch, sems):
        return [
            (m, mats_stream(x_refs[m], o_refs[m], scratch, sems, m, spans[k], orders[k], weights))
            for m in range(count)
            for k in range(len(orders))
        ]

    return Job(
        mats,
        [jax.ShapeDtypeStruct((rows, width), jnp.float32)] * count,
        [
            pltpu.VMEM((min(2, count), blocks // 2, rows, width), jnp.bfloat16),
            pltpu.VMEM((min(3, count), blocks // 2, rows, width), jnp.float32),
            pltpu.VMEM((min(3, count), blocks // 2 - 1, rows, width), jnp.bfloat16),
            pltpu.VMEM((min(3, count), blocks - 1, rows, width), jnp.bfloat16),
        ],
        count * sends,
        count * keeps,
        set(orders[0]),
        steps,
        spaces=(pl.ANY, pltpu.VMEM),
    )


def trade_kernel(count, *refs):
    x_refs, o_refs = refs[:count], refs[count : 2 * count]
    send_sems, recv_sems = refs[2 * count :]
    bit = ("seq", 0)
    greet([bit])
    copies = []
    for k in range(count):
        copy = pltpu.make_async_remote_copy(
            x_refs[k],
            o_refs[k],
            send_sems.at[k],
            recv_sems.at[k],
            device_id=partner(bit),
            device_id_type=MESH,
        )
        copy.start()
        copies.append(copy)
    for copy in copies:
        copy.wait()


def trade(arrays, name, number):
    count = len(arrays)
    return pl.pallas_call(
        partial(trade_kernel, count),
        out_shape=[jax.ShapeDtypeStruct(x.shape, x.dtype) for x in arrays],
        in_specs=[pl.BlockSpec(memory_space=pl.ANY)] * count,
        out_specs=[pl.BlockSpec(memory_space=pl.ANY)] * count,
        scratch_shapes=[pltpu.SemaphoreType.DMA((count,)), pltpu.SemaphoreType.DMA((count,))],
        compiler_params=pltpu.CompilerParams(collective_id=number, has_side_effects=True),
        name=name,
    )(*arrays)


def my_rows(features, own):
    rows = features.shape[0]
    parts = features.reshape(rows, -1, 2, own)
    at = lax.rem(lax.axis_index("seq"), 2)
    mine = lax.dynamic_index_in_dim(parts, at, 2, keepdims=False)
    other = lax.dynamic_index_in_dim(parts, 1 - at, 2, keepdims=False)
    return mine.reshape(rows, -1), other.reshape(rows, -1)


def late_mats(groups, number):
    pairs = [pair for group in groups for pair in group]
    total = lax.axis_size(AXES)
    height = sum(features.shape[1] for features, unused in groups[0])
    own = height // total * lax.axis_size("shard")
    halves = [my_rows(features, own) for features, unused in pairs]
    tails = [tail for unused, tail in pairs]
    got = trade([other for unused, other in halves] + tails, "trade_rows", number)
    parts = []
    for k, (mine, unused) in enumerate(halves):
        grad = dot_cols(
            jnp.concatenate([mine, got[k]], 0),
            jnp.concatenate([tails[k], got[len(halves) + k]], 0),
        )
        parts.append(rows_major(grad.astype(jnp.bfloat16)))
    mats = []
    for group in groups:
        grad = jnp.concatenate(parts[: len(group)], 0) if len(group) > 1 else parts[0]
        parts = parts[len(group) :]
        mats.append(grad.reshape(total // 2, -1, grad.shape[1]))
    return mats


def mats_fit(mats):
    blocks, rows, width = mats[0].shape
    tile = -(-rows // 16) * 16 * -(-width // 128) * 128
    fits = (50 * 2**20 - tile * blocks * 2) // (tile * blocks * 5)
    return len(mats) if fits >= 3 else max(1, fits)


def head_lanes(half, shape):
    lane = lax.broadcasted_iota(jnp.int32, shape, 1)
    return (lane < HEAD) if half == 0 else (lane >= HEAD)


def pair_lanes(p):
    return pl.ds(pl.multiple_of(p * 2 * HEAD, 2 * HEAD), 2 * HEAD)


def seq_places():
    me = lax.axis_index("seq")
    return me, partner(("seq", 0))["seq"], partner(("seq", 1))["seq"]


def to_seq(source, target, sems, k, place):
    return pltpu.make_async_remote_copy(
        source,
        target,
        sems.at[0, k],
        sems.at[1, k],
        device_id={"seq": place},
        device_id_type=MESH,
    )


def attend_kernel(
    q_ref, own_ref, key_ids_ref, query_ids_ref, o_ref, lse_ref, kv_ref, blocked, far, near, pass_on, own_sem
):
    rows = own_ref.shape[0] // 2
    keys = kv_ref.shape[0] * rows
    pairs = q_ref.shape[1] // (2 * HEAD)
    me, near_at, far_at = seq_places()
    beyond = near_at + far_at - me
    greet([("seq", 0), ("seq", 1)])

    def far_copy(p, at):
        return to_seq(own_ref.at[:, pair_lanes(p)], kv_ref.at[at, :, pair_lanes(p)], far, p, far_at)

    def near_copy(p, at):
        return to_seq(own_ref.at[:, pair_lanes(p)], kv_ref.at[at, :, pair_lanes(p)], near, p, near_at)

    def pass_copy(p, at):
        here = kv_ref.at[far_at, :, pair_lanes(p)]
        return to_seq(here, kv_ref.at[at, :, pair_lanes(p)], pass_on, p, near_at)

    def send(p, carry):
        far_copy(p, me).start()
        near_copy(p, me).start()
        return carry

    lax.fori_loop(0, pairs, send, 0)
    own = pltpu.make_async_copy(own_ref, kv_ref.at[me], own_sem)
    own.start()
    blocked[...] = jnp.where(key_ids_ref[...] <= query_ids_ref[...], 0.0, MASK_FILL)
    own.wait()

    def forward_one(p):
        far_copy(p, far_at).wait_recv()
        pass_copy(p, far_at).start()

    forward_one(0)

    def pair(p, carry):
        @pl.when(p + 1 < pairs)
        def _():
            forward_one(p + 1)

        near_copy(p, near_at).wait_recv()
        pass_copy(p, beyond).wait_recv()
        lanes = pair_lanes(p)
        key_pair = kv_ref[:, :rows, lanes].reshape(keys, 2 * HEAD)
        val_turned = kv_ref[:, rows:, lanes].reshape(keys, 2 * HEAD).T
        query_pair = q_ref[:, lanes]
        outs = []
        for half in range(2):
            query = jnp.where(head_lanes(half, query_pair.shape), query_pair, 0)
            scores = dot_rows(key_pair, query.astype(jnp.bfloat16)) * HEAD ** (-0.5) + blocked[...]
            top = jnp.max(scores, 0, keepdims=True)
            raised = jnp.exp(scores - top)
            total = jnp.sum(raised, 0, keepdims=True)
            probs = (raised * (1.0 / total)).astype(jnp.bfloat16)
            outs.append(dot_plain(val_turned[half * HEAD : (half + 1) * HEAD], probs))
            lse_ref[p, half] = (top + jnp.log(total))[0]
        o_ref[:, lanes] = jnp.concatenate(outs, 0).T.astype(o_ref.dtype)
        return carry

    lax.fori_loop(0, pairs, pair, 0)

    def sent(p, carry):
        far_copy(p, me).wait_send()
        near_copy(p, me).wait_send()
        pass_copy(p, far_at).wait_send()
        return carry

    lax.fori_loop(0, pairs, sent, 0)


def attend(queries, own_pair, key_ids, query_ids, number):
    rows, width = queries.shape
    keys = key_ids.shape[0]
    pairs = width // (2 * HEAD)
    groups = lax.axis_size("seq")
    copies = pltpu.SemaphoreType.DMA((2, pairs))
    return pl.pallas_call(
        attend_kernel,
        out_shape=(
            jax.ShapeDtypeStruct((rows, width), jnp.bfloat16),
            jax.ShapeDtypeStruct((pairs, 2, rows), jnp.float32),
            jax.ShapeDtypeStruct((groups,) + own_pair.shape, jnp.bfloat16),
        ),
        in_specs=[pl.BlockSpec(memory_space=pltpu.VMEM)] * 4,
        out_specs=(pl.BlockSpec(memory_space=pltpu.VMEM),) * 3,
        scratch_shapes=[
            pltpu.VMEM((keys, rows), jnp.float32),
            copies,
            copies,
            copies,
            pltpu.SemaphoreType.DMA,
        ],
        compiler_params=pltpu.CompilerParams(
            collective_id=number, has_side_effects=True, vmem_limit_bytes=48 * 2**20
        ),
        cost_estimate=pl.CostEstimate(
            flops=4 * rows * keys * width,
            transcendentals=rows * keys * HEADS,
            bytes_accessed=4 * keys * width,
        ),
        name="attend",
    )(queries, own_pair, key_ids[:, None], query_ids[None, :])


def attend_back_kernel(
    q_ref,
    kv_ref,
    grad_ref,
    lse_ref,
    key_ids_ref,
    query_ids_ref,
    dq_ref,
    own_ref,
    blocked,
    fresh,
    kept,
    near_out,
    near_in,
    far_out,
    far_in,
    near,
    far,
):
    groups, twice, unused = kv_ref.shape
    rows = twice // 2
    keys = groups * rows
    pairs = q_ref.shape[1] // (2 * HEAD)
    scale = HEAD ** (-0.5)
    me, near_at, far_at = seq_places()
    low, high = lax.rem(me, 2), me // 2
    greet([("seq", 0), ("seq", 1)])
    blocked[...] = jnp.where(key_ids_ref[...] <= query_ids_ref[...], 0.0, MASK_FILL)

    def near_copy(p):
        return to_seq(near_out.at[p], near_in.at[p], near, p, near_at)

    def far_copy(p):
        return to_seq(far_out.at[p], far_in.at[p], far, p, far_at)

    def middle(p):
        near_copy(p).wait()
        for k in range(2):
            kept[p, k] = kept[p, k] + near_in[p, k].astype(jnp.float32)
        far_out[p] = kept[p, 1 - high].astype(far_out.dtype)
        far_copy(p).start()

    def last(p):
        far_copy(p).wait()
        total = kept[p, high] + far_in[p].astype(jnp.float32)
        own_ref[:, pair_lanes(p)] = total.astype(own_ref.dtype)

    def pair(p, carry):
        lanes = pair_lanes(p)
        key_pair = kv_ref[:, :rows, lanes].reshape(keys, 2 * HEAD)
        val_pair = kv_ref[:, rows:, lanes].reshape(keys, 2 * HEAD)
        key_turned = key_pair.T
        query_pair = q_ref[:, lanes]
        grad_pair = grad_ref[:, lanes]
        key_grad = jnp.zeros((keys, 2 * HEAD), jnp.float32)
        val_grad = jnp.zeros((keys, 2 * HEAD), jnp.float32)
        outs = []
        for half in range(2):
            here = head_lanes(half, query_pair.shape)
            query = jnp.where(here, query_pair, 0).astype(jnp.bfloat16)
            grad = jnp.where(here, grad_pair, 0).astype(jnp.bfloat16)
            scores = dot_rows(key_pair, query) * scale + blocked[...]
            probs = jnp.exp(scores - lse_ref[p, half][None, :])
            prob_grad = dot_rows(val_pair, grad)
            inner = jnp.sum(probs * prob_grad, 0, keepdims=True)
            score_grad = (probs * (prob_grad - inner)).astype(jnp.bfloat16)
            key_grad = key_grad + dot_plain(score_grad, query)
            val_grad = val_grad + dot_plain(probs.astype(jnp.bfloat16), grad)
            outs.append(dot_plain(key_turned[half * HEAD : (half + 1) * HEAD], score_grad))
        dq_ref[:, lanes] = (jnp.concatenate(outs, 0).T * scale).astype(dq_ref.dtype)
        fresh[:, :rows] = (key_grad * scale).reshape(groups, rows, 2 * HEAD)
        fresh[:, rows:] = val_grad.reshape(groups, rows, 2 * HEAD)
        for k in range(2):
            near_out[p, k] = fresh[2 * k + 1 - low].astype(near_out.dtype)
            kept[p, k] = fresh[2 * k + low]
        near_copy(p).start()

        @pl.when(p >= 1)
        def _():
            middle(p - 1)

        @pl.when(p >= 2)
        def _():
            last(p - 2)

        return carry

    lax.fori_loop(0, pairs, pair, 0)
    middle(pairs - 1)
    last(pairs - 2)
    last(pairs - 1)


def attend_back(queries, key_vals, grad, lse, key_ids, query_ids, number):
    rows, width = queries.shape
    keys = key_ids.shape[0]
    pairs = width // (2 * HEAD)
    piece = (2 * rows, 2 * HEAD)
    copies = pltpu.SemaphoreType.DMA((2, pairs))
    return pl.pallas_call(
        attend_back_kernel,
        out_shape=(
            jax.ShapeDtypeStruct((rows, width), jnp.bfloat16),
            jax.ShapeDtypeStruct((2 * rows, width), jnp.bfloat16),
        ),
        in_specs=[pl.BlockSpec(memory_space=pltpu.VMEM)] * 6,
        out_specs=(pl.BlockSpec(memory_space=pltpu.VMEM),) * 2,
        scratch_shapes=[
            pltpu.VMEM((keys, rows), jnp.float32),
            pltpu.VMEM((lax.axis_size("seq"),) + piece, jnp.float32),
            pltpu.VMEM((pairs, 2) + piece, jnp.float32),
            pltpu.VMEM((pairs, 2) + piece, jnp.bfloat16),
            pltpu.VMEM((pairs, 2) + piece, jnp.bfloat16),
            pltpu.VMEM((pairs,) + piece, jnp.bfloat16),
            pltpu.VMEM((pairs,) + piece, jnp.bfloat16),
            copies,
            copies,
        ],
        compiler_params=pltpu.CompilerParams(
            collective_id=number, has_side_effects=True, vmem_limit_bytes=58 * 2**20
        ),
        cost_estimate=pl.CostEstimate(
            flops=10 * rows * keys * width,
            transcendentals=rows * keys * HEADS,
            bytes_accessed=12 * keys * width,
        ),
        name="attend_back",
    )(queries, key_vals, grad, lse, key_ids[:, None], query_ids[None, :])


def add_pair(first, second):
    return first + second


def merge_soft(first, second):
    highest = jnp.maximum(first[0], second[0])
    total = first[1] * jnp.exp(first[0] - highest) + second[1] * jnp.exp(second[0] - highest)
    return jnp.stack([highest, total, first[2] + second[2]])


def dot_rows(left_op, right_op):
    return lax.dot_general(
        left_op, right_op, (((1,), (1,)), ((), ())), preferred_element_type=jnp.float32
    )


def dot_cols(left_op, right_op):
    return lax.dot_general(
        left_op, right_op, (((0,), (0,)), ((), ())), preferred_element_type=jnp.float32
    )


def dot_plain(left_op, right_op):
    return jnp.dot(left_op, right_op, preferred_element_type=jnp.float32)


def column_sums(values):
    return jnp.sum(values.astype(jnp.float32), 0)


def layer_norm(values, gain, shift):
    center = values - jnp.mean(values, -1, keepdims=True)
    spread = jnp.mean(center * center, -1, keepdims=True)
    return center * lax.rsqrt(spread + NORM_EPS) * gain + shift


def norm_back(values, gain, shift, grad):
    unused, pull = jax.vjp(layer_norm, values, gain, shift)
    return pull(grad)


def one_hot(wanted, length, axis):
    shape = list(wanted.shape)
    shape.insert(axis, length)
    at = lax.broadcasted_iota(jnp.int32, shape, axis)
    return (at == jnp.expand_dims(wanted, axis)).astype(jnp.bfloat16)


def counts_before(flags):
    length = flags.shape[-1]
    earlier = (
        lax.broadcasted_iota(jnp.int32, (length, length), 0)
        < lax.broadcasted_iota(jnp.int32, (length, length), 1)
    ).astype(jnp.bfloat16)
    return dot_plain(flags.astype(jnp.bfloat16), earlier).astype(jnp.int32)


def wide(rows_in):
    return jnp.pad(rows_in, ((0, 0), (0, -rows_in.shape[1] % (2 * HEAD))))


def rows_major(x):
    return with_layout_constraint(x, Layout(major_to_minor=tuple(range(x.ndim))))


def scatter_rows(groups):
    total = lax.axis_size(AXES)
    mats = []
    for group in groups:
        parts = [rows_major(dot_cols(*pair).astype(jnp.bfloat16)) for pair in group]
        grad = jnp.concatenate(parts, 0) if len(parts) > 1 else parts[0]
        mats.append(grad.reshape(total, -1, grad.shape[1]))
    blocks = jnp.concatenate(mats, 1) if len(mats) > 1 else mats[0]
    own = lax.psum_scatter(blocks, AXES, scatter_dimension=0, tiled=True)[0]
    return own.reshape(len(mats), -1, own.shape[1])


def layer_forward(state, weights, params, query_ids, key_ids):
    width = state.shape[1]
    hidden = layer_norm(state, params[0], params[1]).astype(jnp.bfloat16)
    joined = dot_rows(hidden, weights[0][: 3 * width])
    queries = wide((joined[:, :width] + params[2]).astype(jnp.bfloat16))
    key_rows = joined[:, width : 2 * width].astype(jnp.bfloat16)
    val_rows = (joined[:, 2 * width :] + params[3]).astype(jnp.bfloat16)
    own_pair = jnp.concatenate([wide(key_rows), wide(val_rows)], 0)
    attended, lse, key_vals = attend(queries, own_pair, key_ids, query_ids, 4)
    attended = attended[:, :width]
    mid_state = state + dot_plain(attended, weights[0][3 * width :]) + params[4]
    normed = layer_norm(mid_state, params[5], params[6]).astype(jnp.bfloat16)
    upward = dot_rows(normed, weights[1]) + params[8:12].reshape(-1)
    active = jax.nn.gelu(upward, approximate=True).astype(jnp.bfloat16)
    output = mid_state + dot_plain(active, weights[2]) + params[7]
    return (
        output,
        (hidden, queries, key_vals, lse, attended, mid_state, normed, upward, active),
    )


def layer_backward(state, weights, params, saved, query_ids, key_ids, grad_in, arrived):
    width = state.shape[1]
    hidden, queries, key_vals, lse, attended, mid_state, normed, upward, active = saved
    down_grad = grad_in.astype(jnp.bfloat16)
    act_grad = dot_rows(down_grad, weights[2])
    unused_gelu, gelu_pull = jax.vjp(partial(jax.nn.gelu, approximate=True), upward)
    up_grad = gelu_pull(act_grad)[0].astype(jnp.bfloat16)
    mid_back, gain_two, shift_two = norm_back(
        mid_state, params[5], params[6], dot_plain(up_grad, weights[1])
    )
    mid_grad = grad_in + mid_back
    out_grad = mid_grad.astype(jnp.bfloat16)
    att_grad = wide(dot_rows(out_grad, weights[0][3 * width :]).astype(jnp.bfloat16))
    if arrived:
        att_grad, arrived[0] = lax.optimization_barrier((att_grad, arrived[0]))
    query_grad, own = attend_back(queries, key_vals, att_grad, lse, key_ids, query_ids, 8)
    query_grad = query_grad[:, :width]
    key_grad, val_grad = own[: own.shape[0] // 2, :width], own[own.shape[0] // 2 :, :width]
    joined_grad = jnp.concatenate([query_grad, key_grad, val_grad], 1)
    state_back, gain_one, shift_one = norm_back(
        state, params[0], params[1], dot_plain(joined_grad, weights[0][: 3 * width])
    )
    small_grad = jnp.concatenate(
        [
            jnp.stack(
                [
                    gain_one,
                    shift_one,
                    column_sums(query_grad),
                    column_sums(val_grad),
                    column_sums(out_grad),
                    gain_two,
                    shift_two,
                    column_sums(down_grad),
                ]
            ),
            column_sums(up_grad).reshape(4, width),
        ],
        0,
    )
    factors = [
        [(joined_grad, hidden), (attended, out_grad)],
        [(up_grad, normed)],
        [(active, down_grad)],
    ]
    return (mid_grad + state_back, factors, small_grad)


def adam_step(weights, moment, square, grad, rate, decay, step):
    moment = BETA_ONE * moment + (1 - BETA_ONE) * grad
    square = BETA_TWO * square + (1 - BETA_TWO) * grad * grad
    moment_hat = moment / (1 - BETA_ONE**step)
    square_hat = square / (1 - BETA_TWO**step)
    weights = weights - rate * (moment_hat / (jnp.sqrt(square_hat) + ADAM_EPS) + decay * weights)
    return (weights, moment, square)


def pad_rows(x, rows):
    return jnp.pad(x, ((0, rows - x.shape[0]), (0, 0)))


def on_device(
    tokens,
    block_ids,
    completion,
    regroup,
    targets,
    step_count,
    layer_mats,
    mats_moment,
    mats_square,
    embed_table,
    table_moment,
    table_square,
):
    seqs, tok_count = tokens.shape
    seq_length = block_ids.shape[1]
    width = embed_table.shape[1]
    table_local = embed_table.shape[0]
    layers = layer_mats.shape[0]
    replicas, groups, shards = (lax.axis_size(axis) for axis in AXES)
    total = replicas * groups * shards
    seq_at = lax.axis_index("seq")
    shard_at = lax.axis_index("shard")
    device_at = lax.axis_index(AXES)
    seq_bits, dp_bits, shard_bits = bits_of("seq"), bits_of("dp"), bits_of("shard")
    first_row = device_at * table_local
    table_own = embed_table.astype(jnp.bfloat16)
    mats_low = layer_mats.astype(jnp.bfloat16)
    token_ids = tokens.reshape(-1)
    local_rows = token_ids.shape[0]
    small_count = 12 * layers + 2
    small_rows = -(-small_count // 16) * 16

    ids_all = exchange(
        jnp.pad(token_ids, (0, -local_rows % 1024)).reshape(1, -1, 128),
        "share_ids",
        0,
        join_axes=AXES,
        join_orders=[shard_bits[::-1] + dp_bits[::-1] + seq_bits[::-1]],
    )
    ids_all = ids_all.reshape(total, -1)[:, :local_rows]
    owner_all = ids_all // table_local
    loads = jnp.sum(
        (owner_all[:, :, None] == jnp.arange(total)[None, None, :]).astype(jnp.int32), 1
    )
    rounds = (jnp.max(loads) + SLOTS - 1) // SLOTS
    asked = owner_all == device_at
    asked_rank = counts_before(asked)
    asked_row = ids_all - first_row
    own_owner = token_ids // table_local
    same = own_owner[:, None] == own_owner[None, :]
    before = jnp.arange(local_rows)[None, :] < jnp.arange(local_rows)[:, None]
    own_rank = jnp.sum((same & before).astype(jnp.int32), 1)

    def asked_rows(at):
        chosen = asked[:, None, :] & (
            asked_rank[:, None, :] == at * SLOTS + jnp.arange(SLOTS)[None, :, None]
        )
        return (jnp.sum(jnp.where(chosen, asked_row[:, None, :] + 1, 0), 2) - 1).reshape(-1)

    def own_slots(at):
        slot = own_rank - at * SLOTS
        return jnp.where((slot >= 0) & (slot < SLOTS), own_owner * SLOTS + slot, -1)

    def fetch(at, given):
        return dot_plain(
            one_hot(own_slots(at), total * SLOTS, 1), given.reshape(total * SLOTS, width)
        )

    fixed = jnp.arange(seq_length + small_rows, dtype=jnp.int32)
    fixed_row = jnp.where(fixed < seq_length + small_count, VOCAB + fixed - first_row, -1)
    wanted = jnp.concatenate([asked_rows(0), fixed_row])
    rows_out = dot_plain(one_hot(wanted, table_local, 1), table_own).astype(jnp.bfloat16)
    exchanged = total * SLOTS
    piece = seq_length // total
    gathered = []
    for layer_at in range(layers):
        if layer_at == 0:
            whole = lax.all_gather(mats_low[0], AXES, axis=1, tiled=True)
            gathered.append([whole[k] for k in range(3)])
        else:
            first = lax.all_gather(mats_low[layer_at, 0], AXES, axis=0, tiled=True)
            rest = lax.all_gather(mats_low[layer_at, 1:], AXES, axis=1, tiled=True)
            gathered.append([first, rest[0], rest[1]])
    (place_rows,), (small,), (given,) = run_jobs(
        [
            sum_job(
                rows_out[exchanged : exchanged + seq_length].reshape(total, piece, width),
                sum_axes=("seq", "dp", "shard"),
                sum_orders=[seq_bits + dp_bits + shard_bits],
                join_axes=("dp", "shard"),
                join_orders=[shard_bits[::-1] + dp_bits[::-1]],
            ),
            combine_job(rows_out[exchanged + seq_length :], add_pair),
            swap_job(rows_out[:exchanged].reshape(total, SLOTS, width), late=7),
        ],
        "open_rows",
        2,
        32,
    )
    place_rows = place_rows.reshape(tok_count, width)
    small = small[:small_count].astype(jnp.float32)
    place_state = jnp.broadcast_to(place_rows.astype(jnp.float32), (seqs, tok_count, width))
    state = fetch(0, given) + place_state.reshape(local_rows, width)

    def fetch_more(at, held):
        rows = dot_plain(one_hot(asked_rows(at), table_local, 1), table_own).astype(jnp.bfloat16)
        return held + fetch(at, swap(rows.reshape(total, SLOTS, width), "swap_rows", 1))

    state = lax.fori_loop(1, rounds, fetch_more, state)

    query_ids = lax.dynamic_slice_in_dim(block_ids[0], seq_at * tok_count, tok_count, 0)
    inputs, kept, saved = [], [], []
    for layer_at in range(layers):
        weights = gathered[layer_at]
        inputs.append(state)
        kept.append(weights)
        state, held = layer_forward(
            state,
            weights,
            small[12 * layer_at : 12 * layer_at + 12],
            query_ids,
            block_ids[0],
        )
        saved.append(held)
    final_gain = small[12 * layers]
    final_shift = small[12 * layers + 1]
    final = layer_norm(state, final_gain, final_shift).astype(jnp.bfloat16)

    group_mask = completion[0]
    slot_of = regroup[0]
    slots = slot_of.shape[0]
    comp_rows = slots // shards
    rank_all = counts_before(group_mask[None])[0]
    mine = lax.dynamic_slice_in_dim(group_mask, shard_at * local_rows, local_rows)
    my_rank = lax.dynamic_slice_in_dim(rank_all, shard_at * local_rows, local_rows)
    my_slot = jnp.sum(
        jnp.where(my_rank[:, None] == jnp.arange(slots)[None, :], slot_of[None, :], 0), 1
    )
    to_slot = one_hot(jnp.where(mine == 1, my_slot, -1), slots, 0)
    outgoing = dot_plain(to_slot, final).astype(jnp.bfloat16).reshape(shards, comp_rows, width)
    two_ways = [seq_bits[1:] + dp_bits, dp_bits + seq_bits[1:]]
    head_in = exchange(
        outgoing,
        "share_final",
        5,
        sum_axes=("shard",),
        sum_orders=[shard_bits, shard_bits],
        join_axes=AXES,
        join_orders=[shard_bits[::-1] + way[::-1] + seq_bits[:1] for way in two_ways],
        chunks=2,
    ).reshape(-1, width)

    rows_all = targets.shape[0]
    columns = first_row + jnp.arange(table_local, dtype=jnp.int32)
    live = (columns < VOCAB)[None, :]
    logits = dot_rows(head_in, table_own)
    masked = jnp.where(live, logits, MASK_FILL)
    top_local = jnp.max(masked, 1)
    total_local = jnp.sum(jnp.where(live, jnp.exp(masked - top_local[:, None]), 0.0), 1)
    target_hit = columns[None, :] == targets[:, None]
    pick_local = jnp.sum(jnp.where(target_hit, logits, 0.0), 1)
    stats = combine_all(
        jnp.stack([top_local, total_local, pick_local]).reshape(3, -1, 128),
        merge_soft,
        "share_stats",
        6,
    ).reshape(3, rows_all)
    log_total = stats[0] + jnp.log(stats[1])
    loss_value = jnp.sum(log_total - stats[2]) / rows_all
    probs = jnp.where(live, jnp.exp(masked - log_total[:, None]), 0.0)
    logit_grad = ((probs - target_hit.astype(jnp.float32)) / rows_all).astype(jnp.bfloat16)
    head_grad = dot_cols(logit_grad, head_in)
    returned = exchange(
        dot_plain(logit_grad, table_own).reshape(total, comp_rows, width),
        "return_final",
        7,
        sum_axes=AXES,
        sum_orders=[seq_bits[:1] + way + shard_bits for way in two_ways],
        join_axes=("shard",),
        join_orders=[shard_bits[::-1], shard_bits[::-1]],
        chunks=2,
    ).reshape(slots, width)
    final_grad = dot_cols(to_slot, returned)
    state_grad, gain_final, shift_final = norm_back(state, final_gain, final_shift, final_grad)

    late = []
    arrived = []
    small_grads = [None] * layers
    for layer_at in reversed(range(layers)):
        state_grad, factors, small_grads[layer_at] = layer_backward(
            inputs[layer_at],
            kept[layer_at],
            small[12 * layer_at : 12 * layer_at + 12],
            saved[layer_at],
            query_ids,
            block_ids[0],
            state_grad,
            arrived,
        )
        if layer_at > 0:
            arrived = [scatter_rows(factors[2:]), scatter_rows(factors[:2])]
        else:
            late = factors

    low_grad = state_grad.astype(jnp.bfloat16)
    place_grad = jnp.sum(state_grad.reshape(seqs, tok_count, width), 0)
    small_grad = pad_rows(
        jnp.concatenate(small_grads + [jnp.stack([gain_final, shift_final])], 0), small_rows
    )

    def leaving(at):
        rows = dot_cols(one_hot(own_slots(at), total * SLOTS, 1), low_grad).astype(jnp.bfloat16)
        return rows.reshape(total, SLOTS, width)

    (low_grad, arrived[1]) = lax.optimization_barrier((low_grad, arrived[1]))
    upper = jnp.concatenate([arrived[1], arrived[0]], 0).astype(jnp.float32)
    late = late_mats(late, 12)
    fits = mats_fit(late)
    own_mats, (place_grad,), (small_grad,), (came,) = run_jobs(
        [
            mats_job(late[:fits]),
            sum_job(
                place_grad.reshape(replicas * shards, piece, width),
                sum_axes=("dp", "shard"),
                sum_orders=[dp_bits + shard_bits],
                join_axes=("seq", "dp", "shard"),
                join_orders=[shard_bits[::-1] + dp_bits[::-1] + seq_bits[::-1]],
            ),
            combine_job(small_grad, add_pair),
            swap_job(leaving(0), late=5),
        ],
        "close_rows",
        10,
        61,
    )
    for k in range(fits, len(late), fits):
        more = run_jobs([mats_job(late[k : k + fits])], "sum_mats", 14 + k, 61)[0]
        own_mats = list(own_mats) + list(more)
    place_grad = place_grad.reshape(seq_length, width)
    small_high = small_grad.astype(jnp.bfloat16)
    small_low = (small_grad - small_high.astype(jnp.float32)).astype(jnp.bfloat16)
    values = jnp.concatenate([came.reshape(-1, width), place_grad, small_high, small_low], 0)
    value_row = jnp.concatenate([wanted, fixed_row[seq_length:]])
    table_grad = dot_plain(one_hot(value_row, table_local, 0), values) + head_grad

    def return_more(at, held):
        rows = swap(leaving(at), "swap_rows", 1).reshape(-1, width)
        return held + dot_plain(one_hot(asked_rows(at), table_local, 0), rows)

    table_grad = lax.fori_loop(1, rounds, return_more, table_grad)
    mats_grad = jnp.stack([jnp.stack(own_mats), upper])
    local_squares = jnp.sum(mats_grad * mats_grad) + jnp.sum(table_grad * table_grad)
    squares = combine_all(jnp.full((8, 128), local_squares), add_pair, "share_norm", 11)
    grad_norm = jnp.sqrt(squares[0, 0])
    factor = CLIP_NORM / grad_norm
    step = step_count[0].astype(jnp.float32)
    new_mats = adam_step(
        layer_mats, mats_moment, mats_square, factor * mats_grad, RATE_MATS, DECAY_RATE, step
    )
    plain_rows = (columns < VOCAB + seq_length)[:, None]
    rate = jnp.where(plain_rows, RATE_TABLE, RATE_SMALL)
    decay = jnp.where(plain_rows, DECAY_RATE, 0.0)
    new_table = adam_step(
        embed_table, table_moment, table_square, factor * table_grad, rate, decay, step
    )
    return (
        loss_value.reshape(1),
        grad_norm.reshape(1),
        new_mats[0],
        new_mats[1],
        new_mats[2],
        new_table[0],
        new_table[1],
        new_table[2],
    )


def solution(mesh):
    in_specs = (
        P(("dp", "shard"), "seq"),
        P(("dp", "shard"), None),
        P(("dp", "seq"), None),
        P(("dp", "seq"), None),
        P(),
        P(),
        P(None, None, ("dp", "seq", "shard"), None),
        P(None, None, ("dp", "seq", "shard"), None),
        P(None, None, ("dp", "seq", "shard"), None),
        P(("dp", "seq", "shard"), None),
        P(("dp", "seq", "shard"), None),
        P(("dp", "seq", "shard"), None),
    )
    out_specs = (
        P(),
        P(),
        P(None, None, ("dp", "seq", "shard"), None),
        P(None, None, ("dp", "seq", "shard"), None),
        P(None, None, ("dp", "seq", "shard"), None),
        P(("dp", "seq", "shard"), None),
        P(("dp", "seq", "shard"), None),
        P(("dp", "seq", "shard"), None),
    )
    return jax.shard_map(
        on_device, mesh=mesh, in_specs=in_specs, out_specs=out_specs, check_vma=False
    )
```

```python
import itertools
from functools import partial

import jax
import jax.numpy as jnp
from jax import lax
from jax.experimental import pallas as pl
from jax.experimental.layout import Layout, with_layout_constraint
from jax.experimental.pallas import tpu as pltpu
from jax.sharding import PartitionSpec as P

HEADS = 17
HEAD = 64
VOCAB = 50278

NORM_EPS = 1e-05
CLIP_NORM = 0.02
BETA_ONE = 0.9
BETA_TWO = 0.95
ADAM_EPS = 1e-08
DECAY_RATE = 0.1
RATE_MATS = 0.05
RATE_TABLE = 0.1
RATE_SMALL = 0.5
MASK_FILL = -1e30

AXES = ("dp", "seq", "shard")
MESH = pl.DeviceIdType.MESH
SLOTS = 24


def bits_of(axis):
    return [(axis, b) for b in range(lax.axis_size(axis).bit_length() - 1)]


def bit_here(bit):
    return lax.rem(lax.axis_index(bit[0]) // 2 ** bit[1], 2)


def partner(bit):
    at = lax.axis_index(bit[0])
    return {bit[0]: at + (1 - 2 * bit_here(bit)) * 2 ** bit[1]}


def greet(bits):
    barrier = pltpu.get_barrier_semaphore()
    for bit in bits:
        pl.semaphore_signal(barrier, inc=1, device_id=partner(bit), device_id_type=MESH)
    pl.semaphore_wait(barrier, len(bits))


def block_weight(axes, bit):
    weight = 2 ** bit[1]
    for axis in axes[axes.index(bit[0]) + 1 :]:
        weight *= lax.axis_size(axis)
    return weight


def block_runs(weights):
    weights = sorted(weights)
    joined = 0
    while joined < len(weights) and weights[joined] == 2**joined:
        joined += 1
    rest = [(0, w) for w in weights[joined:]]
    return 2**joined, [sum(c) for c in itertools.product(*rest)]


class Job:
    def __init__(
        self, inputs, outputs, scratch, sends, keeps, bits, steps, spaces=(pltpu.VMEM, pltpu.VMEM)
    ):
        self.inputs, self.outputs, self.scratch = inputs, outputs, scratch
        self.sends, self.keeps, self.bits, self.steps, self.spaces = sends, keeps, bits, steps, spaces


def me_and_total():
    seq_size, shard_size = lax.axis_size("seq"), lax.axis_size("shard")
    at = (lax.axis_index("dp") * seq_size + lax.axis_index("seq")) * shard_size
    return at + lax.axis_index("shard"), lax.axis_size("dp") * seq_size * shard_size


def place_of(at):
    seq_size, shard_size = lax.axis_size("seq"), lax.axis_size("shard")
    return {
        "dp": at // (seq_size * shard_size),
        "seq": lax.rem(at // shard_size, seq_size),
        "shard": lax.rem(at, shard_size),
    }


def greet_all():
    me, total = me_and_total()
    barrier = pltpu.get_barrier_semaphore()

    def hello(k, carry):
        pl.semaphore_signal(
            barrier, inc=1, device_id=place_of(lax.rem(me + k, total)), device_id_type=MESH
        )
        return carry

    lax.fori_loop(1, total, hello, 0)
    pl.semaphore_wait(barrier, total - 1)


class Sems:
    def __init__(self, send, recv, keep):
        self.send, self.recv, self.keep = send, recv, keep
        self.used = self.kept = 0

    def copy(self, source, target, device):
        k = self.used
        self.used += 1
        copy = pltpu.make_async_remote_copy(
            source, target, self.send.at[k], self.recv.at[k], device_id=device, device_id_type=MESH
        )
        copy.start()
        return copy

    def local(self, source, target):
        k = self.kept
        self.kept += 1
        copy = pltpu.make_async_copy(source, target, self.keep.at[k])
        copy.start()
        return copy

    def span(self, count):
        first = self.used
        self.used += count
        return first


def jobs_kernel(jobs, *refs):
    refs = list(refs)

    def take(count):
        out = refs[:count]
        del refs[:count]
        return out

    held = [take(len(job.inputs)) for job in jobs]
    made = [take(len(job.outputs)) for job in jobs]
    used = [take(len(job.scratch)) for job in jobs]
    sems = Sems(*refs)
    if any(job.bits is None for job in jobs):
        greet_all()
    else:
        greet(sorted(set(bit for job in jobs for bit in job.bits)))
    active = []
    for job, x, o, w in zip(jobs, held, made, used):
        active += job.steps(x, o, w, sems)
    tick = 0
    while active:
        left = []
        for delay, gen in active:
            if delay > tick or next(gen, "end") != "end":
                left.append((delay, gen))
        active = left
        tick += 1


def run_jobs(jobs, name, number, vmem=60):
    inputs = [x for job in jobs for x in job.inputs]
    outputs = [o for job in jobs for o in job.outputs]
    in_specs = [pl.BlockSpec(memory_space=job.spaces[0]) for job in jobs for unused in job.inputs]
    out_specs = [pl.BlockSpec(memory_space=job.spaces[1]) for job in jobs for unused in job.outputs]
    sends = sum(job.sends for job in jobs)
    keeps = max(1, sum(job.keeps for job in jobs))
    flat = pl.pallas_call(
        partial(jobs_kernel, jobs),
        out_shape=outputs,
        in_specs=in_specs,
        out_specs=out_specs,
        scratch_shapes=[w for job in jobs for w in job.scratch]
        + [
            pltpu.SemaphoreType.DMA((sends,)),
            pltpu.SemaphoreType.DMA((sends,)),
            pltpu.SemaphoreType.DMA((keeps,)),
        ],
        compiler_params=pltpu.CompilerParams(
            collective_id=number, has_side_effects=True, vmem_limit_bytes=vmem * 2**20
        ),
        name=name,
    )(*inputs)
    out = []
    for job in jobs:
        out.append(flat[: len(job.outputs)])
        flat = flat[len(job.outputs) :]
    return out


def sum_stream(x_ref, o_ref, scratch, sems, rows, first_slot, sum_axes, sums, join_axes, joins):
    source = x_ref
    slot = first_slot
    if sums:
        work, parcel, recv = scratch
    for step, bit in enumerate(sums):
        base = sum(bit_here(b) * block_weight(sum_axes, b) for b in sums[:step])
        weight = block_weight(sum_axes, bit)
        mine = bit_here(bit)
        size, offsets = block_runs([block_weight(sum_axes, b) for b in sums[step + 1 :]])
        started = []
        for offset in offsets:
            leave = base + (1 - mine) * weight + offset
            if source.dtype == parcel.dtype:
                packed = source.at[pl.ds(leave, size), rows]
            else:

                def pack(i, carry, leave=leave, at=slot, source=source):
                    parcel[at + i, rows] = source[leave + i, rows].astype(parcel.dtype)
                    return carry

                lax.fori_loop(0, size, pack, 0)
                packed = parcel.at[pl.ds(slot, size), rows]
            copy = sems.copy(packed, recv.at[pl.ds(slot, size), rows], partner(bit))
            started.append((copy, base + mine * weight + offset, slot, size))
            slot += size
        yield
        for copy, keep, at, size in started:
            copy.wait()

            def add(i, carry, keep=keep, at=at, source=source):
                total = source[keep + i, rows].astype(jnp.float32)
                total = total + recv[at + i, rows].astype(jnp.float32)
                work[keep + i, rows] = total.astype(work.dtype)
                return carry

            lax.fori_loop(0, size, add, 0)
        source = work
    own = sum(bit_here(b) * block_weight(sum_axes, b) for b in sums) if sums else 0
    result = source[own, rows].astype(o_ref.dtype)
    if not joins:
        o_ref[rows] = result
        return
    o_ref[sum(bit_here(b) * block_weight(join_axes, b) for b in joins), rows] = result
    for step, bit in enumerate(joins):
        base = sum(bit_here(b) * block_weight(join_axes, b) for b in joins[step:])
        size, offsets = block_runs([block_weight(join_axes, b) for b in joins[:step]])
        started = []
        for offset in offsets:
            here = o_ref.at[pl.ds(base + offset, size), rows]
            started.append(sems.copy(here, here, partner(bit)))
        yield
        for copy in started:
            copy.wait()


def sum_job(x, sum_axes=(), sum_orders=(), join_axes=(), join_orders=(), chunks=1):
    rows, width = x.shape[-2:]
    blocks = 1
    for axis in join_axes:
        blocks *= lax.axis_size(axis)
    kind = jnp.bfloat16 if sum_axes else x.dtype
    streams = max(len(sum_orders), len(join_orders))
    if rows % (streams * chunks * 16):
        chunks = 1
    share = rows // (streams * chunks)
    sends = 0
    for order in sum_orders:
        for step in range(len(order)):
            sends += len(block_runs([block_weight(sum_axes, b) for b in order[step + 1 :]])[1])
    for order in join_orders:
        for step in range(len(order)):
            sends += len(block_runs([block_weight(join_axes, b) for b in order[:step]])[1])
    scratch = []
    if sum_axes:
        if x.size * 14 > 56 * 2**20:
            x = x.astype(jnp.bfloat16)
        exact = x.dtype == jnp.float32 or x.size < 2**22
        scratch = [
            pltpu.VMEM(x.shape, jnp.float32 if exact else kind),
            pltpu.VMEM(x.shape, kind),
            pltpu.VMEM(x.shape, kind),
        ]

    def steps(x_refs, o_refs, scratch_refs, sems):
        gens = []
        for c in range(chunks):
            for k in range(streams):
                rows_here = pl.ds((k * chunks + c) * share, share)
                sums = sum_orders[k] if sum_orders else []
                joins = join_orders[k] if join_orders else []
                gens.append(
                    (
                        c,
                        sum_stream(
                            x_refs[0], o_refs[0], scratch_refs, sems, rows_here, 0,
                            sum_axes, sums, join_axes, joins,
                        ),
                    )
                )
        return gens

    bits = set(bit for order in list(sum_orders) + list(join_orders) for bit in order)
    shape = (blocks, rows, width) if join_axes else (rows, width)
    return Job(
        [x], [jax.ShapeDtypeStruct(shape, kind)], scratch, sends * chunks, 0, bits, steps
    )


def exchange(x, name, number, **how):
    return run_jobs([sum_job(x, **how)], name, number)[0][0]


def combine_job(x, combine):
    bits = [bit for axis in reversed(AXES) for bit in bits_of(axis)]
    slots = (len(bits),) + x.shape

    def steps(x_refs, o_refs, scratch, sems):
        out_buf, in_buf = scratch

        def gen():
            current = x_refs[0][...]
            for i, bit in enumerate(bits):
                out_buf[i] = current
                copy = sems.copy(out_buf.at[i], in_buf.at[i], partner(bit))
                yield
                copy.wait()
                current, other = out_buf[i], in_buf[i]
                low = bit_here(bit) == 0
                current = combine(jnp.where(low, current, other), jnp.where(low, other, current))
            o_refs[0][...] = current

        return [(0, gen())]

    return Job(
        [x],
        [jax.ShapeDtypeStruct(x.shape, x.dtype)],
        [pltpu.VMEM(slots, x.dtype), pltpu.VMEM(slots, x.dtype)],
        len(bits),
        0,
        bits,
        steps,
    )


def combine_all(x, combine, name, number):
    return run_jobs([combine_job(x, combine)], name, number, 16)[0][0]


def swap_job(x, late=0):
    total = x.shape[0]

    def steps(x_refs, o_refs, scratch, sems):
        x_ref, o_ref = x_refs[0], o_refs[0]

        def gen():
            me, unused = me_and_total()
            first = sems.span(total)
            keep = sems.local(x_ref.at[me], o_ref.at[me])

            def copy_to(other, here):
                return pltpu.make_async_remote_copy(
                    x_ref.at[other],
                    o_ref.at[here],
                    sems.send.at[first + other],
                    sems.recv.at[first + here],
                    device_id=place_of(other),
                    device_id_type=MESH,
                )

            def send(k, carry):
                copy_to(lax.rem(me + k, total), me).start()
                return carry

            lax.fori_loop(1, total, send, 0)
            for unused in range(late + 1):
                yield

            def finish(k, carry):
                other = lax.rem(me + k, total)
                copy_to(other, other).wait()
                return carry

            lax.fori_loop(1, total, finish, 0)
            keep.wait()

        return [(0, gen())]

    return Job(
        [x],
        [jax.ShapeDtypeStruct(x.shape, x.dtype)],
        [],
        total,
        1,
        None,
        steps,
        spaces=(pl.ANY, pl.ANY),
    )


def spread_job(x, add):
    total = lax.axis_size(AXES)
    all_shape = (total,) + x.shape

    def steps(x_refs, o_refs, scratch, sems):
        x_ref = x_refs[0]
        target = scratch[0] if add else o_refs[0]

        def gen():
            me, unused = me_and_total()
            first = sems.span(total)
            target[me] = x_ref[...]

            def copy_to(other, here):
                return pltpu.make_async_remote_copy(
                    x_ref,
                    target.at[here],
                    sems.send.at[first + other],
                    sems.recv.at[first + here],
                    device_id=place_of(other),
                    device_id_type=MESH,
                )

            def send(k, carry):
                copy_to(lax.rem(me + k, total), me).start()
                return carry

            lax.fori_loop(1, total, send, 0)
            yield

            def finish(k, carry):
                other = lax.rem(me + k, total)
                copy_to(other, other).wait()
                return carry

            lax.fori_loop(1, total, finish, 0)
            if add:
                o_refs[0][...] = jnp.sum(target[...], 0)

        return [(0, gen())]

    return Job(
        [x],
        [jax.ShapeDtypeStruct(x.shape if add else all_shape, x.dtype)],
        [pltpu.VMEM(all_shape, x.dtype)] if add else [],
        total,
        0,
        None,
        steps,
    )


def swap(x, name, number):
    return run_jobs([swap_job(x)], name, number, 16)[0][0]


def sum_orders_for(rows):
    across, along, deep = bits_of("seq")[1:], bits_of("dp"), bits_of("shard")
    if rows < 64 or rows % 8:
        return [(0, rows)], [across + along + deep]
    one, two = rows * 8 // 17 // 16 * 16, rows * 6 // 17 // 16 * 16
    spans = [(0, one), (one, two), (one + two, rows - one - two)]
    return spans, [across + along + deep, along + across + deep, deep + along + across]


def mats_stream(x_ref, o_ref, scratch, sems, m, span, order, weights):
    kept, work, parcel, recv = scratch
    turn, m = m % 2, m % work.shape[0]
    steps = len(order)
    rows = pl.ds(*span)
    slot = 0
    rest = sorted((b for b in weights if b != order[0]), key=lambda b: weights[b])
    small = {b: 2**k for k, b in enumerate(rest)}
    for step, bit in enumerate(order):
        mine = bit_here(bit)
        base = sum(bit_here(b) * small[b] for b in order[1:step])
        runs, keeps = [], []
        if step == 0:
            size, offsets = block_runs([weights[b] for b in order[1:]])
            for offset in offsets:
                left, place = offset, 0
                for b in reversed(rest):
                    if left >= weights[b]:
                        left -= weights[b]
                        place += small[b]
                keeps.append(
                    sems.local(
                        x_ref.at[pl.ds(mine * weights[bit] + offset, size), rows],
                        kept.at[turn, pl.ds(place, size), rows],
                    )
                )
                runs.append(((1 - mine) * weights[bit] + offset, place))
        else:
            size, offsets = block_runs([small[b] for b in order[step + 1 :]])
            for offset in offsets:
                here = base + offset
                runs.append((here + (1 - mine) * small[bit], here + mine * small[bit]))
        started = []
        for leave, keep_at in runs:
            at = slot
            slot += size
            if step == 0:
                packed = x_ref.at[pl.ds(leave, size), rows]
            else:
                spot = at - 2 ** (steps - 1)

                def pack(i, carry, leave=leave, spot=spot):
                    parcel[m, spot + i, rows] = work[m, leave + i, rows].astype(parcel.dtype)
                    return carry

                lax.fori_loop(0, size, pack, 0)
                packed = parcel.at[m, pl.ds(spot, size), rows]
            copy = sems.copy(packed, recv.at[m, pl.ds(at, size), rows], partner(bit))
            started.append((copy, at, keep_at, size))
        yield
        for keep in keeps:
            keep.wait()
        for copy, at, keep_at, size in started:
            copy.wait()

            def add(i, carry, at=at, keep_at=keep_at, step=step):
                if step == 0:
                    total = kept[turn, keep_at + i, rows].astype(jnp.float32)
                else:
                    total = work[m, keep_at + i, rows]
                work[m, keep_at + i, rows] = total + recv[m, at + i, rows].astype(jnp.float32)
                return carry

            lax.fori_loop(0, size, add, 0)
    o_ref[rows] = work[m, sum(bit_here(b) * small[b] for b in order[1:]), rows]


def mats_job(mats):
    blocks, rows, width = mats[0].shape
    spans, orders = sum_orders_for(rows)
    weights = {}
    for bit in orders[0]:
        weight = block_weight(AXES, bit)
        weights[bit] = weight if bit[0] == "shard" else weight // 2
    keeps = sends = 0
    for order in orders:
        keeps += len(block_runs([weights[b] for b in order[1:]])[1])
        sends += len(block_runs([weights[b] for b in order[1:]])[1])
        rest = sorted((b for b in weights if b != order[0]), key=lambda b: weights[b])
        small = {b: 2**k for k, b in enumerate(rest)}
        for step in range(1, len(order)):
            sends += len(block_runs([small[b] for b in order[step + 1 :]])[1])
    count = len(mats)

    def steps(x_refs, o_refs, scratch, sems):
        return [
            (m, mats_stream(x_refs[m], o_refs[m], scratch, sems, m, spans[k], orders[k], weights))
            for m in range(count)
            for k in range(len(orders))
        ]

    return Job(
        mats,
        [jax.ShapeDtypeStruct((rows, width), jnp.float32)] * count,
        [
            pltpu.VMEM((min(2, count), blocks // 2, rows, width), jnp.bfloat16),
            pltpu.VMEM((min(3, count), blocks // 2, rows, width), jnp.float32),
            pltpu.VMEM((min(3, count), blocks // 2 - 1, rows, width), jnp.bfloat16),
            pltpu.VMEM((min(3, count), blocks - 1, rows, width), jnp.bfloat16),
        ],
        count * sends,
        count * keeps,
        set(orders[0]),
        steps,
        spaces=(pl.ANY, pltpu.VMEM),
    )


def gather_job(parts):
    rows, width = parts[0].shape
    spans, orders = sum_orders_for(rows)
    orders = [order[::-1] + bits_of("seq")[:1] for order in orders]
    total = lax.axis_size(AXES)
    sends = 0
    for order in orders:
        for step in range(len(order)):
            sends += len(block_runs([block_weight(AXES, b) for b in order[:step]])[1])

    def gen(x_ref, o_ref, sems, span, order):
        here = pl.ds(*span)
        own = me_and_total()[0]
        keep = sems.local(x_ref.at[here], o_ref.at[own, here])
        for step, bit in enumerate(order):
            base = sum(bit_here(b) * block_weight(AXES, b) for b in order[step:])
            size, offsets = block_runs([block_weight(AXES, b) for b in order[:step]])
            started = []
            for offset in offsets:
                target = o_ref.at[pl.ds(base + offset, size), here]
                source = x_ref.at[here] if step == 0 else target
                target = o_ref.at[own, here] if step == 0 else target
                started.append(sems.copy(source, target, partner(bit)))
            yield
            if step == 0:
                keep.wait()
            for copy in started:
                copy.wait()

    def steps(x_refs, o_refs, scratch, sems):
        return [
            (m, gen(x_refs[m], o_refs[m], sems, spans[k], orders[k]))
            for m in range(len(parts))
            for k in range(len(orders))
        ]

    return Job(
        parts,
        [jax.ShapeDtypeStruct((total, rows, width), parts[0].dtype)] * len(parts),
        [],
        sends * len(parts),
        len(orders) * len(parts),
        set(orders[0]),
        steps,
        spaces=(pl.ANY, pl.ANY),
    )


def trade_kernel(count, *refs):
    x_refs, o_refs = refs[:count], refs[count : 2 * count]
    send_sems, recv_sems = refs[2 * count :]
    bit = ("seq", 0)
    greet([bit])
    copies = []
    for k in range(count):
        copy = pltpu.make_async_remote_copy(
            x_refs[k],
            o_refs[k],
            send_sems.at[k],
            recv_sems.at[k],
            device_id=partner(bit),
            device_id_type=MESH,
        )
        copy.start()
        copies.append(copy)
    for copy in copies:
        copy.wait()


def trade(arrays, name, number):
    count = len(arrays)
    return pl.pallas_call(
        partial(trade_kernel, count),
        out_shape=[jax.ShapeDtypeStruct(x.shape, x.dtype) for x in arrays],
        in_specs=[pl.BlockSpec(memory_space=pl.ANY)] * count,
        out_specs=[pl.BlockSpec(memory_space=pl.ANY)] * count,
        scratch_shapes=[pltpu.SemaphoreType.DMA((count,)), pltpu.SemaphoreType.DMA((count,))],
        compiler_params=pltpu.CompilerParams(collective_id=number, has_side_effects=True),
        name=name,
    )(*arrays)


def my_rows(features, own):
    rows = features.shape[0]
    parts = features.reshape(rows, -1, 2, own)
    at = lax.rem(lax.axis_index("seq"), 2)
    mine = lax.dynamic_index_in_dim(parts, at, 2, keepdims=False)
    other = lax.dynamic_index_in_dim(parts, 1 - at, 2, keepdims=False)
    return mine.reshape(rows, -1), other.reshape(rows, -1)


def late_mats(groups, number):
    pairs = [pair for group in groups for pair in group]
    total = lax.axis_size(AXES)
    height = sum(features.shape[1] for features, unused in groups[0])
    own = height // total * lax.axis_size("shard")
    halves = [my_rows(features, own) for features, unused in pairs]
    tails = [tail for unused, tail in pairs]
    got = trade([other for unused, other in halves] + tails, "trade_rows", number)
    parts = []
    for k, (mine, unused) in enumerate(halves):
        grad = dot_cols(
            jnp.concatenate([mine, got[k]], 0),
            jnp.concatenate([tails[k], got[len(halves) + k]], 0),
        )
        parts.append(rows_major(grad.astype(jnp.bfloat16)))
    mats = []
    for group in groups:
        grad = jnp.concatenate(parts[: len(group)], 0) if len(group) > 1 else parts[0]
        parts = parts[len(group) :]
        mats.append(grad.reshape(total // 2, -1, grad.shape[1]))
    return mats


def mats_fit(mats):
    blocks, rows, width = mats[0].shape
    tile = -(-rows // 16) * 16 * -(-width // 128) * 128
    fits = (50 * 2**20 - tile * blocks * 2) // (tile * blocks * 5)
    return len(mats) if fits >= 3 else max(1, fits)


def head_lanes(half, shape):
    lane = lax.broadcasted_iota(jnp.int32, shape, 1)
    return (lane < HEAD) if half == 0 else (lane >= HEAD)


def pair_lanes(p):
    return pl.ds(pl.multiple_of(p * 2 * HEAD, 2 * HEAD), 2 * HEAD)


def seq_places():
    me = lax.axis_index("seq")
    return me, partner(("seq", 0))["seq"], partner(("seq", 1))["seq"]


def to_seq(source, target, sems, k, place):
    return pltpu.make_async_remote_copy(
        source,
        target,
        sems.at[0, k],
        sems.at[1, k],
        device_id={"seq": place},
        device_id_type=MESH,
    )


def attend_kernel(
    q_ref, own_ref, key_ids_ref, query_ids_ref, o_ref, lse_ref, kv_ref, blocked, far, near, pass_on, own_sem
):
    rows = own_ref.shape[0] // 2
    keys = kv_ref.shape[0] * rows
    pairs = q_ref.shape[1] // (2 * HEAD)
    me, near_at, far_at = seq_places()
    beyond = near_at + far_at - me
    greet([("seq", 0), ("seq", 1)])

    def far_copy(p, at):
        return to_seq(own_ref.at[:, pair_lanes(p)], kv_ref.at[at, :, pair_lanes(p)], far, p, far_at)

    def near_copy(p, at):
        return to_seq(own_ref.at[:, pair_lanes(p)], kv_ref.at[at, :, pair_lanes(p)], near, p, near_at)

    def pass_copy(p, at):
        here = kv_ref.at[far_at, :, pair_lanes(p)]
        return to_seq(here, kv_ref.at[at, :, pair_lanes(p)], pass_on, p, near_at)

    def send(p, carry):
        far_copy(p, me).start()
        near_copy(p, me).start()
        return carry

    lax.fori_loop(0, pairs, send, 0)
    own = pltpu.make_async_copy(own_ref, kv_ref.at[me], own_sem)
    own.start()
    blocked[...] = jnp.where(key_ids_ref[...] <= query_ids_ref[...], 0.0, MASK_FILL)
    own.wait()

    def forward_one(p):
        far_copy(p, far_at).wait_recv()
        pass_copy(p, far_at).start()

    forward_one(0)

    def pair(p, carry):
        @pl.when(p + 1 < pairs)
        def _():
            forward_one(p + 1)

        near_copy(p, near_at).wait_recv()
        pass_copy(p, beyond).wait_recv()
        lanes = pair_lanes(p)
        key_pair = kv_ref[:, :rows, lanes].reshape(keys, 2 * HEAD)
        val_turned = kv_ref[:, rows:, lanes].reshape(keys, 2 * HEAD).T
        query_pair = q_ref[:, lanes]
        outs = []
        for half in range(2):
            query = jnp.where(head_lanes(half, query_pair.shape), query_pair, 0)
            scores = dot_rows(key_pair, query.astype(jnp.bfloat16)) * HEAD ** (-0.5) + blocked[...]
            top = jnp.max(scores, 0, keepdims=True)
            raised = jnp.exp(scores - top)
            total = jnp.sum(raised, 0, keepdims=True)
            probs = (raised * (1.0 / total)).astype(jnp.bfloat16)
            outs.append(dot_plain(val_turned[half * HEAD : (half + 1) * HEAD], probs))
            lse_ref[p, half] = (top + jnp.log(total))[0]
        o_ref[:, lanes] = jnp.concatenate(outs, 0).T.astype(o_ref.dtype)
        return carry

    lax.fori_loop(0, pairs, pair, 0)

    def sent(p, carry):
        far_copy(p, me).wait_send()
        near_copy(p, me).wait_send()
        pass_copy(p, far_at).wait_send()
        return carry

    lax.fori_loop(0, pairs, sent, 0)


def attend(queries, own_pair, key_ids, query_ids, number):
    rows, width = queries.shape
    keys = key_ids.shape[0]
    pairs = width // (2 * HEAD)
    groups = lax.axis_size("seq")
    copies = pltpu.SemaphoreType.DMA((2, pairs))
    return pl.pallas_call(
        attend_kernel,
        out_shape=(
            jax.ShapeDtypeStruct((rows, width), jnp.bfloat16),
            jax.ShapeDtypeStruct((pairs, 2, rows), jnp.float32),
            jax.ShapeDtypeStruct((groups,) + own_pair.shape, jnp.bfloat16),
        ),
        in_specs=[pl.BlockSpec(memory_space=pltpu.VMEM)] * 4,
        out_specs=(pl.BlockSpec(memory_space=pltpu.VMEM),) * 3,
        scratch_shapes=[
            pltpu.VMEM((keys, rows), jnp.float32),
            copies,
            copies,
            copies,
            pltpu.SemaphoreType.DMA,
        ],
        compiler_params=pltpu.CompilerParams(
            collective_id=number, has_side_effects=True, vmem_limit_bytes=48 * 2**20
        ),
        cost_estimate=pl.CostEstimate(
            flops=4 * rows * keys * width,
            transcendentals=rows * keys * HEADS,
            bytes_accessed=4 * keys * width,
        ),
        name="attend",
    )(queries, own_pair, key_ids[:, None], query_ids[None, :])


def attend_back_kernel(
    q_ref,
    kv_ref,
    grad_ref,
    lse_ref,
    key_ids_ref,
    query_ids_ref,
    dq_ref,
    own_ref,
    blocked,
    fresh,
    kept,
    near_out,
    near_in,
    far_out,
    far_in,
    near,
    far,
):
    groups, twice, unused = kv_ref.shape
    rows = twice // 2
    keys = groups * rows
    pairs = q_ref.shape[1] // (2 * HEAD)
    scale = HEAD ** (-0.5)
    me, near_at, far_at = seq_places()
    low, high = lax.rem(me, 2), me // 2
    greet([("seq", 0), ("seq", 1)])
    blocked[...] = jnp.where(key_ids_ref[...] <= query_ids_ref[...], 0.0, MASK_FILL)

    def near_copy(p):
        return to_seq(near_out.at[p], near_in.at[p], near, p, near_at)

    def far_copy(p):
        return to_seq(far_out.at[p], far_in.at[p], far, p, far_at)

    def middle(p):
        near_copy(p).wait()
        for k in range(2):
            kept[p, k] = kept[p, k] + near_in[p, k].astype(jnp.float32)
        far_out[p] = kept[p, 1 - high].astype(far_out.dtype)
        far_copy(p).start()

    def last(p):
        far_copy(p).wait()
        total = kept[p, high] + far_in[p].astype(jnp.float32)
        own_ref[:, pair_lanes(p)] = total.astype(own_ref.dtype)

    def pair(p, carry):
        lanes = pair_lanes(p)
        key_pair = kv_ref[:, :rows, lanes].reshape(keys, 2 * HEAD)
        val_pair = kv_ref[:, rows:, lanes].reshape(keys, 2 * HEAD)
        key_turned = key_pair.T
        query_pair = q_ref[:, lanes]
        grad_pair = grad_ref[:, lanes]
        key_grad = jnp.zeros((keys, 2 * HEAD), jnp.float32)
        val_grad = jnp.zeros((keys, 2 * HEAD), jnp.float32)
        outs = []
        for half in range(2):
            here = head_lanes(half, query_pair.shape)
            query = jnp.where(here, query_pair, 0).astype(jnp.bfloat16)
            grad = jnp.where(here, grad_pair, 0).astype(jnp.bfloat16)
            scores = dot_rows(key_pair, query) * scale + blocked[...]
            probs = jnp.exp(scores - lse_ref[p, half][None, :])
            prob_grad = dot_rows(val_pair, grad)
            inner = jnp.sum(probs * prob_grad, 0, keepdims=True)
            score_grad = (probs * (prob_grad - inner)).astype(jnp.bfloat16)
            key_grad = key_grad + dot_plain(score_grad, query)
            val_grad = val_grad + dot_plain(probs.astype(jnp.bfloat16), grad)
            outs.append(dot_plain(key_turned[half * HEAD : (half + 1) * HEAD], score_grad))
        dq_ref[:, lanes] = (jnp.concatenate(outs, 0).T * scale).astype(dq_ref.dtype)
        fresh[:, :rows] = (key_grad * scale).reshape(groups, rows, 2 * HEAD)
        fresh[:, rows:] = val_grad.reshape(groups, rows, 2 * HEAD)
        for k in range(2):
            near_out[p, k] = fresh[2 * k + 1 - low].astype(near_out.dtype)
            kept[p, k] = fresh[2 * k + low]
        near_copy(p).start()

        @pl.when(p >= 1)
        def _():
            middle(p - 1)

        @pl.when(p >= 2)
        def _():
            last(p - 2)

        return carry

    lax.fori_loop(0, pairs, pair, 0)
    middle(pairs - 1)
    last(pairs - 2)
    last(pairs - 1)


def attend_back(queries, key_vals, grad, lse, key_ids, query_ids, number):
    rows, width = queries.shape
    keys = key_ids.shape[0]
    pairs = width // (2 * HEAD)
    piece = (2 * rows, 2 * HEAD)
    copies = pltpu.SemaphoreType.DMA((2, pairs))
    return pl.pallas_call(
        attend_back_kernel,
        out_shape=(
            jax.ShapeDtypeStruct((rows, width), jnp.bfloat16),
            jax.ShapeDtypeStruct((2 * rows, width), jnp.bfloat16),
        ),
        in_specs=[pl.BlockSpec(memory_space=pltpu.VMEM)] * 6,
        out_specs=(pl.BlockSpec(memory_space=pltpu.VMEM),) * 2,
        scratch_shapes=[
            pltpu.VMEM((keys, rows), jnp.float32),
            pltpu.VMEM((lax.axis_size("seq"),) + piece, jnp.float32),
            pltpu.VMEM((pairs, 2) + piece, jnp.float32),
            pltpu.VMEM((pairs, 2) + piece, jnp.bfloat16),
            pltpu.VMEM((pairs, 2) + piece, jnp.bfloat16),
            pltpu.VMEM((pairs,) + piece, jnp.bfloat16),
            pltpu.VMEM((pairs,) + piece, jnp.bfloat16),
            copies,
            copies,
        ],
        compiler_params=pltpu.CompilerParams(
            collective_id=number, has_side_effects=True, vmem_limit_bytes=58 * 2**20
        ),
        cost_estimate=pl.CostEstimate(
            flops=10 * rows * keys * width,
            transcendentals=rows * keys * HEADS,
            bytes_accessed=12 * keys * width,
        ),
        name="attend_back",
    )(queries, key_vals, grad, lse, key_ids[:, None], query_ids[None, :])


def add_pair(first, second):
    return first + second


def merge_soft(first, second):
    highest = jnp.maximum(first[0], second[0])
    total = first[1] * jnp.exp(first[0] - highest) + second[1] * jnp.exp(second[0] - highest)
    return jnp.stack([highest, total, first[2] + second[2]])


def dot_rows(left_op, right_op):
    return lax.dot_general(
        left_op, right_op, (((1,), (1,)), ((), ())), preferred_element_type=jnp.float32
    )


def dot_cols(left_op, right_op):
    return lax.dot_general(
        left_op, right_op, (((0,), (0,)), ((), ())), preferred_element_type=jnp.float32
    )


def dot_plain(left_op, right_op):
    return jnp.dot(left_op, right_op, preferred_element_type=jnp.float32)


def column_sums(values):
    return jnp.sum(values.astype(jnp.float32), 0, keepdims=True)


def layer_norm(values, gain, shift):
    center = values - jnp.mean(values, -1, keepdims=True)
    spread = jnp.mean(center * center, -1, keepdims=True)
    return center * lax.rsqrt(spread + NORM_EPS) * gain + shift


def norm_back(values, gain, shift, grad):
    unused, pull = jax.vjp(layer_norm, values, gain, shift)
    return pull(grad)


def one_hot(wanted, length, axis):
    shape = list(wanted.shape)
    shape.insert(axis, length)
    at = lax.broadcasted_iota(jnp.int32, shape, axis)
    return (at == jnp.expand_dims(wanted, axis)).astype(jnp.bfloat16)


def counts_before(flags):
    length = flags.shape[-1]
    earlier = (
        lax.broadcasted_iota(jnp.int32, (length, length), 0)
        < lax.broadcasted_iota(jnp.int32, (length, length), 1)
    ).astype(jnp.bfloat16)
    return dot_plain(flags.astype(jnp.bfloat16), earlier).astype(jnp.int32)


def wide(rows_in):
    return jnp.pad(rows_in, ((0, 0), (0, -rows_in.shape[1] % (2 * HEAD))))


def rows_major(x):
    return with_layout_constraint(x, Layout(major_to_minor=tuple(range(x.ndim))))


def scatter_rows(groups):
    total = lax.axis_size(AXES)
    mats = []
    for group in groups:
        parts = [rows_major(dot_cols(*pair).astype(jnp.bfloat16)) for pair in group]
        grad = jnp.concatenate(parts, 0) if len(parts) > 1 else parts[0]
        mats.append(grad.reshape(total, -1, grad.shape[1]))
    blocks = jnp.concatenate(mats, 1) if len(mats) > 1 else mats[0]
    own = lax.psum_scatter(blocks, AXES, scatter_dimension=0, tiled=True)[0]
    return own.reshape(len(mats), -1, own.shape[1])


def layer_forward(state, weights, params, query_ids, key_ids):
    width = state.shape[1]
    hidden = layer_norm(state, params[0 : 1], params[1 : 2]).astype(jnp.bfloat16)
    joined = rows_major(dot_rows(hidden, weights[0][: 3 * width]))
    queries = wide((joined[:, :width] + params[2 : 3]).astype(jnp.bfloat16))
    key_rows = joined[:, width : 2 * width].astype(jnp.bfloat16)
    val_rows = (joined[:, 2 * width :] + params[3 : 4]).astype(jnp.bfloat16)
    own_pair = jnp.concatenate([wide(key_rows), wide(val_rows)], 0)
    attended, lse, key_vals = attend(queries, own_pair, key_ids, query_ids, 4)
    attended = attended[:, :width]
    mid_state = state + dot_plain(attended, weights[0][3 * width :]) + params[4 : 5]
    normed = layer_norm(mid_state, params[5 : 6], params[6 : 7]).astype(jnp.bfloat16)
    upward = dot_rows(normed, weights[1]) + params[8:12].reshape(1, -1)
    active = jax.nn.gelu(upward, approximate=True).astype(jnp.bfloat16)
    output = mid_state + dot_plain(active, weights[2]) + params[7 : 8]
    return (
        output,
        (hidden, queries, key_vals, lse, attended, mid_state, normed, upward, active),
    )


def layer_backward(state, weights, params, saved, query_ids, key_ids, grad_in, arrived):
    width = state.shape[1]
    hidden, queries, key_vals, lse, attended, mid_state, normed, upward, active = saved
    down_grad = grad_in.astype(jnp.bfloat16)
    act_grad = dot_rows(down_grad, weights[2])
    unused_gelu, gelu_pull = jax.vjp(partial(jax.nn.gelu, approximate=True), upward)
    up_grad = gelu_pull(act_grad)[0].astype(jnp.bfloat16)
    mid_back, gain_two, shift_two = norm_back(
        mid_state, params[5 : 6], params[6 : 7], dot_plain(up_grad, weights[1])
    )
    mid_grad = grad_in + mid_back
    out_grad = mid_grad.astype(jnp.bfloat16)
    att_grad = wide(dot_rows(out_grad, weights[0][3 * width :]).astype(jnp.bfloat16))
    if arrived:
        att_grad, arrived[0] = lax.optimization_barrier((att_grad, arrived[0]))
    query_grad, own = attend_back(queries, key_vals, att_grad, lse, key_ids, query_ids, 8)
    query_grad = query_grad[:, :width]
    key_grad, val_grad = own[: own.shape[0] // 2, :width], own[own.shape[0] // 2 :, :width]
    joined_grad = jnp.concatenate([query_grad, key_grad, val_grad], 1)
    state_back, gain_one, shift_one = norm_back(
        state, params[0 : 1], params[1 : 2], dot_plain(joined_grad, weights[0][: 3 * width])
    )
    up_sums = column_sums(up_grad)
    small_grad = [
        gain_one,
        shift_one,
        column_sums(query_grad),
        column_sums(val_grad),
        column_sums(out_grad),
        gain_two,
        shift_two,
        column_sums(down_grad),
    ] + [up_sums[:, k * width : (k + 1) * width] for k in range(4)]
    factors = [
        [(joined_grad, hidden), (attended, out_grad)],
        [(up_grad, normed)],
        [(active, down_grad)],
    ]
    return (mid_grad + state_back, factors, small_grad)


def adam_step(weights, moment, square, grad, rate, decay, step):
    moment = BETA_ONE * moment + (1 - BETA_ONE) * grad
    square = BETA_TWO * square + (1 - BETA_TWO) * grad * grad
    moment_hat = moment / (1 - BETA_ONE**step)
    square_hat = square / (1 - BETA_TWO**step)
    weights = weights - rate * (moment_hat / (jnp.sqrt(square_hat) + ADAM_EPS) + decay * weights)
    return (weights, moment, square)


def pad_rows(x, rows):
    return jnp.pad(x, ((0, rows - x.shape[0]), (0, 0)))


def on_device(
    tokens,
    block_ids,
    completion,
    regroup,
    targets,
    step_count,
    layer_mats,
    mats_moment,
    mats_square,
    embed_table,
    table_moment,
    table_square,
):
    seqs, tok_count = tokens.shape
    seq_length = block_ids.shape[1]
    width = embed_table.shape[1]
    table_local = embed_table.shape[0]
    layers = layer_mats.shape[0]
    replicas, groups, shards = (lax.axis_size(axis) for axis in AXES)
    total = replicas * groups * shards
    seq_at = lax.axis_index("seq")
    shard_at = lax.axis_index("shard")
    device_at = lax.axis_index(AXES)
    seq_bits, dp_bits, shard_bits = bits_of("seq"), bits_of("dp"), bits_of("shard")
    first_row = device_at * table_local
    table_own = embed_table.astype(jnp.bfloat16)
    mats_low = layer_mats.astype(jnp.bfloat16)
    token_ids = tokens.reshape(-1)
    local_rows = token_ids.shape[0]
    small_count = 12 * layers + 2
    small_rows = -(-small_count // 16) * 16

    packed_ids = jnp.pad(token_ids, (0, -local_rows % 1024)).reshape(-1, 128)
    ids_all = run_jobs([spread_job(packed_ids, False)], "share_ids", 0, 16)[0][0]
    ids_all = ids_all.reshape(total, -1)[:, :local_rows]
    owner_all = ids_all // table_local
    loads = jnp.sum(
        (owner_all[:, :, None] == jnp.arange(total)[None, None, :]).astype(jnp.int32), 1
    )
    rounds = (jnp.max(loads) + SLOTS - 1) // SLOTS
    asked = owner_all == device_at
    asked_rank = counts_before(asked)
    asked_row = ids_all - first_row
    own_owner = token_ids // table_local
    same = own_owner[:, None] == own_owner[None, :]
    before = jnp.arange(local_rows)[None, :] < jnp.arange(local_rows)[:, None]
    own_rank = jnp.sum((same & before).astype(jnp.int32), 1)

    def asked_rows(at):
        chosen = asked[:, None, :] & (
            asked_rank[:, None, :] == at * SLOTS + jnp.arange(SLOTS)[None, :, None]
        )
        return (jnp.sum(jnp.where(chosen, asked_row[:, None, :] + 1, 0), 2) - 1).reshape(-1)

    def own_slots(at):
        slot = own_rank - at * SLOTS
        return jnp.where((slot >= 0) & (slot < SLOTS), own_owner * SLOTS + slot, -1)

    def fetch(at, given):
        return dot_plain(
            one_hot(own_slots(at), total * SLOTS, 1), given.reshape(total * SLOTS, width)
        )

    fixed = jnp.arange(seq_length + small_rows, dtype=jnp.int32)
    fixed_row = jnp.where(fixed < seq_length + small_count, VOCAB + fixed - first_row, -1)
    wanted = jnp.concatenate([asked_rows(0), fixed_row])
    rows_out = dot_plain(one_hot(wanted, table_local, 1), table_own).astype(jnp.bfloat16)
    exchanged = total * SLOTS
    piece = seq_length // total
    gathered = []
    for layer_at in range(layers):
        if layer_at == 0:
            whole = lax.all_gather(mats_low[0], AXES, axis=1, tiled=True)
            gathered.append([whole[k] for k in range(3)])
        else:
            gathered.append(
                [lax.all_gather(mats_low[layer_at, k], AXES, axis=0, tiled=True) for k in range(2)]
            )
    (last_down,), (place_rows,), (small,), (given,) = run_jobs(
        [
            gather_job([mats_low[1, 2]]),
            sum_job(
                rows_out[exchanged : exchanged + seq_length].reshape(total, piece, width),
                sum_axes=("seq", "dp", "shard"),
                sum_orders=[seq_bits + dp_bits + shard_bits],
                join_axes=("dp", "shard"),
                join_orders=[shard_bits[::-1] + dp_bits[::-1]],
            ),
            combine_job(rows_out[exchanged + seq_length :], add_pair),
            swap_job(rows_out[:exchanged].reshape(total, SLOTS, width), late=7),
        ],
        "open_rows",
        2,
        32,
    )
    gathered[1].append(last_down.reshape(-1, width))
    place_rows = place_rows.reshape(tok_count, width)
    small = small[:small_count].astype(jnp.float32)
    place_state = jnp.broadcast_to(place_rows.astype(jnp.float32), (seqs, tok_count, width))
    state = fetch(0, given) + place_state.reshape(local_rows, width)

    def fetch_more(at, held):
        rows = dot_plain(one_hot(asked_rows(at), table_local, 1), table_own).astype(jnp.bfloat16)
        return held + fetch(at, swap(rows.reshape(total, SLOTS, width), "swap_rows", 1))

    state = lax.fori_loop(1, rounds, fetch_more, state)

    query_ids = lax.dynamic_slice_in_dim(block_ids[0], seq_at * tok_count, tok_count, 0)
    inputs, kept, saved = [], [], []
    for layer_at in range(layers):
        weights = gathered[layer_at]
        inputs.append(state)
        kept.append(weights)
        state, held = layer_forward(
            state,
            weights,
            small[12 * layer_at : 12 * layer_at + 12],
            query_ids,
            block_ids[0],
        )
        saved.append(held)
    final_gain = small[12 * layers : 12 * layers + 1]
    final_shift = small[12 * layers + 1 : 12 * layers + 2]
    final = layer_norm(state, final_gain, final_shift).astype(jnp.bfloat16)

    group_mask = completion[0]
    slot_of = regroup[0]
    slots = slot_of.shape[0]
    comp_rows = slots // shards
    rank_all = counts_before(group_mask[None])[0]
    mine = lax.dynamic_slice_in_dim(group_mask, shard_at * local_rows, local_rows)
    my_rank = lax.dynamic_slice_in_dim(rank_all, shard_at * local_rows, local_rows)
    my_slot = jnp.sum(
        jnp.where(my_rank[:, None] == jnp.arange(slots)[None, :], slot_of[None, :], 0), 1
    )
    to_slot = one_hot(jnp.where(mine == 1, my_slot, -1), slots, 0)
    outgoing = dot_plain(to_slot, final).astype(jnp.bfloat16).reshape(shards, comp_rows, width)
    two_ways = [seq_bits[1:] + dp_bits, dp_bits + seq_bits[1:]]
    head_in = exchange(
        outgoing,
        "share_final",
        5,
        sum_axes=("shard",),
        sum_orders=[shard_bits, shard_bits],
        join_axes=AXES,
        join_orders=[shard_bits[::-1] + way[::-1] + seq_bits[:1] for way in two_ways],
        chunks=2,
    ).reshape(-1, width)

    rows_all = targets.shape[0]
    columns = first_row + jnp.arange(table_local, dtype=jnp.int32)
    live = (columns < VOCAB)[None, :]
    logits = dot_rows(head_in, table_own)
    masked = jnp.where(live, logits, MASK_FILL)
    top_local = jnp.max(masked, 1)
    total_local = jnp.sum(jnp.where(live, jnp.exp(masked - top_local[:, None]), 0.0), 1)
    target_hit = columns[None, :] == targets[:, None]
    pick_local = jnp.sum(jnp.where(target_hit, logits, 0.0), 1)
    stats = combine_all(
        jnp.stack([top_local, total_local, pick_local]).reshape(3, -1, 128),
        merge_soft,
        "share_stats",
        6,
    ).reshape(3, rows_all)
    log_total = stats[0] + jnp.log(stats[1])
    loss_value = jnp.sum(log_total - stats[2]) / rows_all
    probs = jnp.where(live, jnp.exp(masked - log_total[:, None]), 0.0)
    logit_grad = ((probs - target_hit.astype(jnp.float32)) / rows_all).astype(jnp.bfloat16)
    head_grad = dot_cols(logit_grad, head_in)
    returned = exchange(
        dot_plain(logit_grad, table_own).reshape(total, comp_rows, width),
        "return_final",
        7,
        sum_axes=AXES,
        sum_orders=[seq_bits[:1] + way + shard_bits for way in two_ways],
        join_axes=("shard",),
        join_orders=[shard_bits[::-1], shard_bits[::-1]],
        chunks=2,
    ).reshape(slots, width)
    final_grad = dot_cols(to_slot, returned)
    state_grad, gain_final, shift_final = norm_back(state, final_gain, final_shift, final_grad)

    late = []
    arrived = []
    small_grads = [None] * layers
    for layer_at in reversed(range(layers)):
        state_grad, factors, small_grads[layer_at] = layer_backward(
            inputs[layer_at],
            kept[layer_at],
            small[12 * layer_at : 12 * layer_at + 12],
            saved[layer_at],
            query_ids,
            block_ids[0],
            state_grad,
            arrived,
        )
        if layer_at > 0:
            arrived = [scatter_rows(factors[2:]), scatter_rows(factors[1:2])]
            late = factors[:1]
        else:
            late = factors + late

    low_grad = state_grad.astype(jnp.bfloat16)
    place_grad = jnp.sum(state_grad.reshape(seqs, tok_count, width), 0)
    small_grad = pad_rows(
        jnp.concatenate(sum(small_grads, []) + [gain_final, shift_final], 0), small_rows
    )

    def leaving(at):
        rows = dot_cols(one_hot(own_slots(at), total * SLOTS, 1), low_grad).astype(jnp.bfloat16)
        return rows.reshape(total, SLOTS, width)

    (low_grad, arrived[1]) = lax.optimization_barrier((low_grad, arrived[1]))
    upper = jnp.concatenate([arrived[1], arrived[0]], 0).astype(jnp.float32)
    late = late_mats(late, 12)
    fits = mats_fit(late)
    own_mats, (place_grad,), (small_grad,), (came,) = run_jobs(
        [
            mats_job(late[:fits]),
            sum_job(
                place_grad.reshape(replicas * shards, piece, width),
                sum_axes=("dp", "shard"),
                sum_orders=[dp_bits + shard_bits],
                join_axes=("seq", "dp", "shard"),
                join_orders=[shard_bits[::-1] + dp_bits[::-1] + seq_bits[::-1]],
            ),
            combine_job(small_grad, add_pair),
            swap_job(leaving(0), late=5),
        ],
        "close_rows",
        10,
        61,
    )
    for k in range(fits, len(late), fits):
        more = run_jobs([mats_job(late[k : k + fits])], "sum_mats", 14 + k, 61)[0]
        own_mats = list(own_mats) + list(lax.optimization_barrier(tuple(more)))
    place_grad = place_grad.reshape(seq_length, width)
    small_high = small_grad.astype(jnp.bfloat16)
    small_low = (small_grad - small_high.astype(jnp.float32)).astype(jnp.bfloat16)
    values = jnp.concatenate([came.reshape(-1, width), place_grad, small_high, small_low], 0)
    value_row = jnp.concatenate([wanted, fixed_row[seq_length:]])
    table_grad = dot_plain(one_hot(value_row, table_local, 0), values) + head_grad

    def return_more(at, held):
        rows = swap(leaving(at), "swap_rows", 1).reshape(-1, width)
        return held + dot_plain(one_hot(asked_rows(at), table_local, 0), rows)

    table_grad = lax.fori_loop(1, rounds, return_more, table_grad)
    mats_grad = jnp.concatenate([jnp.stack(own_mats), upper], 0).reshape(layer_mats.shape)
    local_squares = jnp.sum(mats_grad * mats_grad) + jnp.sum(table_grad * table_grad)
    squares = jnp.full((8, 128), local_squares)
    squares = run_jobs([spread_job(squares, True)], "share_norm", 11, 16)[0][0]
    grad_norm = jnp.sqrt(squares[0, 0])
    factor = CLIP_NORM / grad_norm
    step = step_count[0].astype(jnp.float32)
    new_mats = adam_step(
        layer_mats, mats_moment, mats_square, factor * mats_grad, RATE_MATS, DECAY_RATE, step
    )
    plain_rows = (columns < VOCAB + seq_length)[:, None]
    rate = jnp.where(plain_rows, RATE_TABLE, RATE_SMALL)
    decay = jnp.where(plain_rows, DECAY_RATE, 0.0)
    new_table = adam_step(
        embed_table, table_moment, table_square, factor * table_grad, rate, decay, step
    )
    return (
        loss_value.reshape(1),
        grad_norm.reshape(1),
        new_mats[0],
        new_mats[1],
        new_mats[2],
        new_table[0],
        new_table[1],
        new_table[2],
    )


def solution(mesh):
    in_specs = (
        P(("dp", "shard"), "seq"),
        P(("dp", "shard"), None),
        P(("dp", "seq"), None),
        P(("dp", "seq"), None),
        P(),
        P(),
        P(None, None, ("dp", "seq", "shard"), None),
        P(None, None, ("dp", "seq", "shard"), None),
        P(None, None, ("dp", "seq", "shard"), None),
        P(("dp", "seq", "shard"), None),
        P(("dp", "seq", "shard"), None),
        P(("dp", "seq", "shard"), None),
    )
    out_specs = (
        P(),
        P(),
        P(None, None, ("dp", "seq", "shard"), None),
        P(None, None, ("dp", "seq", "shard"), None),
        P(None, None, ("dp", "seq", "shard"), None),
        P(("dp", "seq", "shard"), None),
        P(("dp", "seq", "shard"), None),
        P(("dp", "seq", "shard"), None),
    )
    return jax.shard_map(
        on_device, mesh=mesh, in_specs=in_specs, out_specs=out_specs, check_vma=False
    )
```

```python
import itertools
from functools import partial

import jax
import jax.numpy as jnp
from jax import lax
from jax.experimental import pallas as pl
from jax.experimental.layout import Layout, with_layout_constraint
from jax.experimental.pallas import tpu as pltpu
from jax.sharding import PartitionSpec as P

HEADS = 17
HEAD = 64
VOCAB = 50278

NORM_EPS = 1e-05
CLIP_NORM = 0.02
BETA_ONE = 0.9
BETA_TWO = 0.95
ADAM_EPS = 1e-08
DECAY_RATE = 0.1
RATE_MATS = 0.05
RATE_TABLE = 0.1
RATE_SMALL = 0.5
MASK_FILL = -1e30

AXES = ("dp", "seq", "shard")
MESH = pl.DeviceIdType.MESH
SLOTS = 24


def bits_of(axis):
    return [(axis, b) for b in range(lax.axis_size(axis).bit_length() - 1)]


def bit_here(bit):
    return lax.rem(lax.axis_index(bit[0]) // 2 ** bit[1], 2)


def partner(bit):
    at = lax.axis_index(bit[0])
    return {bit[0]: at + (1 - 2 * bit_here(bit)) * 2 ** bit[1]}


def greet(bits):
    barrier = pltpu.get_barrier_semaphore()
    for bit in bits:
        pl.semaphore_signal(barrier, inc=1, device_id=partner(bit), device_id_type=MESH)
    pl.semaphore_wait(barrier, len(bits))


def block_weight(axes, bit):
    weight = 2 ** bit[1]
    for axis in axes[axes.index(bit[0]) + 1 :]:
        weight *= lax.axis_size(axis)
    return weight


def block_runs(weights):
    weights = sorted(weights)
    joined = 0
    while joined < len(weights) and weights[joined] == 2**joined:
        joined += 1
    rest = [(0, w) for w in weights[joined:]]
    return 2**joined, [sum(c) for c in itertools.product(*rest)]


class Job:
    def __init__(
        self, inputs, outputs, scratch, sends, keeps, bits, steps, spaces=(pltpu.VMEM, pltpu.VMEM)
    ):
        self.inputs, self.outputs, self.scratch = inputs, outputs, scratch
        self.sends, self.keeps, self.bits, self.steps, self.spaces = sends, keeps, bits, steps, spaces


def me_and_total():
    seq_size, shard_size = lax.axis_size("seq"), lax.axis_size("shard")
    at = (lax.axis_index("dp") * seq_size + lax.axis_index("seq")) * shard_size
    return at + lax.axis_index("shard"), lax.axis_size("dp") * seq_size * shard_size


def place_of(at):
    seq_size, shard_size = lax.axis_size("seq"), lax.axis_size("shard")
    return {
        "dp": at // (seq_size * shard_size),
        "seq": lax.rem(at // shard_size, seq_size),
        "shard": lax.rem(at, shard_size),
    }


def greet_all():
    me, total = me_and_total()
    barrier = pltpu.get_barrier_semaphore()

    def hello(k, carry):
        pl.semaphore_signal(
            barrier, inc=1, device_id=place_of(lax.rem(me + k, total)), device_id_type=MESH
        )
        return carry

    lax.fori_loop(1, total, hello, 0)
    pl.semaphore_wait(barrier, total - 1)


class Sems:
    def __init__(self, send, recv, keep):
        self.send, self.recv, self.keep = send, recv, keep
        self.used = self.kept = 0

    def copy(self, source, target, device):
        k = self.used
        self.used += 1
        copy = pltpu.make_async_remote_copy(
            source, target, self.send.at[k], self.recv.at[k], device_id=device, device_id_type=MESH
        )
        copy.start()
        return copy

    def local(self, source, target):
        k = self.kept
        self.kept += 1
        copy = pltpu.make_async_copy(source, target, self.keep.at[k])
        copy.start()
        return copy

    def span(self, count):
        first = self.used
        self.used += count
        return first


def jobs_kernel(jobs, *refs):
    refs = list(refs)

    def take(count):
        out = refs[:count]
        del refs[:count]
        return out

    held = [take(len(job.inputs)) for job in jobs]
    made = [take(len(job.outputs)) for job in jobs]
    used = [take(len(job.scratch)) for job in jobs]
    sems = Sems(*refs)
    if any(job.bits is None for job in jobs):
        greet_all()
    else:
        greet(sorted(set(bit for job in jobs for bit in job.bits)))
    active = []
    for job, x, o, w in zip(jobs, held, made, used):
        active += job.steps(x, o, w, sems)
    tick = 0
    while active:
        left = []
        for delay, gen in active:
            if delay > tick or next(gen, "end") != "end":
                left.append((delay, gen))
        active = left
        tick += 1


def run_jobs(jobs, name, number, vmem=60):
    inputs = [x for job in jobs for x in job.inputs]
    outputs = [o for job in jobs for o in job.outputs]
    in_specs = [pl.BlockSpec(memory_space=job.spaces[0]) for job in jobs for unused in job.inputs]
    out_specs = [pl.BlockSpec(memory_space=job.spaces[1]) for job in jobs for unused in job.outputs]
    sends = sum(job.sends for job in jobs)
    keeps = max(1, sum(job.keeps for job in jobs))
    flat = pl.pallas_call(
        partial(jobs_kernel, jobs),
        out_shape=outputs,
        in_specs=in_specs,
        out_specs=out_specs,
        scratch_shapes=[w for job in jobs for w in job.scratch]
        + [
            pltpu.SemaphoreType.DMA((sends,)),
            pltpu.SemaphoreType.DMA((sends,)),
            pltpu.SemaphoreType.DMA((keeps,)),
        ],
        compiler_params=pltpu.CompilerParams(
            collective_id=number, has_side_effects=True, vmem_limit_bytes=vmem * 2**20
        ),
        name=name,
    )(*inputs)
    out = []
    for job in jobs:
        out.append(flat[: len(job.outputs)])
        flat = flat[len(job.outputs) :]
    return out


def sum_stream(x_ref, o_ref, scratch, sems, rows, first_slot, sum_axes, sums, join_axes, joins):
    source = x_ref
    slot = first_slot
    if sums:
        work, parcel, recv = scratch
    for step, bit in enumerate(sums):
        base = sum(bit_here(b) * block_weight(sum_axes, b) for b in sums[:step])
        weight = block_weight(sum_axes, bit)
        mine = bit_here(bit)
        size, offsets = block_runs([block_weight(sum_axes, b) for b in sums[step + 1 :]])
        started = []
        for offset in offsets:
            leave = base + (1 - mine) * weight + offset
            if source.dtype == parcel.dtype:
                packed = source.at[pl.ds(leave, size), rows]
            else:

                def pack(i, carry, leave=leave, at=slot, source=source):
                    parcel[at + i, rows] = source[leave + i, rows].astype(parcel.dtype)
                    return carry

                lax.fori_loop(0, size, pack, 0)
                packed = parcel.at[pl.ds(slot, size), rows]
            copy = sems.copy(packed, recv.at[pl.ds(slot, size), rows], partner(bit))
            started.append((copy, base + mine * weight + offset, slot, size))
            slot += size
        yield
        for copy, keep, at, size in started:
            copy.wait()

            def add(i, carry, keep=keep, at=at, source=source):
                total = source[keep + i, rows].astype(jnp.float32)
                total = total + recv[at + i, rows].astype(jnp.float32)
                work[keep + i, rows] = total.astype(work.dtype)
                return carry

            lax.fori_loop(0, size, add, 0)
        source = work
    own = sum(bit_here(b) * block_weight(sum_axes, b) for b in sums) if sums else 0
    result = source[own, rows].astype(o_ref.dtype)
    if not joins:
        o_ref[rows] = result
        return
    o_ref[sum(bit_here(b) * block_weight(join_axes, b) for b in joins), rows] = result
    for step, bit in enumerate(joins):
        base = sum(bit_here(b) * block_weight(join_axes, b) for b in joins[step:])
        size, offsets = block_runs([block_weight(join_axes, b) for b in joins[:step]])
        started = []
        for offset in offsets:
            here = o_ref.at[pl.ds(base + offset, size), rows]
            started.append(sems.copy(here, here, partner(bit)))
        yield
        for copy in started:
            copy.wait()


def sum_job(x, sum_axes=(), sum_orders=(), join_axes=(), join_orders=(), chunks=1):
    rows, width = x.shape[-2:]
    blocks = 1
    for axis in join_axes:
        blocks *= lax.axis_size(axis)
    kind = jnp.bfloat16 if sum_axes else x.dtype
    streams = max(len(sum_orders), len(join_orders))
    if rows % (streams * chunks * 16):
        chunks = 1
    share = rows // (streams * chunks)
    sends = 0
    for order in sum_orders:
        for step in range(len(order)):
            sends += len(block_runs([block_weight(sum_axes, b) for b in order[step + 1 :]])[1])
    for order in join_orders:
        for step in range(len(order)):
            sends += len(block_runs([block_weight(join_axes, b) for b in order[:step]])[1])
    scratch = []
    if sum_axes:
        if x.size * 14 > 56 * 2**20:
            x = x.astype(jnp.bfloat16)
        exact = x.dtype == jnp.float32 or x.size < 2**22
        scratch = [
            pltpu.VMEM(x.shape, jnp.float32 if exact else kind),
            pltpu.VMEM(x.shape, kind),
            pltpu.VMEM(x.shape, kind),
        ]

    def steps(x_refs, o_refs, scratch_refs, sems):
        gens = []
        for c in range(chunks):
            for k in range(streams):
                rows_here = pl.ds((k * chunks + c) * share, share)
                sums = sum_orders[k] if sum_orders else []
                joins = join_orders[k] if join_orders else []
                gens.append(
                    (
                        c,
                        sum_stream(
                            x_refs[0], o_refs[0], scratch_refs, sems, rows_here, 0,
                            sum_axes, sums, join_axes, joins,
                        ),
                    )
                )
        return gens

    bits = set(bit for order in list(sum_orders) + list(join_orders) for bit in order)
    shape = (blocks, rows, width) if join_axes else (rows, width)
    return Job(
        [x], [jax.ShapeDtypeStruct(shape, kind)], scratch, sends * chunks, 0, bits, steps
    )


def exchange(x, name, number, **how):
    return run_jobs([sum_job(x, **how)], name, number)[0][0]


def combine_job(x, combine):
    bits = [bit for axis in reversed(AXES) for bit in bits_of(axis)]
    slots = (len(bits),) + x.shape

    def steps(x_refs, o_refs, scratch, sems):
        out_buf, in_buf = scratch

        def gen():
            current = x_refs[0][...]
            for i, bit in enumerate(bits):
                out_buf[i] = current
                copy = sems.copy(out_buf.at[i], in_buf.at[i], partner(bit))
                yield
                copy.wait()
                current, other = out_buf[i], in_buf[i]
                low = bit_here(bit) == 0
                current = combine(jnp.where(low, current, other), jnp.where(low, other, current))
            o_refs[0][...] = current

        return [(0, gen())]

    return Job(
        [x],
        [jax.ShapeDtypeStruct(x.shape, x.dtype)],
        [pltpu.VMEM(slots, x.dtype), pltpu.VMEM(slots, x.dtype)],
        len(bits),
        0,
        bits,
        steps,
    )


def combine_all(x, combine, name, number):
    return run_jobs([combine_job(x, combine)], name, number, 16)[0][0]


def swap_job(x, late=0):
    total = x.shape[0]

    def steps(x_refs, o_refs, scratch, sems):
        x_ref, o_ref = x_refs[0], o_refs[0]

        def gen():
            me, unused = me_and_total()
            first = sems.span(total)
            keep = sems.local(x_ref.at[me], o_ref.at[me])

            def copy_to(other, here):
                return pltpu.make_async_remote_copy(
                    x_ref.at[other],
                    o_ref.at[here],
                    sems.send.at[first + other],
                    sems.recv.at[first + here],
                    device_id=place_of(other),
                    device_id_type=MESH,
                )

            def send(k, carry):
                copy_to(lax.rem(me + k, total), me).start()
                return carry

            lax.fori_loop(1, total, send, 0)
            for unused in range(late + 1):
                yield

            def finish(k, carry):
                other = lax.rem(me + k, total)
                copy_to(other, other).wait()
                return carry

            lax.fori_loop(1, total, finish, 0)
            keep.wait()

        return [(0, gen())]

    return Job(
        [x],
        [jax.ShapeDtypeStruct(x.shape, x.dtype)],
        [],
        total,
        1,
        None,
        steps,
        spaces=(pl.ANY, pl.ANY),
    )


def spread_job(x, add):
    total = lax.axis_size(AXES)
    all_shape = (total,) + x.shape

    def steps(x_refs, o_refs, scratch, sems):
        x_ref = x_refs[0]
        target = scratch[0] if add else o_refs[0]

        def gen():
            me, unused = me_and_total()
            first = sems.span(total)
            target[me] = x_ref[...]

            def copy_to(other, here):
                return pltpu.make_async_remote_copy(
                    x_ref,
                    target.at[here],
                    sems.send.at[first + other],
                    sems.recv.at[first + here],
                    device_id=place_of(other),
                    device_id_type=MESH,
                )

            def send(k, carry):
                copy_to(lax.rem(me + k, total), me).start()
                return carry

            lax.fori_loop(1, total, send, 0)
            yield

            def finish(k, carry):
                other = lax.rem(me + k, total)
                copy_to(other, other).wait()
                return carry

            lax.fori_loop(1, total, finish, 0)
            if add:
                o_refs[0][...] = jnp.sum(target[...], 0)

        return [(0, gen())]

    return Job(
        [x],
        [jax.ShapeDtypeStruct(x.shape if add else all_shape, x.dtype)],
        [pltpu.VMEM(all_shape, x.dtype)] if add else [],
        total,
        0,
        None,
        steps,
    )


def swap(x, name, number):
    return run_jobs([swap_job(x)], name, number, 16)[0][0]


def sum_orders_for(rows):
    across, along, deep = bits_of("seq")[1:], bits_of("dp"), bits_of("shard")
    if rows < 64 or rows % 8:
        return [(0, rows)], [across + along + deep]
    one, two = rows * 8 // 17 // 16 * 16, rows * 6 // 17 // 16 * 16
    spans = [(0, one), (one, two), (one + two, rows - one - two)]
    return spans, [across + along + deep, along + across + deep, deep + along + across]


def mats_stream(x_ref, o_ref, scratch, sems, m, span, order, weights):
    kept, work, parcel, recv = scratch
    turn, m = m % 2, m % work.shape[0]
    steps = len(order)
    rows = pl.ds(*span)
    slot = 0
    rest = sorted((b for b in weights if b != order[0]), key=lambda b: weights[b])
    small = {b: 2**k for k, b in enumerate(rest)}
    for step, bit in enumerate(order):
        mine = bit_here(bit)
        base = sum(bit_here(b) * small[b] for b in order[1:step])
        runs, keeps = [], []
        if step == 0:
            size, offsets = block_runs([weights[b] for b in order[1:]])
            for offset in offsets:
                left, place = offset, 0
                for b in reversed(rest):
                    if left >= weights[b]:
                        left -= weights[b]
                        place += small[b]
                keeps.append(
                    sems.local(
                        x_ref.at[pl.ds(mine * weights[bit] + offset, size), rows],
                        kept.at[turn, pl.ds(place, size), rows],
                    )
                )
                runs.append(((1 - mine) * weights[bit] + offset, place))
        else:
            size, offsets = block_runs([small[b] for b in order[step + 1 :]])
            for offset in offsets:
                here = base + offset
                runs.append((here + (1 - mine) * small[bit], here + mine * small[bit]))
        started = []
        for leave, keep_at in runs:
            at = slot
            slot += size
            if step == 0:
                packed = x_ref.at[pl.ds(leave, size), rows]
            else:
                spot = at - 2 ** (steps - 1)

                def pack(i, carry, leave=leave, spot=spot):
                    parcel[m, spot + i, rows] = work[m, leave + i, rows].astype(parcel.dtype)
                    return carry

                lax.fori_loop(0, size, pack, 0)
                packed = parcel.at[m, pl.ds(spot, size), rows]
            copy = sems.copy(packed, recv.at[m, pl.ds(at, size), rows], partner(bit))
            started.append((copy, at, keep_at, size))
        yield
        for keep in keeps:
            keep.wait()
        for copy, at, keep_at, size in started:
            copy.wait()

            def add(i, carry, at=at, keep_at=keep_at, step=step):
                if step == 0:
                    total = kept[turn, keep_at + i, rows].astype(jnp.float32)
                else:
                    total = work[m, keep_at + i, rows]
                work[m, keep_at + i, rows] = total + recv[m, at + i, rows].astype(jnp.float32)
                return carry

            lax.fori_loop(0, size, add, 0)
    o_ref[rows] = work[m, sum(bit_here(b) * small[b] for b in order[1:]), rows]


def mats_job(mats):
    blocks, rows, width = mats[0].shape
    spans, orders = sum_orders_for(rows)
    weights = {}
    for bit in orders[0]:
        weight = block_weight(AXES, bit)
        weights[bit] = weight if bit[0] == "shard" else weight // 2
    keeps = sends = 0
    for order in orders:
        keeps += len(block_runs([weights[b] for b in order[1:]])[1])
        sends += len(block_runs([weights[b] for b in order[1:]])[1])
        rest = sorted((b for b in weights if b != order[0]), key=lambda b: weights[b])
        small = {b: 2**k for k, b in enumerate(rest)}
        for step in range(1, len(order)):
            sends += len(block_runs([small[b] for b in order[step + 1 :]])[1])
    count = len(mats)

    def steps(x_refs, o_refs, scratch, sems):
        return [
            (m, mats_stream(x_refs[m], o_refs[m], scratch, sems, m, spans[k], orders[k], weights))
            for m in range(count)
            for k in range(len(orders))
        ]

    return Job(
        mats,
        [jax.ShapeDtypeStruct((rows, width), jnp.float32)] * count,
        [
            pltpu.VMEM((min(2, count), blocks // 2, rows, width), jnp.bfloat16),
            pltpu.VMEM((min(3, count), blocks // 2, rows, width), jnp.float32),
            pltpu.VMEM((min(3, count), blocks // 2 - 1, rows, width), jnp.bfloat16),
            pltpu.VMEM((min(3, count), blocks - 1, rows, width), jnp.bfloat16),
        ],
        count * sends,
        count * keeps,
        set(orders[0]),
        steps,
        spaces=(pl.ANY, pltpu.VMEM),
    )


def gather_job(parts):
    rows, width = parts[0].shape
    spans, orders = sum_orders_for(rows)
    orders = [order[::-1] + bits_of("seq")[:1] for order in orders]
    total = lax.axis_size(AXES)
    sends = 0
    for order in orders:
        for step in range(len(order)):
            sends += len(block_runs([block_weight(AXES, b) for b in order[:step]])[1])

    def gen(x_ref, o_ref, sems, span, order):
        here = pl.ds(*span)
        own = me_and_total()[0]
        keep = sems.local(x_ref.at[here], o_ref.at[own, here])
        for step, bit in enumerate(order):
            base = sum(bit_here(b) * block_weight(AXES, b) for b in order[step:])
            size, offsets = block_runs([block_weight(AXES, b) for b in order[:step]])
            started = []
            for offset in offsets:
                target = o_ref.at[pl.ds(base + offset, size), here]
                source = x_ref.at[here] if step == 0 else target
                target = o_ref.at[own, here] if step == 0 else target
                started.append(sems.copy(source, target, partner(bit)))
            yield
            if step == 0:
                keep.wait()
            for copy in started:
                copy.wait()

    def steps(x_refs, o_refs, scratch, sems):
        return [
            (m, gen(x_refs[m], o_refs[m], sems, spans[k], orders[k]))
            for m in range(len(parts))
            for k in range(len(orders))
        ]

    return Job(
        parts,
        [jax.ShapeDtypeStruct((total, rows, width), parts[0].dtype)] * len(parts),
        [],
        sends * len(parts),
        len(orders) * len(parts),
        set(orders[0]),
        steps,
        spaces=(pl.ANY, pl.ANY),
    )


def trade_kernel(halved, count, *refs):
    x_refs, o_refs = refs[:count], refs[count : 2 * count]
    send_sems, recv_sems, keep_sems = refs[2 * count :]
    bit = ("seq", 0)
    mine = bit_here(bit)
    greet([bit])
    copies = []
    for k in range(count):
        if k < halved:
            tokens = x_refs[k].shape[-1]
            keep, leave = x_refs[k].at[:, mine], x_refs[k].at[:, 1 - mine]
            near = o_refs[k].at[:, :, pl.ds(0, tokens)]
            far = o_refs[k].at[:, :, pl.ds(tokens, tokens)]
        else:
            tokens = x_refs[k].shape[0]
            keep = leave = x_refs[k]
            near, far = o_refs[k].at[pl.ds(0, tokens)], o_refs[k].at[pl.ds(tokens, tokens)]
        local = pltpu.make_async_copy(keep, near, keep_sems.at[k])
        local.start()
        copy = pltpu.make_async_remote_copy(
            leave,
            far,
            send_sems.at[k],
            recv_sems.at[k],
            device_id=partner(bit),
            device_id_type=MESH,
        )
        copy.start()
        copies += [local, copy]
    for copy in copies:
        copy.wait()


def trade(features, cotangents, name, number):
    arrays = features + cotangents
    count = len(arrays)
    outs = []
    for x in features:
        runs, unused, rows, tokens = x.shape
        outs.append(jax.ShapeDtypeStruct((runs, rows, 2 * tokens), x.dtype))
    for x in cotangents:
        outs.append(jax.ShapeDtypeStruct((2 * x.shape[0], x.shape[1]), x.dtype))
    return pl.pallas_call(
        partial(trade_kernel, len(features), count),
        out_shape=outs,
        in_specs=[pl.BlockSpec(memory_space=pl.ANY)] * count,
        out_specs=[pl.BlockSpec(memory_space=pl.ANY)] * count,
        scratch_shapes=[pltpu.SemaphoreType.DMA((count,))] * 3,
        compiler_params=pltpu.CompilerParams(collective_id=number, has_side_effects=True),
        name=name,
    )(*arrays)


def late_mats(groups, number):
    pairs = [pair for group in groups for pair in group]
    total = lax.axis_size(AXES)
    height = sum(features.shape[1] for features, unused in groups[0])
    own = height // total * lax.axis_size("shard")
    features = [x.T.reshape(-1, 2, own, x.shape[0]) for x, unused in pairs]
    got = trade(features, [tail for unused, tail in pairs], "trade_rows", number)
    parts = []
    for k in range(len(pairs)):
        both = got[k].reshape(-1, got[k].shape[2])
        parts.append(rows_major(dot_plain(both, got[len(pairs) + k]).astype(jnp.bfloat16)))
    mats = []
    for group in groups:
        grad = jnp.concatenate(parts[: len(group)], 0) if len(group) > 1 else parts[0]
        parts = parts[len(group) :]
        mats.append(grad.reshape(total // 2, -1, grad.shape[1]))
    return mats


def mats_fit(mats):
    blocks, rows, width = mats[0].shape
    tile = -(-rows // 16) * 16 * -(-width // 128) * 128
    fits = (50 * 2**20 - tile * blocks * 2) // (tile * blocks * 5)
    return len(mats) if fits >= 3 else max(1, fits)


def head_lanes(half, shape):
    lane = lax.broadcasted_iota(jnp.int32, shape, 1)
    return (lane < HEAD) if half == 0 else (lane >= HEAD)


def pair_lanes(p):
    return pl.ds(pl.multiple_of(p * 2 * HEAD, 2 * HEAD), 2 * HEAD)


def seq_places():
    me = lax.axis_index("seq")
    return me, partner(("seq", 0))["seq"], partner(("seq", 1))["seq"]


def to_seq(source, target, sems, k, place):
    return pltpu.make_async_remote_copy(
        source,
        target,
        sems.at[0, k],
        sems.at[1, k],
        device_id={"seq": place},
        device_id_type=MESH,
    )


def attend_kernel(
    q_ref, own_ref, key_ids_ref, query_ids_ref, o_ref, lse_ref, kv_ref, blocked, far, near, pass_on, own_sem
):
    rows = own_ref.shape[0] // 2
    keys = kv_ref.shape[0] * rows
    pairs = q_ref.shape[1] // (2 * HEAD)
    me, near_at, far_at = seq_places()
    beyond = near_at + far_at - me
    greet([("seq", 0), ("seq", 1)])

    def far_copy(p, at):
        return to_seq(own_ref.at[:, pair_lanes(p)], kv_ref.at[at, :, pair_lanes(p)], far, p, far_at)

    def near_copy(p, at):
        return to_seq(own_ref.at[:, pair_lanes(p)], kv_ref.at[at, :, pair_lanes(p)], near, p, near_at)

    def pass_copy(p, at):
        here = kv_ref.at[far_at, :, pair_lanes(p)]
        return to_seq(here, kv_ref.at[at, :, pair_lanes(p)], pass_on, p, near_at)

    def send(p, carry):
        far_copy(p, me).start()
        near_copy(p, me).start()
        return carry

    lax.fori_loop(0, pairs, send, 0)
    own = pltpu.make_async_copy(own_ref, kv_ref.at[me], own_sem)
    own.start()
    blocked[...] = jnp.where(key_ids_ref[...] <= query_ids_ref[...], 0.0, MASK_FILL)
    own.wait()

    def forward_one(p):
        far_copy(p, far_at).wait_recv()
        pass_copy(p, far_at).start()

    forward_one(0)

    def pair(p, carry):
        @pl.when(p + 1 < pairs)
        def _():
            forward_one(p + 1)

        near_copy(p, near_at).wait_recv()
        pass_copy(p, beyond).wait_recv()
        lanes = pair_lanes(p)
        key_pair = kv_ref[:, :rows, lanes].reshape(keys, 2 * HEAD)
        val_turned = kv_ref[:, rows:, lanes].reshape(keys, 2 * HEAD).T
        query_pair = q_ref[:, lanes]
        outs = []
        for half in range(2):
            query = jnp.where(head_lanes(half, query_pair.shape), query_pair, 0)
            scores = dot_rows(key_pair, query.astype(jnp.bfloat16)) * HEAD ** (-0.5) + blocked[...]
            top = jnp.max(scores, 0, keepdims=True)
            raised = jnp.exp(scores - top)
            total = jnp.sum(raised, 0, keepdims=True)
            probs = (raised * (1.0 / total)).astype(jnp.bfloat16)
            outs.append(dot_plain(val_turned[half * HEAD : (half + 1) * HEAD], probs))
            lse_ref[p, half] = (top + jnp.log(total))[0]
        o_ref[:, lanes] = jnp.concatenate(outs, 0).T.astype(o_ref.dtype)
        return carry

    lax.fori_loop(0, pairs, pair, 0)

    def sent(p, carry):
        far_copy(p, me).wait_send()
        near_copy(p, me).wait_send()
        pass_copy(p, far_at).wait_send()
        return carry

    lax.fori_loop(0, pairs, sent, 0)


def attend(queries, own_pair, key_ids, query_ids, number):
    rows, width = queries.shape
    keys = key_ids.shape[0]
    pairs = width // (2 * HEAD)
    groups = lax.axis_size("seq")
    copies = pltpu.SemaphoreType.DMA((2, pairs))
    return pl.pallas_call(
        attend_kernel,
        out_shape=(
            jax.ShapeDtypeStruct((rows, width), jnp.bfloat16),
            jax.ShapeDtypeStruct((pairs, 2, rows), jnp.float32),
            jax.ShapeDtypeStruct((groups,) + own_pair.shape, jnp.bfloat16),
        ),
        in_specs=[pl.BlockSpec(memory_space=pltpu.VMEM)] * 4,
        out_specs=(pl.BlockSpec(memory_space=pltpu.VMEM),) * 3,
        scratch_shapes=[
            pltpu.VMEM((keys, rows), jnp.float32),
            copies,
            copies,
            copies,
            pltpu.SemaphoreType.DMA,
        ],
        compiler_params=pltpu.CompilerParams(
            collective_id=number, has_side_effects=True, vmem_limit_bytes=48 * 2**20
        ),
        cost_estimate=pl.CostEstimate(
            flops=4 * rows * keys * width,
            transcendentals=rows * keys * HEADS,
            bytes_accessed=4 * keys * width,
        ),
        name="attend",
    )(queries, own_pair, key_ids[:, None], query_ids[None, :])


def attend_back_kernel(
    q_ref,
    kv_ref,
    grad_ref,
    lse_ref,
    key_ids_ref,
    query_ids_ref,
    dq_ref,
    own_ref,
    blocked,
    fresh,
    kept,
    near_out,
    near_in,
    far_out,
    far_in,
    near,
    far,
):
    groups, twice, unused = kv_ref.shape
    rows = twice // 2
    keys = groups * rows
    pairs = q_ref.shape[1] // (2 * HEAD)
    scale = HEAD ** (-0.5)
    me, near_at, far_at = seq_places()
    low, high = lax.rem(me, 2), me // 2
    greet([("seq", 0), ("seq", 1)])
    blocked[...] = jnp.where(key_ids_ref[...] <= query_ids_ref[...], 0.0, MASK_FILL)

    def near_copy(p):
        return to_seq(near_out.at[p], near_in.at[p], near, p, near_at)

    def far_copy(p):
        return to_seq(far_out.at[p], far_in.at[p], far, p, far_at)

    def middle(p):
        near_copy(p).wait()
        for k in range(2):
            kept[p, k] = kept[p, k] + near_in[p, k].astype(jnp.float32)
        far_out[p] = kept[p, 1 - high].astype(far_out.dtype)
        far_copy(p).start()

    def last(p):
        far_copy(p).wait()
        total = kept[p, high] + far_in[p].astype(jnp.float32)
        own_ref[:, pair_lanes(p)] = total.astype(own_ref.dtype)

    def pair(p, carry):
        lanes = pair_lanes(p)
        key_pair = kv_ref[:, :rows, lanes].reshape(keys, 2 * HEAD)
        val_pair = kv_ref[:, rows:, lanes].reshape(keys, 2 * HEAD)
        key_turned = key_pair.T
        query_pair = q_ref[:, lanes]
        grad_pair = grad_ref[:, lanes]
        key_grad = jnp.zeros((keys, 2 * HEAD), jnp.float32)
        val_grad = jnp.zeros((keys, 2 * HEAD), jnp.float32)
        outs = []
        for half in range(2):
            here = head_lanes(half, query_pair.shape)
            query = jnp.where(here, query_pair, 0).astype(jnp.bfloat16)
            grad = jnp.where(here, grad_pair, 0).astype(jnp.bfloat16)
            scores = dot_rows(key_pair, query) * scale + blocked[...]
            probs = jnp.exp(scores - lse_ref[p, half][None, :])
            prob_grad = dot_rows(val_pair, grad)
            inner = jnp.sum(probs * prob_grad, 0, keepdims=True)
            score_grad = (probs * (prob_grad - inner)).astype(jnp.bfloat16)
            key_grad = key_grad + dot_plain(score_grad, query)
            val_grad = val_grad + dot_plain(probs.astype(jnp.bfloat16), grad)
            outs.append(dot_plain(key_turned[half * HEAD : (half + 1) * HEAD], score_grad))
        dq_ref[:, lanes] = (jnp.concatenate(outs, 0).T * scale).astype(dq_ref.dtype)
        fresh[:, :rows] = (key_grad * scale).reshape(groups, rows, 2 * HEAD)
        fresh[:, rows:] = val_grad.reshape(groups, rows, 2 * HEAD)
        for k in range(2):
            near_out[p, k] = fresh[2 * k + 1 - low].astype(near_out.dtype)
            kept[p, k] = fresh[2 * k + low]
        near_copy(p).start()

        @pl.when(p >= 1)
        def _():
            middle(p - 1)

        @pl.when(p >= 2)
        def _():
            last(p - 2)

        return carry

    lax.fori_loop(0, pairs, pair, 0)
    middle(pairs - 1)
    last(pairs - 2)
    last(pairs - 1)


def attend_back(queries, key_vals, grad, lse, key_ids, query_ids, number):
    rows, width = queries.shape
    keys = key_ids.shape[0]
    pairs = width // (2 * HEAD)
    piece = (2 * rows, 2 * HEAD)
    copies = pltpu.SemaphoreType.DMA((2, pairs))
    return pl.pallas_call(
        attend_back_kernel,
        out_shape=(
            jax.ShapeDtypeStruct((rows, width), jnp.bfloat16),
            jax.ShapeDtypeStruct((2 * rows, width), jnp.bfloat16),
        ),
        in_specs=[pl.BlockSpec(memory_space=pltpu.VMEM)] * 6,
        out_specs=(pl.BlockSpec(memory_space=pltpu.VMEM),) * 2,
        scratch_shapes=[
            pltpu.VMEM((keys, rows), jnp.float32),
            pltpu.VMEM((lax.axis_size("seq"),) + piece, jnp.float32),
            pltpu.VMEM((pairs, 2) + piece, jnp.float32),
            pltpu.VMEM((pairs, 2) + piece, jnp.bfloat16),
            pltpu.VMEM((pairs, 2) + piece, jnp.bfloat16),
            pltpu.VMEM((pairs,) + piece, jnp.bfloat16),
            pltpu.VMEM((pairs,) + piece, jnp.bfloat16),
            copies,
            copies,
        ],
        compiler_params=pltpu.CompilerParams(
            collective_id=number, has_side_effects=True, vmem_limit_bytes=58 * 2**20
        ),
        cost_estimate=pl.CostEstimate(
            flops=10 * rows * keys * width,
            transcendentals=rows * keys * HEADS,
            bytes_accessed=12 * keys * width,
        ),
        name="attend_back",
    )(queries, key_vals, grad, lse, key_ids[:, None], query_ids[None, :])


def add_pair(first, second):
    return first + second


def merge_soft(first, second):
    highest = jnp.maximum(first[0], second[0])
    total = first[1] * jnp.exp(first[0] - highest) + second[1] * jnp.exp(second[0] - highest)
    return jnp.stack([highest, total, first[2] + second[2]])


def dot_rows(left_op, right_op):
    return lax.dot_general(
        left_op, right_op, (((1,), (1,)), ((), ())), preferred_element_type=jnp.float32
    )


def dot_cols(left_op, right_op):
    return lax.dot_general(
        left_op, right_op, (((0,), (0,)), ((), ())), preferred_element_type=jnp.float32
    )


def dot_plain(left_op, right_op):
    return jnp.dot(left_op, right_op, preferred_element_type=jnp.float32)


def column_sums(values):
    return jnp.sum(values.astype(jnp.float32), 0)


def layer_norm(values, gain, shift):
    center = values - jnp.mean(values, -1, keepdims=True)
    spread = jnp.mean(center * center, -1, keepdims=True)
    return center * lax.rsqrt(spread + NORM_EPS) * gain + shift


def norm_back(values, gain, shift, grad):
    unused, pull = jax.vjp(layer_norm, values, gain, shift)
    return pull(grad)


def one_hot(wanted, length, axis):
    shape = list(wanted.shape)
    shape.insert(axis, length)
    at = lax.broadcasted_iota(jnp.int32, shape, axis)
    return (at == jnp.expand_dims(wanted, axis)).astype(jnp.bfloat16)


def counts_before(flags):
    length = flags.shape[-1]
    earlier = (
        lax.broadcasted_iota(jnp.int32, (length, length), 0)
        < lax.broadcasted_iota(jnp.int32, (length, length), 1)
    ).astype(jnp.bfloat16)
    return dot_plain(flags.astype(jnp.bfloat16), earlier).astype(jnp.int32)


def wide(rows_in):
    return jnp.pad(rows_in, ((0, 0), (0, -rows_in.shape[1] % (2 * HEAD))))


def rows_major(x):
    return with_layout_constraint(x, Layout(major_to_minor=tuple(range(x.ndim))))


def scatter_rows(groups):
    total = lax.axis_size(AXES)
    mats = []
    for group in groups:
        parts = [rows_major(dot_cols(*pair).astype(jnp.bfloat16)) for pair in group]
        grad = jnp.concatenate(parts, 0) if len(parts) > 1 else parts[0]
        mats.append(grad.reshape(total, -1, grad.shape[1]))
    blocks = jnp.concatenate(mats, 1) if len(mats) > 1 else mats[0]
    own = lax.psum_scatter(blocks, AXES, scatter_dimension=0, tiled=True)[0]
    return own.reshape(len(mats), -1, own.shape[1])


def layer_forward(state, weights, params, query_ids, key_ids):
    width = state.shape[1]
    hidden = layer_norm(state, params[0 : 1], params[1 : 2]).astype(jnp.bfloat16)
    joined = rows_major(dot_rows(hidden, weights[0][: 3 * width]))
    queries = wide((joined[:, :width] + params[2 : 3]).astype(jnp.bfloat16))
    key_rows = joined[:, width : 2 * width].astype(jnp.bfloat16)
    val_rows = (joined[:, 2 * width :] + params[3 : 4]).astype(jnp.bfloat16)
    own_pair = jnp.concatenate([wide(key_rows), wide(val_rows)], 0)
    attended, lse, key_vals = attend(queries, own_pair, key_ids, query_ids, 4)
    attended = attended[:, :width]
    mid_state = state + dot_plain(attended, weights[0][3 * width :]) + params[4 : 5]
    normed = layer_norm(mid_state, params[5 : 6], params[6 : 7]).astype(jnp.bfloat16)
    upward = dot_rows(normed, weights[1]) + params[8:12].reshape(1, -1)
    active = jax.nn.gelu(upward, approximate=True).astype(jnp.bfloat16)
    output = mid_state + dot_plain(active, weights[2]) + params[7 : 8]
    return (
        output,
        (hidden, queries, key_vals, lse, attended, mid_state, normed, upward, active),
    )


def layer_backward(state, weights, params, saved, query_ids, key_ids, grad_in, arrived):
    width = state.shape[1]
    hidden, queries, key_vals, lse, attended, mid_state, normed, upward, active = saved
    down_grad = grad_in.astype(jnp.bfloat16)
    act_grad = dot_rows(down_grad, weights[2])
    unused_gelu, gelu_pull = jax.vjp(partial(jax.nn.gelu, approximate=True), upward)
    up_grad = gelu_pull(act_grad)[0].astype(jnp.bfloat16)
    mid_back, gain_two, shift_two = norm_back(
        mid_state, params[5 : 6], params[6 : 7], rows_major(dot_plain(up_grad, weights[1]))
    )
    mid_grad = grad_in + mid_back
    out_grad = mid_grad.astype(jnp.bfloat16)
    att_grad = wide(rows_major(dot_rows(out_grad, weights[0][3 * width :]).astype(jnp.bfloat16)))
    if arrived:
        att_grad, arrived[0] = lax.optimization_barrier((att_grad, arrived[0]))
    query_grad, own = attend_back(queries, key_vals, att_grad, lse, key_ids, query_ids, 8)
    query_grad = query_grad[:, :width]
    key_grad, val_grad = own[: own.shape[0] // 2, :width], own[own.shape[0] // 2 :, :width]
    joined_grad = jnp.concatenate([query_grad, key_grad, val_grad], 1)
    state_back, gain_one, shift_one = norm_back(
        state,
        params[0 : 1],
        params[1 : 2],
        rows_major(dot_plain(joined_grad, weights[0][: 3 * width])),
    )
    up_sums = column_sums(up_grad)
    small_grad = [
        gain_one,
        shift_one,
        column_sums(query_grad),
        column_sums(val_grad),
        column_sums(out_grad),
        gain_two,
        shift_two,
        column_sums(down_grad),
        up_sums,
    ]
    factors = [
        [(joined_grad, hidden), (attended, out_grad)],
        [(up_grad, normed)],
        [(active, down_grad)],
    ]
    return (mid_grad + state_back, factors, small_grad)


def adam_step(weights, moment, square, grad, rate, decay, step):
    moment = BETA_ONE * moment + (1 - BETA_ONE) * grad
    square = BETA_TWO * square + (1 - BETA_TWO) * grad * grad
    moment_hat = moment / (1 - BETA_ONE**step)
    square_hat = square / (1 - BETA_TWO**step)
    weights = weights - rate * (moment_hat / (jnp.sqrt(square_hat) + ADAM_EPS) + decay * weights)
    return (weights, moment, square)


def pad_rows(x, rows):
    return jnp.pad(x, ((0, rows - x.shape[0]), (0, 0)))


def on_device(
    tokens,
    block_ids,
    completion,
    regroup,
    targets,
    step_count,
    layer_mats,
    mats_moment,
    mats_square,
    embed_table,
    table_moment,
    table_square,
):
    seqs, tok_count = tokens.shape
    seq_length = block_ids.shape[1]
    width = embed_table.shape[1]
    table_local = embed_table.shape[0]
    layers = layer_mats.shape[0]
    replicas, groups, shards = (lax.axis_size(axis) for axis in AXES)
    total = replicas * groups * shards
    seq_at = lax.axis_index("seq")
    shard_at = lax.axis_index("shard")
    device_at = lax.axis_index(AXES)
    seq_bits, dp_bits, shard_bits = bits_of("seq"), bits_of("dp"), bits_of("shard")
    first_row = device_at * table_local
    table_own = embed_table.astype(jnp.bfloat16)
    mats_low = layer_mats.astype(jnp.bfloat16)
    token_ids = tokens.reshape(-1)
    local_rows = token_ids.shape[0]
    small_count = 12 * layers + 2
    small_rows = -(-small_count // 16) * 16

    packed_ids = jnp.pad(token_ids, (0, -local_rows % 1024)).reshape(-1, 128)
    ids_all = run_jobs([spread_job(packed_ids, False)], "share_ids", 0, 16)[0][0]
    ids_all = ids_all.reshape(total, -1)[:, :local_rows]
    owner_all = ids_all // table_local
    loads = jnp.sum(
        (owner_all[:, :, None] == jnp.arange(total)[None, None, :]).astype(jnp.int32), 1
    )
    rounds = (jnp.max(loads) + SLOTS - 1) // SLOTS
    asked = owner_all == device_at
    asked_rank = counts_before(asked)
    asked_row = ids_all - first_row
    own_owner = token_ids // table_local
    same = own_owner[:, None] == own_owner[None, :]
    before = jnp.arange(local_rows)[None, :] < jnp.arange(local_rows)[:, None]
    own_rank = jnp.sum((same & before).astype(jnp.int32), 1)

    def asked_rows(at):
        chosen = asked[:, None, :] & (
            asked_rank[:, None, :] == at * SLOTS + jnp.arange(SLOTS)[None, :, None]
        )
        return (jnp.sum(jnp.where(chosen, asked_row[:, None, :] + 1, 0), 2) - 1).reshape(-1)

    def own_slots(at):
        slot = own_rank - at * SLOTS
        return jnp.where((slot >= 0) & (slot < SLOTS), own_owner * SLOTS + slot, -1)

    def fetch(at, given):
        return dot_plain(
            one_hot(own_slots(at), total * SLOTS, 1), given.reshape(total * SLOTS, width)
        )

    fixed = jnp.arange(seq_length + small_rows, dtype=jnp.int32)
    fixed_row = jnp.where(fixed < seq_length + small_count, VOCAB + fixed - first_row, -1)
    wanted = jnp.concatenate([asked_rows(0), fixed_row])
    rows_out = dot_plain(one_hot(wanted, table_local, 1), table_own).astype(jnp.bfloat16)
    exchanged = total * SLOTS
    piece = seq_length // total
    gathered = []
    for layer_at in range(layers):
        if layer_at == 0:
            whole = lax.all_gather(mats_low[0], AXES, axis=1, tiled=True)
            gathered.append([whole[k] for k in range(3)])
        else:
            rest = lax.all_gather(mats_low[layer_at, 1:], AXES, axis=1, tiled=True)
            gathered.append([rest[0], rest[1]])
    (upper_first,), (place_rows,), (small,), (given,) = run_jobs(
        [
            gather_job([mats_low[1, 0]]),
            sum_job(
                rows_out[exchanged : exchanged + seq_length].reshape(total, piece, width),
                sum_axes=("seq", "dp", "shard"),
                sum_orders=[seq_bits + dp_bits + shard_bits],
                join_axes=("dp", "shard"),
                join_orders=[shard_bits[::-1] + dp_bits[::-1]],
            ),
            combine_job(rows_out[exchanged + seq_length :], add_pair),
            swap_job(rows_out[:exchanged].reshape(total, SLOTS, width), late=7),
        ],
        "open_rows",
        2,
        32,
    )
    gathered[1].insert(0, upper_first.reshape(-1, width))
    place_rows = place_rows.reshape(tok_count, width)
    small = small[:small_count].astype(jnp.float32)
    place_state = jnp.broadcast_to(place_rows.astype(jnp.float32), (seqs, tok_count, width))
    state = fetch(0, given) + place_state.reshape(local_rows, width)

    def fetch_more(at, held):
        rows = dot_plain(one_hot(asked_rows(at), table_local, 1), table_own).astype(jnp.bfloat16)
        return held + fetch(at, swap(rows.reshape(total, SLOTS, width), "swap_rows", 1))

    state = lax.fori_loop(1, rounds, fetch_more, state)

    query_ids = lax.dynamic_slice_in_dim(block_ids[0], seq_at * tok_count, tok_count, 0)
    inputs, kept, saved = [], [], []
    for layer_at in range(layers):
        weights = gathered[layer_at]
        inputs.append(state)
        kept.append(weights)
        state, held = layer_forward(
            state,
            weights,
            small[12 * layer_at : 12 * layer_at + 12],
            query_ids,
            block_ids[0],
        )
        saved.append(held)
    final_gain = small[12 * layers : 12 * layers + 1]
    final_shift = small[12 * layers + 1 : 12 * layers + 2]
    final = layer_norm(state, final_gain, final_shift).astype(jnp.bfloat16)

    group_mask = completion[0]
    slot_of = regroup[0]
    slots = slot_of.shape[0]
    comp_rows = slots // shards
    rank_all = counts_before(group_mask[None])[0]
    mine = lax.dynamic_slice_in_dim(group_mask, shard_at * local_rows, local_rows)
    my_rank = lax.dynamic_slice_in_dim(rank_all, shard_at * local_rows, local_rows)
    my_slot = jnp.sum(
        jnp.where(my_rank[:, None] == jnp.arange(slots)[None, :], slot_of[None, :], 0), 1
    )
    to_slot = one_hot(jnp.where(mine == 1, my_slot, -1), slots, 0)
    outgoing = dot_plain(to_slot, final).astype(jnp.bfloat16).reshape(shards, comp_rows, width)
    two_ways = [seq_bits[1:] + dp_bits, dp_bits + seq_bits[1:]]
    head_in = exchange(
        outgoing,
        "share_final",
        5,
        sum_axes=("shard",),
        sum_orders=[shard_bits, shard_bits],
        join_axes=AXES,
        join_orders=[shard_bits[::-1] + way[::-1] + seq_bits[:1] for way in two_ways],
        chunks=2,
    ).reshape(-1, width)

    rows_all = targets.shape[0]
    columns = first_row + jnp.arange(table_local, dtype=jnp.int32)
    live = (columns < VOCAB)[None, :]
    logits = dot_rows(head_in, table_own)
    masked = jnp.where(live, logits, MASK_FILL)
    top_local = jnp.max(masked, 1)
    total_local = jnp.sum(jnp.where(live, jnp.exp(masked - top_local[:, None]), 0.0), 1)
    target_hit = columns[None, :] == targets[:, None]
    pick_local = jnp.sum(jnp.where(target_hit, logits, 0.0), 1)
    stats = combine_all(
        jnp.stack([top_local, total_local, pick_local]).reshape(3, -1, 128),
        merge_soft,
        "share_stats",
        6,
    ).reshape(3, rows_all)
    log_total = stats[0] + jnp.log(stats[1])
    loss_value = jnp.sum(log_total - stats[2]) / rows_all
    probs = jnp.where(live, jnp.exp(masked - log_total[:, None]), 0.0)
    logit_grad = ((probs - target_hit.astype(jnp.float32)) / rows_all).astype(jnp.bfloat16)
    head_grad = dot_cols(logit_grad, head_in)
    returned = exchange(
        dot_plain(logit_grad, table_own).reshape(total, comp_rows, width),
        "return_final",
        7,
        sum_axes=AXES,
        sum_orders=[seq_bits[:1] + way + shard_bits for way in two_ways],
        join_axes=("shard",),
        join_orders=[shard_bits[::-1], shard_bits[::-1]],
        chunks=2,
    ).reshape(slots, width)
    final_grad = rows_major(dot_cols(to_slot, returned))
    state_grad, gain_final, shift_final = norm_back(state, final_gain, final_shift, final_grad)

    late = []
    arrived = []
    small_grads = [None] * layers
    for layer_at in reversed(range(layers)):
        state_grad, factors, small_grads[layer_at] = layer_backward(
            inputs[layer_at],
            kept[layer_at],
            small[12 * layer_at : 12 * layer_at + 12],
            saved[layer_at],
            query_ids,
            block_ids[0],
            state_grad,
            arrived,
        )
        if layer_at > 0:
            arrived = [scatter_rows(factors[2:]), scatter_rows(factors[1:2])]
            late = factors[:1]
        else:
            late = factors + late

    low_grad = state_grad.astype(jnp.bfloat16)
    place_grad = jnp.sum(state_grad.reshape(seqs, tok_count, width), 0)
    small_grad = jnp.concatenate(
        [x.reshape(-1) for x in sum(small_grads, []) + [gain_final, shift_final]]
    )
    small_size = small_grad.shape[0]
    small_grad = jnp.pad(small_grad, (0, -small_size % 1024)).reshape(-1, 128)

    def leaving(at):
        rows = dot_cols(one_hot(own_slots(at), total * SLOTS, 1), low_grad).astype(jnp.bfloat16)
        return rows.reshape(total, SLOTS, width)

    (low_grad, arrived[1]) = lax.optimization_barrier((low_grad, arrived[1]))
    upper = jnp.concatenate([arrived[1], arrived[0]], 0).astype(jnp.float32)
    late = late_mats(late, 12)
    fits = mats_fit(late)
    own_mats, (place_grad,), (small_grad,), (came,) = run_jobs(
        [
            mats_job(late[:fits]),
            sum_job(
                place_grad.reshape(replicas * shards, piece, width),
                sum_axes=("dp", "shard"),
                sum_orders=[dp_bits + shard_bits],
                join_axes=("seq", "dp", "shard"),
                join_orders=[shard_bits[::-1] + dp_bits[::-1] + seq_bits[::-1]],
            ),
            combine_job(small_grad, add_pair),
            swap_job(leaving(0), late=5),
        ],
        "close_rows",
        10,
        61,
    )
    for k in range(fits, len(late), fits):
        more = run_jobs([mats_job(late[k : k + fits])], "sum_mats", 14 + k, 61)[0]
        own_mats = list(own_mats) + list(lax.optimization_barrier(tuple(more)))
    place_grad = place_grad.reshape(seq_length, width)
    small_grad = pad_rows(small_grad.reshape(-1)[:small_size].reshape(-1, width), small_rows)
    small_high = small_grad.astype(jnp.bfloat16)
    small_low = (small_grad - small_high.astype(jnp.float32)).astype(jnp.bfloat16)
    values = jnp.concatenate([came.reshape(-1, width), place_grad, small_high, small_low], 0)
    value_row = jnp.concatenate([wanted, fixed_row[seq_length:]])
    table_grad = dot_plain(one_hot(value_row, table_local, 0), values) + head_grad

    def return_more(at, held):
        rows = swap(leaving(at), "swap_rows", 1).reshape(-1, width)
        return held + dot_plain(one_hot(asked_rows(at), table_local, 0), rows)

    table_grad = lax.fori_loop(1, rounds, return_more, table_grad)
    mats_grad = jnp.concatenate([jnp.stack(own_mats), upper], 0).reshape(layer_mats.shape)
    local_squares = jnp.sum(mats_grad * mats_grad) + jnp.sum(table_grad * table_grad)
    squares = jnp.full((8, 128), local_squares)
    squares = run_jobs([spread_job(squares, True)], "share_norm", 11, 16)[0][0]
    grad_norm = jnp.sqrt(squares[0, 0])
    factor = CLIP_NORM / grad_norm
    step = step_count[0].astype(jnp.float32)
    new_mats = adam_step(
        layer_mats, mats_moment, mats_square, factor * mats_grad, RATE_MATS, DECAY_RATE, step
    )
    plain_rows = (columns < VOCAB + seq_length)[:, None]
    rate = jnp.where(plain_rows, RATE_TABLE, RATE_SMALL)
    decay = jnp.where(plain_rows, DECAY_RATE, 0.0)
    new_table = adam_step(
        embed_table, table_moment, table_square, factor * table_grad, rate, decay, step
    )
    return (
        loss_value.reshape(1),
        grad_norm.reshape(1),
        new_mats[0],
        new_mats[1],
        new_mats[2],
        new_table[0],
        new_table[1],
        new_table[2],
    )


def solution(mesh):
    in_specs = (
        P(("dp", "shard"), "seq"),
        P(("dp", "shard"), None),
        P(("dp", "seq"), None),
        P(("dp", "seq"), None),
        P(),
        P(),
        P(None, None, ("dp", "seq", "shard"), None),
        P(None, None, ("dp", "seq", "shard"), None),
        P(None, None, ("dp", "seq", "shard"), None),
        P(("dp", "seq", "shard"), None),
        P(("dp", "seq", "shard"), None),
        P(("dp", "seq", "shard"), None),
    )
    out_specs = (
        P(),
        P(),
        P(None, None, ("dp", "seq", "shard"), None),
        P(None, None, ("dp", "seq", "shard"), None),
        P(None, None, ("dp", "seq", "shard"), None),
        P(("dp", "seq", "shard"), None),
        P(("dp", "seq", "shard"), None),
        P(("dp", "seq", "shard"), None),
    )
    return jax.shard_map(
        on_device, mesh=mesh, in_specs=in_specs, out_specs=out_specs, check_vma=False
    )
```

```python
import itertools
from functools import partial

import jax
import jax.numpy as jnp
from jax import lax
from jax.experimental import pallas as pl
from jax.experimental.layout import Layout, with_layout_constraint
from jax.experimental.pallas import tpu as pltpu
from jax.sharding import PartitionSpec as P

HEADS = 17
HEAD = 64
VOCAB = 50278

NORM_EPS = 1e-05
CLIP_NORM = 0.02
BETA_ONE = 0.9
BETA_TWO = 0.95
ADAM_EPS = 1e-08
DECAY_RATE = 0.1
RATE_MATS = 0.05
RATE_TABLE = 0.1
RATE_SMALL = 0.5
MASK_FILL = -1e30

AXES = ("dp", "seq", "shard")
MESH = pl.DeviceIdType.MESH
SLOTS = 24


def bits_of(axis):
    return [(axis, b) for b in range(lax.axis_size(axis).bit_length() - 1)]


def bit_here(bit):
    return lax.rem(lax.axis_index(bit[0]) // 2 ** bit[1], 2)


def partner(bit):
    at = lax.axis_index(bit[0])
    return {bit[0]: at + (1 - 2 * bit_here(bit)) * 2 ** bit[1]}


def greet(bits):
    barrier = pltpu.get_barrier_semaphore()
    for bit in bits:
        pl.semaphore_signal(barrier, inc=1, device_id=partner(bit), device_id_type=MESH)
    pl.semaphore_wait(barrier, len(bits))


def block_weight(axes, bit):
    weight = 2 ** bit[1]
    for axis in axes[axes.index(bit[0]) + 1 :]:
        weight *= lax.axis_size(axis)
    return weight


def block_runs(weights):
    weights = sorted(weights)
    joined = 0
    while joined < len(weights) and weights[joined] == 2**joined:
        joined += 1
    rest = [(0, w) for w in weights[joined:]]
    return 2**joined, [sum(c) for c in itertools.product(*rest)]


class Job:
    def __init__(
        self, inputs, outputs, scratch, sends, keeps, bits, steps, spaces=(pltpu.VMEM, pltpu.VMEM)
    ):
        self.inputs, self.outputs, self.scratch = inputs, outputs, scratch
        self.sends, self.keeps, self.bits, self.steps, self.spaces = sends, keeps, bits, steps, spaces


def me_and_total():
    seq_size, shard_size = lax.axis_size("seq"), lax.axis_size("shard")
    at = (lax.axis_index("dp") * seq_size + lax.axis_index("seq")) * shard_size
    return at + lax.axis_index("shard"), lax.axis_size("dp") * seq_size * shard_size


def place_of(at):
    seq_size, shard_size = lax.axis_size("seq"), lax.axis_size("shard")
    return {
        "dp": at // (seq_size * shard_size),
        "seq": lax.rem(at // shard_size, seq_size),
        "shard": lax.rem(at, shard_size),
    }


def greet_all():
    me, total = me_and_total()
    barrier = pltpu.get_barrier_semaphore()

    def hello(k, carry):
        pl.semaphore_signal(
            barrier, inc=1, device_id=place_of(lax.rem(me + k, total)), device_id_type=MESH
        )
        return carry

    lax.fori_loop(1, total, hello, 0)
    pl.semaphore_wait(barrier, total - 1)


class Sems:
    def __init__(self, send, recv, keep):
        self.send, self.recv, self.keep = send, recv, keep
        self.used = self.kept = 0

    def copy(self, source, target, device):
        k = self.used
        self.used += 1
        copy = pltpu.make_async_remote_copy(
            source, target, self.send.at[k], self.recv.at[k], device_id=device, device_id_type=MESH
        )
        copy.start()
        return copy

    def local(self, source, target):
        k = self.kept
        self.kept += 1
        copy = pltpu.make_async_copy(source, target, self.keep.at[k])
        copy.start()
        return copy

    def span(self, count):
        first = self.used
        self.used += count
        return first


def jobs_kernel(jobs, *refs):
    refs = list(refs)

    def take(count):
        out = refs[:count]
        del refs[:count]
        return out

    held = [take(len(job.inputs)) for job in jobs]
    made = [take(len(job.outputs)) for job in jobs]
    used = [take(len(job.scratch)) for job in jobs]
    sems = Sems(*refs)
    if any(job.bits is None for job in jobs):
        greet_all()
    else:
        greet(sorted(set(bit for job in jobs for bit in job.bits)))
    active = []
    for job, x, o, w in zip(jobs, held, made, used):
        active += job.steps(x, o, w, sems)
    tick = 0
    while active:
        left = []
        for delay, gen in active:
            if delay > tick or next(gen, "end") != "end":
                left.append((delay, gen))
        active = left
        tick += 1


def run_jobs(jobs, name, number, vmem=60):
    inputs = [x for job in jobs for x in job.inputs]
    outputs = [o for job in jobs for o in job.outputs]
    in_specs = [pl.BlockSpec(memory_space=job.spaces[0]) for job in jobs for unused in job.inputs]
    out_specs = [pl.BlockSpec(memory_space=job.spaces[1]) for job in jobs for unused in job.outputs]
    sends = sum(job.sends for job in jobs)
    keeps = max(1, sum(job.keeps for job in jobs))
    flat = pl.pallas_call(
        partial(jobs_kernel, jobs),
        out_shape=outputs,
        in_specs=in_specs,
        out_specs=out_specs,
        scratch_shapes=[w for job in jobs for w in job.scratch]
        + [
            pltpu.SemaphoreType.DMA((sends,)),
            pltpu.SemaphoreType.DMA((sends,)),
            pltpu.SemaphoreType.DMA((keeps,)),
        ],
        compiler_params=pltpu.CompilerParams(
            collective_id=number, has_side_effects=True, vmem_limit_bytes=vmem * 2**20
        ),
        name=name,
    )(*inputs)
    out = []
    for job in jobs:
        out.append(flat[: len(job.outputs)])
        flat = flat[len(job.outputs) :]
    return out


def sum_stream(x_ref, o_ref, scratch, sems, rows, first_slot, sum_axes, sums, join_axes, joins):
    source = x_ref
    slot = first_slot
    if sums:
        work, parcel, recv = scratch
    for step, bit in enumerate(sums):
        base = sum(bit_here(b) * block_weight(sum_axes, b) for b in sums[:step])
        weight = block_weight(sum_axes, bit)
        mine = bit_here(bit)
        size, offsets = block_runs([block_weight(sum_axes, b) for b in sums[step + 1 :]])
        started = []
        for offset in offsets:
            leave = base + (1 - mine) * weight + offset
            if source.dtype == parcel.dtype:
                packed = source.at[pl.ds(leave, size), rows]
            else:

                def pack(i, carry, leave=leave, at=slot, source=source):
                    parcel[at + i, rows] = source[leave + i, rows].astype(parcel.dtype)
                    return carry

                lax.fori_loop(0, size, pack, 0)
                packed = parcel.at[pl.ds(slot, size), rows]
            copy = sems.copy(packed, recv.at[pl.ds(slot, size), rows], partner(bit))
            started.append((copy, base + mine * weight + offset, slot, size))
            slot += size
        yield
        for copy, keep, at, size in started:
            copy.wait()

            def add(i, carry, keep=keep, at=at, source=source):
                total = source[keep + i, rows].astype(jnp.float32)
                total = total + recv[at + i, rows].astype(jnp.float32)
                work[keep + i, rows] = total.astype(work.dtype)
                return carry

            lax.fori_loop(0, size, add, 0)
        source = work
    own = sum(bit_here(b) * block_weight(sum_axes, b) for b in sums) if sums else 0
    result = source[own, rows].astype(o_ref.dtype)
    if not joins:
        o_ref[rows] = result
        return
    o_ref[sum(bit_here(b) * block_weight(join_axes, b) for b in joins), rows] = result
    for step, bit in enumerate(joins):
        base = sum(bit_here(b) * block_weight(join_axes, b) for b in joins[step:])
        size, offsets = block_runs([block_weight(join_axes, b) for b in joins[:step]])
        started = []
        for offset in offsets:
            here = o_ref.at[pl.ds(base + offset, size), rows]
            started.append(sems.copy(here, here, partner(bit)))
        yield
        for copy in started:
            copy.wait()


def sum_job(x, sum_axes=(), sum_orders=(), join_axes=(), join_orders=(), chunks=1):
    rows, width = x.shape[-2:]
    blocks = 1
    for axis in join_axes:
        blocks *= lax.axis_size(axis)
    kind = jnp.bfloat16 if sum_axes else x.dtype
    streams = max(len(sum_orders), len(join_orders))
    if rows % (streams * chunks * 16):
        chunks = 1
    share = rows // (streams * chunks)
    sends = 0
    for order in sum_orders:
        for step in range(len(order)):
            sends += len(block_runs([block_weight(sum_axes, b) for b in order[step + 1 :]])[1])
    for order in join_orders:
        for step in range(len(order)):
            sends += len(block_runs([block_weight(join_axes, b) for b in order[:step]])[1])
    scratch = []
    if sum_axes:
        if x.size * 14 > 56 * 2**20:
            x = x.astype(jnp.bfloat16)
        exact = x.dtype == jnp.float32 or x.size < 2**22
        scratch = [
            pltpu.VMEM(x.shape, jnp.float32 if exact else kind),
            pltpu.VMEM(x.shape, kind),
            pltpu.VMEM(x.shape, kind),
        ]

    def steps(x_refs, o_refs, scratch_refs, sems):
        gens = []
        for c in range(chunks):
            for k in range(streams):
                rows_here = pl.ds((k * chunks + c) * share, share)
                sums = sum_orders[k] if sum_orders else []
                joins = join_orders[k] if join_orders else []
                gens.append(
                    (
                        c,
                        sum_stream(
                            x_refs[0], o_refs[0], scratch_refs, sems, rows_here, 0,
                            sum_axes, sums, join_axes, joins,
                        ),
                    )
                )
        return gens

    bits = set(bit for order in list(sum_orders) + list(join_orders) for bit in order)
    shape = (blocks, rows, width) if join_axes else (rows, width)
    return Job(
        [x], [jax.ShapeDtypeStruct(shape, kind)], scratch, sends * chunks, 0, bits, steps
    )


def exchange(x, name, number, **how):
    return run_jobs([sum_job(x, **how)], name, number)[0][0]


def combine_job(x, combine):
    bits = [bit for axis in reversed(AXES) for bit in bits_of(axis)]
    slots = (len(bits),) + x.shape

    def steps(x_refs, o_refs, scratch, sems):
        out_buf, in_buf = scratch

        def gen():
            current = x_refs[0][...]
            for i, bit in enumerate(bits):
                out_buf[i] = current
                copy = sems.copy(out_buf.at[i], in_buf.at[i], partner(bit))
                yield
                copy.wait()
                current, other = out_buf[i], in_buf[i]
                low = bit_here(bit) == 0
                current = combine(jnp.where(low, current, other), jnp.where(low, other, current))
            o_refs[0][...] = current

        return [(0, gen())]

    return Job(
        [x],
        [jax.ShapeDtypeStruct(x.shape, x.dtype)],
        [pltpu.VMEM(slots, x.dtype), pltpu.VMEM(slots, x.dtype)],
        len(bits),
        0,
        bits,
        steps,
    )


def combine_all(x, combine, name, number):
    return run_jobs([combine_job(x, combine)], name, number, 16)[0][0]


def swap_job(x, late=0):
    total = x.shape[0]

    def steps(x_refs, o_refs, scratch, sems):
        x_ref, o_ref = x_refs[0], o_refs[0]

        def gen():
            me, unused = me_and_total()
            first = sems.span(total)
            keep = sems.local(x_ref.at[me], o_ref.at[me])

            def copy_to(other, here):
                return pltpu.make_async_remote_copy(
                    x_ref.at[other],
                    o_ref.at[here],
                    sems.send.at[first + other],
                    sems.recv.at[first + here],
                    device_id=place_of(other),
                    device_id_type=MESH,
                )

            def send(k, carry):
                copy_to(lax.rem(me + k, total), me).start()
                return carry

            lax.fori_loop(1, total, send, 0)
            for unused in range(late + 1):
                yield

            def finish(k, carry):
                other = lax.rem(me + k, total)
                copy_to(other, other).wait()
                return carry

            lax.fori_loop(1, total, finish, 0)
            keep.wait()

        return [(0, gen())]

    return Job(
        [x],
        [jax.ShapeDtypeStruct(x.shape, x.dtype)],
        [],
        total,
        1,
        None,
        steps,
        spaces=(pl.ANY, pl.ANY),
    )


def spread_job(x, add):
    total = lax.axis_size(AXES)
    all_shape = (total,) + x.shape

    def steps(x_refs, o_refs, scratch, sems):
        x_ref = x_refs[0]
        target = scratch[0] if add else o_refs[0]

        def gen():
            me, unused = me_and_total()
            first = sems.span(total)
            target[me] = x_ref[...]

            def copy_to(other, here):
                return pltpu.make_async_remote_copy(
                    x_ref,
                    target.at[here],
                    sems.send.at[first + other],
                    sems.recv.at[first + here],
                    device_id=place_of(other),
                    device_id_type=MESH,
                )

            def send(k, carry):
                copy_to(lax.rem(me + k, total), me).start()
                return carry

            lax.fori_loop(1, total, send, 0)
            yield

            def finish(k, carry):
                other = lax.rem(me + k, total)
                copy_to(other, other).wait()
                return carry

            lax.fori_loop(1, total, finish, 0)
            if add:
                o_refs[0][...] = jnp.sum(target[...], 0)

        return [(0, gen())]

    return Job(
        [x],
        [jax.ShapeDtypeStruct(x.shape if add else all_shape, x.dtype)],
        [pltpu.VMEM(all_shape, x.dtype)] if add else [],
        total,
        0,
        None,
        steps,
    )


def swap(x, name, number):
    return run_jobs([swap_job(x)], name, number, 16)[0][0]


def sum_orders_for(rows):
    across, along, deep = bits_of("seq")[1:], bits_of("dp"), bits_of("shard")
    if rows < 64 or rows % 8:
        return [(0, rows)], [across + along + deep]
    one, two = rows * 8 // 17 // 16 * 16, rows * 6 // 17 // 16 * 16
    spans = [(0, one), (one, two), (one + two, rows - one - two)]
    return spans, [across + along + deep, along + across + deep, deep + along + across]


def mats_stream(x_ref, o_ref, scratch, sems, m, span, order, weights):
    kept, work, parcel, recv = scratch
    turn, m = m % 2, m % work.shape[0]
    steps = len(order)
    rows = pl.ds(*span)
    slot = 0
    rest = sorted((b for b in weights if b != order[0]), key=lambda b: weights[b])
    small = {b: 2**k for k, b in enumerate(rest)}
    for step, bit in enumerate(order):
        mine = bit_here(bit)
        base = sum(bit_here(b) * small[b] for b in order[1:step])
        runs, keeps = [], []
        if step == 0:
            size, offsets = block_runs([weights[b] for b in order[1:]])
            for offset in offsets:
                left, place = offset, 0
                for b in reversed(rest):
                    if left >= weights[b]:
                        left -= weights[b]
                        place += small[b]
                keeps.append(
                    sems.local(
                        x_ref.at[pl.ds(mine * weights[bit] + offset, size), rows],
                        kept.at[turn, pl.ds(place, size), rows],
                    )
                )
                runs.append(((1 - mine) * weights[bit] + offset, place))
        else:
            size, offsets = block_runs([small[b] for b in order[step + 1 :]])
            for offset in offsets:
                here = base + offset
                runs.append((here + (1 - mine) * small[bit], here + mine * small[bit]))
        started = []
        for leave, keep_at in runs:
            at = slot
            slot += size
            if step == 0:
                packed = x_ref.at[pl.ds(leave, size), rows]
            else:
                spot = at - 2 ** (steps - 1)

                def pack(i, carry, leave=leave, spot=spot):
                    parcel[m, spot + i, rows] = work[m, leave + i, rows].astype(parcel.dtype)
                    return carry

                lax.fori_loop(0, size, pack, 0)
                packed = parcel.at[m, pl.ds(spot, size), rows]
            copy = sems.copy(packed, recv.at[m, pl.ds(at, size), rows], partner(bit))
            started.append((copy, at, keep_at, size))
        yield
        for keep in keeps:
            keep.wait()
        for copy, at, keep_at, size in started:
            copy.wait()

            def add(i, carry, at=at, keep_at=keep_at, step=step):
                if step == 0:
                    total = kept[turn, keep_at + i, rows].astype(jnp.float32)
                else:
                    total = work[m, keep_at + i, rows]
                work[m, keep_at + i, rows] = total + recv[m, at + i, rows].astype(jnp.float32)
                return carry

            lax.fori_loop(0, size, add, 0)
    o_ref[rows] = work[m, sum(bit_here(b) * small[b] for b in order[1:]), rows]


def mats_job(mats):
    blocks, rows, width = mats[0].shape
    spans, orders = sum_orders_for(rows)
    weights = {}
    for bit in orders[0]:
        weight = block_weight(AXES, bit)
        weights[bit] = weight if bit[0] == "shard" else weight // 2
    keeps = sends = 0
    for order in orders:
        keeps += len(block_runs([weights[b] for b in order[1:]])[1])
        sends += len(block_runs([weights[b] for b in order[1:]])[1])
        rest = sorted((b for b in weights if b != order[0]), key=lambda b: weights[b])
        small = {b: 2**k for k, b in enumerate(rest)}
        for step in range(1, len(order)):
            sends += len(block_runs([small[b] for b in order[step + 1 :]])[1])
    count = len(mats)

    def steps(x_refs, o_refs, scratch, sems):
        return [
            (m, mats_stream(x_refs[m], o_refs[m], scratch, sems, m, spans[k], orders[k], weights))
            for m in range(count)
            for k in range(len(orders))
        ]

    return Job(
        mats,
        [jax.ShapeDtypeStruct((rows, width), jnp.float32)] * count,
        [
            pltpu.VMEM((min(2, count), blocks // 2, rows, width), jnp.bfloat16),
            pltpu.VMEM((min(3, count), blocks // 2, rows, width), jnp.float32),
            pltpu.VMEM((min(3, count), blocks // 2 - 1, rows, width), jnp.bfloat16),
            pltpu.VMEM((min(3, count), blocks - 1, rows, width), jnp.bfloat16),
        ],
        count * sends,
        count * keeps,
        set(orders[0]),
        steps,
        spaces=(pl.ANY, pltpu.VMEM),
    )


def gather_job(parts):
    rows, width = parts[0].shape
    spans, orders = sum_orders_for(rows)
    orders = [order[::-1] + bits_of("seq")[:1] for order in orders]
    total = lax.axis_size(AXES)
    sends = 0
    for order in orders:
        for step in range(len(order)):
            sends += len(block_runs([block_weight(AXES, b) for b in order[:step]])[1])

    def gen(x_ref, o_ref, sems, span, order):
        here = pl.ds(*span)
        own = me_and_total()[0]
        keep = sems.local(x_ref.at[here], o_ref.at[own, here])
        for step, bit in enumerate(order):
            base = sum(bit_here(b) * block_weight(AXES, b) for b in order[step:])
            size, offsets = block_runs([block_weight(AXES, b) for b in order[:step]])
            started = []
            for offset in offsets:
                target = o_ref.at[pl.ds(base + offset, size), here]
                source = x_ref.at[here] if step == 0 else target
                target = o_ref.at[own, here] if step == 0 else target
                started.append(sems.copy(source, target, partner(bit)))
            yield
            if step == 0:
                keep.wait()
            for copy in started:
                copy.wait()

    def steps(x_refs, o_refs, scratch, sems):
        return [
            (m, gen(x_refs[m], o_refs[m], sems, spans[k], orders[k]))
            for m in range(len(parts))
            for k in range(len(orders))
        ]

    return Job(
        parts,
        [jax.ShapeDtypeStruct((total, rows, width), parts[0].dtype)] * len(parts),
        [],
        sends * len(parts),
        len(orders) * len(parts),
        set(orders[0]),
        steps,
        spaces=(pl.ANY, pl.ANY),
    )


def trade_kernel(halved, count, *refs):
    x_refs, o_refs = refs[:count], refs[count : 2 * count]
    send_sems, recv_sems, keep_sems = refs[2 * count :]
    bit = ("seq", 0)
    mine = bit_here(bit)
    greet([bit])
    copies = []
    for k in range(count):
        if k < halved:
            tokens = x_refs[k].shape[-1]
            keep, leave = x_refs[k].at[:, mine], x_refs[k].at[:, 1 - mine]
            near = o_refs[k].at[:, :, pl.ds(0, tokens)]
            far = o_refs[k].at[:, :, pl.ds(tokens, tokens)]
        else:
            tokens = x_refs[k].shape[0]
            keep = leave = x_refs[k]
            near, far = o_refs[k].at[pl.ds(0, tokens)], o_refs[k].at[pl.ds(tokens, tokens)]
        local = pltpu.make_async_copy(keep, near, keep_sems.at[k])
        local.start()
        copy = pltpu.make_async_remote_copy(
            leave,
            far,
            send_sems.at[k],
            recv_sems.at[k],
            device_id=partner(bit),
            device_id_type=MESH,
        )
        copy.start()
        copies += [local, copy]
    for copy in copies:
        copy.wait()


def trade(features, cotangents, name, number):
    arrays = features + cotangents
    count = len(arrays)
    outs = []
    for x in features:
        runs, unused, rows, tokens = x.shape
        outs.append(jax.ShapeDtypeStruct((runs, rows, 2 * tokens), x.dtype))
    for x in cotangents:
        outs.append(jax.ShapeDtypeStruct((2 * x.shape[0], x.shape[1]), x.dtype))
    return pl.pallas_call(
        partial(trade_kernel, len(features), count),
        out_shape=outs,
        in_specs=[pl.BlockSpec(memory_space=pl.ANY)] * count,
        out_specs=[pl.BlockSpec(memory_space=pltpu.VMEM)] * count,
        scratch_shapes=[pltpu.SemaphoreType.DMA((count,))] * 3,
        compiler_params=pltpu.CompilerParams(
            collective_id=number, has_side_effects=True, vmem_limit_bytes=40 * 2**20
        ),
        name=name,
    )(*arrays)


def late_mats(groups, number):
    pairs = [pair for group in groups for pair in group]
    total = lax.axis_size(AXES)
    height = sum(features.shape[1] for features, unused in groups[0])
    own = height // total * lax.axis_size("shard")
    features = [x.T.reshape(-1, 2, own, x.shape[0]) for x, unused in pairs]
    got = trade(features, [tail for unused, tail in pairs], "trade_rows", number)
    parts = []
    for k in range(len(pairs)):
        both = got[k].reshape(-1, got[k].shape[2])
        parts.append(rows_major(dot_plain(both, got[len(pairs) + k]).astype(jnp.bfloat16)))
    mats = []
    for group in groups:
        grad = jnp.concatenate(parts[: len(group)], 0) if len(group) > 1 else parts[0]
        parts = parts[len(group) :]
        mats.append(grad.reshape(total // 2, -1, grad.shape[1]))
    return mats


def mats_fit(mats):
    blocks, rows, width = mats[0].shape
    tile = -(-rows // 16) * 16 * -(-width // 128) * 128
    fits = (50 * 2**20 - tile * blocks * 2) // (tile * blocks * 5)
    return len(mats) if fits >= 3 else max(1, fits)


def head_lanes(half, shape):
    lane = lax.broadcasted_iota(jnp.int32, shape, 1)
    return (lane < HEAD) if half == 0 else (lane >= HEAD)


def pair_lanes(p):
    return pl.ds(pl.multiple_of(p * 2 * HEAD, 2 * HEAD), 2 * HEAD)


def seq_places():
    me = lax.axis_index("seq")
    return me, partner(("seq", 0))["seq"], partner(("seq", 1))["seq"]


def to_seq(source, target, sems, k, place):
    return pltpu.make_async_remote_copy(
        source,
        target,
        sems.at[0, k],
        sems.at[1, k],
        device_id={"seq": place},
        device_id_type=MESH,
    )


def attend_kernel(
    q_ref, own_ref, key_ids_ref, query_ids_ref, o_ref, lse_ref, kv_ref, blocked, far, near, pass_on, own_sem
):
    rows = own_ref.shape[0] // 2
    keys = kv_ref.shape[0] * rows
    pairs = q_ref.shape[1] // (2 * HEAD)
    me, near_at, far_at = seq_places()
    beyond = near_at + far_at - me
    greet([("seq", 0), ("seq", 1)])

    def far_copy(p, at):
        return to_seq(own_ref.at[:, pair_lanes(p)], kv_ref.at[at, :, pair_lanes(p)], far, p, far_at)

    def near_copy(p, at):
        return to_seq(own_ref.at[:, pair_lanes(p)], kv_ref.at[at, :, pair_lanes(p)], near, p, near_at)

    def pass_copy(p, at):
        here = kv_ref.at[far_at, :, pair_lanes(p)]
        return to_seq(here, kv_ref.at[at, :, pair_lanes(p)], pass_on, p, near_at)

    def send(p, carry):
        far_copy(p, me).start()
        near_copy(p, me).start()
        return carry

    lax.fori_loop(0, pairs, send, 0)
    own = pltpu.make_async_copy(own_ref, kv_ref.at[me], own_sem)
    own.start()
    blocked[...] = jnp.where(key_ids_ref[...] <= query_ids_ref[...], 0.0, MASK_FILL)
    own.wait()

    def forward_one(p):
        far_copy(p, far_at).wait_recv()
        pass_copy(p, far_at).start()

    forward_one(0)

    def pair(p, carry):
        @pl.when(p + 1 < pairs)
        def _():
            forward_one(p + 1)

        near_copy(p, near_at).wait_recv()
        pass_copy(p, beyond).wait_recv()
        lanes = pair_lanes(p)
        key_pair = kv_ref[:, :rows, lanes].reshape(keys, 2 * HEAD)
        val_turned = kv_ref[:, rows:, lanes].reshape(keys, 2 * HEAD).T
        query_pair = q_ref[:, lanes]
        outs = []
        for half in range(2):
            query = jnp.where(head_lanes(half, query_pair.shape), query_pair, 0)
            scores = dot_rows(key_pair, query.astype(jnp.bfloat16)) * HEAD ** (-0.5) + blocked[...]
            top = jnp.max(scores, 0, keepdims=True)
            raised = jnp.exp(scores - top)
            total = jnp.sum(raised, 0, keepdims=True)
            probs = (raised * (1.0 / total)).astype(jnp.bfloat16)
            outs.append(dot_plain(val_turned[half * HEAD : (half + 1) * HEAD], probs))
            lse_ref[p, half] = (top + jnp.log(total))[0]
        o_ref[:, lanes] = jnp.concatenate(outs, 0).T.astype(o_ref.dtype)
        return carry

    lax.fori_loop(0, pairs, pair, 0)

    def sent(p, carry):
        far_copy(p, me).wait_send()
        near_copy(p, me).wait_send()
        pass_copy(p, far_at).wait_send()
        return carry

    lax.fori_loop(0, pairs, sent, 0)


def attend(queries, own_pair, key_ids, query_ids, number):
    rows, width = queries.shape
    keys = key_ids.shape[0]
    pairs = width // (2 * HEAD)
    groups = lax.axis_size("seq")
    copies = pltpu.SemaphoreType.DMA((2, pairs))
    return pl.pallas_call(
        attend_kernel,
        out_shape=(
            jax.ShapeDtypeStruct((rows, width), jnp.bfloat16),
            jax.ShapeDtypeStruct((pairs, 2, rows), jnp.float32),
            jax.ShapeDtypeStruct((groups,) + own_pair.shape, jnp.bfloat16),
        ),
        in_specs=[pl.BlockSpec(memory_space=pltpu.VMEM)] * 4,
        out_specs=(pl.BlockSpec(memory_space=pltpu.VMEM),) * 3,
        scratch_shapes=[
            pltpu.VMEM((keys, rows), jnp.float32),
            copies,
            copies,
            copies,
            pltpu.SemaphoreType.DMA,
        ],
        compiler_params=pltpu.CompilerParams(
            collective_id=number, has_side_effects=True, vmem_limit_bytes=48 * 2**20
        ),
        cost_estimate=pl.CostEstimate(
            flops=4 * rows * keys * width,
            transcendentals=rows * keys * HEADS,
            bytes_accessed=4 * keys * width,
        ),
        name="attend",
    )(queries, own_pair, key_ids[:, None], query_ids[None, :])


def attend_back_kernel(
    q_ref,
    kv_ref,
    grad_ref,
    lse_ref,
    key_ids_ref,
    query_ids_ref,
    dq_ref,
    own_ref,
    blocked,
    fresh,
    kept,
    near_out,
    near_in,
    far_out,
    far_in,
    near,
    far,
):
    groups, twice, unused = kv_ref.shape
    rows = twice // 2
    keys = groups * rows
    pairs = q_ref.shape[1] // (2 * HEAD)
    scale = HEAD ** (-0.5)
    me, near_at, far_at = seq_places()
    low, high = lax.rem(me, 2), me // 2
    greet([("seq", 0), ("seq", 1)])
    blocked[...] = jnp.where(key_ids_ref[...] <= query_ids_ref[...], 0.0, MASK_FILL)

    def near_copy(p):
        return to_seq(near_out.at[p], near_in.at[p], near, p, near_at)

    def far_copy(p):
        return to_seq(far_out.at[p], far_in.at[p], far, p, far_at)

    def middle(p):
        near_copy(p).wait()
        for k in range(2):
            kept[p, k] = kept[p, k] + near_in[p, k].astype(jnp.float32)
        far_out[p] = kept[p, 1 - high].astype(far_out.dtype)
        far_copy(p).start()

    def last(p):
        far_copy(p).wait()
        total = kept[p, high] + far_in[p].astype(jnp.float32)
        own_ref[:, pair_lanes(p)] = total.astype(own_ref.dtype)

    def pair(p, carry):
        lanes = pair_lanes(p)
        key_pair = kv_ref[:, :rows, lanes].reshape(keys, 2 * HEAD)
        val_pair = kv_ref[:, rows:, lanes].reshape(keys, 2 * HEAD)
        key_turned = key_pair.T
        query_pair = q_ref[:, lanes]
        grad_pair = grad_ref[:, lanes]
        key_grad = jnp.zeros((keys, 2 * HEAD), jnp.float32)
        val_grad = jnp.zeros((keys, 2 * HEAD), jnp.float32)
        outs = []
        for half in range(2):
            here = head_lanes(half, query_pair.shape)
            query = jnp.where(here, query_pair, 0).astype(jnp.bfloat16)
            grad = jnp.where(here, grad_pair, 0).astype(jnp.bfloat16)
            scores = dot_rows(key_pair, query) * scale + blocked[...]
            probs = jnp.exp(scores - lse_ref[p, half][None, :])
            prob_grad = dot_rows(val_pair, grad)
            inner = jnp.sum(probs * prob_grad, 0, keepdims=True)
            score_grad = (probs * (prob_grad - inner)).astype(jnp.bfloat16)
            key_grad = key_grad + dot_plain(score_grad, query)
            val_grad = val_grad + dot_plain(probs.astype(jnp.bfloat16), grad)
            outs.append(dot_plain(key_turned[half * HEAD : (half + 1) * HEAD], score_grad))
        dq_ref[:, lanes] = (jnp.concatenate(outs, 0).T * scale).astype(dq_ref.dtype)
        fresh[:, :rows] = (key_grad * scale).reshape(groups, rows, 2 * HEAD)
        fresh[:, rows:] = val_grad.reshape(groups, rows, 2 * HEAD)
        for k in range(2):
            near_out[p, k] = fresh[2 * k + 1 - low].astype(near_out.dtype)
            kept[p, k] = fresh[2 * k + low]
        near_copy(p).start()

        @pl.when(p >= 1)
        def _():
            middle(p - 1)

        @pl.when(p >= 2)
        def _():
            last(p - 2)

        return carry

    lax.fori_loop(0, pairs, pair, 0)
    middle(pairs - 1)
    last(pairs - 2)
    last(pairs - 1)


def attend_back(queries, key_vals, grad, lse, key_ids, query_ids, number):
    rows, width = queries.shape
    keys = key_ids.shape[0]
    pairs = width // (2 * HEAD)
    piece = (2 * rows, 2 * HEAD)
    copies = pltpu.SemaphoreType.DMA((2, pairs))
    return pl.pallas_call(
        attend_back_kernel,
        out_shape=(
            jax.ShapeDtypeStruct((rows, width), jnp.bfloat16),
            jax.ShapeDtypeStruct((2 * rows, width), jnp.bfloat16),
        ),
        in_specs=[pl.BlockSpec(memory_space=pltpu.VMEM)] * 6,
        out_specs=(pl.BlockSpec(memory_space=pltpu.VMEM),) * 2,
        scratch_shapes=[
            pltpu.VMEM((keys, rows), jnp.float32),
            pltpu.VMEM((lax.axis_size("seq"),) + piece, jnp.float32),
            pltpu.VMEM((pairs, 2) + piece, jnp.float32),
            pltpu.VMEM((pairs, 2) + piece, jnp.bfloat16),
            pltpu.VMEM((pairs, 2) + piece, jnp.bfloat16),
            pltpu.VMEM((pairs,) + piece, jnp.bfloat16),
            pltpu.VMEM((pairs,) + piece, jnp.bfloat16),
            copies,
            copies,
        ],
        compiler_params=pltpu.CompilerParams(
            collective_id=number, has_side_effects=True, vmem_limit_bytes=58 * 2**20
        ),
        cost_estimate=pl.CostEstimate(
            flops=10 * rows * keys * width,
            transcendentals=rows * keys * HEADS,
            bytes_accessed=12 * keys * width,
        ),
        name="attend_back",
    )(queries, key_vals, grad, lse, key_ids[:, None], query_ids[None, :])


def add_pair(first, second):
    return first + second


def merge_soft(first, second):
    highest = jnp.maximum(first[0], second[0])
    total = first[1] * jnp.exp(first[0] - highest) + second[1] * jnp.exp(second[0] - highest)
    return jnp.stack([highest, total, first[2] + second[2]])


def dot_rows(left_op, right_op):
    return lax.dot_general(
        left_op, right_op, (((1,), (1,)), ((), ())), preferred_element_type=jnp.float32
    )


def dot_cols(left_op, right_op):
    return lax.dot_general(
        left_op, right_op, (((0,), (0,)), ((), ())), preferred_element_type=jnp.float32
    )


def dot_plain(left_op, right_op):
    return jnp.dot(left_op, right_op, preferred_element_type=jnp.float32)


def column_sums(values):
    return jnp.sum(values.astype(jnp.float32), 0)


def layer_norm(values, gain, shift):
    center = values - jnp.mean(values, -1, keepdims=True)
    spread = jnp.mean(center * center, -1, keepdims=True)
    return center * lax.rsqrt(spread + NORM_EPS) * gain + shift


def norm_back(values, gain, shift, grad):
    unused, pull = jax.vjp(layer_norm, values, gain, shift)
    return pull(grad)


def one_hot(wanted, length, axis):
    shape = list(wanted.shape)
    shape.insert(axis, length)
    at = lax.broadcasted_iota(jnp.int32, shape, axis)
    return (at == jnp.expand_dims(wanted, axis)).astype(jnp.bfloat16)


def counts_before(flags):
    length = flags.shape[-1]
    earlier = (
        lax.broadcasted_iota(jnp.int32, (length, length), 0)
        < lax.broadcasted_iota(jnp.int32, (length, length), 1)
    ).astype(jnp.bfloat16)
    return dot_plain(flags.astype(jnp.bfloat16), earlier).astype(jnp.int32)


def wide(rows_in):
    return jnp.pad(rows_in, ((0, 0), (0, -rows_in.shape[1] % (2 * HEAD))))


def rows_major(x):
    return with_layout_constraint(x, Layout(major_to_minor=tuple(range(x.ndim))))


def scatter_rows(groups):
    total = lax.axis_size(AXES)
    mats = []
    for group in groups:
        parts = [rows_major(dot_cols(*pair).astype(jnp.bfloat16)) for pair in group]
        grad = jnp.concatenate(parts, 0) if len(parts) > 1 else parts[0]
        mats.append(grad.reshape(total, -1, grad.shape[1]))
    blocks = jnp.concatenate(mats, 1) if len(mats) > 1 else mats[0]
    own = lax.psum_scatter(blocks, AXES, scatter_dimension=0, tiled=True)[0]
    return own.reshape(len(mats), -1, own.shape[1])


def layer_forward(state, weights, params, query_ids, key_ids):
    width = state.shape[1]
    hidden = layer_norm(state, params[0 : 1], params[1 : 2]).astype(jnp.bfloat16)
    joined = rows_major(dot_rows(hidden, weights[0][: 3 * width]))
    queries = wide((joined[:, :width] + params[2 : 3]).astype(jnp.bfloat16))
    key_rows = joined[:, width : 2 * width].astype(jnp.bfloat16)
    val_rows = (joined[:, 2 * width :] + params[3 : 4]).astype(jnp.bfloat16)
    own_pair = jnp.concatenate([wide(key_rows), wide(val_rows)], 0)
    attended, lse, key_vals = attend(queries, own_pair, key_ids, query_ids, 4)
    attended = attended[:, :width]
    mid_state = state + dot_plain(attended, weights[0][3 * width :]) + params[4 : 5]
    normed = layer_norm(mid_state, params[5 : 6], params[6 : 7]).astype(jnp.bfloat16)
    upward = dot_rows(normed, weights[1]) + params[8:12].reshape(1, -1)
    active = jax.nn.gelu(upward, approximate=True).astype(jnp.bfloat16)
    output = mid_state + dot_plain(active, weights[2]) + params[7 : 8]
    return (
        output,
        (hidden, queries, key_vals, lse, attended, mid_state, normed, upward, active),
    )


def layer_backward(state, weights, params, saved, query_ids, key_ids, grad_in, arrived):
    width = state.shape[1]
    hidden, queries, key_vals, lse, attended, mid_state, normed, upward, active = saved
    down_grad = grad_in.astype(jnp.bfloat16)
    act_grad = dot_rows(down_grad, weights[2])
    unused_gelu, gelu_pull = jax.vjp(partial(jax.nn.gelu, approximate=True), upward)
    up_grad = gelu_pull(act_grad)[0].astype(jnp.bfloat16)
    mid_back, gain_two, shift_two = norm_back(
        mid_state, params[5 : 6], params[6 : 7], rows_major(dot_plain(up_grad, weights[1]))
    )
    mid_grad = grad_in + mid_back
    out_grad = mid_grad.astype(jnp.bfloat16)
    att_grad = wide(rows_major(dot_rows(out_grad, weights[0][3 * width :]).astype(jnp.bfloat16)))
    if arrived:
        att_grad, arrived[0] = lax.optimization_barrier((att_grad, arrived[0]))
    query_grad, own = attend_back(queries, key_vals, att_grad, lse, key_ids, query_ids, 8)
    query_grad = query_grad[:, :width]
    key_grad, val_grad = own[: own.shape[0] // 2, :width], own[own.shape[0] // 2 :, :width]
    joined_grad = jnp.concatenate([query_grad, key_grad, val_grad], 1)
    state_back, gain_one, shift_one = norm_back(
        state,
        params[0 : 1],
        params[1 : 2],
        rows_major(dot_plain(joined_grad, weights[0][: 3 * width])),
    )
    up_sums = column_sums(up_grad)
    small_grad = [
        gain_one,
        shift_one,
        column_sums(query_grad),
        column_sums(val_grad),
        column_sums(out_grad),
        gain_two,
        shift_two,
        column_sums(down_grad),
        up_sums,
    ]
    factors = [
        [(joined_grad, hidden), (attended, out_grad)],
        [(up_grad, normed)],
        [(active, down_grad)],
    ]
    return (mid_grad + state_back, factors, small_grad)


def adam_step(weights, moment, square, grad, rate, decay, step):
    moment = BETA_ONE * moment + (1 - BETA_ONE) * grad
    square = BETA_TWO * square + (1 - BETA_TWO) * grad * grad
    moment_hat = moment / (1 - BETA_ONE**step)
    square_hat = square / (1 - BETA_TWO**step)
    weights = weights - rate * (moment_hat / (jnp.sqrt(square_hat) + ADAM_EPS) + decay * weights)
    return (weights, moment, square)


def pad_rows(x, rows):
    return jnp.pad(x, ((0, rows - x.shape[0]), (0, 0)))


def on_device(
    tokens,
    block_ids,
    completion,
    regroup,
    targets,
    step_count,
    layer_mats,
    mats_moment,
    mats_square,
    embed_table,
    table_moment,
    table_square,
):
    seqs, tok_count = tokens.shape
    seq_length = block_ids.shape[1]
    width = embed_table.shape[1]
    table_local = embed_table.shape[0]
    layers = layer_mats.shape[0]
    replicas, groups, shards = (lax.axis_size(axis) for axis in AXES)
    total = replicas * groups * shards
    seq_at = lax.axis_index("seq")
    shard_at = lax.axis_index("shard")
    device_at = lax.axis_index(AXES)
    seq_bits, dp_bits, shard_bits = bits_of("seq"), bits_of("dp"), bits_of("shard")
    first_row = device_at * table_local
    table_own = embed_table.astype(jnp.bfloat16)
    mats_low = layer_mats.astype(jnp.bfloat16)
    token_ids = tokens.reshape(-1)
    local_rows = token_ids.shape[0]
    small_count = 12 * layers + 2
    small_rows = -(-small_count // 16) * 16

    packed_ids = jnp.pad(token_ids, (0, -local_rows % 1024)).reshape(-1, 128)
    ids_all = run_jobs([spread_job(packed_ids, False)], "share_ids", 0, 16)[0][0]
    ids_all = ids_all.reshape(total, -1)[:, :local_rows]
    owner_all = ids_all // table_local
    loads = jnp.sum(
        (owner_all[:, :, None] == jnp.arange(total)[None, None, :]).astype(jnp.int32), 1
    )
    rounds = (jnp.max(loads) + SLOTS - 1) // SLOTS
    asked = owner_all == device_at
    asked_rank = counts_before(asked)
    asked_row = ids_all - first_row
    own_owner = token_ids // table_local
    same = own_owner[:, None] == own_owner[None, :]
    before = jnp.arange(local_rows)[None, :] < jnp.arange(local_rows)[:, None]
    own_rank = jnp.sum((same & before).astype(jnp.int32), 1)

    def asked_rows(at):
        chosen = asked[:, None, :] & (
            asked_rank[:, None, :] == at * SLOTS + jnp.arange(SLOTS)[None, :, None]
        )
        return (jnp.sum(jnp.where(chosen, asked_row[:, None, :] + 1, 0), 2) - 1).reshape(-1)

    def own_slots(at):
        slot = own_rank - at * SLOTS
        return jnp.where((slot >= 0) & (slot < SLOTS), own_owner * SLOTS + slot, -1)

    def fetch(at, given):
        return dot_plain(
            one_hot(own_slots(at), total * SLOTS, 1), given.reshape(total * SLOTS, width)
        )

    fixed = jnp.arange(seq_length + small_rows, dtype=jnp.int32)
    fixed_row = jnp.where(fixed < seq_length + small_count, VOCAB + fixed - first_row, -1)
    wanted = jnp.concatenate([asked_rows(0), fixed_row])
    rows_out = dot_plain(one_hot(wanted, table_local, 1), table_own).astype(jnp.bfloat16)
    exchanged = total * SLOTS
    piece = seq_length // total
    gathered = []
    for layer_at in range(layers):
        if layer_at == 0:
            whole = lax.all_gather(mats_low[0], AXES, axis=1, tiled=True)
            gathered.append([whole[k] for k in range(3)])
        else:
            rest = lax.all_gather(mats_low[layer_at, 1:], AXES, axis=1, tiled=True)
            gathered.append([rest[0], rest[1]])
    (upper_first,), (place_rows,), (small,), (given,) = run_jobs(
        [
            gather_job([mats_low[1, 0]]),
            sum_job(
                rows_out[exchanged : exchanged + seq_length].reshape(total, piece, width),
                sum_axes=("seq", "dp", "shard"),
                sum_orders=[seq_bits + dp_bits + shard_bits],
                join_axes=("dp", "shard"),
                join_orders=[shard_bits[::-1] + dp_bits[::-1]],
            ),
            combine_job(rows_out[exchanged + seq_length :], add_pair),
            swap_job(rows_out[:exchanged].reshape(total, SLOTS, width), late=7),
        ],
        "open_rows",
        2,
        32,
    )
    gathered[1].insert(0, upper_first.reshape(-1, width))
    place_rows = place_rows.reshape(tok_count, width)
    small = small[:small_count].astype(jnp.float32)
    place_state = jnp.broadcast_to(place_rows.astype(jnp.float32), (seqs, tok_count, width))
    state = fetch(0, given) + place_state.reshape(local_rows, width)

    def fetch_more(at, held):
        rows = dot_plain(one_hot(asked_rows(at), table_local, 1), table_own).astype(jnp.bfloat16)
        return held + fetch(at, swap(rows.reshape(total, SLOTS, width), "swap_rows", 1))

    state = lax.fori_loop(1, rounds, fetch_more, state)

    query_ids = lax.dynamic_slice_in_dim(block_ids[0], seq_at * tok_count, tok_count, 0)
    inputs, kept, saved = [], [], []
    for layer_at in range(layers):
        weights = gathered[layer_at]
        inputs.append(state)
        kept.append(weights)
        state, held = layer_forward(
            state,
            weights,
            small[12 * layer_at : 12 * layer_at + 12],
            query_ids,
            block_ids[0],
        )
        saved.append(held)
    final_gain = small[12 * layers : 12 * layers + 1]
    final_shift = small[12 * layers + 1 : 12 * layers + 2]
    final = layer_norm(state, final_gain, final_shift).astype(jnp.bfloat16)

    group_mask = completion[0]
    slot_of = regroup[0]
    slots = slot_of.shape[0]
    comp_rows = slots // shards
    rank_all = counts_before(group_mask[None])[0]
    mine = lax.dynamic_slice_in_dim(group_mask, shard_at * local_rows, local_rows)
    my_rank = lax.dynamic_slice_in_dim(rank_all, shard_at * local_rows, local_rows)
    my_slot = jnp.sum(
        jnp.where(my_rank[:, None] == jnp.arange(slots)[None, :], slot_of[None, :], 0), 1
    )
    to_slot = one_hot(jnp.where(mine == 1, my_slot, -1), slots, 0)
    outgoing = dot_plain(to_slot, final).astype(jnp.bfloat16).reshape(shards, comp_rows, width)
    two_ways = [seq_bits[1:] + dp_bits, dp_bits + seq_bits[1:]]
    head_in = exchange(
        outgoing,
        "share_final",
        5,
        sum_axes=("shard",),
        sum_orders=[shard_bits, shard_bits],
        join_axes=AXES,
        join_orders=[shard_bits[::-1] + way[::-1] + seq_bits[:1] for way in two_ways],
        chunks=2,
    ).reshape(-1, width)

    rows_all = targets.shape[0]
    columns = first_row + jnp.arange(table_local, dtype=jnp.int32)
    live = (columns < VOCAB)[None, :]
    logits = dot_rows(head_in, table_own)
    masked = jnp.where(live, logits, MASK_FILL)
    top_local = jnp.max(masked, 1)
    total_local = jnp.sum(jnp.where(live, jnp.exp(masked - top_local[:, None]), 0.0), 1)
    target_hit = columns[None, :] == targets[:, None]
    pick_local = jnp.sum(jnp.where(target_hit, logits, 0.0), 1)
    stats = combine_all(
        jnp.stack([top_local, total_local, pick_local]).reshape(3, -1, 128),
        merge_soft,
        "share_stats",
        6,
    ).reshape(3, rows_all)
    log_total = stats[0] + jnp.log(stats[1])
    loss_value = jnp.sum(log_total - stats[2]) / rows_all
    probs = jnp.where(live, jnp.exp(masked - log_total[:, None]), 0.0)
    logit_grad = ((probs - target_hit.astype(jnp.float32)) / rows_all).astype(jnp.bfloat16)
    head_grad = dot_cols(logit_grad, head_in)
    returned = exchange(
        dot_plain(logit_grad, table_own).reshape(total, comp_rows, width),
        "return_final",
        7,
        sum_axes=AXES,
        sum_orders=[seq_bits[:1] + way + shard_bits for way in two_ways],
        join_axes=("shard",),
        join_orders=[shard_bits[::-1], shard_bits[::-1]],
        chunks=2,
    ).reshape(slots, width)
    final_grad = rows_major(dot_cols(to_slot, returned))
    state_grad, gain_final, shift_final = norm_back(state, final_gain, final_shift, final_grad)

    late = []
    arrived = []
    small_grads = [None] * layers
    for layer_at in reversed(range(layers)):
        state_grad, factors, small_grads[layer_at] = layer_backward(
            inputs[layer_at],
            kept[layer_at],
            small[12 * layer_at : 12 * layer_at + 12],
            saved[layer_at],
            query_ids,
            block_ids[0],
            state_grad,
            arrived,
        )
        if layer_at > 0:
            arrived = [scatter_rows(factors[2:]), scatter_rows(factors[1:2])]
            late = factors[:1]
        else:
            late = factors + late

    low_grad = state_grad.astype(jnp.bfloat16)
    place_grad = jnp.sum(state_grad.reshape(seqs, tok_count, width), 0)
    small_grad = jnp.concatenate(
        [x.reshape(-1) for x in sum(small_grads, []) + [gain_final, shift_final]]
    )
    small_size = small_grad.shape[0]
    small_grad = jnp.pad(small_grad, (0, -small_size % 1024)).reshape(-1, 128)

    def leaving(at):
        rows = dot_cols(one_hot(own_slots(at), total * SLOTS, 1), low_grad).astype(jnp.bfloat16)
        return rows.reshape(total, SLOTS, width)

    late = late_mats(late, 12)
    late, arrived[1] = lax.optimization_barrier((late, arrived[1]))
    upper = jnp.concatenate([arrived[1], arrived[0]], 0).astype(jnp.float32)
    fits = mats_fit(late)
    own_mats, (place_grad,), (small_grad,), (came,) = run_jobs(
        [
            mats_job(late[:fits]),
            sum_job(
                place_grad.reshape(replicas * shards, piece, width),
                sum_axes=("dp", "shard"),
                sum_orders=[dp_bits + shard_bits],
                join_axes=("seq", "dp", "shard"),
                join_orders=[shard_bits[::-1] + dp_bits[::-1] + seq_bits[::-1]],
            ),
            combine_job(small_grad, add_pair),
            swap_job(leaving(0), late=5),
        ],
        "close_rows",
        10,
        61,
    )
    for k in range(fits, len(late), fits):
        more = run_jobs([mats_job(late[k : k + fits])], "sum_mats", 14 + k, 61)[0]
        own_mats = list(own_mats) + list(lax.optimization_barrier(tuple(more)))
    place_grad = place_grad.reshape(seq_length, width)
    small_grad = pad_rows(small_grad.reshape(-1)[:small_size].reshape(-1, width), small_rows)
    small_high = small_grad.astype(jnp.bfloat16)
    small_low = (small_grad - small_high.astype(jnp.float32)).astype(jnp.bfloat16)
    values = jnp.concatenate([came.reshape(-1, width), place_grad, small_high, small_low], 0)
    value_row = jnp.concatenate([wanted, fixed_row[seq_length:]])
    table_grad = dot_plain(one_hot(value_row, table_local, 0), values) + head_grad

    def return_more(at, held):
        rows = swap(leaving(at), "swap_rows", 1).reshape(-1, width)
        return held + dot_plain(one_hot(asked_rows(at), table_local, 0), rows)

    table_grad = lax.fori_loop(1, rounds, return_more, table_grad)
    mats_grad = jnp.concatenate([jnp.stack(own_mats), upper], 0).reshape(layer_mats.shape)
    local_squares = jnp.sum(mats_grad * mats_grad) + jnp.sum(table_grad * table_grad)
    squares = jnp.full((8, 128), local_squares)
    squares = run_jobs([spread_job(squares, True)], "share_norm", 11, 16)[0][0]
    grad_norm = jnp.sqrt(squares[0, 0])
    factor = CLIP_NORM / grad_norm
    step = step_count[0].astype(jnp.float32)
    new_mats = adam_step(
        layer_mats, mats_moment, mats_square, factor * mats_grad, RATE_MATS, DECAY_RATE, step
    )
    plain_rows = (columns < VOCAB + seq_length)[:, None]
    rate = jnp.where(plain_rows, RATE_TABLE, RATE_SMALL)
    decay = jnp.where(plain_rows, DECAY_RATE, 0.0)
    new_table = adam_step(
        embed_table, table_moment, table_square, factor * table_grad, rate, decay, step
    )
    return (
        loss_value.reshape(1),
        grad_norm.reshape(1),
        new_mats[0],
        new_mats[1],
        new_mats[2],
        new_table[0],
        new_table[1],
        new_table[2],
    )


def solution(mesh):
    in_specs = (
        P(("dp", "shard"), "seq"),
        P(("dp", "shard"), None),
        P(("dp", "seq"), None),
        P(("dp", "seq"), None),
        P(),
        P(),
        P(None, None, ("dp", "seq", "shard"), None),
        P(None, None, ("dp", "seq", "shard"), None),
        P(None, None, ("dp", "seq", "shard"), None),
        P(("dp", "seq", "shard"), None),
        P(("dp", "seq", "shard"), None),
        P(("dp", "seq", "shard"), None),
    )
    out_specs = (
        P(),
        P(),
        P(None, None, ("dp", "seq", "shard"), None),
        P(None, None, ("dp", "seq", "shard"), None),
        P(None, None, ("dp", "seq", "shard"), None),
        P(("dp", "seq", "shard"), None),
        P(("dp", "seq", "shard"), None),
        P(("dp", "seq", "shard"), None),
    )
    return jax.shard_map(
        on_device, mesh=mesh, in_specs=in_specs, out_specs=out_specs, check_vma=False
    )
```

```python
import itertools
from functools import partial

import jax
import jax.numpy as jnp
from jax import lax
from jax.experimental import pallas as pl
from jax.experimental.layout import Layout, with_layout_constraint
from jax.experimental.pallas import tpu as pltpu
from jax.sharding import PartitionSpec as P

HEADS = 17
HEAD = 64
VOCAB = 50278

NORM_EPS = 1e-05
CLIP_NORM = 0.02
BETA_ONE = 0.9
BETA_TWO = 0.95
ADAM_EPS = 1e-08
DECAY_RATE = 0.1
RATE_MATS = 0.05
RATE_TABLE = 0.1
RATE_SMALL = 0.5
MASK_FILL = -1e30

AXES = ("dp", "seq", "shard")
MESH = pl.DeviceIdType.MESH
SLOTS = 24


def bits_of(axis):
    return [(axis, b) for b in range(lax.axis_size(axis).bit_length() - 1)]


def bit_here(bit):
    return lax.rem(lax.axis_index(bit[0]) // 2 ** bit[1], 2)


def partner(bit):
    at = lax.axis_index(bit[0])
    return {bit[0]: at + (1 - 2 * bit_here(bit)) * 2 ** bit[1]}


def greet(bits):
    barrier = pltpu.get_barrier_semaphore()
    for bit in bits:
        pl.semaphore_signal(barrier, inc=1, device_id=partner(bit), device_id_type=MESH)
    pl.semaphore_wait(barrier, len(bits))


def block_weight(axes, bit):
    weight = 2 ** bit[1]
    for axis in axes[axes.index(bit[0]) + 1 :]:
        weight *= lax.axis_size(axis)
    return weight


def block_runs(weights):
    weights = sorted(weights)
    joined = 0
    while joined < len(weights) and weights[joined] == 2**joined:
        joined += 1
    rest = [(0, w) for w in weights[joined:]]
    return 2**joined, [sum(c) for c in itertools.product(*rest)]


class Job:
    def __init__(
        self, inputs, outputs, scratch, sends, keeps, bits, steps, spaces=(pltpu.VMEM, pltpu.VMEM)
    ):
        self.inputs, self.outputs, self.scratch = inputs, outputs, scratch
        self.sends, self.keeps, self.bits, self.steps, self.spaces = sends, keeps, bits, steps, spaces


def me_and_total():
    seq_size, shard_size = lax.axis_size("seq"), lax.axis_size("shard")
    at = (lax.axis_index("dp") * seq_size + lax.axis_index("seq")) * shard_size
    return at + lax.axis_index("shard"), lax.axis_size("dp") * seq_size * shard_size


def place_of(at):
    seq_size, shard_size = lax.axis_size("seq"), lax.axis_size("shard")
    return {
        "dp": at // (seq_size * shard_size),
        "seq": lax.rem(at // shard_size, seq_size),
        "shard": lax.rem(at, shard_size),
    }


def greet_all():
    me, total = me_and_total()
    barrier = pltpu.get_barrier_semaphore()

    def hello(k, carry):
        pl.semaphore_signal(
            barrier, inc=1, device_id=place_of(lax.rem(me + k, total)), device_id_type=MESH
        )
        return carry

    lax.fori_loop(1, total, hello, 0)
    pl.semaphore_wait(barrier, total - 1)


class Sems:
    def __init__(self, send, recv, keep):
        self.send, self.recv, self.keep = send, recv, keep
        self.used = self.kept = 0

    def copy(self, source, target, device):
        k = self.used
        self.used += 1
        copy = pltpu.make_async_remote_copy(
            source, target, self.send.at[k], self.recv.at[k], device_id=device, device_id_type=MESH
        )
        copy.start()
        return copy

    def local(self, source, target):
        k = self.kept
        self.kept += 1
        copy = pltpu.make_async_copy(source, target, self.keep.at[k])
        copy.start()
        return copy

    def span(self, count):
        first = self.used
        self.used += count
        return first


def jobs_kernel(jobs, *refs):
    refs = list(refs)

    def take(count):
        out = refs[:count]
        del refs[:count]
        return out

    held = [take(len(job.inputs)) for job in jobs]
    made = [take(len(job.outputs)) for job in jobs]
    used = [take(len(job.scratch)) for job in jobs]
    sems = Sems(*refs)
    if any(job.bits is None for job in jobs):
        greet_all()
    else:
        greet(sorted(set(bit for job in jobs for bit in job.bits)))
    active = []
    for job, x, o, w in zip(jobs, held, made, used):
        active += job.steps(x, o, w, sems)
    tick = 0
    while active:
        left = []
        for delay, gen in active:
            if delay > tick or next(gen, "end") != "end":
                left.append((delay, gen))
        active = left
        tick += 1


def run_jobs(jobs, name, number, vmem=60):
    inputs = [x for job in jobs for x in job.inputs]
    outputs = [o for job in jobs for o in job.outputs]
    in_specs = [pl.BlockSpec(memory_space=job.spaces[0]) for job in jobs for unused in job.inputs]
    out_specs = [pl.BlockSpec(memory_space=job.spaces[1]) for job in jobs for unused in job.outputs]
    sends = sum(job.sends for job in jobs)
    keeps = max(1, sum(job.keeps for job in jobs))
    flat = pl.pallas_call(
        partial(jobs_kernel, jobs),
        out_shape=outputs,
        in_specs=in_specs,
        out_specs=out_specs,
        scratch_shapes=[w for job in jobs for w in job.scratch]
        + [
            pltpu.SemaphoreType.DMA((sends,)),
            pltpu.SemaphoreType.DMA((sends,)),
            pltpu.SemaphoreType.DMA((keeps,)),
        ],
        compiler_params=pltpu.CompilerParams(
            collective_id=number, has_side_effects=True, vmem_limit_bytes=vmem * 2**20
        ),
        name=name,
    )(*inputs)
    out = []
    for job in jobs:
        out.append(flat[: len(job.outputs)])
        flat = flat[len(job.outputs) :]
    return out


def sum_stream(x_ref, o_ref, scratch, sems, rows, first_slot, sum_axes, sums, join_axes, joins):
    source = x_ref
    slot = first_slot
    if sums:
        work, parcel, recv = scratch
    for step, bit in enumerate(sums):
        base = sum(bit_here(b) * block_weight(sum_axes, b) for b in sums[:step])
        weight = block_weight(sum_axes, bit)
        mine = bit_here(bit)
        size, offsets = block_runs([block_weight(sum_axes, b) for b in sums[step + 1 :]])
        started = []
        for offset in offsets:
            leave = base + (1 - mine) * weight + offset
            if source.dtype == parcel.dtype:
                packed = source.at[pl.ds(leave, size), rows]
            else:

                def pack(i, carry, leave=leave, at=slot, source=source):
                    parcel[at + i, rows] = source[leave + i, rows].astype(parcel.dtype)
                    return carry

                lax.fori_loop(0, size, pack, 0)
                packed = parcel.at[pl.ds(slot, size), rows]
            copy = sems.copy(packed, recv.at[pl.ds(slot, size), rows], partner(bit))
            started.append((copy, base + mine * weight + offset, slot, size))
            slot += size
        yield
        for copy, keep, at, size in started:
            copy.wait()

            def add(i, carry, keep=keep, at=at, source=source):
                total = source[keep + i, rows].astype(jnp.float32)
                total = total + recv[at + i, rows].astype(jnp.float32)
                work[keep + i, rows] = total.astype(work.dtype)
                return carry

            lax.fori_loop(0, size, add, 0)
        source = work
    own = sum(bit_here(b) * block_weight(sum_axes, b) for b in sums) if sums else 0
    result = source[own, rows].astype(o_ref.dtype)
    if not joins:
        o_ref[rows] = result
        return
    o_ref[sum(bit_here(b) * block_weight(join_axes, b) for b in joins), rows] = result
    for step, bit in enumerate(joins):
        base = sum(bit_here(b) * block_weight(join_axes, b) for b in joins[step:])
        size, offsets = block_runs([block_weight(join_axes, b) for b in joins[:step]])
        started = []
        for offset in offsets:
            here = o_ref.at[pl.ds(base + offset, size), rows]
            started.append(sems.copy(here, here, partner(bit)))
        yield
        for copy in started:
            copy.wait()


def sum_job(x, sum_axes=(), sum_orders=(), join_axes=(), join_orders=(), chunks=1):
    rows, width = x.shape[-2:]
    blocks = 1
    for axis in join_axes:
        blocks *= lax.axis_size(axis)
    kind = jnp.bfloat16 if sum_axes else x.dtype
    streams = max(len(sum_orders), len(join_orders))
    if rows % (streams * chunks * 16):
        chunks = 1
    share = rows // (streams * chunks)
    sends = 0
    for order in sum_orders:
        for step in range(len(order)):
            sends += len(block_runs([block_weight(sum_axes, b) for b in order[step + 1 :]])[1])
    for order in join_orders:
        for step in range(len(order)):
            sends += len(block_runs([block_weight(join_axes, b) for b in order[:step]])[1])
    scratch = []
    if sum_axes:
        if x.size * 14 > 56 * 2**20:
            x = x.astype(jnp.bfloat16)
        exact = x.dtype == jnp.float32 or x.size < 2**22
        scratch = [
            pltpu.VMEM(x.shape, jnp.float32 if exact else kind),
            pltpu.VMEM(x.shape, kind),
            pltpu.VMEM(x.shape, kind),
        ]

    def steps(x_refs, o_refs, scratch_refs, sems):
        gens = []
        for c in range(chunks):
            for k in range(streams):
                rows_here = pl.ds((k * chunks + c) * share, share)
                sums = sum_orders[k] if sum_orders else []
                joins = join_orders[k] if join_orders else []
                gens.append(
                    (
                        c,
                        sum_stream(
                            x_refs[0], o_refs[0], scratch_refs, sems, rows_here, 0,
                            sum_axes, sums, join_axes, joins,
                        ),
                    )
                )
        return gens

    bits = set(bit for order in list(sum_orders) + list(join_orders) for bit in order)
    shape = (blocks, rows, width) if join_axes else (rows, width)
    return Job(
        [x], [jax.ShapeDtypeStruct(shape, kind)], scratch, sends * chunks, 0, bits, steps
    )


def exchange(x, name, number, **how):
    return run_jobs([sum_job(x, **how)], name, number)[0][0]


def combine_job(x, combine):
    bits = [bit for axis in reversed(AXES) for bit in bits_of(axis)]
    slots = (len(bits),) + x.shape

    def steps(x_refs, o_refs, scratch, sems):
        out_buf, in_buf = scratch

        def gen():
            current = x_refs[0][...]
            for i, bit in enumerate(bits):
                out_buf[i] = current
                copy = sems.copy(out_buf.at[i], in_buf.at[i], partner(bit))
                yield
                copy.wait()
                current, other = out_buf[i], in_buf[i]
                low = bit_here(bit) == 0
                current = combine(jnp.where(low, current, other), jnp.where(low, other, current))
            o_refs[0][...] = current

        return [(0, gen())]

    return Job(
        [x],
        [jax.ShapeDtypeStruct(x.shape, x.dtype)],
        [pltpu.VMEM(slots, x.dtype), pltpu.VMEM(slots, x.dtype)],
        len(bits),
        0,
        bits,
        steps,
    )


def combine_all(x, combine, name, number):
    return run_jobs([combine_job(x, combine)], name, number, 16)[0][0]


def swap_job(x, late=0):
    total = x.shape[0]

    def steps(x_refs, o_refs, scratch, sems):
        x_ref, o_ref = x_refs[0], o_refs[0]

        def gen():
            me, unused = me_and_total()
            first = sems.span(total)
            keep = sems.local(x_ref.at[me], o_ref.at[me])

            def copy_to(other, here):
                return pltpu.make_async_remote_copy(
                    x_ref.at[other],
                    o_ref.at[here],
                    sems.send.at[first + other],
                    sems.recv.at[first + here],
                    device_id=place_of(other),
                    device_id_type=MESH,
                )

            def send(k, carry):
                copy_to(lax.rem(me + k, total), me).start()
                return carry

            lax.fori_loop(1, total, send, 0)
            for unused in range(late + 1):
                yield

            def finish(k, carry):
                other = lax.rem(me + k, total)
                copy_to(other, other).wait()
                return carry

            lax.fori_loop(1, total, finish, 0)
            keep.wait()

        return [(0, gen())]

    return Job(
        [x],
        [jax.ShapeDtypeStruct(x.shape, x.dtype)],
        [],
        total,
        1,
        None,
        steps,
        spaces=(pl.ANY, pl.ANY),
    )


def spread_job(x, add):
    total = lax.axis_size(AXES)
    all_shape = (total,) + x.shape

    def steps(x_refs, o_refs, scratch, sems):
        x_ref = x_refs[0]
        target = scratch[0] if add else o_refs[0]

        def gen():
            me, unused = me_and_total()
            first = sems.span(total)
            target[me] = x_ref[...]

            def copy_to(other, here):
                return pltpu.make_async_remote_copy(
                    x_ref,
                    target.at[here],
                    sems.send.at[first + other],
                    sems.recv.at[first + here],
                    device_id=place_of(other),
                    device_id_type=MESH,
                )

            def send(k, carry):
                copy_to(lax.rem(me + k, total), me).start()
                return carry

            lax.fori_loop(1, total, send, 0)
            yield

            def finish(k, carry):
                other = lax.rem(me + k, total)
                copy_to(other, other).wait()
                return carry

            lax.fori_loop(1, total, finish, 0)
            if add:
                o_refs[0][...] = jnp.sum(target[...], 0)

        return [(0, gen())]

    return Job(
        [x],
        [jax.ShapeDtypeStruct(x.shape if add else all_shape, x.dtype)],
        [pltpu.VMEM(all_shape, x.dtype)] if add else [],
        total,
        0,
        None,
        steps,
    )


def swap(x, name, number):
    return run_jobs([swap_job(x)], name, number, 16)[0][0]


def sum_orders_for(rows):
    across, along, deep = bits_of("seq")[1:], bits_of("dp"), bits_of("shard")
    if rows < 64 or rows % 8:
        return [(0, rows)], [across + along + deep]
    one, two = rows * 8 // 17 // 16 * 16, rows * 6 // 17 // 16 * 16
    spans = [(0, one), (one, two), (one + two, rows - one - two)]
    return spans, [across + along + deep, along + across + deep, deep + along + across]


def mats_stream(x_ref, o_ref, scratch, sems, m, span, order, weights):
    kept, work, parcel, recv = scratch
    which, turn, m = m, m % 2, m % work.shape[0]
    steps = len(order)
    rows = pl.ds(*span)
    slot = 0
    rest = sorted((b for b in weights if b != order[0]), key=lambda b: weights[b])
    small = {b: 2**k for k, b in enumerate(rest)}
    for step, bit in enumerate(order):
        mine = bit_here(bit)
        base = sum(bit_here(b) * small[b] for b in order[1:step])
        runs, keeps = [], []
        if step == 0:
            size, offsets = block_runs([weights[b] for b in order[1:]])
            for offset in offsets:
                left, place = offset, 0
                for b in reversed(rest):
                    if left >= weights[b]:
                        left -= weights[b]
                        place += small[b]
                keeps.append(
                    sems.local(
                        x_ref.at[pl.ds(mine * weights[bit] + offset, size), rows],
                        kept.at[turn, pl.ds(place, size), rows],
                    )
                )
                runs.append(((1 - mine) * weights[bit] + offset, place))
        else:
            size, offsets = block_runs([small[b] for b in order[step + 1 :]])
            for offset in offsets:
                here = base + offset
                runs.append((here + (1 - mine) * small[bit], here + mine * small[bit]))
        started = []
        for leave, keep_at in runs:
            at = slot
            slot += size
            if step == 0:
                packed = x_ref.at[pl.ds(leave, size), rows]
            else:
                spot = at - 2 ** (steps - 1)

                def pack(i, carry, leave=leave, spot=spot):
                    parcel[m, spot + i, rows] = work[m, leave + i, rows].astype(parcel.dtype)
                    return carry

                lax.fori_loop(0, size, pack, 0)
                packed = parcel.at[m, pl.ds(spot, size), rows]
            copy = sems.copy(packed, recv.at[m, pl.ds(at, size), rows], partner(bit))
            started.append((copy, at, keep_at, size))
        yield
        for keep in keeps:
            keep.wait()
        for copy, at, keep_at, size in started:
            copy.wait()

            def add(i, carry, at=at, keep_at=keep_at, step=step):
                if step == 0:
                    total = kept[turn, keep_at + i, rows].astype(jnp.float32)
                else:
                    total = work[m, keep_at + i, rows]
                work[m, keep_at + i, rows] = total + recv[m, at + i, rows].astype(jnp.float32)
                return carry

            lax.fori_loop(0, size, add, 0)
    o_ref[which, rows] = work[m, sum(bit_here(b) * small[b] for b in order[1:]), rows]


def mats_job(mats):
    blocks, rows, width = mats[0].shape
    spans, orders = sum_orders_for(rows)
    weights = {}
    for bit in orders[0]:
        weight = block_weight(AXES, bit)
        weights[bit] = weight if bit[0] == "shard" else weight // 2
    keeps = sends = 0
    for order in orders:
        keeps += len(block_runs([weights[b] for b in order[1:]])[1])
        sends += len(block_runs([weights[b] for b in order[1:]])[1])
        rest = sorted((b for b in weights if b != order[0]), key=lambda b: weights[b])
        small = {b: 2**k for k, b in enumerate(rest)}
        for step in range(1, len(order)):
            sends += len(block_runs([small[b] for b in order[step + 1 :]])[1])
    count = len(mats)

    def steps(x_refs, o_refs, scratch, sems):
        o_ref = o_refs[0]
        return [
            (m, mats_stream(x_refs[m], o_ref, scratch, sems, m, spans[k], orders[k], weights))
            for m in range(count)
            for k in range(len(orders))
        ]

    return Job(
        mats,
        [jax.ShapeDtypeStruct((count, rows, width), jnp.float32)],
        [
            pltpu.VMEM((min(2, count), blocks // 2, rows, width), jnp.bfloat16),
            pltpu.VMEM((min(3, count), blocks // 2, rows, width), jnp.float32),
            pltpu.VMEM((min(3, count), blocks // 2 - 1, rows, width), jnp.bfloat16),
            pltpu.VMEM((min(3, count), blocks - 1, rows, width), jnp.bfloat16),
        ],
        count * sends,
        count * keeps,
        set(orders[0]),
        steps,
        spaces=(pl.ANY, pltpu.VMEM),
    )


def gather_job(parts):
    rows, width = parts[0].shape
    spans, orders = sum_orders_for(rows)
    orders = [order[::-1] + bits_of("seq")[:1] for order in orders]
    total = lax.axis_size(AXES)
    sends = 0
    for order in orders:
        for step in range(len(order)):
            sends += len(block_runs([block_weight(AXES, b) for b in order[:step]])[1])

    def gen(x_ref, o_ref, sems, span, order):
        here = pl.ds(*span)
        own = me_and_total()[0]
        keep = sems.local(x_ref.at[here], o_ref.at[own, here])
        for step, bit in enumerate(order):
            base = sum(bit_here(b) * block_weight(AXES, b) for b in order[step:])
            size, offsets = block_runs([block_weight(AXES, b) for b in order[:step]])
            started = []
            for offset in offsets:
                target = o_ref.at[pl.ds(base + offset, size), here]
                source = x_ref.at[here] if step == 0 else target
                target = o_ref.at[own, here] if step == 0 else target
                started.append(sems.copy(source, target, partner(bit)))
            yield
            if step == 0:
                keep.wait()
            for copy in started:
                copy.wait()

    def steps(x_refs, o_refs, scratch, sems):
        return [
            (m, gen(x_refs[m], o_refs[m], sems, spans[k], orders[k]))
            for m in range(len(parts))
            for k in range(len(orders))
        ]

    return Job(
        parts,
        [jax.ShapeDtypeStruct((total, rows, width), parts[0].dtype)] * len(parts),
        [],
        sends * len(parts),
        len(orders) * len(parts),
        set(orders[0]),
        steps,
        spaces=(pl.ANY, pl.ANY),
    )


def trade_kernel(halved, count, *refs):
    x_refs, o_refs = refs[:count], refs[count : 2 * count]
    send_sems, recv_sems, keep_sems = refs[2 * count :]
    bit = ("seq", 0)
    mine = bit_here(bit)
    greet([bit])
    copies = []
    for k in range(count):
        if k < halved:
            tokens = x_refs[k].shape[-1]
            keep, leave = x_refs[k].at[:, mine], x_refs[k].at[:, 1 - mine]
            near = o_refs[k].at[:, :, pl.ds(0, tokens)]
            far = o_refs[k].at[:, :, pl.ds(tokens, tokens)]
        else:
            tokens = x_refs[k].shape[0]
            keep = leave = x_refs[k]
            near, far = o_refs[k].at[pl.ds(0, tokens)], o_refs[k].at[pl.ds(tokens, tokens)]
        local = pltpu.make_async_copy(keep, near, keep_sems.at[k])
        local.start()
        copy = pltpu.make_async_remote_copy(
            leave,
            far,
            send_sems.at[k],
            recv_sems.at[k],
            device_id=partner(bit),
            device_id_type=MESH,
        )
        copy.start()
        copies += [local, copy]
    for copy in copies:
        copy.wait()


def trade(features, cotangents, name, number):
    arrays = features + cotangents
    count = len(arrays)
    outs = []
    for x in features:
        runs, unused, rows, tokens = x.shape
        outs.append(jax.ShapeDtypeStruct((runs, rows, 2 * tokens), x.dtype))
    for x in cotangents:
        outs.append(jax.ShapeDtypeStruct((2 * x.shape[0], x.shape[1]), x.dtype))
    return pl.pallas_call(
        partial(trade_kernel, len(features), count),
        out_shape=outs,
        in_specs=[pl.BlockSpec(memory_space=pl.ANY)] * count,
        out_specs=[pl.BlockSpec(memory_space=pltpu.VMEM)] * count,
        scratch_shapes=[pltpu.SemaphoreType.DMA((count,))] * 3,
        compiler_params=pltpu.CompilerParams(
            collective_id=number, has_side_effects=True, vmem_limit_bytes=40 * 2**20
        ),
        name=name,
    )(*arrays)


def late_mats(groups, number):
    pairs = [pair for group in groups for pair in group]
    total = lax.axis_size(AXES)
    height = sum(features.shape[1] for features, unused in groups[0])
    own = height // total * lax.axis_size("shard")
    features = [x.T.reshape(-1, 2, own, x.shape[0]) for x, unused in pairs]
    got = trade(features, [tail for unused, tail in pairs], "trade_rows", number)
    parts = []
    for k in range(len(pairs)):
        both = got[k].reshape(-1, got[k].shape[2])
        parts.append(rows_major(dot_plain(both, got[len(pairs) + k]).astype(jnp.bfloat16)))
    mats = []
    for group in groups:
        grad = jnp.concatenate(parts[: len(group)], 0) if len(group) > 1 else parts[0]
        parts = parts[len(group) :]
        mats.append(grad.reshape(total // 2, -1, grad.shape[1]))
    return mats


def mats_fit(mats):
    blocks, rows, width = mats[0].shape
    tile = -(-rows // 16) * 16 * -(-width // 128) * 128
    fits = (50 * 2**20 - tile * blocks * 2) // (tile * blocks * 5)
    return len(mats) if fits >= 3 else max(1, fits)


def head_lanes(half, shape):
    lane = lax.broadcasted_iota(jnp.int32, shape, 1)
    return (lane < HEAD) if half == 0 else (lane >= HEAD)


def pair_lanes(p):
    return pl.ds(pl.multiple_of(p * 2 * HEAD, 2 * HEAD), 2 * HEAD)


def seq_places():
    me = lax.axis_index("seq")
    return me, partner(("seq", 0))["seq"], partner(("seq", 1))["seq"]


def to_seq(source, target, sems, k, place):
    return pltpu.make_async_remote_copy(
        source,
        target,
        sems.at[0, k],
        sems.at[1, k],
        device_id={"seq": place},
        device_id_type=MESH,
    )


def attend_kernel(
    q_ref, own_ref, key_ids_ref, query_ids_ref, o_ref, lse_ref, kv_ref, blocked, far, near, pass_on, own_sem
):
    rows = own_ref.shape[0] // 2
    keys = kv_ref.shape[0] * rows
    pairs = q_ref.shape[1] // (2 * HEAD)
    me, near_at, far_at = seq_places()
    beyond = near_at + far_at - me
    greet([("seq", 0), ("seq", 1)])

    def far_copy(p, at):
        return to_seq(own_ref.at[:, pair_lanes(p)], kv_ref.at[at, :, pair_lanes(p)], far, p, far_at)

    def near_copy(p, at):
        return to_seq(own_ref.at[:, pair_lanes(p)], kv_ref.at[at, :, pair_lanes(p)], near, p, near_at)

    def pass_copy(p, at):
        here = kv_ref.at[far_at, :, pair_lanes(p)]
        return to_seq(here, kv_ref.at[at, :, pair_lanes(p)], pass_on, p, near_at)

    def send(p, carry):
        far_copy(p, me).start()
        near_copy(p, me).start()
        return carry

    lax.fori_loop(0, pairs, send, 0)
    own = pltpu.make_async_copy(own_ref, kv_ref.at[me], own_sem)
    own.start()
    blocked[...] = jnp.where(key_ids_ref[...] <= query_ids_ref[...], 0.0, MASK_FILL)
    own.wait()

    def forward_one(p):
        far_copy(p, far_at).wait_recv()
        pass_copy(p, far_at).start()

    forward_one(0)

    def pair(p, carry):
        @pl.when(p + 1 < pairs)
        def _():
            forward_one(p + 1)

        near_copy(p, near_at).wait_recv()
        pass_copy(p, beyond).wait_recv()
        lanes = pair_lanes(p)
        key_pair = kv_ref[:, :rows, lanes].reshape(keys, 2 * HEAD)
        val_turned = kv_ref[:, rows:, lanes].reshape(keys, 2 * HEAD).T
        query_pair = q_ref[:, lanes]
        outs = []
        for half in range(2):
            query = jnp.where(head_lanes(half, query_pair.shape), query_pair, 0)
            scores = dot_rows(key_pair, query.astype(jnp.bfloat16)) * HEAD ** (-0.5) + blocked[...]
            top = jnp.max(scores, 0, keepdims=True)
            raised = jnp.exp(scores - top)
            total = jnp.sum(raised, 0, keepdims=True)
            probs = (raised * (1.0 / total)).astype(jnp.bfloat16)
            outs.append(dot_plain(val_turned[half * HEAD : (half + 1) * HEAD], probs))
            lse_ref[p, half] = (top + jnp.log(total))[0]
        o_ref[:, lanes] = jnp.concatenate(outs, 0).T.astype(o_ref.dtype)
        return carry

    lax.fori_loop(0, pairs, pair, 0)

    def sent(p, carry):
        far_copy(p, me).wait_send()
        near_copy(p, me).wait_send()
        pass_copy(p, far_at).wait_send()
        return carry

    lax.fori_loop(0, pairs, sent, 0)


def attend(queries, own_pair, key_ids, query_ids, number):
    rows, width = queries.shape
    keys = key_ids.shape[0]
    pairs = width // (2 * HEAD)
    groups = lax.axis_size("seq")
    copies = pltpu.SemaphoreType.DMA((2, pairs))
    return pl.pallas_call(
        attend_kernel,
        out_shape=(
            jax.ShapeDtypeStruct((rows, width), jnp.bfloat16),
            jax.ShapeDtypeStruct((pairs, 2, rows), jnp.float32),
            jax.ShapeDtypeStruct((groups,) + own_pair.shape, jnp.bfloat16),
        ),
        in_specs=[pl.BlockSpec(memory_space=pltpu.VMEM)] * 4,
        out_specs=(pl.BlockSpec(memory_space=pltpu.VMEM),) * 3,
        scratch_shapes=[
            pltpu.VMEM((keys, rows), jnp.float32),
            copies,
            copies,
            copies,
            pltpu.SemaphoreType.DMA,
        ],
        compiler_params=pltpu.CompilerParams(
            collective_id=number, has_side_effects=True, vmem_limit_bytes=48 * 2**20
        ),
        cost_estimate=pl.CostEstimate(
            flops=4 * rows * keys * width,
            transcendentals=rows * keys * HEADS,
            bytes_accessed=4 * keys * width,
        ),
        name="attend",
    )(queries, own_pair, key_ids[:, None], query_ids[None, :])


def attend_back_kernel(
    q_ref,
    kv_ref,
    grad_ref,
    lse_ref,
    key_ids_ref,
    query_ids_ref,
    dq_ref,
    own_ref,
    blocked,
    fresh,
    kept,
    near_out,
    near_in,
    far_out,
    far_in,
    near,
    far,
):
    groups, twice, unused = kv_ref.shape
    rows = twice // 2
    keys = groups * rows
    pairs = q_ref.shape[1] // (2 * HEAD)
    scale = HEAD ** (-0.5)
    me, near_at, far_at = seq_places()
    low, high = lax.rem(me, 2), me // 2
    greet([("seq", 0), ("seq", 1)])
    blocked[...] = jnp.where(key_ids_ref[...] <= query_ids_ref[...], 0.0, MASK_FILL)

    def near_copy(p):
        return to_seq(near_out.at[p], near_in.at[p], near, p, near_at)

    def far_copy(p):
        return to_seq(far_out.at[p], far_in.at[p], far, p, far_at)

    def middle(p):
        near_copy(p).wait()
        for k in range(2):
            kept[p, k] = kept[p, k] + near_in[p, k].astype(jnp.float32)
        far_out[p] = kept[p, 1 - high].astype(far_out.dtype)
        far_copy(p).start()

    def last(p):
        far_copy(p).wait()
        total = kept[p, high] + far_in[p].astype(jnp.float32)
        own_ref[:, pair_lanes(p)] = total.astype(own_ref.dtype)

    def pair(p, carry):
        lanes = pair_lanes(p)
        key_pair = kv_ref[:, :rows, lanes].reshape(keys, 2 * HEAD)
        val_pair = kv_ref[:, rows:, lanes].reshape(keys, 2 * HEAD)
        key_turned = key_pair.T
        query_pair = q_ref[:, lanes]
        grad_pair = grad_ref[:, lanes]
        key_grad = jnp.zeros((keys, 2 * HEAD), jnp.float32)
        val_grad = jnp.zeros((keys, 2 * HEAD), jnp.float32)
        outs = []
        for half in range(2):
            here = head_lanes(half, query_pair.shape)
            query = jnp.where(here, query_pair, 0).astype(jnp.bfloat16)
            grad = jnp.where(here, grad_pair, 0).astype(jnp.bfloat16)
            scores = dot_rows(key_pair, query) * scale + blocked[...]
            probs = jnp.exp(scores - lse_ref[p, half][None, :])
            prob_grad = dot_rows(val_pair, grad)
            inner = jnp.sum(probs * prob_grad, 0, keepdims=True)
            score_grad = (probs * (prob_grad - inner)).astype(jnp.bfloat16)
            key_grad = key_grad + dot_plain(score_grad, query)
            val_grad = val_grad + dot_plain(probs.astype(jnp.bfloat16), grad)
            outs.append(dot_plain(key_turned[half * HEAD : (half + 1) * HEAD], score_grad))
        dq_ref[:, lanes] = (jnp.concatenate(outs, 0).T * scale).astype(dq_ref.dtype)
        fresh[:, :rows] = (key_grad * scale).reshape(groups, rows, 2 * HEAD)
        fresh[:, rows:] = val_grad.reshape(groups, rows, 2 * HEAD)
        for k in range(2):
            near_out[p, k] = fresh[2 * k + 1 - low].astype(near_out.dtype)
            kept[p, k] = fresh[2 * k + low]
        near_copy(p).start()

        @pl.when(p >= 1)
        def _():
            middle(p - 1)

        @pl.when(p >= 2)
        def _():
            last(p - 2)

        return carry

    lax.fori_loop(0, pairs, pair, 0)
    middle(pairs - 1)
    last(pairs - 2)
    last(pairs - 1)


def attend_back(queries, key_vals, grad, lse, key_ids, query_ids, number):
    rows, width = queries.shape
    keys = key_ids.shape[0]
    pairs = width // (2 * HEAD)
    piece = (2 * rows, 2 * HEAD)
    copies = pltpu.SemaphoreType.DMA((2, pairs))
    return pl.pallas_call(
        attend_back_kernel,
        out_shape=(
            jax.ShapeDtypeStruct((rows, width), jnp.bfloat16),
            jax.ShapeDtypeStruct((2 * rows, width), jnp.bfloat16),
        ),
        in_specs=[pl.BlockSpec(memory_space=pltpu.VMEM)] * 6,
        out_specs=(pl.BlockSpec(memory_space=pltpu.VMEM),) * 2,
        scratch_shapes=[
            pltpu.VMEM((keys, rows), jnp.float32),
            pltpu.VMEM((lax.axis_size("seq"),) + piece, jnp.float32),
            pltpu.VMEM((pairs, 2) + piece, jnp.float32),
            pltpu.VMEM((pairs, 2) + piece, jnp.bfloat16),
            pltpu.VMEM((pairs, 2) + piece, jnp.bfloat16),
            pltpu.VMEM((pairs,) + piece, jnp.bfloat16),
            pltpu.VMEM((pairs,) + piece, jnp.bfloat16),
            copies,
            copies,
        ],
        compiler_params=pltpu.CompilerParams(
            collective_id=number, has_side_effects=True, vmem_limit_bytes=58 * 2**20
        ),
        cost_estimate=pl.CostEstimate(
            flops=10 * rows * keys * width,
            transcendentals=rows * keys * HEADS,
            bytes_accessed=12 * keys * width,
        ),
        name="attend_back",
    )(queries, key_vals, grad, lse, key_ids[:, None], query_ids[None, :])


def add_pair(first, second):
    return first + second


def merge_soft(first, second):
    highest = jnp.maximum(first[0], second[0])
    total = first[1] * jnp.exp(first[0] - highest) + second[1] * jnp.exp(second[0] - highest)
    return jnp.stack([highest, total, first[2] + second[2]])


def dot_rows(left_op, right_op):
    return lax.dot_general(
        left_op, right_op, (((1,), (1,)), ((), ())), preferred_element_type=jnp.float32
    )


def dot_cols(left_op, right_op):
    return lax.dot_general(
        left_op, right_op, (((0,), (0,)), ((), ())), preferred_element_type=jnp.float32
    )


def dot_plain(left_op, right_op):
    return jnp.dot(left_op, right_op, preferred_element_type=jnp.float32)


def column_sums(values):
    return jnp.sum(values.astype(jnp.float32), 0)


def layer_norm(values, gain, shift):
    center = values - jnp.mean(values, -1, keepdims=True)
    spread = jnp.mean(center * center, -1, keepdims=True)
    return center * lax.rsqrt(spread + NORM_EPS) * gain + shift


def norm_back(values, gain, shift, grad):
    unused, pull = jax.vjp(layer_norm, values, gain, shift)
    return pull(grad)


def one_hot(wanted, length, axis):
    shape = list(wanted.shape)
    shape.insert(axis, length)
    at = lax.broadcasted_iota(jnp.int32, shape, axis)
    return (at == jnp.expand_dims(wanted, axis)).astype(jnp.bfloat16)


def counts_before(flags):
    length = flags.shape[-1]
    earlier = (
        lax.broadcasted_iota(jnp.int32, (length, length), 0)
        < lax.broadcasted_iota(jnp.int32, (length, length), 1)
    ).astype(jnp.bfloat16)
    return dot_plain(flags.astype(jnp.bfloat16), earlier).astype(jnp.int32)


def wide(rows_in):
    return jnp.pad(rows_in, ((0, 0), (0, -rows_in.shape[1] % (2 * HEAD))))


def rows_major(x):
    return with_layout_constraint(x, Layout(major_to_minor=tuple(range(x.ndim))))


def turned(x):
    return with_layout_constraint(x, Layout(major_to_minor=(1, 0)))


def scatter_rows(groups):
    total = lax.axis_size(AXES)
    mats = []
    for group in groups:
        parts = [rows_major(dot_cols(*pair).astype(jnp.bfloat16)) for pair in group]
        grad = jnp.concatenate(parts, 0) if len(parts) > 1 else parts[0]
        mats.append(grad.reshape(total, -1, grad.shape[1]))
    blocks = jnp.concatenate(mats, 1) if len(mats) > 1 else mats[0]
    own = lax.psum_scatter(blocks, AXES, scatter_dimension=0, tiled=True)[0]
    return own.reshape(len(mats), -1, own.shape[1])


def layer_forward(state, weights, params, query_ids, key_ids):
    width = state.shape[1]
    hidden = layer_norm(state, params[0 : 1], params[1 : 2]).astype(jnp.bfloat16)
    joined = rows_major(dot_rows(hidden, weights[0][: 3 * width]))
    queries = wide((joined[:, :width] + params[2 : 3]).astype(jnp.bfloat16))
    key_rows = joined[:, width : 2 * width].astype(jnp.bfloat16)
    val_rows = (joined[:, 2 * width :] + params[3 : 4]).astype(jnp.bfloat16)
    own_pair = jnp.concatenate([wide(key_rows), wide(val_rows)], 0)
    attended, lse, key_vals = attend(queries, own_pair, key_ids, query_ids, 4)
    attended = attended[:, :width]
    mid_state = state + dot_plain(attended, weights[0][3 * width :]) + params[4 : 5]
    normed = layer_norm(mid_state, params[5 : 6], params[6 : 7]).astype(jnp.bfloat16)
    upward = turned(dot_rows(normed, weights[1]) + params[8:12].reshape(1, -1))
    active = turned(jax.nn.gelu(upward, approximate=True).astype(jnp.bfloat16))
    output = mid_state + dot_plain(active, weights[2]) + params[7 : 8]
    return (
        output,
        (hidden, queries, key_vals, lse, attended, mid_state, normed, upward, active),
    )


def layer_backward(state, weights, params, saved, query_ids, key_ids, grad_in, arrived):
    width = state.shape[1]
    hidden, queries, key_vals, lse, attended, mid_state, normed, upward, active = saved
    down_grad = grad_in.astype(jnp.bfloat16)
    act_grad = dot_rows(down_grad, weights[2])
    unused_gelu, gelu_pull = jax.vjp(partial(jax.nn.gelu, approximate=True), upward)
    up_grad = turned(gelu_pull(act_grad)[0].astype(jnp.bfloat16))
    mid_back, gain_two, shift_two = norm_back(
        mid_state, params[5 : 6], params[6 : 7], rows_major(dot_plain(up_grad, weights[1]))
    )
    mid_grad = grad_in + mid_back
    out_grad = mid_grad.astype(jnp.bfloat16)
    att_grad = wide(rows_major(dot_rows(out_grad, weights[0][3 * width :]).astype(jnp.bfloat16)))
    if arrived:
        att_grad, arrived[0] = lax.optimization_barrier((att_grad, arrived[0]))
    query_grad, own = attend_back(queries, key_vals, att_grad, lse, key_ids, query_ids, 8)
    query_grad = query_grad[:, :width]
    key_grad, val_grad = own[: own.shape[0] // 2, :width], own[own.shape[0] // 2 :, :width]
    joined_grad = jnp.concatenate([query_grad, key_grad, val_grad], 1)
    state_back, gain_one, shift_one = norm_back(
        state,
        params[0 : 1],
        params[1 : 2],
        rows_major(dot_plain(joined_grad, weights[0][: 3 * width])),
    )
    up_sums = column_sums(up_grad)
    small_grad = [
        gain_one,
        shift_one,
        column_sums(query_grad),
        column_sums(val_grad),
        column_sums(out_grad),
        gain_two,
        shift_two,
        column_sums(down_grad),
        up_sums,
    ]
    factors = [
        [(joined_grad, hidden), (attended, out_grad)],
        [(up_grad, normed)],
        [(active, down_grad)],
    ]
    return (mid_grad + state_back, factors, small_grad)


def adam_step(weights, moment, square, grad, rate, decay, step):
    moment = BETA_ONE * moment + (1 - BETA_ONE) * grad
    square = BETA_TWO * square + (1 - BETA_TWO) * grad * grad
    moment_hat = moment / (1 - BETA_ONE**step)
    square_hat = square / (1 - BETA_TWO**step)
    weights = weights - rate * (moment_hat / (jnp.sqrt(square_hat) + ADAM_EPS) + decay * weights)
    return (weights, moment, square)


def pad_rows(x, rows):
    return jnp.pad(x, ((0, rows - x.shape[0]), (0, 0)))


def on_device(
    tokens,
    block_ids,
    completion,
    regroup,
    targets,
    step_count,
    layer_mats,
    mats_moment,
    mats_square,
    embed_table,
    table_moment,
    table_square,
):
    seqs, tok_count = tokens.shape
    seq_length = block_ids.shape[1]
    width = embed_table.shape[1]
    table_local = embed_table.shape[0]
    layers = layer_mats.shape[0]
    replicas, groups, shards = (lax.axis_size(axis) for axis in AXES)
    total = replicas * groups * shards
    seq_at = lax.axis_index("seq")
    shard_at = lax.axis_index("shard")
    device_at = lax.axis_index(AXES)
    seq_bits, dp_bits, shard_bits = bits_of("seq"), bits_of("dp"), bits_of("shard")
    first_row = device_at * table_local
    table_own = embed_table.astype(jnp.bfloat16)
    mats_low = layer_mats.astype(jnp.bfloat16)
    token_ids = tokens.reshape(-1)
    local_rows = token_ids.shape[0]
    small_count = 12 * layers + 2
    small_rows = -(-small_count // 16) * 16

    packed_ids = jnp.pad(token_ids, (0, -local_rows % 1024)).reshape(-1, 128)
    ids_all = run_jobs([spread_job(packed_ids, False)], "share_ids", 0, 16)[0][0]
    ids_all = ids_all.reshape(total, -1)[:, :local_rows]
    owner_all = ids_all // table_local
    loads = jnp.sum(
        (owner_all[:, :, None] == jnp.arange(total)[None, None, :]).astype(jnp.int32), 1
    )
    rounds = (jnp.max(loads) + SLOTS - 1) // SLOTS
    asked = owner_all == device_at
    asked_rank = counts_before(asked)
    asked_row = ids_all - first_row
    own_owner = token_ids // table_local
    same = own_owner[:, None] == own_owner[None, :]
    before = jnp.arange(local_rows)[None, :] < jnp.arange(local_rows)[:, None]
    own_rank = jnp.sum((same & before).astype(jnp.int32), 1)

    def asked_rows(at):
        chosen = asked[:, None, :] & (
            asked_rank[:, None, :] == at * SLOTS + jnp.arange(SLOTS)[None, :, None]
        )
        return (jnp.sum(jnp.where(chosen, asked_row[:, None, :] + 1, 0), 2) - 1).reshape(-1)

    def own_slots(at):
        slot = own_rank - at * SLOTS
        return jnp.where((slot >= 0) & (slot < SLOTS), own_owner * SLOTS + slot, -1)

    def fetch(at, given):
        return dot_plain(
            one_hot(own_slots(at), total * SLOTS, 1), given.reshape(total * SLOTS, width)
        )

    fixed = jnp.arange(seq_length + small_rows, dtype=jnp.int32)
    fixed_row = jnp.where(fixed < seq_length + small_count, VOCAB + fixed - first_row, -1)
    wanted = jnp.concatenate([asked_rows(0), fixed_row])
    rows_out = dot_plain(one_hot(wanted, table_local, 1), table_own).astype(jnp.bfloat16)
    exchanged = total * SLOTS
    piece = seq_length // total
    gathered = []
    for layer_at in range(layers):
        if layer_at == 0:
            whole = lax.all_gather(mats_low[0], AXES, axis=1, tiled=True)
            gathered.append([whole[k] for k in range(3)])
        else:
            rest = lax.all_gather(mats_low[layer_at, 1:], AXES, axis=1, tiled=True)
            gathered.append([rest[0], rest[1]])
    (upper_first,), (place_rows,), (small,), (given,) = run_jobs(
        [
            gather_job([mats_low[1, 0]]),
            sum_job(
                rows_out[exchanged : exchanged + seq_length].reshape(total, piece, width),
                sum_axes=("seq", "dp", "shard"),
                sum_orders=[seq_bits + dp_bits + shard_bits],
                join_axes=("dp", "shard"),
                join_orders=[shard_bits[::-1] + dp_bits[::-1]],
            ),
            combine_job(rows_out[exchanged + seq_length :], add_pair),
            swap_job(rows_out[:exchanged].reshape(total, SLOTS, width), late=7),
        ],
        "open_rows",
        2,
        32,
    )
    gathered[1].insert(0, upper_first.reshape(-1, width))
    place_rows = place_rows.reshape(tok_count, width)
    small = small[:small_count].astype(jnp.float32)
    place_state = jnp.broadcast_to(place_rows.astype(jnp.float32), (seqs, tok_count, width))
    state = fetch(0, given) + place_state.reshape(local_rows, width)

    def fetch_more(at, held):
        rows = dot_plain(one_hot(asked_rows(at), table_local, 1), table_own).astype(jnp.bfloat16)
        return held + fetch(at, swap(rows.reshape(total, SLOTS, width), "swap_rows", 1))

    state = lax.fori_loop(1, rounds, fetch_more, state)

    query_ids = lax.dynamic_slice_in_dim(block_ids[0], seq_at * tok_count, tok_count, 0)
    inputs, kept, saved = [], [], []
    for layer_at in range(layers):
        weights = gathered[layer_at]
        inputs.append(state)
        kept.append(weights)
        state, held = layer_forward(
            state,
            weights,
            small[12 * layer_at : 12 * layer_at + 12],
            query_ids,
            block_ids[0],
        )
        saved.append(held)
    final_gain = small[12 * layers : 12 * layers + 1]
    final_shift = small[12 * layers + 1 : 12 * layers + 2]
    final = layer_norm(state, final_gain, final_shift).astype(jnp.bfloat16)

    group_mask = completion[0]
    slot_of = regroup[0]
    slots = slot_of.shape[0]
    comp_rows = slots // shards
    rank_all = counts_before(group_mask[None])[0]
    mine = lax.dynamic_slice_in_dim(group_mask, shard_at * local_rows, local_rows)
    my_rank = lax.dynamic_slice_in_dim(rank_all, shard_at * local_rows, local_rows)
    my_slot = jnp.sum(
        jnp.where(my_rank[:, None] == jnp.arange(slots)[None, :], slot_of[None, :], 0), 1
    )
    to_slot = one_hot(jnp.where(mine == 1, my_slot, -1), slots, 0)
    outgoing = dot_plain(to_slot, final).astype(jnp.bfloat16).reshape(shards, comp_rows, width)
    two_ways = [seq_bits[1:] + dp_bits, dp_bits + seq_bits[1:]]
    head_in = exchange(
        outgoing,
        "share_final",
        5,
        sum_axes=("shard",),
        sum_orders=[shard_bits, shard_bits],
        join_axes=AXES,
        join_orders=[shard_bits[::-1] + way[::-1] + seq_bits[:1] for way in two_ways],
        chunks=2,
    ).reshape(-1, width)

    rows_all = targets.shape[0]
    columns = first_row + jnp.arange(table_local, dtype=jnp.int32)
    live = (columns < VOCAB)[None, :]
    logits = dot_rows(head_in, table_own)
    masked = jnp.where(live, logits, MASK_FILL)
    top_local = jnp.max(masked, 1)
    total_local = jnp.sum(jnp.where(live, jnp.exp(masked - top_local[:, None]), 0.0), 1)
    target_hit = columns[None, :] == targets[:, None]
    pick_local = jnp.sum(jnp.where(target_hit, logits, 0.0), 1)
    stats = combine_all(
        jnp.stack([top_local, total_local, pick_local]).reshape(3, -1, 128),
        merge_soft,
        "share_stats",
        6,
    ).reshape(3, rows_all)
    log_total = stats[0] + jnp.log(stats[1])
    loss_value = jnp.sum(log_total - stats[2]) / rows_all
    probs = jnp.where(live, jnp.exp(masked - log_total[:, None]), 0.0)
    logit_grad = ((probs - target_hit.astype(jnp.float32)) / rows_all).astype(jnp.bfloat16)
    head_grad = dot_cols(logit_grad, head_in)
    returned = exchange(
        dot_plain(logit_grad, table_own).reshape(total, comp_rows, width),
        "return_final",
        7,
        sum_axes=AXES,
        sum_orders=[seq_bits[:1] + way + shard_bits for way in two_ways],
        join_axes=("shard",),
        join_orders=[shard_bits[::-1], shard_bits[::-1]],
        chunks=2,
    ).reshape(slots, width)
    final_grad = rows_major(dot_cols(to_slot, returned))
    state_grad, gain_final, shift_final = norm_back(state, final_gain, final_shift, final_grad)

    late = []
    arrived = []
    small_grads = [None] * layers
    for layer_at in reversed(range(layers)):
        state_grad, factors, small_grads[layer_at] = layer_backward(
            inputs[layer_at],
            kept[layer_at],
            small[12 * layer_at : 12 * layer_at + 12],
            saved[layer_at],
            query_ids,
            block_ids[0],
            state_grad,
            arrived,
        )
        if layer_at > 0:
            arrived = [scatter_rows(factors[2:]), scatter_rows(factors[1:2])]
            late = factors[:1]
        else:
            late = factors + late

    low_grad = state_grad.astype(jnp.bfloat16)
    place_grad = jnp.sum(state_grad.reshape(seqs, tok_count, width), 0)
    small_grad = jnp.concatenate(
        [x.reshape(-1) for x in sum(small_grads, []) + [gain_final, shift_final]]
    )
    small_size = small_grad.shape[0]
    small_grad = jnp.pad(small_grad, (0, -small_size % 1024)).reshape(-1, 128)

    def leaving(at):
        rows = dot_cols(one_hot(own_slots(at), total * SLOTS, 1), low_grad).astype(jnp.bfloat16)
        return rows.reshape(total, SLOTS, width)

    late = late_mats(late, 12)
    late, arrived[1] = lax.optimization_barrier((late, arrived[1]))
    upper = jnp.concatenate([arrived[1], arrived[0]], 0).astype(jnp.float32)
    fits = mats_fit(late)
    (own_mats,), (place_grad,), (small_grad,), (came,) = run_jobs(
        [
            mats_job(late[:fits]),
            sum_job(
                place_grad.reshape(replicas * shards, piece, width),
                sum_axes=("dp", "shard"),
                sum_orders=[dp_bits + shard_bits],
                join_axes=("seq", "dp", "shard"),
                join_orders=[shard_bits[::-1] + dp_bits[::-1] + seq_bits[::-1]],
            ),
            combine_job(small_grad, add_pair),
            swap_job(leaving(0), late=5),
        ],
        "close_rows",
        10,
        61,
    )
    for k in range(fits, len(late), fits):
        more = run_jobs([mats_job(late[k : k + fits])], "sum_mats", 14 + k, 61)[0][0]
        own_mats = jnp.concatenate([own_mats, lax.optimization_barrier(more)], 0)
    place_grad = place_grad.reshape(seq_length, width)
    small_grad = pad_rows(small_grad.reshape(-1)[:small_size].reshape(-1, width), small_rows)
    small_high = small_grad.astype(jnp.bfloat16)
    small_low = (small_grad - small_high.astype(jnp.float32)).astype(jnp.bfloat16)
    values = jnp.concatenate([came.reshape(-1, width), place_grad, small_high, small_low], 0)
    value_row = jnp.concatenate([wanted, fixed_row[seq_length:]])
    table_grad = dot_plain(one_hot(value_row, table_local, 0), values) + head_grad

    def return_more(at, held):
        rows = swap(leaving(at), "swap_rows", 1).reshape(-1, width)
        return held + dot_plain(one_hot(asked_rows(at), table_local, 0), rows)

    table_grad = lax.fori_loop(1, rounds, return_more, table_grad)
    mats_grad = jnp.concatenate([own_mats, upper], 0).reshape(layer_mats.shape)
    local_squares = jnp.sum(mats_grad * mats_grad) + jnp.sum(table_grad * table_grad)
    squares = jnp.full((8, 128), local_squares)
    squares = run_jobs([spread_job(squares, True)], "share_norm", 11, 16)[0][0]
    grad_norm = jnp.sqrt(squares[0, 0])
    factor = CLIP_NORM / grad_norm
    step = step_count[0].astype(jnp.float32)
    new_mats = adam_step(
        layer_mats, mats_moment, mats_square, factor * mats_grad, RATE_MATS, DECAY_RATE, step
    )
    plain_rows = (columns < VOCAB + seq_length)[:, None]
    rate = jnp.where(plain_rows, RATE_TABLE, RATE_SMALL)
    decay = jnp.where(plain_rows, DECAY_RATE, 0.0)
    new_table = adam_step(
        embed_table, table_moment, table_square, factor * table_grad, rate, decay, step
    )
    return (
        loss_value.reshape(1),
        grad_norm.reshape(1),
        new_mats[0],
        new_mats[1],
        new_mats[2],
        new_table[0],
        new_table[1],
        new_table[2],
    )


def solution(mesh):
    in_specs = (
        P(("dp", "shard"), "seq"),
        P(("dp", "shard"), None),
        P(("dp", "seq"), None),
        P(("dp", "seq"), None),
        P(),
        P(),
        P(None, None, ("dp", "seq", "shard"), None),
        P(None, None, ("dp", "seq", "shard"), None),
        P(None, None, ("dp", "seq", "shard"), None),
        P(("dp", "seq", "shard"), None),
        P(("dp", "seq", "shard"), None),
        P(("dp", "seq", "shard"), None),
    )
    out_specs = (
        P(),
        P(),
        P(None, None, ("dp", "seq", "shard"), None),
        P(None, None, ("dp", "seq", "shard"), None),
        P(None, None, ("dp", "seq", "shard"), None),
        P(("dp", "seq", "shard"), None),
        P(("dp", "seq", "shard"), None),
        P(("dp", "seq", "shard"), None),
    )
    return jax.shard_map(
        on_device, mesh=mesh, in_specs=in_specs, out_specs=out_specs, check_vma=False
    )
```

```python
import itertools
from functools import partial

import jax
import jax.numpy as jnp
from jax import lax
from jax.experimental import pallas as pl
from jax.experimental.layout import Layout, with_layout_constraint
from jax.experimental.pallas import tpu as pltpu
from jax.sharding import PartitionSpec as P

HEADS = 17
HEAD = 64
VOCAB = 50278

NORM_EPS = 1e-05
CLIP_NORM = 0.02
BETA_ONE = 0.9
BETA_TWO = 0.95
ADAM_EPS = 1e-08
DECAY_RATE = 0.1
RATE_MATS = 0.05
RATE_TABLE = 0.1
RATE_SMALL = 0.5
MASK_FILL = -1e30

AXES = ("dp", "seq", "shard")
MESH = pl.DeviceIdType.MESH
SLOTS = 24


def bits_of(axis):
    return [(axis, b) for b in range(lax.axis_size(axis).bit_length() - 1)]


def bit_here(bit):
    return lax.rem(lax.axis_index(bit[0]) // 2 ** bit[1], 2)


def partner(bit):
    at = lax.axis_index(bit[0])
    return {bit[0]: at + (1 - 2 * bit_here(bit)) * 2 ** bit[1]}


def greet(bits):
    barrier = pltpu.get_barrier_semaphore()
    for bit in bits:
        pl.semaphore_signal(barrier, inc=1, device_id=partner(bit), device_id_type=MESH)
    pl.semaphore_wait(barrier, len(bits))


def block_weight(axes, bit):
    weight = 2 ** bit[1]
    for axis in axes[axes.index(bit[0]) + 1 :]:
        weight *= lax.axis_size(axis)
    return weight


def block_runs(weights):
    weights = sorted(weights)
    joined = 0
    while joined < len(weights) and weights[joined] == 2**joined:
        joined += 1
    rest = [(0, w) for w in weights[joined:]]
    return 2**joined, [sum(c) for c in itertools.product(*rest)]


class Job:
    def __init__(
        self, inputs, outputs, scratch, sends, keeps, bits, steps, spaces=(pltpu.VMEM, pltpu.VMEM)
    ):
        self.inputs, self.outputs, self.scratch = inputs, outputs, scratch
        self.sends, self.keeps, self.bits, self.steps, self.spaces = sends, keeps, bits, steps, spaces


def me_and_total():
    seq_size, shard_size = lax.axis_size("seq"), lax.axis_size("shard")
    at = (lax.axis_index("dp") * seq_size + lax.axis_index("seq")) * shard_size
    return at + lax.axis_index("shard"), lax.axis_size("dp") * seq_size * shard_size


def place_of(at):
    seq_size, shard_size = lax.axis_size("seq"), lax.axis_size("shard")
    return {
        "dp": at // (seq_size * shard_size),
        "seq": lax.rem(at // shard_size, seq_size),
        "shard": lax.rem(at, shard_size),
    }


def greet_all():
    me, total = me_and_total()
    barrier = pltpu.get_barrier_semaphore()

    def hello(k, carry):
        pl.semaphore_signal(
            barrier, inc=1, device_id=place_of(lax.rem(me + k, total)), device_id_type=MESH
        )
        return carry

    lax.fori_loop(1, total, hello, 0)
    pl.semaphore_wait(barrier, total - 1)


class Sems:
    def __init__(self, send, recv, keep):
        self.send, self.recv, self.keep = send, recv, keep
        self.used = self.kept = 0

    def copy(self, source, target, device):
        k = self.used
        self.used += 1
        copy = pltpu.make_async_remote_copy(
            source, target, self.send.at[k], self.recv.at[k], device_id=device, device_id_type=MESH
        )
        copy.start()
        return copy

    def local(self, source, target):
        k = self.kept
        self.kept += 1
        copy = pltpu.make_async_copy(source, target, self.keep.at[k])
        copy.start()
        return copy

    def span(self, count):
        first = self.used
        self.used += count
        return first


def jobs_kernel(jobs, *refs):
    refs = list(refs)

    def take(count):
        out = refs[:count]
        del refs[:count]
        return out

    held = [take(len(job.inputs)) for job in jobs]
    made = [take(len(job.outputs)) for job in jobs]
    used = [take(len(job.scratch)) for job in jobs]
    sems = Sems(*refs)
    if any(job.bits is None for job in jobs):
        greet_all()
    else:
        greet(sorted(set(bit for job in jobs for bit in job.bits)))
    active = []
    for job, x, o, w in zip(jobs, held, made, used):
        active += job.steps(x, o, w, sems)
    tick = 0
    while active:
        left = []
        for delay, gen in active:
            if delay > tick or next(gen, "end") != "end":
                left.append((delay, gen))
        active = left
        tick += 1


def run_jobs(jobs, name, number, vmem=60):
    inputs = [x for job in jobs for x in job.inputs]
    outputs = [o for job in jobs for o in job.outputs]
    in_specs = [pl.BlockSpec(memory_space=job.spaces[0]) for job in jobs for unused in job.inputs]
    out_specs = [pl.BlockSpec(memory_space=job.spaces[1]) for job in jobs for unused in job.outputs]
    sends = sum(job.sends for job in jobs)
    keeps = max(1, sum(job.keeps for job in jobs))
    flat = pl.pallas_call(
        partial(jobs_kernel, jobs),
        out_shape=outputs,
        in_specs=in_specs,
        out_specs=out_specs,
        scratch_shapes=[w for job in jobs for w in job.scratch]
        + [
            pltpu.SemaphoreType.DMA((sends,)),
            pltpu.SemaphoreType.DMA((sends,)),
            pltpu.SemaphoreType.DMA((keeps,)),
        ],
        compiler_params=pltpu.CompilerParams(
            collective_id=number, has_side_effects=True, vmem_limit_bytes=vmem * 2**20
        ),
        name=name,
    )(*inputs)
    out = []
    for job in jobs:
        out.append(flat[: len(job.outputs)])
        flat = flat[len(job.outputs) :]
    return out


def sum_stream(x_ref, o_ref, scratch, sems, rows, first_slot, sum_axes, sums, join_axes, joins):
    source = x_ref
    slot = first_slot
    if sums:
        work, parcel, recv = scratch
    for step, bit in enumerate(sums):
        base = sum(bit_here(b) * block_weight(sum_axes, b) for b in sums[:step])
        weight = block_weight(sum_axes, bit)
        mine = bit_here(bit)
        size, offsets = block_runs([block_weight(sum_axes, b) for b in sums[step + 1 :]])
        started = []
        for offset in offsets:
            leave = base + (1 - mine) * weight + offset
            if source.dtype == parcel.dtype:
                packed = source.at[pl.ds(leave, size), rows]
            else:

                def pack(i, carry, leave=leave, at=slot, source=source):
                    parcel[at + i, rows] = source[leave + i, rows].astype(parcel.dtype)
                    return carry

                lax.fori_loop(0, size, pack, 0)
                packed = parcel.at[pl.ds(slot, size), rows]
            copy = sems.copy(packed, recv.at[pl.ds(slot, size), rows], partner(bit))
            started.append((copy, base + mine * weight + offset, slot, size))
            slot += size
        yield
        for copy, keep, at, size in started:
            copy.wait()

            def add(i, carry, keep=keep, at=at, source=source):
                total = source[keep + i, rows].astype(jnp.float32)
                total = total + recv[at + i, rows].astype(jnp.float32)
                work[keep + i, rows] = total.astype(work.dtype)
                return carry

            lax.fori_loop(0, size, add, 0)
        source = work
    own = sum(bit_here(b) * block_weight(sum_axes, b) for b in sums) if sums else 0
    result = source[own, rows].astype(o_ref.dtype)
    if not joins:
        o_ref[rows] = result
        return
    o_ref[sum(bit_here(b) * block_weight(join_axes, b) for b in joins), rows] = result
    for step, bit in enumerate(joins):
        base = sum(bit_here(b) * block_weight(join_axes, b) for b in joins[step:])
        size, offsets = block_runs([block_weight(join_axes, b) for b in joins[:step]])
        started = []
        for offset in offsets:
            here = o_ref.at[pl.ds(base + offset, size), rows]
            started.append(sems.copy(here, here, partner(bit)))
        yield
        for copy in started:
            copy.wait()


def sum_job(x, sum_axes=(), sum_orders=(), join_axes=(), join_orders=(), chunks=1):
    rows, width = x.shape[-2:]
    blocks = 1
    for axis in join_axes:
        blocks *= lax.axis_size(axis)
    kind = jnp.bfloat16 if sum_axes else x.dtype
    streams = max(len(sum_orders), len(join_orders))
    if rows % (streams * chunks * 16):
        chunks = 1
    share = rows // (streams * chunks)
    sends = 0
    for order in sum_orders:
        for step in range(len(order)):
            sends += len(block_runs([block_weight(sum_axes, b) for b in order[step + 1 :]])[1])
    for order in join_orders:
        for step in range(len(order)):
            sends += len(block_runs([block_weight(join_axes, b) for b in order[:step]])[1])
    scratch = []
    if sum_axes:
        if x.size * 14 > 56 * 2**20:
            x = x.astype(jnp.bfloat16)
        exact = x.dtype == jnp.float32 or x.size < 2**22
        scratch = [
            pltpu.VMEM(x.shape, jnp.float32 if exact else kind),
            pltpu.VMEM(x.shape, kind),
            pltpu.VMEM(x.shape, kind),
        ]

    def steps(x_refs, o_refs, scratch_refs, sems):
        gens = []
        for c in range(chunks):
            for k in range(streams):
                rows_here = pl.ds((k * chunks + c) * share, share)
                sums = sum_orders[k] if sum_orders else []
                joins = join_orders[k] if join_orders else []
                gens.append(
                    (
                        c,
                        sum_stream(
                            x_refs[0], o_refs[0], scratch_refs, sems, rows_here, 0,
                            sum_axes, sums, join_axes, joins,
                        ),
                    )
                )
        return gens

    bits = set(bit for order in list(sum_orders) + list(join_orders) for bit in order)
    shape = (blocks, rows, width) if join_axes else (rows, width)
    return Job(
        [x], [jax.ShapeDtypeStruct(shape, kind)], scratch, sends * chunks, 0, bits, steps
    )


def exchange(x, name, number, **how):
    return run_jobs([sum_job(x, **how)], name, number)[0][0]


def combine_job(x, combine):
    bits = [bit for axis in reversed(AXES) for bit in bits_of(axis)]
    slots = (len(bits),) + x.shape

    def steps(x_refs, o_refs, scratch, sems):
        out_buf, in_buf = scratch

        def gen():
            current = x_refs[0][...]
            for i, bit in enumerate(bits):
                out_buf[i] = current
                copy = sems.copy(out_buf.at[i], in_buf.at[i], partner(bit))
                yield
                copy.wait()
                current, other = out_buf[i], in_buf[i]
                low = bit_here(bit) == 0
                current = combine(jnp.where(low, current, other), jnp.where(low, other, current))
            o_refs[0][...] = current

        return [(0, gen())]

    return Job(
        [x],
        [jax.ShapeDtypeStruct(x.shape, x.dtype)],
        [pltpu.VMEM(slots, x.dtype), pltpu.VMEM(slots, x.dtype)],
        len(bits),
        0,
        bits,
        steps,
    )


def combine_all(x, combine, name, number):
    return run_jobs([combine_job(x, combine)], name, number, 16)[0][0]


def swap_job(x, late=0):
    total = x.shape[0]

    def steps(x_refs, o_refs, scratch, sems):
        x_ref, o_ref = x_refs[0], o_refs[0]

        def gen():
            me, unused = me_and_total()
            first = sems.span(total)
            keep = sems.local(x_ref.at[me], o_ref.at[me])

            def copy_to(other, here):
                return pltpu.make_async_remote_copy(
                    x_ref.at[other],
                    o_ref.at[here],
                    sems.send.at[first + other],
                    sems.recv.at[first + here],
                    device_id=place_of(other),
                    device_id_type=MESH,
                )

            def send(k, carry):
                copy_to(lax.rem(me + k, total), me).start()
                return carry

            lax.fori_loop(1, total, send, 0)
            for unused in range(late + 1):
                yield

            def finish(k, carry):
                other = lax.rem(me + k, total)
                copy_to(other, other).wait()
                return carry

            lax.fori_loop(1, total, finish, 0)
            keep.wait()

        return [(0, gen())]

    return Job(
        [x],
        [jax.ShapeDtypeStruct(x.shape, x.dtype)],
        [],
        total,
        1,
        None,
        steps,
        spaces=(pl.ANY, pl.ANY),
    )


def spread_job(x, add):
    total = lax.axis_size(AXES)
    all_shape = (total,) + x.shape

    def steps(x_refs, o_refs, scratch, sems):
        x_ref = x_refs[0]
        target = scratch[0] if add else o_refs[0]

        def gen():
            me, unused = me_and_total()
            first = sems.span(total)
            target[me] = x_ref[...]

            def copy_to(other, here):
                return pltpu.make_async_remote_copy(
                    x_ref,
                    target.at[here],
                    sems.send.at[first + other],
                    sems.recv.at[first + here],
                    device_id=place_of(other),
                    device_id_type=MESH,
                )

            def send(k, carry):
                copy_to(lax.rem(me + k, total), me).start()
                return carry

            lax.fori_loop(1, total, send, 0)
            yield

            def finish(k, carry):
                other = lax.rem(me + k, total)
                copy_to(other, other).wait()
                return carry

            lax.fori_loop(1, total, finish, 0)
            if add:
                o_refs[0][...] = jnp.sum(target[...], 0)

        return [(0, gen())]

    return Job(
        [x],
        [jax.ShapeDtypeStruct(x.shape if add else all_shape, x.dtype)],
        [pltpu.VMEM(all_shape, x.dtype)] if add else [],
        total,
        0,
        None,
        steps,
    )


def swap(x, name, number):
    return run_jobs([swap_job(x)], name, number, 16)[0][0]


def sum_orders_for(rows):
    across, along, deep = bits_of("seq")[1:], bits_of("dp"), bits_of("shard")
    if rows < 64 or rows % 8:
        return [(0, rows)], [across + along + deep]
    one, two = rows * 8 // 17 // 16 * 16, rows * 6 // 17 // 16 * 16
    spans = [(0, one), (one, two), (one + two, rows - one - two)]
    return spans, [across + along + deep, along + across + deep, deep + along + across]


def mats_stream(x_ref, o_ref, scratch, sems, m, span, order, weights):
    kept, work, parcel, recv = scratch
    which, turn, m = m, m % 2, m % work.shape[0]
    steps = len(order)
    rows = pl.ds(*span)
    slot = 0
    rest = sorted((b for b in weights if b != order[0]), key=lambda b: weights[b])
    small = {b: 2**k for k, b in enumerate(rest)}
    for step, bit in enumerate(order):
        mine = bit_here(bit)
        base = sum(bit_here(b) * small[b] for b in order[1:step])
        runs, keeps = [], []
        if step == 0:
            size, offsets = block_runs([weights[b] for b in order[1:]])
            for offset in offsets:
                left, place = offset, 0
                for b in reversed(rest):
                    if left >= weights[b]:
                        left -= weights[b]
                        place += small[b]
                keeps.append(
                    sems.local(
                        x_ref.at[pl.ds(mine * weights[bit] + offset, size), rows],
                        kept.at[turn, pl.ds(place, size), rows],
                    )
                )
                runs.append(((1 - mine) * weights[bit] + offset, place))
        else:
            size, offsets = block_runs([small[b] for b in order[step + 1 :]])
            for offset in offsets:
                here = base + offset
                runs.append((here + (1 - mine) * small[bit], here + mine * small[bit]))
        started = []
        for leave, keep_at in runs:
            at = slot
            slot += size
            if step == 0:
                packed = x_ref.at[pl.ds(leave, size), rows]
            else:
                spot = at - 2 ** (steps - 1)

                def pack(i, carry, leave=leave, spot=spot):
                    parcel[m, spot + i, rows] = work[m, leave + i, rows].astype(parcel.dtype)
                    return carry

                lax.fori_loop(0, size, pack, 0)
                packed = parcel.at[m, pl.ds(spot, size), rows]
            copy = sems.copy(packed, recv.at[m, pl.ds(at, size), rows], partner(bit))
            started.append((copy, at, keep_at, size))
        yield
        for keep in keeps:
            keep.wait()
        for copy, at, keep_at, size in started:
            copy.wait()

            def add(i, carry, at=at, keep_at=keep_at, step=step):
                if step == 0:
                    total = kept[turn, keep_at + i, rows].astype(jnp.float32)
                else:
                    total = work[m, keep_at + i, rows]
                work[m, keep_at + i, rows] = total + recv[m, at + i, rows].astype(jnp.float32)
                return carry

            lax.fori_loop(0, size, add, 0)
    o_ref[which, rows] = work[m, sum(bit_here(b) * small[b] for b in order[1:]), rows]


def mats_job(mats):
    blocks, rows, width = mats[0].shape
    spans, orders = sum_orders_for(rows)
    weights = {}
    for bit in orders[0]:
        weight = block_weight(AXES, bit)
        weights[bit] = weight if bit[0] == "shard" else weight // 2
    keeps = sends = 0
    for order in orders:
        keeps += len(block_runs([weights[b] for b in order[1:]])[1])
        sends += len(block_runs([weights[b] for b in order[1:]])[1])
        rest = sorted((b for b in weights if b != order[0]), key=lambda b: weights[b])
        small = {b: 2**k for k, b in enumerate(rest)}
        for step in range(1, len(order)):
            sends += len(block_runs([small[b] for b in order[step + 1 :]])[1])
    count = len(mats)

    def steps(x_refs, o_refs, scratch, sems):
        o_ref = o_refs[0]
        return [
            (m, mats_stream(x_refs[m], o_ref, scratch, sems, m, spans[k], orders[k], weights))
            for m in range(count)
            for k in range(len(orders))
        ]

    return Job(
        mats,
        [jax.ShapeDtypeStruct((count, rows, width), jnp.float32)],
        [
            pltpu.VMEM((min(2, count), blocks // 2, rows, width), jnp.bfloat16),
            pltpu.VMEM((min(3, count), blocks // 2, rows, width), jnp.float32),
            pltpu.VMEM((min(3, count), blocks // 2 - 1, rows, width), jnp.bfloat16),
            pltpu.VMEM((min(3, count), blocks - 1, rows, width), jnp.bfloat16),
        ],
        count * sends,
        count * keeps,
        set(orders[0]),
        steps,
        spaces=(pl.ANY, pltpu.VMEM),
    )


def gather_job(parts):
    rows, width = parts[0].shape
    spans, orders = sum_orders_for(rows)
    orders = [order[::-1] + bits_of("seq")[:1] for order in orders]
    total = lax.axis_size(AXES)
    sends = 0
    for order in orders:
        for step in range(len(order)):
            sends += len(block_runs([block_weight(AXES, b) for b in order[:step]])[1])

    def gen(x_ref, o_ref, sems, span, order):
        here = pl.ds(*span)
        own = me_and_total()[0]
        keep = sems.local(x_ref.at[here], o_ref.at[own, here])
        for step, bit in enumerate(order):
            base = sum(bit_here(b) * block_weight(AXES, b) for b in order[step:])
            size, offsets = block_runs([block_weight(AXES, b) for b in order[:step]])
            started = []
            for offset in offsets:
                target = o_ref.at[pl.ds(base + offset, size), here]
                source = x_ref.at[here] if step == 0 else target
                target = o_ref.at[own, here] if step == 0 else target
                started.append(sems.copy(source, target, partner(bit)))
            yield
            if step == 0:
                keep.wait()
            for copy in started:
                copy.wait()

    def steps(x_refs, o_refs, scratch, sems):
        return [
            (m, gen(x_refs[m], o_refs[m], sems, spans[k], orders[k]))
            for m in range(len(parts))
            for k in range(len(orders))
        ]

    return Job(
        parts,
        [jax.ShapeDtypeStruct((total, rows, width), parts[0].dtype)] * len(parts),
        [],
        sends * len(parts),
        len(orders) * len(parts),
        set(orders[0]),
        steps,
        spaces=(pl.ANY, pl.ANY),
    )


def trade_kernel(halved, count, *refs):
    x_refs, o_refs = refs[:count], refs[count : 2 * count]
    send_sems, recv_sems, keep_sems = refs[2 * count :]
    bit = ("seq", 0)
    mine = bit_here(bit)
    greet([bit])
    copies = []
    for k in range(count):
        if k < halved:
            tokens = x_refs[k].shape[-1]
            keep, leave = x_refs[k].at[:, mine], x_refs[k].at[:, 1 - mine]
            near = o_refs[k].at[:, :, pl.ds(0, tokens)]
            far = o_refs[k].at[:, :, pl.ds(tokens, tokens)]
        else:
            tokens = x_refs[k].shape[0]
            keep = leave = x_refs[k]
            near, far = o_refs[k].at[pl.ds(0, tokens)], o_refs[k].at[pl.ds(tokens, tokens)]
        local = pltpu.make_async_copy(keep, near, keep_sems.at[k])
        local.start()
        copy = pltpu.make_async_remote_copy(
            leave,
            far,
            send_sems.at[k],
            recv_sems.at[k],
            device_id=partner(bit),
            device_id_type=MESH,
        )
        copy.start()
        copies += [local, copy]
    for copy in copies:
        copy.wait()


def trade(features, cotangents, name, number):
    arrays = features + cotangents
    count = len(arrays)
    outs = []
    for x in features:
        runs, unused, rows, tokens = x.shape
        outs.append(jax.ShapeDtypeStruct((runs, rows, 2 * tokens), x.dtype))
    for x in cotangents:
        outs.append(jax.ShapeDtypeStruct((2 * x.shape[0], x.shape[1]), x.dtype))
    return pl.pallas_call(
        partial(trade_kernel, len(features), count),
        out_shape=outs,
        in_specs=[pl.BlockSpec(memory_space=pl.ANY)] * count,
        out_specs=[pl.BlockSpec(memory_space=pltpu.VMEM)] * count,
        scratch_shapes=[pltpu.SemaphoreType.DMA((count,))] * 3,
        compiler_params=pltpu.CompilerParams(
            collective_id=number, has_side_effects=True, vmem_limit_bytes=40 * 2**20
        ),
        name=name,
    )(*arrays)


def late_mats(groups, number):
    pairs = [pair for group in groups for pair in group]
    total = lax.axis_size(AXES)
    height = sum(features.shape[1] for features, unused in groups[0])
    own = height // total * lax.axis_size("shard")
    features = [x.T.reshape(-1, 2, own, x.shape[0]) for x, unused in pairs]
    got = trade(features, [tail for unused, tail in pairs], "trade_rows", number)
    parts = []
    for k in range(len(pairs)):
        both = got[k].reshape(-1, got[k].shape[2])
        parts.append(rows_major(dot_plain(both, got[len(pairs) + k]).astype(jnp.bfloat16)))
    mats = []
    for group in groups:
        grad = jnp.concatenate(parts[: len(group)], 0) if len(group) > 1 else parts[0]
        parts = parts[len(group) :]
        mats.append(grad.reshape(total // 2, -1, grad.shape[1]))
    return mats


def mats_fit(mats):
    blocks, rows, width = mats[0].shape
    tile = -(-rows // 16) * 16 * -(-width // 128) * 128
    fits = (50 * 2**20 - tile * blocks * 2) // (tile * blocks * 5)
    return len(mats) if fits >= 3 else max(1, fits)


def head_lanes(half, shape):
    lane = lax.broadcasted_iota(jnp.int32, shape, 1)
    return (lane < HEAD) if half == 0 else (lane >= HEAD)


def pair_lanes(p):
    return pl.ds(pl.multiple_of(p * 2 * HEAD, 2 * HEAD), 2 * HEAD)


def seq_places():
    me = lax.axis_index("seq")
    return me, partner(("seq", 0))["seq"], partner(("seq", 1))["seq"]


def to_seq(source, target, sems, k, place):
    return pltpu.make_async_remote_copy(
        source,
        target,
        sems.at[0, k],
        sems.at[1, k],
        device_id={"seq": place},
        device_id_type=MESH,
    )


def attend_kernel(
    q_ref, own_ref, key_ids_ref, query_ids_ref, o_ref, lse_ref, kv_ref, blocked, far, near, pass_on, own_sem
):
    rows = own_ref.shape[0] // 2
    keys = kv_ref.shape[0] * rows
    pairs = q_ref.shape[1] // (2 * HEAD)
    me, near_at, far_at = seq_places()
    beyond = near_at + far_at - me
    greet([("seq", 0), ("seq", 1)])

    def far_copy(p, at):
        return to_seq(own_ref.at[:, pair_lanes(p)], kv_ref.at[at, :, pair_lanes(p)], far, p, far_at)

    def near_copy(p, at):
        return to_seq(own_ref.at[:, pair_lanes(p)], kv_ref.at[at, :, pair_lanes(p)], near, p, near_at)

    def pass_copy(p, at):
        here = kv_ref.at[far_at, :, pair_lanes(p)]
        return to_seq(here, kv_ref.at[at, :, pair_lanes(p)], pass_on, p, near_at)

    def send(p, carry):
        far_copy(p, me).start()
        near_copy(p, me).start()
        return carry

    lax.fori_loop(0, pairs, send, 0)
    own = pltpu.make_async_copy(own_ref, kv_ref.at[me], own_sem)
    own.start()
    blocked[...] = jnp.where(key_ids_ref[...] <= query_ids_ref[...], 0.0, MASK_FILL)
    own.wait()

    def forward_one(p):
        far_copy(p, far_at).wait_recv()
        pass_copy(p, far_at).start()

    forward_one(0)

    def pair(p, carry):
        @pl.when(p + 1 < pairs)
        def _():
            forward_one(p + 1)

        near_copy(p, near_at).wait_recv()
        pass_copy(p, beyond).wait_recv()
        lanes = pair_lanes(p)
        key_pair = kv_ref[:, :rows, lanes].reshape(keys, 2 * HEAD)
        val_turned = kv_ref[:, rows:, lanes].reshape(keys, 2 * HEAD).T
        query_pair = q_ref[:, lanes]
        outs = []
        for half in range(2):
            query = jnp.where(head_lanes(half, query_pair.shape), query_pair, 0)
            scores = dot_rows(key_pair, query.astype(jnp.bfloat16)) * HEAD ** (-0.5) + blocked[...]
            top = jnp.max(scores, 0, keepdims=True)
            raised = jnp.exp(scores - top)
            total = jnp.sum(raised, 0, keepdims=True)
            probs = (raised * (1.0 / total)).astype(jnp.bfloat16)
            outs.append(dot_plain(val_turned[half * HEAD : (half + 1) * HEAD], probs))
            lse_ref[p, half] = (top + jnp.log(total))[0]
        o_ref[:, lanes] = jnp.concatenate(outs, 0).T.astype(o_ref.dtype)
        return carry

    lax.fori_loop(0, pairs, pair, 0)

    def sent(p, carry):
        far_copy(p, me).wait_send()
        near_copy(p, me).wait_send()
        pass_copy(p, far_at).wait_send()
        return carry

    lax.fori_loop(0, pairs, sent, 0)


def attend(queries, own_pair, key_ids, query_ids, number):
    rows, width = queries.shape
    keys = key_ids.shape[0]
    pairs = width // (2 * HEAD)
    groups = lax.axis_size("seq")
    copies = pltpu.SemaphoreType.DMA((2, pairs))
    return pl.pallas_call(
        attend_kernel,
        out_shape=(
            jax.ShapeDtypeStruct((rows, width), jnp.bfloat16),
            jax.ShapeDtypeStruct((pairs, 2, rows), jnp.float32),
            jax.ShapeDtypeStruct((groups,) + own_pair.shape, jnp.bfloat16),
        ),
        in_specs=[pl.BlockSpec(memory_space=pltpu.VMEM)] * 4,
        out_specs=(pl.BlockSpec(memory_space=pltpu.VMEM),) * 3,
        scratch_shapes=[
            pltpu.VMEM((keys, rows), jnp.float32),
            copies,
            copies,
            copies,
            pltpu.SemaphoreType.DMA,
        ],
        compiler_params=pltpu.CompilerParams(
            collective_id=number, has_side_effects=True, vmem_limit_bytes=48 * 2**20
        ),
        cost_estimate=pl.CostEstimate(
            flops=4 * rows * keys * width,
            transcendentals=rows * keys * HEADS,
            bytes_accessed=4 * keys * width,
        ),
        name="attend",
    )(queries, own_pair, key_ids[:, None], query_ids[None, :])


def attend_back_kernel(
    q_ref,
    kv_ref,
    grad_ref,
    lse_ref,
    key_ids_ref,
    query_ids_ref,
    dq_ref,
    own_ref,
    blocked,
    fresh,
    kept,
    near_out,
    near_in,
    far_out,
    far_in,
    near,
    far,
):
    groups, twice, unused = kv_ref.shape
    rows = twice // 2
    keys = groups * rows
    pairs = q_ref.shape[1] // (2 * HEAD)
    scale = HEAD ** (-0.5)
    me, near_at, far_at = seq_places()
    low, high = lax.rem(me, 2), me // 2
    greet([("seq", 0), ("seq", 1)])
    blocked[...] = jnp.where(key_ids_ref[...] <= query_ids_ref[...], 0.0, MASK_FILL)

    def near_copy(p):
        return to_seq(near_out.at[p], near_in.at[p], near, p, near_at)

    def far_copy(p):
        return to_seq(far_out.at[p], far_in.at[p], far, p, far_at)

    def middle(p):
        near_copy(p).wait()
        for k in range(2):
            kept[p, k] = kept[p, k] + near_in[p, k].astype(jnp.float32)
        far_out[p] = kept[p, 1 - high].astype(far_out.dtype)
        far_copy(p).start()

    def last(p):
        far_copy(p).wait()
        total = kept[p, high] + far_in[p].astype(jnp.float32)
        own_ref[:, pair_lanes(p)] = total.astype(own_ref.dtype)

    def pair(p, carry):
        lanes = pair_lanes(p)
        key_pair = kv_ref[:, :rows, lanes].reshape(keys, 2 * HEAD)
        val_pair = kv_ref[:, rows:, lanes].reshape(keys, 2 * HEAD)
        key_turned = key_pair.T
        query_pair = q_ref[:, lanes]
        grad_pair = grad_ref[:, lanes]
        key_grad = jnp.zeros((keys, 2 * HEAD), jnp.float32)
        val_grad = jnp.zeros((keys, 2 * HEAD), jnp.float32)
        outs = []
        for half in range(2):
            here = head_lanes(half, query_pair.shape)
            query = jnp.where(here, query_pair, 0).astype(jnp.bfloat16)
            grad = jnp.where(here, grad_pair, 0).astype(jnp.bfloat16)
            scores = dot_rows(key_pair, query) * scale + blocked[...]
            probs = jnp.exp(scores - lse_ref[p, half][None, :])
            prob_grad = dot_rows(val_pair, grad)
            inner = jnp.sum(probs * prob_grad, 0, keepdims=True)
            score_grad = (probs * (prob_grad - inner)).astype(jnp.bfloat16)
            key_grad = key_grad + dot_plain(score_grad, query)
            val_grad = val_grad + dot_plain(probs.astype(jnp.bfloat16), grad)
            outs.append(dot_plain(key_turned[half * HEAD : (half + 1) * HEAD], score_grad))
        dq_ref[:, lanes] = (jnp.concatenate(outs, 0).T * scale).astype(dq_ref.dtype)
        fresh[:, :rows] = (key_grad * scale).reshape(groups, rows, 2 * HEAD)
        fresh[:, rows:] = val_grad.reshape(groups, rows, 2 * HEAD)
        for k in range(2):
            near_out[p, k] = fresh[2 * k + 1 - low].astype(near_out.dtype)
            kept[p, k] = fresh[2 * k + low]
        near_copy(p).start()

        @pl.when(p >= 1)
        def _():
            middle(p - 1)

        @pl.when(p >= 2)
        def _():
            last(p - 2)

        return carry

    lax.fori_loop(0, pairs, pair, 0)
    middle(pairs - 1)
    last(pairs - 2)
    last(pairs - 1)


def attend_back(queries, key_vals, grad, lse, key_ids, query_ids, number):
    rows, width = queries.shape
    keys = key_ids.shape[0]
    pairs = width // (2 * HEAD)
    piece = (2 * rows, 2 * HEAD)
    copies = pltpu.SemaphoreType.DMA((2, pairs))
    return pl.pallas_call(
        attend_back_kernel,
        out_shape=(
            jax.ShapeDtypeStruct((rows, width), jnp.bfloat16),
            jax.ShapeDtypeStruct((2 * rows, width), jnp.bfloat16),
        ),
        in_specs=[pl.BlockSpec(memory_space=pltpu.VMEM)] * 6,
        out_specs=(pl.BlockSpec(memory_space=pltpu.VMEM),) * 2,
        scratch_shapes=[
            pltpu.VMEM((keys, rows), jnp.float32),
            pltpu.VMEM((lax.axis_size("seq"),) + piece, jnp.float32),
            pltpu.VMEM((pairs, 2) + piece, jnp.float32),
            pltpu.VMEM((pairs, 2) + piece, jnp.bfloat16),
            pltpu.VMEM((pairs, 2) + piece, jnp.bfloat16),
            pltpu.VMEM((pairs,) + piece, jnp.bfloat16),
            pltpu.VMEM((pairs,) + piece, jnp.bfloat16),
            copies,
            copies,
        ],
        compiler_params=pltpu.CompilerParams(
            collective_id=number, has_side_effects=True, vmem_limit_bytes=58 * 2**20
        ),
        cost_estimate=pl.CostEstimate(
            flops=10 * rows * keys * width,
            transcendentals=rows * keys * HEADS,
            bytes_accessed=12 * keys * width,
        ),
        name="attend_back",
    )(queries, key_vals, grad, lse, key_ids[:, None], query_ids[None, :])


def add_pair(first, second):
    return first + second


def merge_soft(first, second):
    highest = jnp.maximum(first[0], second[0])
    total = first[1] * jnp.exp(first[0] - highest) + second[1] * jnp.exp(second[0] - highest)
    return jnp.stack([highest, total, first[2] + second[2]])


def dot_rows(left_op, right_op):
    return lax.dot_general(
        left_op, right_op, (((1,), (1,)), ((), ())), preferred_element_type=jnp.float32
    )


def dot_cols(left_op, right_op):
    return lax.dot_general(
        left_op, right_op, (((0,), (0,)), ((), ())), preferred_element_type=jnp.float32
    )


def dot_plain(left_op, right_op):
    return jnp.dot(left_op, right_op, preferred_element_type=jnp.float32)


def column_sums(values):
    return jnp.sum(values.astype(jnp.float32), 0)


def layer_norm(values, gain, shift):
    center = values - jnp.mean(values, -1, keepdims=True)
    spread = jnp.mean(center * center, -1, keepdims=True)
    return center * lax.rsqrt(spread + NORM_EPS) * gain + shift


def norm_back(values, gain, shift, grad):
    unused, pull = jax.vjp(layer_norm, values, gain, shift)
    return pull(grad)


def one_hot(wanted, length, axis):
    shape = list(wanted.shape)
    shape.insert(axis, length)
    at = lax.broadcasted_iota(jnp.int32, shape, axis)
    return (at == jnp.expand_dims(wanted, axis)).astype(jnp.bfloat16)


def counts_before(flags):
    length = flags.shape[-1]
    earlier = (
        lax.broadcasted_iota(jnp.int32, (length, length), 0)
        < lax.broadcasted_iota(jnp.int32, (length, length), 1)
    ).astype(jnp.bfloat16)
    return dot_plain(flags.astype(jnp.bfloat16), earlier).astype(jnp.int32)


def wide(rows_in):
    return jnp.pad(rows_in, ((0, 0), (0, -rows_in.shape[1] % (2 * HEAD))))


def rows_major(x):
    return with_layout_constraint(x, Layout(major_to_minor=tuple(range(x.ndim))))


def turned(x):
    return with_layout_constraint(x, Layout(major_to_minor=(1, 0)))


def scatter_rows(groups):
    total = lax.axis_size(AXES)
    mats = []
    for group in groups:
        parts = [rows_major(dot_cols(*pair).astype(jnp.bfloat16)) for pair in group]
        grad = jnp.concatenate(parts, 0) if len(parts) > 1 else parts[0]
        mats.append(grad.reshape(total, -1, grad.shape[1]))
    blocks = jnp.concatenate(mats, 1) if len(mats) > 1 else mats[0]
    own = lax.psum_scatter(blocks, AXES, scatter_dimension=0, tiled=True)[0]
    return own.reshape(len(mats), -1, own.shape[1])


def layer_forward(state, weights, params, query_ids, key_ids):
    width = state.shape[1]
    hidden = layer_norm(state, params[0 : 1], params[1 : 2]).astype(jnp.bfloat16)
    joined = rows_major(dot_rows(hidden, weights[0][: 3 * width]))
    queries = wide((joined[:, :width] + params[2 : 3]).astype(jnp.bfloat16))
    key_rows = joined[:, width : 2 * width].astype(jnp.bfloat16)
    val_rows = (joined[:, 2 * width :] + params[3 : 4]).astype(jnp.bfloat16)
    own_pair = jnp.concatenate([wide(key_rows), wide(val_rows)], 0)
    attended, lse, key_vals = attend(queries, own_pair, key_ids, query_ids, 4)
    attended = attended[:, :width]
    mid_state = state + dot_plain(attended, weights[0][3 * width :]) + params[4 : 5]
    normed = layer_norm(mid_state, params[5 : 6], params[6 : 7]).astype(jnp.bfloat16)
    upward = turned(dot_rows(normed, weights[1]) + params[8:12].reshape(1, -1))
    active = turned(jax.nn.gelu(upward, approximate=True).astype(jnp.bfloat16))
    output = mid_state + dot_plain(active, weights[2]) + params[7 : 8]
    return (
        output,
        (hidden, queries, key_vals, lse, attended, mid_state, normed, upward, active),
    )


def layer_backward(state, weights, params, saved, query_ids, key_ids, grad_in, arrived):
    width = state.shape[1]
    hidden, queries, key_vals, lse, attended, mid_state, normed, upward, active = saved
    down_grad = grad_in.astype(jnp.bfloat16)
    act_grad = dot_rows(down_grad, weights[2])
    unused_gelu, gelu_pull = jax.vjp(partial(jax.nn.gelu, approximate=True), upward)
    up_grad = turned(gelu_pull(act_grad)[0].astype(jnp.bfloat16))
    mid_back, gain_two, shift_two = norm_back(
        mid_state, params[5 : 6], params[6 : 7], rows_major(dot_plain(up_grad, weights[1]))
    )
    mid_grad = grad_in + mid_back
    out_grad = mid_grad.astype(jnp.bfloat16)
    att_grad = wide(rows_major(dot_rows(out_grad, weights[0][3 * width :]).astype(jnp.bfloat16)))
    if arrived:
        att_grad, arrived[0] = lax.optimization_barrier((att_grad, arrived[0]))
    query_grad, own = attend_back(queries, key_vals, att_grad, lse, key_ids, query_ids, 8)
    query_grad = query_grad[:, :width]
    key_grad, val_grad = own[: own.shape[0] // 2, :width], own[own.shape[0] // 2 :, :width]
    joined_grad = jnp.concatenate([query_grad, key_grad, val_grad], 1)
    state_back, gain_one, shift_one = norm_back(
        state,
        params[0 : 1],
        params[1 : 2],
        rows_major(dot_plain(joined_grad, weights[0][: 3 * width])),
    )
    up_sums = column_sums(up_grad)
    small_grad = [
        gain_one,
        shift_one,
        column_sums(query_grad),
        column_sums(val_grad),
        column_sums(out_grad),
        gain_two,
        shift_two,
        column_sums(down_grad),
        up_sums,
    ]
    factors = [
        [(joined_grad, hidden), (attended, out_grad)],
        [(up_grad, normed)],
        [(active, down_grad)],
    ]
    return (mid_grad + state_back, factors, small_grad)


def adam_step(weights, moment, square, grad, rate, decay, step):
    moment = BETA_ONE * moment + (1 - BETA_ONE) * grad
    square = BETA_TWO * square + (1 - BETA_TWO) * grad * grad
    moment_hat = moment / (1 - BETA_ONE**step)
    square_hat = square / (1 - BETA_TWO**step)
    weights = weights - rate * (moment_hat / (jnp.sqrt(square_hat) + ADAM_EPS) + decay * weights)
    return (weights, moment, square)


def pad_rows(x, rows):
    return jnp.pad(x, ((0, rows - x.shape[0]), (0, 0)))


def on_device(
    tokens,
    block_ids,
    completion,
    regroup,
    targets,
    step_count,
    layer_mats,
    mats_moment,
    mats_square,
    embed_table,
    table_moment,
    table_square,
):
    seqs, tok_count = tokens.shape
    seq_length = block_ids.shape[1]
    width = embed_table.shape[1]
    table_local = embed_table.shape[0]
    layers = layer_mats.shape[0]
    replicas, groups, shards = (lax.axis_size(axis) for axis in AXES)
    total = replicas * groups * shards
    seq_at = lax.axis_index("seq")
    shard_at = lax.axis_index("shard")
    device_at = lax.axis_index(AXES)
    seq_bits, dp_bits, shard_bits = bits_of("seq"), bits_of("dp"), bits_of("shard")
    first_row = device_at * table_local
    table_own = embed_table.astype(jnp.bfloat16)
    mats_low = layer_mats.astype(jnp.bfloat16)
    token_ids = tokens.reshape(-1)
    local_rows = token_ids.shape[0]
    small_count = 12 * layers + 2
    small_rows = -(-small_count // 16) * 16

    packed_ids = jnp.pad(token_ids, (0, -local_rows % 1024)).reshape(-1, 128)
    ids_all = run_jobs([spread_job(packed_ids, False)], "share_ids", 0, 16)[0][0]
    ids_all = ids_all.reshape(total, -1)[:, :local_rows]
    owner_all = ids_all // table_local
    loads = jnp.sum(
        (owner_all[:, :, None] == jnp.arange(total)[None, None, :]).astype(jnp.int32), 1
    )
    rounds = (jnp.max(loads) + SLOTS - 1) // SLOTS
    asked = owner_all == device_at
    asked_rank = counts_before(asked)
    asked_row = ids_all - first_row
    own_owner = token_ids // table_local
    same = own_owner[:, None] == own_owner[None, :]
    before = jnp.arange(local_rows)[None, :] < jnp.arange(local_rows)[:, None]
    own_rank = jnp.sum((same & before).astype(jnp.int32), 1)

    def asked_rows(at):
        chosen = asked[:, None, :] & (
            asked_rank[:, None, :] == at * SLOTS + jnp.arange(SLOTS)[None, :, None]
        )
        return (jnp.sum(jnp.where(chosen, asked_row[:, None, :] + 1, 0), 2) - 1).reshape(-1)

    def own_slots(at):
        slot = own_rank - at * SLOTS
        return jnp.where((slot >= 0) & (slot < SLOTS), own_owner * SLOTS + slot, -1)

    def fetch(at, given):
        return dot_plain(
            one_hot(own_slots(at), total * SLOTS, 1), given.reshape(total * SLOTS, width)
        )

    fixed = jnp.arange(seq_length + small_rows, dtype=jnp.int32)
    fixed_row = jnp.where(fixed < seq_length + small_count, VOCAB + fixed - first_row, -1)
    wanted = jnp.concatenate([asked_rows(0), fixed_row])
    rows_out = dot_plain(one_hot(wanted, table_local, 1), table_own).astype(jnp.bfloat16)
    exchanged = total * SLOTS
    piece = seq_length // total
    gathered = []
    for layer_at in range(layers):
        if layer_at == 0:
            whole = lax.all_gather(mats_low[0], AXES, axis=1, tiled=True)
            gathered.append([whole[k] for k in range(3)])
        else:
            rest = lax.all_gather(mats_low[layer_at, 1:], AXES, axis=1, tiled=True)
            gathered.append([rest[0], rest[1]])
    (upper_first,), (place_rows,), (small,), (given,) = run_jobs(
        [
            gather_job([mats_low[1, 0]]),
            sum_job(
                rows_out[exchanged : exchanged + seq_length].reshape(total, piece, width),
                sum_axes=("seq", "dp", "shard"),
                sum_orders=[seq_bits + dp_bits + shard_bits],
                join_axes=("dp", "shard"),
                join_orders=[shard_bits[::-1] + dp_bits[::-1]],
            ),
            combine_job(rows_out[exchanged + seq_length :], add_pair),
            swap_job(rows_out[:exchanged].reshape(total, SLOTS, width), late=7),
        ],
        "open_rows",
        2,
        32,
    )
    gathered[1].insert(0, upper_first.reshape(-1, width))
    place_rows = place_rows.reshape(tok_count, width)
    small = small[:small_count].astype(jnp.float32)
    place_state = jnp.broadcast_to(place_rows.astype(jnp.float32), (seqs, tok_count, width))
    state = fetch(0, given) + place_state.reshape(local_rows, width)

    def fetch_more(at, held):
        rows = dot_plain(one_hot(asked_rows(at), table_local, 1), table_own).astype(jnp.bfloat16)
        return held + fetch(at, swap(rows.reshape(total, SLOTS, width), "swap_rows", 1))

    state = lax.fori_loop(1, rounds, fetch_more, state)

    query_ids = lax.dynamic_slice_in_dim(block_ids[0], seq_at * tok_count, tok_count, 0)
    inputs, kept, saved = [], [], []
    for layer_at in range(layers):
        weights = gathered[layer_at]
        inputs.append(state)
        kept.append(weights)
        state, held = layer_forward(
            state,
            weights,
            small[12 * layer_at : 12 * layer_at + 12],
            query_ids,
            block_ids[0],
        )
        saved.append(held)
    final_gain = small[12 * layers : 12 * layers + 1]
    final_shift = small[12 * layers + 1 : 12 * layers + 2]
    final = layer_norm(state, final_gain, final_shift).astype(jnp.bfloat16)

    group_mask = completion[0]
    slot_of = regroup[0]
    slots = slot_of.shape[0]
    comp_rows = slots // shards
    rank_all = counts_before(group_mask[None])[0]
    mine = lax.dynamic_slice_in_dim(group_mask, shard_at * local_rows, local_rows)
    my_rank = lax.dynamic_slice_in_dim(rank_all, shard_at * local_rows, local_rows)
    my_slot = jnp.sum(
        jnp.where(my_rank[:, None] == jnp.arange(slots)[None, :], slot_of[None, :], 0), 1
    )
    to_slot = one_hot(jnp.where(mine == 1, my_slot, -1), slots, 0)
    outgoing = dot_plain(to_slot, final).astype(jnp.bfloat16).reshape(shards, comp_rows, width)
    two_ways = [seq_bits[1:] + dp_bits, dp_bits + seq_bits[1:]]
    head_in = exchange(
        outgoing,
        "share_final",
        5,
        sum_axes=("shard",),
        sum_orders=[shard_bits, shard_bits],
        join_axes=AXES,
        join_orders=[shard_bits[::-1] + way[::-1] + seq_bits[:1] for way in two_ways],
        chunks=2,
    ).reshape(-1, width)

    rows_all = targets.shape[0]
    columns = first_row + jnp.arange(table_local, dtype=jnp.int32)
    live = (columns < VOCAB)[None, :]
    logits = dot_rows(head_in, table_own)
    masked = jnp.where(live, logits, MASK_FILL)
    top_local = jnp.max(masked, 1)
    total_local = jnp.sum(jnp.where(live, jnp.exp(masked - top_local[:, None]), 0.0), 1)
    target_hit = columns[None, :] == targets[:, None]
    pick_local = jnp.sum(jnp.where(target_hit, logits, 0.0), 1)
    stats = combine_all(
        jnp.stack([top_local, total_local, pick_local]).reshape(3, -1, 128),
        merge_soft,
        "share_stats",
        6,
    ).reshape(3, rows_all)
    log_total = stats[0] + jnp.log(stats[1])
    loss_value = jnp.sum(log_total - stats[2]) / rows_all
    probs = jnp.where(live, jnp.exp(masked - log_total[:, None]), 0.0)
    logit_grad = ((probs - target_hit.astype(jnp.float32)) / rows_all).astype(jnp.bfloat16)
    head_grad = dot_cols(logit_grad, head_in)
    returned = exchange(
        dot_plain(logit_grad, table_own).reshape(total, comp_rows, width),
        "return_final",
        7,
        sum_axes=AXES,
        sum_orders=[seq_bits[:1] + way + shard_bits for way in two_ways],
        join_axes=("shard",),
        join_orders=[shard_bits[::-1], shard_bits[::-1]],
        chunks=2,
    ).reshape(slots, width)
    final_grad = rows_major(dot_cols(to_slot, returned))
    state_grad, gain_final, shift_final = norm_back(state, final_gain, final_shift, final_grad)

    late = []
    arrived = []
    small_grads = [None] * layers
    for layer_at in reversed(range(layers)):
        state_grad, factors, small_grads[layer_at] = layer_backward(
            inputs[layer_at],
            kept[layer_at],
            small[12 * layer_at : 12 * layer_at + 12],
            saved[layer_at],
            query_ids,
            block_ids[0],
            state_grad,
            arrived,
        )
        if layer_at > 0:
            arrived = [scatter_rows(factors[2:]), scatter_rows(factors[1:2])]
            late = factors[:1]
        else:
            late = factors + late

    low_grad = state_grad.astype(jnp.bfloat16)
    place_grad = jnp.sum(state_grad.reshape(seqs, tok_count, width), 0)
    small_grad = jnp.concatenate(
        [x.reshape(-1) for x in sum(small_grads, []) + [gain_final, shift_final]]
    )
    small_size = small_grad.shape[0]
    small_grad = jnp.pad(small_grad, (0, -small_size % 1024)).reshape(-1, 128)

    def leaving(at):
        rows = dot_cols(one_hot(own_slots(at), total * SLOTS, 1), low_grad).astype(jnp.bfloat16)
        return rows.reshape(total, SLOTS, width)

    late = late_mats(late, 12)
    fits = mats_fit(late)
    (own_mats,), (place_grad,), (small_grad,), (came,) = run_jobs(
        [
            mats_job(late[:fits]),
            sum_job(
                place_grad.reshape(replicas * shards, piece, width),
                sum_axes=("dp", "shard"),
                sum_orders=[dp_bits + shard_bits],
                join_axes=("seq", "dp", "shard"),
                join_orders=[shard_bits[::-1] + dp_bits[::-1] + seq_bits[::-1]],
            ),
            combine_job(small_grad, add_pair),
            swap_job(leaving(0), late=5),
        ],
        "close_rows",
        10,
        61,
    )
    for k in range(fits, len(late), fits):
        more = run_jobs([mats_job(late[k : k + fits])], "sum_mats", 14 + k, 61)[0][0]
        own_mats = jnp.concatenate([own_mats, lax.optimization_barrier(more)], 0)
    place_grad = place_grad.reshape(seq_length, width)
    came, arrived[1] = lax.optimization_barrier((came, arrived[1]))
    upper = jnp.concatenate([arrived[1], arrived[0]], 0).astype(jnp.float32)
    small_grad = pad_rows(small_grad.reshape(-1)[:small_size].reshape(-1, width), small_rows)
    small_high = small_grad.astype(jnp.bfloat16)
    small_low = (small_grad - small_high.astype(jnp.float32)).astype(jnp.bfloat16)
    values = jnp.concatenate([came.reshape(-1, width), place_grad, small_high, small_low], 0)
    value_row = jnp.concatenate([wanted, fixed_row[seq_length:]])
    table_grad = dot_plain(one_hot(value_row, table_local, 0), values) + head_grad

    def return_more(at, held):
        rows = swap(leaving(at), "swap_rows", 1).reshape(-1, width)
        return held + dot_plain(one_hot(asked_rows(at), table_local, 0), rows)

    table_grad = lax.fori_loop(1, rounds, return_more, table_grad)
    mats_grad = jnp.concatenate([own_mats, upper], 0).reshape(layer_mats.shape)
    local_squares = jnp.sum(mats_grad * mats_grad) + jnp.sum(table_grad * table_grad)
    squares = jnp.full((8, 128), local_squares)
    squares = run_jobs([spread_job(squares, True)], "share_norm", 11, 16)[0][0]
    grad_norm = jnp.sqrt(squares[0, 0])
    factor = CLIP_NORM / grad_norm
    step = step_count[0].astype(jnp.float32)
    new_mats = adam_step(
        layer_mats, mats_moment, mats_square, factor * mats_grad, RATE_MATS, DECAY_RATE, step
    )
    plain_rows = (columns < VOCAB + seq_length)[:, None]
    rate = jnp.where(plain_rows, RATE_TABLE, RATE_SMALL)
    decay = jnp.where(plain_rows, DECAY_RATE, 0.0)
    new_table = adam_step(
        embed_table, table_moment, table_square, factor * table_grad, rate, decay, step
    )
    return (
        loss_value.reshape(1),
        grad_norm.reshape(1),
        new_mats[0],
        new_mats[1],
        new_mats[2],
        new_table[0],
        new_table[1],
        new_table[2],
    )


def solution(mesh):
    in_specs = (
        P(("dp", "shard"), "seq"),
        P(("dp", "shard"), None),
        P(("dp", "seq"), None),
        P(("dp", "seq"), None),
        P(),
        P(),
        P(None, None, ("dp", "seq", "shard"), None),
        P(None, None, ("dp", "seq", "shard"), None),
        P(None, None, ("dp", "seq", "shard"), None),
        P(("dp", "seq", "shard"), None),
        P(("dp", "seq", "shard"), None),
        P(("dp", "seq", "shard"), None),
    )
    out_specs = (
        P(),
        P(),
        P(None, None, ("dp", "seq", "shard"), None),
        P(None, None, ("dp", "seq", "shard"), None),
        P(None, None, ("dp", "seq", "shard"), None),
        P(("dp", "seq", "shard"), None),
        P(("dp", "seq", "shard"), None),
        P(("dp", "seq", "shard"), None),
    )
    return jax.shard_map(
        on_device, mesh=mesh, in_specs=in_specs, out_specs=out_specs, check_vma=False
    )
```

```python
import itertools
from functools import partial

import jax
import jax.numpy as jnp
from jax import lax
from jax.experimental import pallas as pl
from jax.experimental.layout import Layout, with_layout_constraint
from jax.experimental.pallas import tpu as pltpu
from jax.sharding import PartitionSpec as P

HEADS = 17
HEAD = 64
VOCAB = 50278

NORM_EPS = 1e-05
CLIP_NORM = 0.02
BETA_ONE = 0.9
BETA_TWO = 0.95
ADAM_EPS = 1e-08
DECAY_RATE = 0.1
RATE_MATS = 0.05
RATE_TABLE = 0.1
RATE_SMALL = 0.5
MASK_FILL = -1e30

AXES = ("dp", "seq", "shard")
MESH = pl.DeviceIdType.MESH
SLOTS = 24


def bits_of(axis):
    return [(axis, b) for b in range(lax.axis_size(axis).bit_length() - 1)]


def bit_here(bit):
    return lax.rem(lax.axis_index(bit[0]) // 2 ** bit[1], 2)


def partner(bit):
    at = lax.axis_index(bit[0])
    return {bit[0]: at + (1 - 2 * bit_here(bit)) * 2 ** bit[1]}


def greet(bits):
    barrier = pltpu.get_barrier_semaphore()
    for bit in bits:
        pl.semaphore_signal(barrier, inc=1, device_id=partner(bit), device_id_type=MESH)
    pl.semaphore_wait(barrier, len(bits))


def block_weight(axes, bit):
    weight = 2 ** bit[1]
    for axis in axes[axes.index(bit[0]) + 1 :]:
        weight *= lax.axis_size(axis)
    return weight


def block_runs(weights):
    weights = sorted(weights)
    joined = 0
    while joined < len(weights) and weights[joined] == 2**joined:
        joined += 1
    rest = [(0, w) for w in weights[joined:]]
    return 2**joined, [sum(c) for c in itertools.product(*rest)]


class Job:
    def __init__(
        self, inputs, outputs, scratch, sends, keeps, bits, steps, spaces=(pltpu.VMEM, pltpu.VMEM)
    ):
        self.inputs, self.outputs, self.scratch = inputs, outputs, scratch
        self.sends, self.keeps, self.bits, self.steps, self.spaces = sends, keeps, bits, steps, spaces


def me_and_total():
    seq_size, shard_size = lax.axis_size("seq"), lax.axis_size("shard")
    at = (lax.axis_index("dp") * seq_size + lax.axis_index("seq")) * shard_size
    return at + lax.axis_index("shard"), lax.axis_size("dp") * seq_size * shard_size


def place_of(at):
    seq_size, shard_size = lax.axis_size("seq"), lax.axis_size("shard")
    return {
        "dp": at // (seq_size * shard_size),
        "seq": lax.rem(at // shard_size, seq_size),
        "shard": lax.rem(at, shard_size),
    }


def greet_all():
    me, total = me_and_total()
    barrier = pltpu.get_barrier_semaphore()

    def hello(k, carry):
        pl.semaphore_signal(
            barrier, inc=1, device_id=place_of(lax.rem(me + k, total)), device_id_type=MESH
        )
        return carry

    lax.fori_loop(1, total, hello, 0)
    pl.semaphore_wait(barrier, total - 1)


class Sems:
    def __init__(self, send, recv, keep):
        self.send, self.recv, self.keep = send, recv, keep
        self.used = self.kept = 0

    def copy(self, source, target, device):
        k = self.used
        self.used += 1
        copy = pltpu.make_async_remote_copy(
            source, target, self.send.at[k], self.recv.at[k], device_id=device, device_id_type=MESH
        )
        copy.start()
        return copy

    def local(self, source, target):
        k = self.kept
        self.kept += 1
        copy = pltpu.make_async_copy(source, target, self.keep.at[k])
        copy.start()
        return copy

    def span(self, count):
        first = self.used
        self.used += count
        return first


def jobs_kernel(jobs, *refs):
    refs = list(refs)

    def take(count):
        out = refs[:count]
        del refs[:count]
        return out

    held = [take(len(job.inputs)) for job in jobs]
    made = [take(len(job.outputs)) for job in jobs]
    used = [take(len(job.scratch)) for job in jobs]
    sems = Sems(*refs)
    if any(job.bits is None for job in jobs):
        greet_all()
    else:
        greet(sorted(set(bit for job in jobs for bit in job.bits)))
    active = []
    for job, x, o, w in zip(jobs, held, made, used):
        active += job.steps(x, o, w, sems)
    tick = 0
    while active:
        left = []
        for delay, gen in active:
            if delay > tick or next(gen, "end") != "end":
                left.append((delay, gen))
        active = left
        tick += 1


def run_jobs(jobs, name, number, vmem=60):
    inputs = [x for job in jobs for x in job.inputs]
    outputs = [o for job in jobs for o in job.outputs]
    in_specs = [pl.BlockSpec(memory_space=job.spaces[0]) for job in jobs for unused in job.inputs]
    out_specs = [pl.BlockSpec(memory_space=job.spaces[1]) for job in jobs for unused in job.outputs]
    sends = sum(job.sends for job in jobs)
    keeps = max(1, sum(job.keeps for job in jobs))
    flat = pl.pallas_call(
        partial(jobs_kernel, jobs),
        out_shape=outputs,
        in_specs=in_specs,
        out_specs=out_specs,
        scratch_shapes=[w for job in jobs for w in job.scratch]
        + [
            pltpu.SemaphoreType.DMA((sends,)),
            pltpu.SemaphoreType.DMA((sends,)),
            pltpu.SemaphoreType.DMA((keeps,)),
        ],
        compiler_params=pltpu.CompilerParams(
            collective_id=number, has_side_effects=True, vmem_limit_bytes=vmem * 2**20
        ),
        name=name,
    )(*inputs)
    out = []
    for job in jobs:
        out.append(flat[: len(job.outputs)])
        flat = flat[len(job.outputs) :]
    return out


def sum_stream(x_ref, o_ref, scratch, sems, rows, first_slot, sum_axes, sums, join_axes, joins):
    source = x_ref
    slot = first_slot
    if sums:
        work, parcel, recv = scratch
    for step, bit in enumerate(sums):
        base = sum(bit_here(b) * block_weight(sum_axes, b) for b in sums[:step])
        weight = block_weight(sum_axes, bit)
        mine = bit_here(bit)
        size, offsets = block_runs([block_weight(sum_axes, b) for b in sums[step + 1 :]])
        started = []
        for offset in offsets:
            leave = base + (1 - mine) * weight + offset
            if source.dtype == parcel.dtype:
                packed = source.at[pl.ds(leave, size), rows]
            else:

                def pack(i, carry, leave=leave, at=slot, source=source):
                    parcel[at + i, rows] = source[leave + i, rows].astype(parcel.dtype)
                    return carry

                lax.fori_loop(0, size, pack, 0)
                packed = parcel.at[pl.ds(slot, size), rows]
            copy = sems.copy(packed, recv.at[pl.ds(slot, size), rows], partner(bit))
            started.append((copy, base + mine * weight + offset, slot, size))
            slot += size
        yield
        for copy, keep, at, size in started:
            copy.wait()

            def add(i, carry, keep=keep, at=at, source=source):
                total = source[keep + i, rows].astype(jnp.float32)
                total = total + recv[at + i, rows].astype(jnp.float32)
                work[keep + i, rows] = total.astype(work.dtype)
                return carry

            lax.fori_loop(0, size, add, 0)
        source = work
    own = sum(bit_here(b) * block_weight(sum_axes, b) for b in sums) if sums else 0
    result = source[own, rows].astype(o_ref.dtype)
    if not joins:
        o_ref[rows] = result
        return
    o_ref[sum(bit_here(b) * block_weight(join_axes, b) for b in joins), rows] = result
    for step, bit in enumerate(joins):
        base = sum(bit_here(b) * block_weight(join_axes, b) for b in joins[step:])
        size, offsets = block_runs([block_weight(join_axes, b) for b in joins[:step]])
        started = []
        for offset in offsets:
            here = o_ref.at[pl.ds(base + offset, size), rows]
            started.append(sems.copy(here, here, partner(bit)))
        yield
        for copy in started:
            copy.wait()


def sum_job(x, sum_axes=(), sum_orders=(), join_axes=(), join_orders=(), chunks=1):
    rows, width = x.shape[-2:]
    blocks = 1
    for axis in join_axes:
        blocks *= lax.axis_size(axis)
    kind = jnp.bfloat16 if sum_axes else x.dtype
    streams = max(len(sum_orders), len(join_orders))
    if rows % (streams * chunks * 16):
        chunks = 1
    share = rows // (streams * chunks)
    sends = 0
    for order in sum_orders:
        for step in range(len(order)):
            sends += len(block_runs([block_weight(sum_axes, b) for b in order[step + 1 :]])[1])
    for order in join_orders:
        for step in range(len(order)):
            sends += len(block_runs([block_weight(join_axes, b) for b in order[:step]])[1])
    scratch = []
    if sum_axes:
        if x.size * 14 > 56 * 2**20:
            x = x.astype(jnp.bfloat16)
        exact = x.dtype == jnp.float32 or x.size < 2**22
        scratch = [
            pltpu.VMEM(x.shape, jnp.float32 if exact else kind),
            pltpu.VMEM(x.shape, kind),
            pltpu.VMEM(x.shape, kind),
        ]

    def steps(x_refs, o_refs, scratch_refs, sems):
        gens = []
        for c in range(chunks):
            for k in range(streams):
                rows_here = pl.ds((k * chunks + c) * share, share)
                sums = sum_orders[k] if sum_orders else []
                joins = join_orders[k] if join_orders else []
                gens.append(
                    (
                        c,
                        sum_stream(
                            x_refs[0], o_refs[0], scratch_refs, sems, rows_here, 0,
                            sum_axes, sums, join_axes, joins,
                        ),
                    )
                )
        return gens

    bits = set(bit for order in list(sum_orders) + list(join_orders) for bit in order)
    shape = (blocks, rows, width) if join_axes else (rows, width)
    return Job(
        [x], [jax.ShapeDtypeStruct(shape, kind)], scratch, sends * chunks, 0, bits, steps
    )


def exchange(x, name, number, **how):
    return run_jobs([sum_job(x, **how)], name, number)[0][0]


def combine_job(x, combine):
    bits = [bit for axis in reversed(AXES) for bit in bits_of(axis)]
    slots = (len(bits),) + x.shape

    def steps(x_refs, o_refs, scratch, sems):
        out_buf, in_buf = scratch

        def gen():
            current = x_refs[0][...]
            for i, bit in enumerate(bits):
                out_buf[i] = current
                copy = sems.copy(out_buf.at[i], in_buf.at[i], partner(bit))
                yield
                copy.wait()
                current, other = out_buf[i], in_buf[i]
                low = bit_here(bit) == 0
                current = combine(jnp.where(low, current, other), jnp.where(low, other, current))
            o_refs[0][...] = current

        return [(0, gen())]

    return Job(
        [x],
        [jax.ShapeDtypeStruct(x.shape, x.dtype)],
        [pltpu.VMEM(slots, x.dtype), pltpu.VMEM(slots, x.dtype)],
        len(bits),
        0,
        bits,
        steps,
    )


def combine_all(x, combine, name, number):
    return run_jobs([combine_job(x, combine)], name, number, 16)[0][0]


def swap_job(x, late=0):
    total = x.shape[0]

    def steps(x_refs, o_refs, scratch, sems):
        x_ref, o_ref = x_refs[0], o_refs[0]

        def gen():
            me, unused = me_and_total()
            first = sems.span(total)
            keep = sems.local(x_ref.at[me], o_ref.at[me])

            def copy_to(other, here):
                return pltpu.make_async_remote_copy(
                    x_ref.at[other],
                    o_ref.at[here],
                    sems.send.at[first + other],
                    sems.recv.at[first + here],
                    device_id=place_of(other),
                    device_id_type=MESH,
                )

            def send(k, carry):
                copy_to(lax.rem(me + k, total), me).start()
                return carry

            lax.fori_loop(1, total, send, 0)
            for unused in range(late + 1):
                yield

            def finish(k, carry):
                other = lax.rem(me + k, total)
                copy_to(other, other).wait()
                return carry

            lax.fori_loop(1, total, finish, 0)
            keep.wait()

        return [(0, gen())]

    return Job(
        [x],
        [jax.ShapeDtypeStruct(x.shape, x.dtype)],
        [],
        total,
        1,
        None,
        steps,
        spaces=(pl.ANY, pl.ANY),
    )


def spread_job(x, add):
    total = lax.axis_size(AXES)
    all_shape = (total,) + x.shape

    def steps(x_refs, o_refs, scratch, sems):
        x_ref = x_refs[0]
        target = scratch[0] if add else o_refs[0]

        def gen():
            me, unused = me_and_total()
            first = sems.span(total)
            target[me] = x_ref[...]

            def copy_to(other, here):
                return pltpu.make_async_remote_copy(
                    x_ref,
                    target.at[here],
                    sems.send.at[first + other],
                    sems.recv.at[first + here],
                    device_id=place_of(other),
                    device_id_type=MESH,
                )

            def send(k, carry):
                copy_to(lax.rem(me + k, total), me).start()
                return carry

            lax.fori_loop(1, total, send, 0)
            yield

            def finish(k, carry):
                other = lax.rem(me + k, total)
                copy_to(other, other).wait()
                return carry

            lax.fori_loop(1, total, finish, 0)
            if add:
                o_refs[0][...] = jnp.sum(target[...], 0)

        return [(0, gen())]

    return Job(
        [x],
        [jax.ShapeDtypeStruct(x.shape if add else all_shape, x.dtype)],
        [pltpu.VMEM(all_shape, x.dtype)] if add else [],
        total,
        0,
        None,
        steps,
    )


def swap(x, name, number):
    return run_jobs([swap_job(x)], name, number, 16)[0][0]


def sum_orders_for(rows):
    across, along, deep = bits_of("seq")[1:], bits_of("dp"), bits_of("shard")
    if rows < 64 or rows % 8:
        return [(0, rows)], [across + along + deep]
    one, two = rows * 8 // 17 // 16 * 16, rows * 6 // 17 // 16 * 16
    spans = [(0, one), (one, two), (one + two, rows - one - two)]
    return spans, [across + along + deep, along + across + deep, deep + along + across]


def mats_stream(x_ref, o_ref, scratch, sems, m, span, order, weights):
    kept, work, parcel, recv = scratch
    which, turn, m = m, m % 2, m % work.shape[0]
    steps = len(order)
    rows = pl.ds(*span)
    slot = 0
    rest = sorted((b for b in weights if b != order[0]), key=lambda b: weights[b])
    small = {b: 2**k for k, b in enumerate(rest)}
    for step, bit in enumerate(order):
        mine = bit_here(bit)
        base = sum(bit_here(b) * small[b] for b in order[1:step])
        runs, keeps = [], []
        if step == 0:
            size, offsets = block_runs([weights[b] for b in order[1:]])
            for offset in offsets:
                left, place = offset, 0
                for b in reversed(rest):
                    if left >= weights[b]:
                        left -= weights[b]
                        place += small[b]
                keeps.append(
                    sems.local(
                        x_ref.at[pl.ds(mine * weights[bit] + offset, size), rows],
                        kept.at[turn, pl.ds(place, size), rows],
                    )
                )
                runs.append(((1 - mine) * weights[bit] + offset, place))
        else:
            size, offsets = block_runs([small[b] for b in order[step + 1 :]])
            for offset in offsets:
                here = base + offset
                runs.append((here + (1 - mine) * small[bit], here + mine * small[bit]))
        started = []
        for leave, keep_at in runs:
            at = slot
            slot += size
            if step == 0:
                packed = x_ref.at[pl.ds(leave, size), rows]
            else:
                spot = at - 2 ** (steps - 1)

                def pack(i, carry, leave=leave, spot=spot):
                    parcel[m, spot + i, rows] = work[m, leave + i, rows].astype(parcel.dtype)
                    return carry

                lax.fori_loop(0, size, pack, 0)
                packed = parcel.at[m, pl.ds(spot, size), rows]
            copy = sems.copy(packed, recv.at[m, pl.ds(at, size), rows], partner(bit))
            started.append((copy, at, keep_at, size))
        yield
        for keep in keeps:
            keep.wait()
        for copy, at, keep_at, size in started:
            copy.wait()

            def add(i, carry, at=at, keep_at=keep_at, step=step):
                if step == 0:
                    total = kept[turn, keep_at + i, rows].astype(jnp.float32)
                else:
                    total = work[m, keep_at + i, rows]
                work[m, keep_at + i, rows] = total + recv[m, at + i, rows].astype(jnp.float32)
                return carry

            lax.fori_loop(0, size, add, 0)
    o_ref[which, rows] = work[m, sum(bit_here(b) * small[b] for b in order[1:]), rows]


def mats_job(mats):
    blocks, rows, width = mats[0].shape
    spans, orders = sum_orders_for(rows)
    weights = {}
    for bit in orders[0]:
        weight = block_weight(AXES, bit)
        weights[bit] = weight if bit[0] == "shard" else weight // 2
    keeps = sends = 0
    for order in orders:
        keeps += len(block_runs([weights[b] for b in order[1:]])[1])
        sends += len(block_runs([weights[b] for b in order[1:]])[1])
        rest = sorted((b for b in weights if b != order[0]), key=lambda b: weights[b])
        small = {b: 2**k for k, b in enumerate(rest)}
        for step in range(1, len(order)):
            sends += len(block_runs([small[b] for b in order[step + 1 :]])[1])
    count = len(mats)

    def steps(x_refs, o_refs, scratch, sems):
        o_ref = o_refs[0]
        return [
            (m, mats_stream(x_refs[m], o_ref, scratch, sems, m, spans[k], orders[k], weights))
            for m in range(count)
            for k in range(len(orders))
        ]

    return Job(
        mats,
        [jax.ShapeDtypeStruct((count, rows, width), jnp.float32)],
        [
            pltpu.VMEM((min(2, count), blocks // 2, rows, width), jnp.bfloat16),
            pltpu.VMEM((min(3, count), blocks // 2, rows, width), jnp.float32),
            pltpu.VMEM((min(3, count), blocks // 2 - 1, rows, width), jnp.bfloat16),
            pltpu.VMEM((min(3, count), blocks - 1, rows, width), jnp.bfloat16),
        ],
        count * sends,
        count * keeps,
        set(orders[0]),
        steps,
        spaces=(pl.ANY, pltpu.VMEM),
    )


def gather_job(parts):
    rows, width = parts[0].shape
    across, along, deep = bits_of("seq")[1:], bits_of("dp"), bits_of("shard")
    spans, ways = [(0, rows)], [across + along]
    if rows >= 64 and rows % 8 == 0:
        half = rows // 32 * 16
        spans, ways = [(0, half), (half, rows - half)], [across + along, along + across]
    orders = [deep[::-1] + way[::-1] + bits_of("seq")[:1] for way in ways]
    total = lax.axis_size(AXES)
    sends = 0
    for order in orders:
        for step in range(len(order)):
            sends += len(block_runs([block_weight(AXES, b) for b in order[:step]])[1])

    def gen(x_ref, o_ref, sems, span, order):
        here = pl.ds(*span)
        own = me_and_total()[0]
        keep = sems.local(x_ref.at[here], o_ref.at[own, here])
        for step, bit in enumerate(order):
            base = sum(bit_here(b) * block_weight(AXES, b) for b in order[step:])
            size, offsets = block_runs([block_weight(AXES, b) for b in order[:step]])
            started = []
            for offset in offsets:
                target = o_ref.at[pl.ds(base + offset, size), here]
                source = x_ref.at[here] if step == 0 else target
                target = o_ref.at[own, here] if step == 0 else target
                started.append(sems.copy(source, target, partner(bit)))
            yield
            if step == 0:
                keep.wait()
            for copy in started:
                copy.wait()

    def steps(x_refs, o_refs, scratch, sems):
        return [
            (m, gen(x_refs[m], o_refs[m], sems, spans[k], orders[k]))
            for m in range(len(parts))
            for k in range(len(orders))
        ]

    return Job(
        parts,
        [jax.ShapeDtypeStruct((total, rows, width), parts[0].dtype)] * len(parts),
        [],
        sends * len(parts),
        len(orders) * len(parts),
        set(orders[0]),
        steps,
        spaces=(pl.ANY, pl.ANY),
    )


def trade_kernel(halved, count, *refs):
    x_refs, o_refs = refs[:count], refs[count : 2 * count]
    send_sems, recv_sems, keep_sems = refs[2 * count :]
    bit = ("seq", 0)
    mine = bit_here(bit)
    greet([bit])
    copies = []
    for k in range(count):
        if k < halved:
            tokens = x_refs[k].shape[-1]
            keep, leave = x_refs[k].at[:, mine], x_refs[k].at[:, 1 - mine]
            near = o_refs[k].at[:, :, pl.ds(0, tokens)]
            far = o_refs[k].at[:, :, pl.ds(tokens, tokens)]
        else:
            tokens = x_refs[k].shape[0]
            keep = leave = x_refs[k]
            near, far = o_refs[k].at[pl.ds(0, tokens)], o_refs[k].at[pl.ds(tokens, tokens)]
        local = pltpu.make_async_copy(keep, near, keep_sems.at[k])
        local.start()
        copy = pltpu.make_async_remote_copy(
            leave,
            far,
            send_sems.at[k],
            recv_sems.at[k],
            device_id=partner(bit),
            device_id_type=MESH,
        )
        copy.start()
        copies += [local, copy]
    for copy in copies:
        copy.wait()


def trade(features, cotangents, name, number):
    arrays = features + cotangents
    count = len(arrays)
    outs = []
    for x in features:
        runs, unused, rows, tokens = x.shape
        outs.append(jax.ShapeDtypeStruct((runs, rows, 2 * tokens), x.dtype))
    for x in cotangents:
        outs.append(jax.ShapeDtypeStruct((2 * x.shape[0], x.shape[1]), x.dtype))
    return pl.pallas_call(
        partial(trade_kernel, len(features), count),
        out_shape=outs,
        in_specs=[pl.BlockSpec(memory_space=pl.ANY)] * count,
        out_specs=[pl.BlockSpec(memory_space=pltpu.VMEM)] * count,
        scratch_shapes=[pltpu.SemaphoreType.DMA((count,))] * 3,
        compiler_params=pltpu.CompilerParams(
            collective_id=number, has_side_effects=True, vmem_limit_bytes=40 * 2**20
        ),
        name=name,
    )(*arrays)


def late_mats(groups, number):
    pairs = [pair for group in groups for pair in group]
    total = lax.axis_size(AXES)
    height = sum(features.shape[1] for features, unused in groups[0])
    own = height // total * lax.axis_size("shard")
    features = [x.T.reshape(-1, 2, own, x.shape[0]) for x, unused in pairs]
    got = trade(features, [tail for unused, tail in pairs], "trade_rows", number)
    parts = []
    for k in range(len(pairs)):
        both = got[k].reshape(-1, got[k].shape[2])
        parts.append(rows_major(dot_plain(both, got[len(pairs) + k]).astype(jnp.bfloat16)))
    mats = []
    for group in groups:
        grad = jnp.concatenate(parts[: len(group)], 0) if len(group) > 1 else parts[0]
        parts = parts[len(group) :]
        mats.append(grad.reshape(total // 2, -1, grad.shape[1]))
    return mats


def mats_fit(mats):
    blocks, rows, width = mats[0].shape
    tile = -(-rows // 16) * 16 * -(-width // 128) * 128
    fits = (50 * 2**20 - tile * blocks * 2) // (tile * blocks * 5)
    return len(mats) if fits >= 3 else max(1, fits)


def head_lanes(half, shape):
    lane = lax.broadcasted_iota(jnp.int32, shape, 1)
    return (lane < HEAD) if half == 0 else (lane >= HEAD)


def pair_lanes(p):
    return pl.ds(pl.multiple_of(p * 2 * HEAD, 2 * HEAD), 2 * HEAD)


def seq_places():
    me = lax.axis_index("seq")
    return me, partner(("seq", 0))["seq"], partner(("seq", 1))["seq"]


def to_seq(source, target, sems, k, place):
    return pltpu.make_async_remote_copy(
        source,
        target,
        sems.at[0, k],
        sems.at[1, k],
        device_id={"seq": place},
        device_id_type=MESH,
    )


def attend_kernel(
    q_ref, own_ref, key_ids_ref, query_ids_ref, o_ref, lse_ref, kv_ref, blocked, far, near, pass_on, own_sem
):
    rows = own_ref.shape[0] // 2
    keys = kv_ref.shape[0] * rows
    pairs = q_ref.shape[1] // (2 * HEAD)
    me, near_at, far_at = seq_places()
    beyond = near_at + far_at - me
    greet([("seq", 0), ("seq", 1)])

    def far_copy(p, at):
        return to_seq(own_ref.at[:, pair_lanes(p)], kv_ref.at[at, :, pair_lanes(p)], far, p, far_at)

    def near_copy(p, at):
        return to_seq(own_ref.at[:, pair_lanes(p)], kv_ref.at[at, :, pair_lanes(p)], near, p, near_at)

    def pass_copy(p, at):
        here = kv_ref.at[far_at, :, pair_lanes(p)]
        return to_seq(here, kv_ref.at[at, :, pair_lanes(p)], pass_on, p, near_at)

    def send(p, carry):
        far_copy(p, me).start()
        near_copy(p, me).start()
        return carry

    lax.fori_loop(0, pairs, send, 0)
    own = pltpu.make_async_copy(own_ref, kv_ref.at[me], own_sem)
    own.start()
    blocked[...] = jnp.where(key_ids_ref[...] <= query_ids_ref[...], 0.0, MASK_FILL)
    own.wait()

    def forward_one(p):
        far_copy(p, far_at).wait_recv()
        pass_copy(p, far_at).start()

    forward_one(0)

    def pair(p, carry):
        @pl.when(p + 1 < pairs)
        def _():
            forward_one(p + 1)

        near_copy(p, near_at).wait_recv()
        pass_copy(p, beyond).wait_recv()
        lanes = pair_lanes(p)
        key_pair = kv_ref[:, :rows, lanes].reshape(keys, 2 * HEAD)
        val_turned = kv_ref[:, rows:, lanes].reshape(keys, 2 * HEAD).T
        query_pair = q_ref[:, lanes]
        outs = []
        for half in range(2):
            query = jnp.where(head_lanes(half, query_pair.shape), query_pair, 0)
            scores = dot_rows(key_pair, query.astype(jnp.bfloat16)) * HEAD ** (-0.5) + blocked[...]
            top = jnp.max(scores, 0, keepdims=True)
            raised = jnp.exp(scores - top)
            total = jnp.sum(raised, 0, keepdims=True)
            probs = (raised * (1.0 / total)).astype(jnp.bfloat16)
            outs.append(dot_plain(val_turned[half * HEAD : (half + 1) * HEAD], probs))
            lse_ref[p, half] = (top + jnp.log(total))[0]
        o_ref[:, lanes] = jnp.concatenate(outs, 0).T.astype(o_ref.dtype)
        return carry

    lax.fori_loop(0, pairs, pair, 0)

    def sent(p, carry):
        far_copy(p, me).wait_send()
        near_copy(p, me).wait_send()
        pass_copy(p, far_at).wait_send()
        return carry

    lax.fori_loop(0, pairs, sent, 0)


def attend(queries, own_pair, key_ids, query_ids, number):
    rows, width = queries.shape
    keys = key_ids.shape[0]
    pairs = width // (2 * HEAD)
    groups = lax.axis_size("seq")
    copies = pltpu.SemaphoreType.DMA((2, pairs))
    return pl.pallas_call(
        attend_kernel,
        out_shape=(
            jax.ShapeDtypeStruct((rows, width), jnp.bfloat16),
            jax.ShapeDtypeStruct((pairs, 2, rows), jnp.float32),
            jax.ShapeDtypeStruct((groups,) + own_pair.shape, jnp.bfloat16),
        ),
        in_specs=[pl.BlockSpec(memory_space=pltpu.VMEM)] * 4,
        out_specs=(pl.BlockSpec(memory_space=pltpu.VMEM),) * 3,
        scratch_shapes=[
            pltpu.VMEM((keys, rows), jnp.float32),
            copies,
            copies,
            copies,
            pltpu.SemaphoreType.DMA,
        ],
        compiler_params=pltpu.CompilerParams(
            collective_id=number, has_side_effects=True, vmem_limit_bytes=48 * 2**20
        ),
        cost_estimate=pl.CostEstimate(
            flops=4 * rows * keys * width,
            transcendentals=rows * keys * HEADS,
            bytes_accessed=4 * keys * width,
        ),
        name="attend",
    )(queries, own_pair, key_ids[:, None], query_ids[None, :])


def attend_back_kernel(
    q_ref,
    kv_ref,
    grad_ref,
    lse_ref,
    key_ids_ref,
    query_ids_ref,
    dq_ref,
    own_ref,
    blocked,
    fresh,
    kept,
    near_out,
    near_in,
    far_out,
    far_in,
    near,
    far,
):
    groups, twice, unused = kv_ref.shape
    rows = twice // 2
    keys = groups * rows
    pairs = q_ref.shape[1] // (2 * HEAD)
    scale = HEAD ** (-0.5)
    me, near_at, far_at = seq_places()
    low, high = lax.rem(me, 2), me // 2
    greet([("seq", 0), ("seq", 1)])
    blocked[...] = jnp.where(key_ids_ref[...] <= query_ids_ref[...], 0.0, MASK_FILL)

    def near_copy(p):
        return to_seq(near_out.at[p], near_in.at[p], near, p, near_at)

    def far_copy(p):
        return to_seq(far_out.at[p], far_in.at[p], far, p, far_at)

    def middle(p):
        near_copy(p).wait()
        for k in range(2):
            kept[p, k] = kept[p, k] + near_in[p, k].astype(jnp.float32)
        far_out[p] = kept[p, 1 - high].astype(far_out.dtype)
        far_copy(p).start()

    def last(p):
        far_copy(p).wait()
        total = kept[p, high] + far_in[p].astype(jnp.float32)
        own_ref[:, pair_lanes(p)] = total.astype(own_ref.dtype)

    def pair(p, carry):
        lanes = pair_lanes(p)
        key_pair = kv_ref[:, :rows, lanes].reshape(keys, 2 * HEAD)
        val_pair = kv_ref[:, rows:, lanes].reshape(keys, 2 * HEAD)
        key_turned = key_pair.T
        query_pair = q_ref[:, lanes]
        grad_pair = grad_ref[:, lanes]
        key_grad = jnp.zeros((keys, 2 * HEAD), jnp.float32)
        val_grad = jnp.zeros((keys, 2 * HEAD), jnp.float32)
        outs = []
        for half in range(2):
            here = head_lanes(half, query_pair.shape)
            query = jnp.where(here, query_pair, 0).astype(jnp.bfloat16)
            grad = jnp.where(here, grad_pair, 0).astype(jnp.bfloat16)
            scores = dot_rows(key_pair, query) * scale + blocked[...]
            probs = jnp.exp(scores - lse_ref[p, half][None, :])
            prob_grad = dot_rows(val_pair, grad)
            inner = jnp.sum(probs * prob_grad, 0, keepdims=True)
            score_grad = (probs * (prob_grad - inner)).astype(jnp.bfloat16)
            key_grad = key_grad + dot_plain(score_grad, query)
            val_grad = val_grad + dot_plain(probs.astype(jnp.bfloat16), grad)
            outs.append(dot_plain(key_turned[half * HEAD : (half + 1) * HEAD], score_grad))
        dq_ref[:, lanes] = (jnp.concatenate(outs, 0).T * scale).astype(dq_ref.dtype)
        fresh[:, :rows] = (key_grad * scale).reshape(groups, rows, 2 * HEAD)
        fresh[:, rows:] = val_grad.reshape(groups, rows, 2 * HEAD)
        for k in range(2):
            near_out[p, k] = fresh[2 * k + 1 - low].astype(near_out.dtype)
            kept[p, k] = fresh[2 * k + low]
        near_copy(p).start()

        @pl.when(p >= 1)
        def _():
            middle(p - 1)

        @pl.when(p >= 2)
        def _():
            last(p - 2)

        return carry

    lax.fori_loop(0, pairs, pair, 0)
    middle(pairs - 1)
    last(pairs - 2)
    last(pairs - 1)


def attend_back(queries, key_vals, grad, lse, key_ids, query_ids, number):
    rows, width = queries.shape
    keys = key_ids.shape[0]
    pairs = width // (2 * HEAD)
    piece = (2 * rows, 2 * HEAD)
    copies = pltpu.SemaphoreType.DMA((2, pairs))
    return pl.pallas_call(
        attend_back_kernel,
        out_shape=(
            jax.ShapeDtypeStruct((rows, width), jnp.bfloat16),
            jax.ShapeDtypeStruct((2 * rows, width), jnp.bfloat16),
        ),
        in_specs=[pl.BlockSpec(memory_space=pltpu.VMEM)] * 6,
        out_specs=(pl.BlockSpec(memory_space=pltpu.VMEM),) * 2,
        scratch_shapes=[
            pltpu.VMEM((keys, rows), jnp.float32),
            pltpu.VMEM((lax.axis_size("seq"),) + piece, jnp.float32),
            pltpu.VMEM((pairs, 2) + piece, jnp.float32),
            pltpu.VMEM((pairs, 2) + piece, jnp.bfloat16),
            pltpu.VMEM((pairs, 2) + piece, jnp.bfloat16),
            pltpu.VMEM((pairs,) + piece, jnp.bfloat16),
            pltpu.VMEM((pairs,) + piece, jnp.bfloat16),
            copies,
            copies,
        ],
        compiler_params=pltpu.CompilerParams(
            collective_id=number, has_side_effects=True, vmem_limit_bytes=58 * 2**20
        ),
        cost_estimate=pl.CostEstimate(
            flops=10 * rows * keys * width,
            transcendentals=rows * keys * HEADS,
            bytes_accessed=12 * keys * width,
        ),
        name="attend_back",
    )(queries, key_vals, grad, lse, key_ids[:, None], query_ids[None, :])


def add_pair(first, second):
    return first + second


def merge_soft(first, second):
    highest = jnp.maximum(first[0], second[0])
    total = first[1] * jnp.exp(first[0] - highest) + second[1] * jnp.exp(second[0] - highest)
    return jnp.stack([highest, total, first[2] + second[2]])


def dot_rows(left_op, right_op):
    return lax.dot_general(
        left_op, right_op, (((1,), (1,)), ((), ())), preferred_element_type=jnp.float32
    )


def dot_cols(left_op, right_op):
    return lax.dot_general(
        left_op, right_op, (((0,), (0,)), ((), ())), preferred_element_type=jnp.float32
    )


def dot_plain(left_op, right_op):
    return jnp.dot(left_op, right_op, preferred_element_type=jnp.float32)


def column_sums(values):
    return jnp.sum(values.astype(jnp.float32), 0)


def layer_norm(values, gain, shift):
    center = values - jnp.mean(values, -1, keepdims=True)
    spread = jnp.mean(center * center, -1, keepdims=True)
    return center * lax.rsqrt(spread + NORM_EPS) * gain + shift


def norm_back(values, gain, shift, grad):
    unused, pull = jax.vjp(layer_norm, values, gain, shift)
    return pull(grad)


def one_hot(wanted, length, axis):
    shape = list(wanted.shape)
    shape.insert(axis, length)
    at = lax.broadcasted_iota(jnp.int32, shape, axis)
    return (at == jnp.expand_dims(wanted, axis)).astype(jnp.bfloat16)


def counts_before(flags):
    length = flags.shape[-1]
    earlier = (
        lax.broadcasted_iota(jnp.int32, (length, length), 0)
        < lax.broadcasted_iota(jnp.int32, (length, length), 1)
    ).astype(jnp.bfloat16)
    return dot_plain(flags.astype(jnp.bfloat16), earlier).astype(jnp.int32)


def wide(rows_in):
    return jnp.pad(rows_in, ((0, 0), (0, -rows_in.shape[1] % (2 * HEAD))))


def rows_major(x):
    return with_layout_constraint(x, Layout(major_to_minor=tuple(range(x.ndim))))


def turned(x):
    return with_layout_constraint(x, Layout(major_to_minor=(1, 0)))


def scatter_rows(groups):
    total = lax.axis_size(AXES)
    mats = []
    for group in groups:
        parts = [rows_major(dot_cols(*pair).astype(jnp.bfloat16)) for pair in group]
        grad = jnp.concatenate(parts, 0) if len(parts) > 1 else parts[0]
        mats.append(grad.reshape(total, -1, grad.shape[1]))
    blocks = jnp.concatenate(mats, 1) if len(mats) > 1 else mats[0]
    own = lax.psum_scatter(blocks, AXES, scatter_dimension=0, tiled=True)[0]
    return own.reshape(len(mats), -1, own.shape[1])


def layer_forward(state, weights, params, query_ids, key_ids):
    width = state.shape[1]
    hidden = layer_norm(state, params[0 : 1], params[1 : 2]).astype(jnp.bfloat16)
    joined = rows_major(dot_rows(hidden, weights[0][: 3 * width]))
    queries = wide((joined[:, :width] + params[2 : 3]).astype(jnp.bfloat16))
    key_rows = joined[:, width : 2 * width].astype(jnp.bfloat16)
    val_rows = (joined[:, 2 * width :] + params[3 : 4]).astype(jnp.bfloat16)
    own_pair = jnp.concatenate([wide(key_rows), wide(val_rows)], 0)
    attended, lse, key_vals = attend(queries, own_pair, key_ids, query_ids, 4)
    attended = attended[:, :width]
    mid_state = state + dot_plain(attended, weights[0][3 * width :]) + params[4 : 5]
    normed = layer_norm(mid_state, params[5 : 6], params[6 : 7]).astype(jnp.bfloat16)
    upward = turned(dot_rows(normed, weights[1]) + params[8:12].reshape(1, -1))
    active = turned(jax.nn.gelu(upward, approximate=True).astype(jnp.bfloat16))
    output = mid_state + dot_plain(active, weights[2]) + params[7 : 8]
    return (
        output,
        (hidden, queries, key_vals, lse, attended, mid_state, normed, upward, active),
    )


def layer_backward(state, weights, params, saved, query_ids, key_ids, grad_in, arrived):
    width = state.shape[1]
    hidden, queries, key_vals, lse, attended, mid_state, normed, upward, active = saved
    down_grad = grad_in.astype(jnp.bfloat16)
    act_grad = dot_rows(down_grad, weights[2])
    unused_gelu, gelu_pull = jax.vjp(partial(jax.nn.gelu, approximate=True), upward)
    up_grad = turned(gelu_pull(act_grad)[0].astype(jnp.bfloat16))
    mid_back, gain_two, shift_two = norm_back(
        mid_state, params[5 : 6], params[6 : 7], rows_major(dot_plain(up_grad, weights[1]))
    )
    mid_grad = grad_in + mid_back
    out_grad = mid_grad.astype(jnp.bfloat16)
    att_grad = wide(rows_major(dot_rows(out_grad, weights[0][3 * width :]).astype(jnp.bfloat16)))
    if arrived:
        att_grad, arrived[0] = lax.optimization_barrier((att_grad, arrived[0]))
    query_grad, own = attend_back(queries, key_vals, att_grad, lse, key_ids, query_ids, 8)
    query_grad = query_grad[:, :width]
    key_grad, val_grad = own[: own.shape[0] // 2, :width], own[own.shape[0] // 2 :, :width]
    joined_grad = jnp.concatenate([query_grad, key_grad, val_grad], 1)
    state_back, gain_one, shift_one = norm_back(
        state,
        params[0 : 1],
        params[1 : 2],
        rows_major(dot_plain(joined_grad, weights[0][: 3 * width])),
    )
    up_sums = column_sums(up_grad)
    small_grad = [
        gain_one,
        shift_one,
        column_sums(query_grad),
        column_sums(val_grad),
        column_sums(out_grad),
        gain_two,
        shift_two,
        column_sums(down_grad),
        up_sums,
    ]
    factors = [
        [(joined_grad, hidden), (attended, out_grad)],
        [(up_grad, normed)],
        [(active, down_grad)],
    ]
    return (mid_grad + state_back, factors, small_grad)


def adam_step(weights, moment, square, grad, rate, decay, step):
    moment = BETA_ONE * moment + (1 - BETA_ONE) * grad
    square = BETA_TWO * square + (1 - BETA_TWO) * grad * grad
    moment_hat = moment / (1 - BETA_ONE**step)
    square_hat = square / (1 - BETA_TWO**step)
    weights = weights - rate * (moment_hat / (jnp.sqrt(square_hat) + ADAM_EPS) + decay * weights)
    return (weights, moment, square)


def pad_rows(x, rows):
    return jnp.pad(x, ((0, rows - x.shape[0]), (0, 0)))


def on_device(
    tokens,
    block_ids,
    completion,
    regroup,
    targets,
    step_count,
    layer_mats,
    mats_moment,
    mats_square,
    embed_table,
    table_moment,
    table_square,
):
    seqs, tok_count = tokens.shape
    seq_length = block_ids.shape[1]
    width = embed_table.shape[1]
    table_local = embed_table.shape[0]
    layers = layer_mats.shape[0]
    replicas, groups, shards = (lax.axis_size(axis) for axis in AXES)
    total = replicas * groups * shards
    seq_at = lax.axis_index("seq")
    shard_at = lax.axis_index("shard")
    device_at = lax.axis_index(AXES)
    seq_bits, dp_bits, shard_bits = bits_of("seq"), bits_of("dp"), bits_of("shard")
    first_row = device_at * table_local
    table_own = embed_table.astype(jnp.bfloat16)
    mats_low = layer_mats.astype(jnp.bfloat16)
    token_ids = tokens.reshape(-1)
    local_rows = token_ids.shape[0]
    small_count = 12 * layers + 2
    small_rows = -(-small_count // 16) * 16

    packed_ids = jnp.pad(token_ids, (0, -local_rows % 1024)).reshape(-1, 128)
    ids_all = run_jobs([spread_job(packed_ids, False)], "share_ids", 0, 16)[0][0]
    ids_all = ids_all.reshape(total, -1)[:, :local_rows]
    owner_all = ids_all // table_local
    loads = jnp.sum(
        (owner_all[:, :, None] == jnp.arange(total)[None, None, :]).astype(jnp.int32), 1
    )
    rounds = (jnp.max(loads) + SLOTS - 1) // SLOTS
    asked = owner_all == device_at
    asked_rank = counts_before(asked)
    asked_row = ids_all - first_row
    own_owner = token_ids // table_local
    same = own_owner[:, None] == own_owner[None, :]
    before = jnp.arange(local_rows)[None, :] < jnp.arange(local_rows)[:, None]
    own_rank = jnp.sum((same & before).astype(jnp.int32), 1)

    def asked_rows(at):
        chosen = asked[:, None, :] & (
            asked_rank[:, None, :] == at * SLOTS + jnp.arange(SLOTS)[None, :, None]
        )
        return (jnp.sum(jnp.where(chosen, asked_row[:, None, :] + 1, 0), 2) - 1).reshape(-1)

    def own_slots(at):
        slot = own_rank - at * SLOTS
        return jnp.where((slot >= 0) & (slot < SLOTS), own_owner * SLOTS + slot, -1)

    def fetch(at, given):
        return dot_plain(
            one_hot(own_slots(at), total * SLOTS, 1), given.reshape(total * SLOTS, width)
        )

    fixed = jnp.arange(seq_length + small_rows, dtype=jnp.int32)
    fixed_row = jnp.where(fixed < seq_length + small_count, VOCAB + fixed - first_row, -1)
    wanted = jnp.concatenate([asked_rows(0), fixed_row])
    rows_out = dot_plain(one_hot(wanted, table_local, 1), table_own).astype(jnp.bfloat16)
    exchanged = total * SLOTS
    piece = seq_length // total
    gathered = []
    for layer_at in range(layers):
        if layer_at == 0:
            whole = lax.all_gather(mats_low[0], AXES, axis=1, tiled=True)
            gathered.append([whole[k] for k in range(3)])
        else:
            rest = lax.all_gather(mats_low[layer_at, 1:], AXES, axis=1, tiled=True)
            gathered.append([rest[0], rest[1]])
    (upper_first,), (place_rows,), (small,), (given,) = run_jobs(
        [
            gather_job([mats_low[1, 0]]),
            sum_job(
                rows_out[exchanged : exchanged + seq_length].reshape(total, piece, width),
                sum_axes=("seq", "dp", "shard"),
                sum_orders=[seq_bits + dp_bits + shard_bits],
                join_axes=("dp", "shard"),
                join_orders=[shard_bits[::-1] + dp_bits[::-1]],
            ),
            combine_job(rows_out[exchanged + seq_length :], add_pair),
            swap_job(rows_out[:exchanged].reshape(total, SLOTS, width), late=7),
        ],
        "open_rows",
        2,
        32,
    )
    gathered[1].insert(0, upper_first.reshape(-1, width))
    place_rows = place_rows.reshape(tok_count, width)
    small = small[:small_count].astype(jnp.float32)
    place_state = jnp.broadcast_to(place_rows.astype(jnp.float32), (seqs, tok_count, width))
    state = fetch(0, given) + place_state.reshape(local_rows, width)

    def fetch_more(at, held):
        rows = dot_plain(one_hot(asked_rows(at), table_local, 1), table_own).astype(jnp.bfloat16)
        return held + fetch(at, swap(rows.reshape(total, SLOTS, width), "swap_rows", 1))

    state = lax.fori_loop(1, rounds, fetch_more, state)

    query_ids = lax.dynamic_slice_in_dim(block_ids[0], seq_at * tok_count, tok_count, 0)
    inputs, kept, saved = [], [], []
    for layer_at in range(layers):
        weights = gathered[layer_at]
        inputs.append(state)
        kept.append(weights)
        state, held = layer_forward(
            state,
            weights,
            small[12 * layer_at : 12 * layer_at + 12],
            query_ids,
            block_ids[0],
        )
        saved.append(held)
    final_gain = small[12 * layers : 12 * layers + 1]
    final_shift = small[12 * layers + 1 : 12 * layers + 2]
    final = layer_norm(state, final_gain, final_shift).astype(jnp.bfloat16)

    group_mask = completion[0]
    slot_of = regroup[0]
    slots = slot_of.shape[0]
    comp_rows = slots // shards
    rank_all = counts_before(group_mask[None])[0]
    mine = lax.dynamic_slice_in_dim(group_mask, shard_at * local_rows, local_rows)
    my_rank = lax.dynamic_slice_in_dim(rank_all, shard_at * local_rows, local_rows)
    my_slot = jnp.sum(
        jnp.where(my_rank[:, None] == jnp.arange(slots)[None, :], slot_of[None, :], 0), 1
    )
    to_slot = one_hot(jnp.where(mine == 1, my_slot, -1), slots, 0)
    outgoing = dot_plain(to_slot, final).astype(jnp.bfloat16).reshape(shards, comp_rows, width)
    two_ways = [seq_bits[1:] + dp_bits, dp_bits + seq_bits[1:]]
    head_in = exchange(
        outgoing,
        "share_final",
        5,
        sum_axes=("shard",),
        sum_orders=[shard_bits, shard_bits],
        join_axes=AXES,
        join_orders=[shard_bits[::-1] + way[::-1] + seq_bits[:1] for way in two_ways],
        chunks=2,
    ).reshape(-1, width)

    rows_all = targets.shape[0]
    columns = first_row + jnp.arange(table_local, dtype=jnp.int32)
    live = (columns < VOCAB)[None, :]
    logits = dot_rows(head_in, table_own)
    masked = jnp.where(live, logits, MASK_FILL)
    top_local = jnp.max(masked, 1)
    total_local = jnp.sum(jnp.where(live, jnp.exp(masked - top_local[:, None]), 0.0), 1)
    target_hit = columns[None, :] == targets[:, None]
    pick_local = jnp.sum(jnp.where(target_hit, logits, 0.0), 1)
    stats = combine_all(
        jnp.stack([top_local, total_local, pick_local]).reshape(3, -1, 128),
        merge_soft,
        "share_stats",
        6,
    ).reshape(3, rows_all)
    log_total = stats[0] + jnp.log(stats[1])
    loss_value = jnp.sum(log_total - stats[2]) / rows_all
    probs = jnp.where(live, jnp.exp(masked - log_total[:, None]), 0.0)
    logit_grad = ((probs - target_hit.astype(jnp.float32)) / rows_all).astype(jnp.bfloat16)
    head_grad = dot_cols(logit_grad, head_in)
    returned = exchange(
        dot_plain(logit_grad, table_own).reshape(total, comp_rows, width),
        "return_final",
        7,
        sum_axes=AXES,
        sum_orders=[seq_bits[:1] + way + shard_bits for way in two_ways],
        join_axes=("shard",),
        join_orders=[shard_bits[::-1], shard_bits[::-1]],
        chunks=2,
    ).reshape(slots, width)
    final_grad = rows_major(dot_cols(to_slot, returned))
    state_grad, gain_final, shift_final = norm_back(state, final_gain, final_shift, final_grad)

    late = []
    arrived = []
    small_grads = [None] * layers
    for layer_at in reversed(range(layers)):
        state_grad, factors, small_grads[layer_at] = layer_backward(
            inputs[layer_at],
            kept[layer_at],
            small[12 * layer_at : 12 * layer_at + 12],
            saved[layer_at],
            query_ids,
            block_ids[0],
            state_grad,
            arrived,
        )
        if layer_at > 0:
            arrived = [scatter_rows(factors[2:]), scatter_rows(factors[1:2])]
            late = factors[:1]
        else:
            late = factors + late

    low_grad = state_grad.astype(jnp.bfloat16)
    place_grad = jnp.sum(state_grad.reshape(seqs, tok_count, width), 0)
    small_grad = jnp.concatenate(
        [x.reshape(-1) for x in sum(small_grads, []) + [gain_final, shift_final]]
    )
    small_size = small_grad.shape[0]
    small_grad = jnp.pad(small_grad, (0, -small_size % 1024)).reshape(-1, 128)

    def leaving(at):
        rows = dot_cols(one_hot(own_slots(at), total * SLOTS, 1), low_grad).astype(jnp.bfloat16)
        return rows_major(rows).reshape(total, SLOTS, width)

    late = late_mats(late, 12)
    fits = mats_fit(late)
    (own_mats,), (place_grad,), (small_grad,), (came,) = run_jobs(
        [
            mats_job(late[:fits]),
            sum_job(
                place_grad.reshape(replicas * shards, piece, width),
                sum_axes=("dp", "shard"),
                sum_orders=[dp_bits + shard_bits],
                join_axes=("seq", "dp", "shard"),
                join_orders=[shard_bits[::-1] + dp_bits[::-1] + seq_bits[::-1]],
            ),
            combine_job(small_grad, add_pair),
            swap_job(leaving(0), late=5),
        ],
        "close_rows",
        10,
        61,
    )
    for k in range(fits, len(late), fits):
        more = run_jobs([mats_job(late[k : k + fits])], "sum_mats", 14 + k, 61)[0][0]
        own_mats = jnp.concatenate([own_mats, lax.optimization_barrier(more)], 0)
    place_grad = place_grad.reshape(seq_length, width)
    came, arrived[1] = lax.optimization_barrier((came, arrived[1]))
    upper = jnp.concatenate([arrived[1], arrived[0]], 0).astype(jnp.float32)
    small_grad = pad_rows(small_grad.reshape(-1)[:small_size].reshape(-1, width), small_rows)
    small_high = small_grad.astype(jnp.bfloat16)
    small_low = (small_grad - small_high.astype(jnp.float32)).astype(jnp.bfloat16)
    values = jnp.concatenate([came.reshape(-1, width), place_grad, small_high, small_low], 0)
    value_row = jnp.concatenate([wanted, fixed_row[seq_length:]])
    table_grad = dot_plain(one_hot(value_row, table_local, 0), values) + head_grad

    def return_more(at, held):
        rows = swap(leaving(at), "swap_rows", 1).reshape(-1, width)
        return held + dot_plain(one_hot(asked_rows(at), table_local, 0), rows)

    table_grad = lax.fori_loop(1, rounds, return_more, table_grad)
    mats_grad = jnp.concatenate([own_mats, upper], 0).reshape(layer_mats.shape)
    local_squares = jnp.sum(mats_grad * mats_grad) + jnp.sum(table_grad * table_grad)
    squares = jnp.full((8, 128), local_squares)
    squares = run_jobs([spread_job(squares, True)], "share_norm", 11, 16)[0][0]
    grad_norm = jnp.sqrt(squares[0, 0])
    factor = CLIP_NORM / grad_norm
    step = step_count[0].astype(jnp.float32)
    new_mats = adam_step(
        layer_mats, mats_moment, mats_square, factor * mats_grad, RATE_MATS, DECAY_RATE, step
    )
    plain_rows = (columns < VOCAB + seq_length)[:, None]
    rate = jnp.where(plain_rows, RATE_TABLE, RATE_SMALL)
    decay = jnp.where(plain_rows, DECAY_RATE, 0.0)
    new_table = adam_step(
        embed_table, table_moment, table_square, factor * table_grad, rate, decay, step
    )
    return (
        loss_value.reshape(1),
        grad_norm.reshape(1),
        new_mats[0],
        new_mats[1],
        new_mats[2],
        new_table[0],
        new_table[1],
        new_table[2],
    )


def solution(mesh):
    in_specs = (
        P(("dp", "shard"), "seq"),
        P(("dp", "shard"), None),
        P(("dp", "seq"), None),
        P(("dp", "seq"), None),
        P(),
        P(),
        P(None, None, ("dp", "seq", "shard"), None),
        P(None, None, ("dp", "seq", "shard"), None),
        P(None, None, ("dp", "seq", "shard"), None),
        P(("dp", "seq", "shard"), None),
        P(("dp", "seq", "shard"), None),
        P(("dp", "seq", "shard"), None),
    )
    out_specs = (
        P(),
        P(),
        P(None, None, ("dp", "seq", "shard"), None),
        P(None, None, ("dp", "seq", "shard"), None),
        P(None, None, ("dp", "seq", "shard"), None),
        P(("dp", "seq", "shard"), None),
        P(("dp", "seq", "shard"), None),
        P(("dp", "seq", "shard"), None),
    )
    return jax.shard_map(
        on_device, mesh=mesh, in_specs=in_specs, out_specs=out_specs, check_vma=False
    )
```

```python
import itertools
from functools import partial

import jax
import jax.numpy as jnp
from jax import lax
from jax.experimental import pallas as pl
from jax.experimental.layout import Layout, with_layout_constraint
from jax.experimental.pallas import tpu as pltpu
from jax.sharding import PartitionSpec as P

HEADS = 17
HEAD = 64
VOCAB = 50278

NORM_EPS = 1e-05
CLIP_NORM = 0.02
BETA_ONE = 0.9
BETA_TWO = 0.95
ADAM_EPS = 1e-08
DECAY_RATE = 0.1
RATE_MATS = 0.05
RATE_TABLE = 0.1
RATE_SMALL = 0.5
MASK_FILL = -1e30

AXES = ("dp", "seq", "shard")
MESH = pl.DeviceIdType.MESH
SLOTS = 24


def bits_of(axis):
    return [(axis, b) for b in range(lax.axis_size(axis).bit_length() - 1)]


def bit_here(bit):
    return lax.rem(lax.axis_index(bit[0]) // 2 ** bit[1], 2)


def partner(bit):
    at = lax.axis_index(bit[0])
    return {bit[0]: at + (1 - 2 * bit_here(bit)) * 2 ** bit[1]}


def greet(bits):
    barrier = pltpu.get_barrier_semaphore()
    for bit in bits:
        pl.semaphore_signal(barrier, inc=1, device_id=partner(bit), device_id_type=MESH)
    pl.semaphore_wait(barrier, len(bits))


def block_weight(axes, bit):
    weight = 2 ** bit[1]
    for axis in axes[axes.index(bit[0]) + 1 :]:
        weight *= lax.axis_size(axis)
    return weight


def block_runs(weights):
    weights = sorted(weights)
    joined = 0
    while joined < len(weights) and weights[joined] == 2**joined:
        joined += 1
    rest = [(0, w) for w in weights[joined:]]
    return 2**joined, [sum(c) for c in itertools.product(*rest)]


class Job:
    def __init__(
        self, inputs, outputs, scratch, sends, keeps, bits, steps, spaces=(pltpu.VMEM, pltpu.VMEM)
    ):
        self.inputs, self.outputs, self.scratch = inputs, outputs, scratch
        self.sends, self.keeps, self.bits, self.steps, self.spaces = sends, keeps, bits, steps, spaces


def me_and_total():
    seq_size, shard_size = lax.axis_size("seq"), lax.axis_size("shard")
    at = (lax.axis_index("dp") * seq_size + lax.axis_index("seq")) * shard_size
    return at + lax.axis_index("shard"), lax.axis_size("dp") * seq_size * shard_size


def place_of(at):
    seq_size, shard_size = lax.axis_size("seq"), lax.axis_size("shard")
    return {
        "dp": at // (seq_size * shard_size),
        "seq": lax.rem(at // shard_size, seq_size),
        "shard": lax.rem(at, shard_size),
    }


def greet_all():
    me, total = me_and_total()
    barrier = pltpu.get_barrier_semaphore()

    def hello(k, carry):
        pl.semaphore_signal(
            barrier, inc=1, device_id=place_of(lax.rem(me + k, total)), device_id_type=MESH
        )
        return carry

    lax.fori_loop(1, total, hello, 0)
    pl.semaphore_wait(barrier, total - 1)


class Sems:
    def __init__(self, send, recv, keep):
        self.send, self.recv, self.keep = send, recv, keep
        self.used = self.kept = 0

    def copy(self, source, target, device):
        k = self.used
        self.used += 1
        copy = pltpu.make_async_remote_copy(
            source, target, self.send.at[k], self.recv.at[k], device_id=device, device_id_type=MESH
        )
        copy.start()
        return copy

    def local(self, source, target):
        k = self.kept
        self.kept += 1
        copy = pltpu.make_async_copy(source, target, self.keep.at[k])
        copy.start()
        return copy

    def span(self, count):
        first = self.used
        self.used += count
        return first


def jobs_kernel(jobs, *refs):
    refs = list(refs)

    def take(count):
        out = refs[:count]
        del refs[:count]
        return out

    held = [take(len(job.inputs)) for job in jobs]
    made = [take(len(job.outputs)) for job in jobs]
    used = [take(len(job.scratch)) for job in jobs]
    sems = Sems(*refs)
    if any(job.bits is None for job in jobs):
        greet_all()
    else:
        greet(sorted(set(bit for job in jobs for bit in job.bits)))
    active = []
    for job, x, o, w in zip(jobs, held, made, used):
        active += job.steps(x, o, w, sems)
    tick = 0
    while active:
        left = []
        for delay, gen in active:
            if delay > tick or next(gen, "end") != "end":
                left.append((delay, gen))
        active = left
        tick += 1


def run_jobs(jobs, name, number, vmem=60):
    inputs = [x for job in jobs for x in job.inputs]
    outputs = [o for job in jobs for o in job.outputs]
    in_specs = [pl.BlockSpec(memory_space=job.spaces[0]) for job in jobs for unused in job.inputs]
    out_specs = [pl.BlockSpec(memory_space=job.spaces[1]) for job in jobs for unused in job.outputs]
    sends = sum(job.sends for job in jobs)
    keeps = max(1, sum(job.keeps for job in jobs))
    flat = pl.pallas_call(
        partial(jobs_kernel, jobs),
        out_shape=outputs,
        in_specs=in_specs,
        out_specs=out_specs,
        scratch_shapes=[w for job in jobs for w in job.scratch]
        + [
            pltpu.SemaphoreType.DMA((sends,)),
            pltpu.SemaphoreType.DMA((sends,)),
            pltpu.SemaphoreType.DMA((keeps,)),
        ],
        compiler_params=pltpu.CompilerParams(
            collective_id=number, has_side_effects=True, vmem_limit_bytes=vmem * 2**20
        ),
        name=name,
    )(*inputs)
    out = []
    for job in jobs:
        out.append(flat[: len(job.outputs)])
        flat = flat[len(job.outputs) :]
    return out


def sum_stream(x_ref, o_ref, scratch, sems, rows, first_slot, sum_axes, sums, join_axes, joins):
    source = x_ref
    slot = first_slot
    if sums:
        work, parcel, recv = scratch
    for step, bit in enumerate(sums):
        base = sum(bit_here(b) * block_weight(sum_axes, b) for b in sums[:step])
        weight = block_weight(sum_axes, bit)
        mine = bit_here(bit)
        size, offsets = block_runs([block_weight(sum_axes, b) for b in sums[step + 1 :]])
        started = []
        for offset in offsets:
            leave = base + (1 - mine) * weight + offset
            if source.dtype == parcel.dtype:
                packed = source.at[pl.ds(leave, size), rows]
            else:

                def pack(i, carry, leave=leave, at=slot, source=source):
                    parcel[at + i, rows] = source[leave + i, rows].astype(parcel.dtype)
                    return carry

                lax.fori_loop(0, size, pack, 0)
                packed = parcel.at[pl.ds(slot, size), rows]
            copy = sems.copy(packed, recv.at[pl.ds(slot, size), rows], partner(bit))
            started.append((copy, base + mine * weight + offset, slot, size))
            slot += size
        yield
        for copy, keep, at, size in started:
            copy.wait()

            def add(i, carry, keep=keep, at=at, source=source):
                total = source[keep + i, rows].astype(jnp.float32)
                total = total + recv[at + i, rows].astype(jnp.float32)
                work[keep + i, rows] = total.astype(work.dtype)
                return carry

            lax.fori_loop(0, size, add, 0)
        source = work
    own = sum(bit_here(b) * block_weight(sum_axes, b) for b in sums) if sums else 0
    result = source[own, rows].astype(o_ref.dtype)
    if not joins:
        o_ref[rows] = result
        return
    o_ref[sum(bit_here(b) * block_weight(join_axes, b) for b in joins), rows] = result
    for step, bit in enumerate(joins):
        base = sum(bit_here(b) * block_weight(join_axes, b) for b in joins[step:])
        size, offsets = block_runs([block_weight(join_axes, b) for b in joins[:step]])
        started = []
        for offset in offsets:
            here = o_ref.at[pl.ds(base + offset, size), rows]
            started.append(sems.copy(here, here, partner(bit)))
        yield
        for copy in started:
            copy.wait()


def sum_job(x, sum_axes=(), sum_orders=(), join_axes=(), join_orders=(), chunks=1):
    rows, width = x.shape[-2:]
    blocks = 1
    for axis in join_axes:
        blocks *= lax.axis_size(axis)
    kind = jnp.bfloat16 if sum_axes else x.dtype
    streams = max(len(sum_orders), len(join_orders))
    if rows % (streams * chunks * 16):
        chunks = 1
    share = rows // (streams * chunks)
    sends = 0
    for order in sum_orders:
        for step in range(len(order)):
            sends += len(block_runs([block_weight(sum_axes, b) for b in order[step + 1 :]])[1])
    for order in join_orders:
        for step in range(len(order)):
            sends += len(block_runs([block_weight(join_axes, b) for b in order[:step]])[1])
    scratch = []
    if sum_axes:
        if x.size * 14 > 56 * 2**20:
            x = x.astype(jnp.bfloat16)
        exact = x.dtype == jnp.float32 or x.size < 2**22
        scratch = [
            pltpu.VMEM(x.shape, jnp.float32 if exact else kind),
            pltpu.VMEM(x.shape, kind),
            pltpu.VMEM(x.shape, kind),
        ]

    def steps(x_refs, o_refs, scratch_refs, sems):
        gens = []
        for c in range(chunks):
            for k in range(streams):
                rows_here = pl.ds((k * chunks + c) * share, share)
                sums = sum_orders[k] if sum_orders else []
                joins = join_orders[k] if join_orders else []
                gens.append(
                    (
                        c,
                        sum_stream(
                            x_refs[0], o_refs[0], scratch_refs, sems, rows_here, 0,
                            sum_axes, sums, join_axes, joins,
                        ),
                    )
                )
        return gens

    bits = set(bit for order in list(sum_orders) + list(join_orders) for bit in order)
    shape = (blocks, rows, width) if join_axes else (rows, width)
    return Job(
        [x], [jax.ShapeDtypeStruct(shape, kind)], scratch, sends * chunks, 0, bits, steps
    )


def exchange(x, name, number, **how):
    return run_jobs([sum_job(x, **how)], name, number)[0][0]


def combine_job(x, combine):
    bits = [bit for axis in reversed(AXES) for bit in bits_of(axis)]
    slots = (len(bits),) + x.shape

    def steps(x_refs, o_refs, scratch, sems):
        out_buf, in_buf = scratch

        def gen():
            current = x_refs[0][...]
            for i, bit in enumerate(bits):
                out_buf[i] = current
                copy = sems.copy(out_buf.at[i], in_buf.at[i], partner(bit))
                yield
                copy.wait()
                current, other = out_buf[i], in_buf[i]
                low = bit_here(bit) == 0
                current = combine(jnp.where(low, current, other), jnp.where(low, other, current))
            o_refs[0][...] = current

        return [(0, gen())]

    return Job(
        [x],
        [jax.ShapeDtypeStruct(x.shape, x.dtype)],
        [pltpu.VMEM(slots, x.dtype), pltpu.VMEM(slots, x.dtype)],
        len(bits),
        0,
        bits,
        steps,
    )


def combine_all(x, combine, name, number):
    return run_jobs([combine_job(x, combine)], name, number, 16)[0][0]


def swap_job(x, late=0):
    total = x.shape[0]

    def steps(x_refs, o_refs, scratch, sems):
        x_ref, o_ref = x_refs[0], o_refs[0]

        def gen():
            me, unused = me_and_total()
            first = sems.span(total)
            keep = sems.local(x_ref.at[me], o_ref.at[me])

            def copy_to(other, here):
                return pltpu.make_async_remote_copy(
                    x_ref.at[other],
                    o_ref.at[here],
                    sems.send.at[first + other],
                    sems.recv.at[first + here],
                    device_id=place_of(other),
                    device_id_type=MESH,
                )

            def send(k, carry):
                copy_to(lax.rem(me + k, total), me).start()
                return carry

            lax.fori_loop(1, total, send, 0)
            for unused in range(late + 1):
                yield

            def finish(k, carry):
                other = lax.rem(me + k, total)
                copy_to(other, other).wait()
                return carry

            lax.fori_loop(1, total, finish, 0)
            keep.wait()

        return [(0, gen())]

    return Job(
        [x],
        [jax.ShapeDtypeStruct(x.shape, x.dtype)],
        [],
        total,
        1,
        None,
        steps,
        spaces=(pl.ANY, pl.ANY),
    )


def spread_job(x, add):
    total = lax.axis_size(AXES)
    all_shape = (total,) + x.shape

    def steps(x_refs, o_refs, scratch, sems):
        x_ref = x_refs[0]
        target = scratch[0] if add else o_refs[0]

        def gen():
            me, unused = me_and_total()
            first = sems.span(total)
            target[me] = x_ref[...]

            def copy_to(other, here):
                return pltpu.make_async_remote_copy(
                    x_ref,
                    target.at[here],
                    sems.send.at[first + other],
                    sems.recv.at[first + here],
                    device_id=place_of(other),
                    device_id_type=MESH,
                )

            def send(k, carry):
                copy_to(lax.rem(me + k, total), me).start()
                return carry

            lax.fori_loop(1, total, send, 0)
            yield

            def finish(k, carry):
                other = lax.rem(me + k, total)
                copy_to(other, other).wait()
                return carry

            lax.fori_loop(1, total, finish, 0)
            if add:
                o_refs[0][...] = jnp.sum(target[...], 0)

        return [(0, gen())]

    return Job(
        [x],
        [jax.ShapeDtypeStruct(x.shape if add else all_shape, x.dtype)],
        [pltpu.VMEM(all_shape, x.dtype)] if add else [],
        total,
        0,
        None,
        steps,
    )


def swap(x, name, number):
    return run_jobs([swap_job(x)], name, number, 16)[0][0]


def sum_orders_for(rows):
    across, along, deep = bits_of("seq")[1:], bits_of("dp"), bits_of("shard")
    if rows < 64 or rows % 8:
        return [(0, rows)], [across + along + deep]
    one, two = rows * 8 // 17 // 16 * 16, rows * 6 // 17 // 16 * 16
    spans = [(0, one), (one, two), (one + two, rows - one - two)]
    return spans, [across + along + deep, along + across + deep, deep + along + across]


def mats_stream(x_ref, o_ref, scratch, sems, m, span, order, weights):
    kept, work, parcel, recv = scratch
    which, turn, m = m, m % 2, m % work.shape[0]
    steps = len(order)
    rows = pl.ds(*span)
    slot = 0
    rest = sorted((b for b in weights if b != order[0]), key=lambda b: weights[b])
    small = {b: 2**k for k, b in enumerate(rest)}
    for step, bit in enumerate(order):
        mine = bit_here(bit)
        base = sum(bit_here(b) * small[b] for b in order[1:step])
        runs, keeps = [], []
        if step == 0:
            size, offsets = block_runs([weights[b] for b in order[1:]])
            for offset in offsets:
                left, place = offset, 0
                for b in reversed(rest):
                    if left >= weights[b]:
                        left -= weights[b]
                        place += small[b]
                keeps.append(
                    sems.local(
                        x_ref.at[pl.ds(mine * weights[bit] + offset, size), rows],
                        kept.at[turn, pl.ds(place, size), rows],
                    )
                )
                runs.append(((1 - mine) * weights[bit] + offset, place))
        else:
            size, offsets = block_runs([small[b] for b in order[step + 1 :]])
            for offset in offsets:
                here = base + offset
                runs.append((here + (1 - mine) * small[bit], here + mine * small[bit]))
        started = []
        for leave, keep_at in runs:
            at = slot
            slot += size
            if step == 0:
                packed = x_ref.at[pl.ds(leave, size), rows]
            else:
                spot = at - 2 ** (steps - 1)

                def pack(i, carry, leave=leave, spot=spot):
                    parcel[m, spot + i, rows] = work[m, leave + i, rows].astype(parcel.dtype)
                    return carry

                lax.fori_loop(0, size, pack, 0)
                packed = parcel.at[m, pl.ds(spot, size), rows]
            copy = sems.copy(packed, recv.at[m, pl.ds(at, size), rows], partner(bit))
            started.append((copy, at, keep_at, size))
        yield
        for keep in keeps:
            keep.wait()
        for copy, at, keep_at, size in started:
            copy.wait()

            def add(i, carry, at=at, keep_at=keep_at, step=step):
                if step == 0:
                    total = kept[turn, keep_at + i, rows].astype(jnp.float32)
                else:
                    total = work[m, keep_at + i, rows]
                work[m, keep_at + i, rows] = total + recv[m, at + i, rows].astype(jnp.float32)
                return carry

            lax.fori_loop(0, size, add, 0)
    o_ref[which, rows] = work[m, sum(bit_here(b) * small[b] for b in order[1:]), rows]


def mats_job(mats):
    blocks, rows, width = mats[0].shape
    spans, orders = sum_orders_for(rows)
    weights = {}
    for bit in orders[0]:
        weight = block_weight(AXES, bit)
        weights[bit] = weight if bit[0] == "shard" else weight // 2
    keeps = sends = 0
    for order in orders:
        keeps += len(block_runs([weights[b] for b in order[1:]])[1])
        sends += len(block_runs([weights[b] for b in order[1:]])[1])
        rest = sorted((b for b in weights if b != order[0]), key=lambda b: weights[b])
        small = {b: 2**k for k, b in enumerate(rest)}
        for step in range(1, len(order)):
            sends += len(block_runs([small[b] for b in order[step + 1 :]])[1])
    count = len(mats)

    def steps(x_refs, o_refs, scratch, sems):
        o_ref = o_refs[0]
        return [
            (m, mats_stream(x_refs[m], o_ref, scratch, sems, m, spans[k], orders[k], weights))
            for m in range(count)
            for k in range(len(orders))
        ]

    return Job(
        mats,
        [jax.ShapeDtypeStruct((count, rows, width), jnp.float32)],
        [
            pltpu.VMEM((min(2, count), blocks // 2, rows, width), jnp.bfloat16),
            pltpu.VMEM((min(3, count), blocks // 2, rows, width), jnp.float32),
            pltpu.VMEM((min(3, count), blocks // 2 - 1, rows, width), jnp.bfloat16),
            pltpu.VMEM((min(3, count), blocks - 1, rows, width), jnp.bfloat16),
        ],
        count * sends,
        count * keeps,
        set(orders[0]),
        steps,
        spaces=(pl.ANY, pltpu.VMEM),
    )


def gather_job(parts):
    rows, width = parts[0].shape
    spans, orders = sum_orders_for(rows)
    orders = [order[::-1] + bits_of("seq")[:1] for order in orders]
    total = lax.axis_size(AXES)
    sends = 0
    for order in orders:
        for step in range(len(order)):
            sends += len(block_runs([block_weight(AXES, b) for b in order[:step]])[1])

    def gen(x_ref, o_ref, sems, span, order):
        here = pl.ds(*span)
        own = me_and_total()[0]
        keep = sems.local(x_ref.at[here], o_ref.at[own, here])
        for step, bit in enumerate(order):
            base = sum(bit_here(b) * block_weight(AXES, b) for b in order[step:])
            size, offsets = block_runs([block_weight(AXES, b) for b in order[:step]])
            started = []
            for offset in offsets:
                target = o_ref.at[pl.ds(base + offset, size), here]
                source = x_ref.at[here] if step == 0 else target
                target = o_ref.at[own, here] if step == 0 else target
                started.append(sems.copy(source, target, partner(bit)))
            yield
            if step == 0:
                keep.wait()
            for copy in started:
                copy.wait()

    def steps(x_refs, o_refs, scratch, sems):
        return [
            (m, gen(x_refs[m], o_refs[m], sems, spans[k], orders[k]))
            for m in range(len(parts))
            for k in range(len(orders))
        ]

    return Job(
        parts,
        [jax.ShapeDtypeStruct((total, rows, width), parts[0].dtype)] * len(parts),
        [],
        sends * len(parts),
        len(orders) * len(parts),
        set(orders[0]),
        steps,
        spaces=(pl.ANY, pl.ANY),
    )


def trade_kernel(halved, count, *refs):
    x_refs, o_refs = refs[:count], refs[count : 2 * count]
    send_sems, recv_sems, keep_sems = refs[2 * count :]
    bit = ("seq", 0)
    mine = bit_here(bit)
    greet([bit])
    copies = []
    for k in range(count):
        if k < halved:
            tokens = x_refs[k].shape[-1]
            keep, leave = x_refs[k].at[:, mine], x_refs[k].at[:, 1 - mine]
            near = o_refs[k].at[:, :, pl.ds(0, tokens)]
            far = o_refs[k].at[:, :, pl.ds(tokens, tokens)]
        else:
            tokens = x_refs[k].shape[0]
            keep = leave = x_refs[k]
            near, far = o_refs[k].at[pl.ds(0, tokens)], o_refs[k].at[pl.ds(tokens, tokens)]
        local = pltpu.make_async_copy(keep, near, keep_sems.at[k])
        local.start()
        copy = pltpu.make_async_remote_copy(
            leave,
            far,
            send_sems.at[k],
            recv_sems.at[k],
            device_id=partner(bit),
            device_id_type=MESH,
        )
        copy.start()
        copies += [local, copy]
    for copy in copies:
        copy.wait()


def trade(features, cotangents, name, number):
    arrays = features + cotangents
    count = len(arrays)
    outs = []
    for x in features:
        runs, unused, rows, tokens = x.shape
        outs.append(jax.ShapeDtypeStruct((runs, rows, 2 * tokens), x.dtype))
    for x in cotangents:
        outs.append(jax.ShapeDtypeStruct((2 * x.shape[0], x.shape[1]), x.dtype))
    return pl.pallas_call(
        partial(trade_kernel, len(features), count),
        out_shape=outs,
        in_specs=[pl.BlockSpec(memory_space=pl.ANY)] * count,
        out_specs=[pl.BlockSpec(memory_space=pltpu.VMEM)] * count,
        scratch_shapes=[pltpu.SemaphoreType.DMA((count,))] * 3,
        compiler_params=pltpu.CompilerParams(
            collective_id=number, has_side_effects=True, vmem_limit_bytes=40 * 2**20
        ),
        name=name,
    )(*arrays)


def late_mats(groups, number):
    pairs = [pair for group in groups for pair in group]
    total = lax.axis_size(AXES)
    height = sum(features.shape[1] for features, unused in groups[0])
    own = height // total * lax.axis_size("shard")
    features = [x.T.reshape(-1, 2, own, x.shape[0]) for x, unused in pairs]
    got = trade(features, [tail for unused, tail in pairs], "trade_rows", number)
    parts = []
    for k in range(len(pairs)):
        both = got[k].reshape(-1, got[k].shape[2])
        parts.append(rows_major(dot_plain(both, got[len(pairs) + k]).astype(jnp.bfloat16)))
    mats = []
    for group in groups:
        grad = jnp.concatenate(parts[: len(group)], 0) if len(group) > 1 else parts[0]
        parts = parts[len(group) :]
        mats.append(grad.reshape(total // 2, -1, grad.shape[1]))
    return mats


def mats_fit(mats):
    blocks, rows, width = mats[0].shape
    tile = -(-rows // 16) * 16 * -(-width // 128) * 128
    fits = (50 * 2**20 - tile * blocks * 2) // (tile * blocks * 5)
    return len(mats) if fits >= 3 else max(1, fits)


def head_lanes(half, shape):
    lane = lax.broadcasted_iota(jnp.int32, shape, 1)
    return (lane < HEAD) if half == 0 else (lane >= HEAD)


def pair_lanes(p):
    return pl.ds(pl.multiple_of(p * 2 * HEAD, 2 * HEAD), 2 * HEAD)


def seq_places():
    me = lax.axis_index("seq")
    return me, partner(("seq", 0))["seq"], partner(("seq", 1))["seq"]


def to_seq(source, target, sems, k, place):
    return pltpu.make_async_remote_copy(
        source,
        target,
        sems.at[0, k],
        sems.at[1, k],
        device_id={"seq": place},
        device_id_type=MESH,
    )


def attend_kernel(
    q_ref, own_ref, key_ids_ref, query_ids_ref, o_ref, lse_ref, kv_ref, blocked, far, near, pass_on, own_sem
):
    rows = own_ref.shape[0] // 2
    keys = kv_ref.shape[0] * rows
    pairs = q_ref.shape[1] // (2 * HEAD)
    me, near_at, far_at = seq_places()
    beyond = near_at + far_at - me
    greet([("seq", 0), ("seq", 1)])

    def far_copy(p, at):
        return to_seq(own_ref.at[:, pair_lanes(p)], kv_ref.at[at, :, pair_lanes(p)], far, p, far_at)

    def near_copy(p, at):
        return to_seq(own_ref.at[:, pair_lanes(p)], kv_ref.at[at, :, pair_lanes(p)], near, p, near_at)

    def pass_copy(p, at):
        here = kv_ref.at[far_at, :, pair_lanes(p)]
        return to_seq(here, kv_ref.at[at, :, pair_lanes(p)], pass_on, p, near_at)

    def send(p, carry):
        far_copy(p, me).start()
        near_copy(p, me).start()
        return carry

    lax.fori_loop(0, pairs, send, 0)
    own = pltpu.make_async_copy(own_ref, kv_ref.at[me], own_sem)
    own.start()
    blocked[...] = jnp.where(key_ids_ref[...] <= query_ids_ref[...], 0.0, MASK_FILL)
    own.wait()

    def forward_one(p):
        far_copy(p, far_at).wait_recv()
        pass_copy(p, far_at).start()

    forward_one(0)

    def pair(p, carry):
        @pl.when(p + 1 < pairs)
        def _():
            forward_one(p + 1)

        near_copy(p, near_at).wait_recv()
        pass_copy(p, beyond).wait_recv()
        lanes = pair_lanes(p)
        key_pair = kv_ref[:, :rows, lanes].reshape(keys, 2 * HEAD)
        val_turned = kv_ref[:, rows:, lanes].reshape(keys, 2 * HEAD).T
        query_pair = q_ref[:, lanes]
        outs = []
        for half in range(2):
            query = jnp.where(head_lanes(half, query_pair.shape), query_pair, 0)
            scores = dot_rows(key_pair, query.astype(jnp.bfloat16)) * HEAD ** (-0.5) + blocked[...]
            top = jnp.max(scores, 0, keepdims=True)
            raised = jnp.exp(scores - top)
            total = jnp.sum(raised, 0, keepdims=True)
            probs = (raised * (1.0 / total)).astype(jnp.bfloat16)
            outs.append(dot_plain(val_turned[half * HEAD : (half + 1) * HEAD], probs))
            lse_ref[p, half] = (top + jnp.log(total))[0]
        o_ref[:, lanes] = jnp.concatenate(outs, 0).T.astype(o_ref.dtype)
        return carry

    lax.fori_loop(0, pairs, pair, 0)

    def sent(p, carry):
        far_copy(p, me).wait_send()
        near_copy(p, me).wait_send()
        pass_copy(p, far_at).wait_send()
        return carry

    lax.fori_loop(0, pairs, sent, 0)


def attend(queries, own_pair, key_ids, query_ids, number):
    rows, width = queries.shape
    keys = key_ids.shape[0]
    pairs = width // (2 * HEAD)
    groups = lax.axis_size("seq")
    copies = pltpu.SemaphoreType.DMA((2, pairs))
    return pl.pallas_call(
        attend_kernel,
        out_shape=(
            jax.ShapeDtypeStruct((rows, width), jnp.bfloat16),
            jax.ShapeDtypeStruct((pairs, 2, rows), jnp.float32),
            jax.ShapeDtypeStruct((groups,) + own_pair.shape, jnp.bfloat16),
        ),
        in_specs=[pl.BlockSpec(memory_space=pltpu.VMEM)] * 4,
        out_specs=(pl.BlockSpec(memory_space=pltpu.VMEM),) * 3,
        scratch_shapes=[
            pltpu.VMEM((keys, rows), jnp.float32),
            copies,
            copies,
            copies,
            pltpu.SemaphoreType.DMA,
        ],
        compiler_params=pltpu.CompilerParams(
            collective_id=number, has_side_effects=True, vmem_limit_bytes=48 * 2**20
        ),
        cost_estimate=pl.CostEstimate(
            flops=4 * rows * keys * width,
            transcendentals=rows * keys * HEADS,
            bytes_accessed=4 * keys * width,
        ),
        name="attend",
    )(queries, own_pair, key_ids[:, None], query_ids[None, :])


def attend_back_kernel(
    q_ref,
    kv_ref,
    grad_ref,
    lse_ref,
    key_ids_ref,
    query_ids_ref,
    dq_ref,
    own_ref,
    blocked,
    fresh,
    kept,
    near_out,
    near_in,
    far_out,
    far_in,
    near,
    far,
):
    groups, twice, unused = kv_ref.shape
    rows = twice // 2
    keys = groups * rows
    pairs = q_ref.shape[1] // (2 * HEAD)
    scale = HEAD ** (-0.5)
    me, near_at, far_at = seq_places()
    low, high = lax.rem(me, 2), me // 2
    greet([("seq", 0), ("seq", 1)])
    blocked[...] = jnp.where(key_ids_ref[...] <= query_ids_ref[...], 0.0, MASK_FILL)

    def near_copy(p):
        return to_seq(near_out.at[p], near_in.at[p], near, p, near_at)

    def far_copy(p):
        return to_seq(far_out.at[p], far_in.at[p], far, p, far_at)

    def middle(p):
        near_copy(p).wait()
        for k in range(2):
            kept[p, k] = kept[p, k] + near_in[p, k].astype(jnp.float32)
        far_out[p] = kept[p, 1 - high].astype(far_out.dtype)
        far_copy(p).start()

    def last(p):
        far_copy(p).wait()
        total = kept[p, high] + far_in[p].astype(jnp.float32)
        own_ref[:, pair_lanes(p)] = total.astype(own_ref.dtype)

    def pair(p, carry):
        lanes = pair_lanes(p)
        key_pair = kv_ref[:, :rows, lanes].reshape(keys, 2 * HEAD)
        val_pair = kv_ref[:, rows:, lanes].reshape(keys, 2 * HEAD)
        key_turned = key_pair.T
        query_pair = q_ref[:, lanes]
        grad_pair = grad_ref[:, lanes]
        key_grad = jnp.zeros((keys, 2 * HEAD), jnp.float32)
        val_grad = jnp.zeros((keys, 2 * HEAD), jnp.float32)
        outs = []
        for half in range(2):
            here = head_lanes(half, query_pair.shape)
            query = jnp.where(here, query_pair, 0).astype(jnp.bfloat16)
            grad = jnp.where(here, grad_pair, 0).astype(jnp.bfloat16)
            scores = dot_rows(key_pair, query) * scale + blocked[...]
            probs = jnp.exp(scores - lse_ref[p, half][None, :])
            prob_grad = dot_rows(val_pair, grad)
            inner = jnp.sum(probs * prob_grad, 0, keepdims=True)
            score_grad = (probs * (prob_grad - inner)).astype(jnp.bfloat16)
            key_grad = key_grad + dot_plain(score_grad, query)
            val_grad = val_grad + dot_plain(probs.astype(jnp.bfloat16), grad)
            outs.append(dot_plain(key_turned[half * HEAD : (half + 1) * HEAD], score_grad))
        dq_ref[:, lanes] = (jnp.concatenate(outs, 0).T * scale).astype(dq_ref.dtype)
        fresh[:, :rows] = (key_grad * scale).reshape(groups, rows, 2 * HEAD)
        fresh[:, rows:] = val_grad.reshape(groups, rows, 2 * HEAD)
        for k in range(2):
            near_out[p, k] = fresh[2 * k + 1 - low].astype(near_out.dtype)
            kept[p, k] = fresh[2 * k + low]
        near_copy(p).start()

        @pl.when(p >= 1)
        def _():
            middle(p - 1)

        @pl.when(p >= 2)
        def _():
            last(p - 2)

        return carry

    lax.fori_loop(0, pairs, pair, 0)
    middle(pairs - 1)
    last(pairs - 2)
    last(pairs - 1)


def attend_back(queries, key_vals, grad, lse, key_ids, query_ids, number):
    rows, width = queries.shape
    keys = key_ids.shape[0]
    pairs = width // (2 * HEAD)
    piece = (2 * rows, 2 * HEAD)
    copies = pltpu.SemaphoreType.DMA((2, pairs))
    return pl.pallas_call(
        attend_back_kernel,
        out_shape=(
            jax.ShapeDtypeStruct((rows, width), jnp.bfloat16),
            jax.ShapeDtypeStruct((2 * rows, width), jnp.bfloat16),
        ),
        in_specs=[pl.BlockSpec(memory_space=pltpu.VMEM)] * 6,
        out_specs=(pl.BlockSpec(memory_space=pltpu.VMEM),) * 2,
        scratch_shapes=[
            pltpu.VMEM((keys, rows), jnp.float32),
            pltpu.VMEM((lax.axis_size("seq"),) + piece, jnp.float32),
            pltpu.VMEM((pairs, 2) + piece, jnp.float32),
            pltpu.VMEM((pairs, 2) + piece, jnp.bfloat16),
            pltpu.VMEM((pairs, 2) + piece, jnp.bfloat16),
            pltpu.VMEM((pairs,) + piece, jnp.bfloat16),
            pltpu.VMEM((pairs,) + piece, jnp.bfloat16),
            copies,
            copies,
        ],
        compiler_params=pltpu.CompilerParams(
            collective_id=number, has_side_effects=True, vmem_limit_bytes=58 * 2**20
        ),
        cost_estimate=pl.CostEstimate(
            flops=10 * rows * keys * width,
            transcendentals=rows * keys * HEADS,
            bytes_accessed=12 * keys * width,
        ),
        name="attend_back",
    )(queries, key_vals, grad, lse, key_ids[:, None], query_ids[None, :])


def add_pair(first, second):
    return first + second


def merge_soft(first, second):
    highest = jnp.maximum(first[0], second[0])
    total = first[1] * jnp.exp(first[0] - highest) + second[1] * jnp.exp(second[0] - highest)
    return jnp.stack([highest, total, first[2] + second[2]])


def dot_rows(left_op, right_op):
    return lax.dot_general(
        left_op, right_op, (((1,), (1,)), ((), ())), preferred_element_type=jnp.float32
    )


def dot_cols(left_op, right_op):
    return lax.dot_general(
        left_op, right_op, (((0,), (0,)), ((), ())), preferred_element_type=jnp.float32
    )


def dot_plain(left_op, right_op):
    return jnp.dot(left_op, right_op, preferred_element_type=jnp.float32)


def column_sums(values):
    return jnp.sum(values.astype(jnp.float32), 0)


def layer_norm(values, gain, shift):
    center = values - jnp.mean(values, -1, keepdims=True)
    spread = jnp.mean(center * center, -1, keepdims=True)
    return center * lax.rsqrt(spread + NORM_EPS) * gain + shift


def norm_back(values, gain, shift, grad):
    unused, pull = jax.vjp(layer_norm, values, gain, shift)
    return pull(grad)


def one_hot(wanted, length, axis):
    shape = list(wanted.shape)
    shape.insert(axis, length)
    at = lax.broadcasted_iota(jnp.int32, shape, axis)
    return (at == jnp.expand_dims(wanted, axis)).astype(jnp.bfloat16)


def counts_before(flags):
    length = flags.shape[-1]
    earlier = (
        lax.broadcasted_iota(jnp.int32, (length, length), 0)
        < lax.broadcasted_iota(jnp.int32, (length, length), 1)
    ).astype(jnp.bfloat16)
    return dot_plain(flags.astype(jnp.bfloat16), earlier).astype(jnp.int32)


def wide(rows_in):
    return jnp.pad(rows_in, ((0, 0), (0, -rows_in.shape[1] % (2 * HEAD))))


def rows_major(x):
    return with_layout_constraint(x, Layout(major_to_minor=tuple(range(x.ndim))))


def turned(x):
    return with_layout_constraint(x, Layout(major_to_minor=(1, 0)))


def scatter_rows(groups):
    total = lax.axis_size(AXES)
    mats = []
    for group in groups:
        parts = [rows_major(dot_cols(*pair).astype(jnp.bfloat16)) for pair in group]
        grad = jnp.concatenate(parts, 0) if len(parts) > 1 else parts[0]
        mats.append(grad.reshape(total, -1, grad.shape[1]))
    blocks = jnp.concatenate(mats, 1) if len(mats) > 1 else mats[0]
    own = lax.psum_scatter(blocks, AXES, scatter_dimension=0, tiled=True)[0]
    return own.reshape(len(mats), -1, own.shape[1])


def layer_forward(state, weights, params, query_ids, key_ids):
    width = state.shape[1]
    hidden = layer_norm(state, params[0 : 1], params[1 : 2]).astype(jnp.bfloat16)
    joined = rows_major(dot_rows(hidden, weights[0][: 3 * width]))
    queries = wide((joined[:, :width] + params[2 : 3]).astype(jnp.bfloat16))
    key_rows = joined[:, width : 2 * width].astype(jnp.bfloat16)
    val_rows = (joined[:, 2 * width :] + params[3 : 4]).astype(jnp.bfloat16)
    own_pair = jnp.concatenate([wide(key_rows), wide(val_rows)], 0)
    attended, lse, key_vals = attend(queries, own_pair, key_ids, query_ids, 4)
    attended = attended[:, :width]
    mid_state = state + dot_plain(attended, weights[0][3 * width :]) + params[4 : 5]
    normed = layer_norm(mid_state, params[5 : 6], params[6 : 7]).astype(jnp.bfloat16)
    upward = turned(dot_rows(normed, weights[1]) + params[8:12].reshape(1, -1))
    active = turned(jax.nn.gelu(upward, approximate=True).astype(jnp.bfloat16))
    output = mid_state + dot_plain(active, weights[2]) + params[7 : 8]
    return (
        output,
        (hidden, queries, key_vals, lse, attended, mid_state, normed, upward, active),
    )


def layer_backward(state, weights, params, saved, query_ids, key_ids, grad_in, arrived):
    width = state.shape[1]
    hidden, queries, key_vals, lse, attended, mid_state, normed, upward, active = saved
    down_grad = grad_in.astype(jnp.bfloat16)
    act_grad = dot_rows(down_grad, weights[2])
    unused_gelu, gelu_pull = jax.vjp(partial(jax.nn.gelu, approximate=True), upward)
    up_grad = turned(gelu_pull(act_grad)[0].astype(jnp.bfloat16))
    mid_back, gain_two, shift_two = norm_back(
        mid_state, params[5 : 6], params[6 : 7], rows_major(dot_plain(up_grad, weights[1]))
    )
    mid_grad = grad_in + mid_back
    out_grad = mid_grad.astype(jnp.bfloat16)
    att_grad = wide(rows_major(dot_rows(out_grad, weights[0][3 * width :]).astype(jnp.bfloat16)))
    if arrived:
        att_grad, arrived[0] = lax.optimization_barrier((att_grad, arrived[0]))
    query_grad, own = attend_back(queries, key_vals, att_grad, lse, key_ids, query_ids, 8)
    query_grad = query_grad[:, :width]
    key_grad, val_grad = own[: own.shape[0] // 2, :width], own[own.shape[0] // 2 :, :width]
    joined_grad = jnp.concatenate([query_grad, key_grad, val_grad], 1)
    state_back, gain_one, shift_one = norm_back(
        state,
        params[0 : 1],
        params[1 : 2],
        rows_major(dot_plain(joined_grad, weights[0][: 3 * width])),
    )
    up_sums = column_sums(up_grad)
    small_grad = [
        gain_one,
        shift_one,
        column_sums(query_grad),
        column_sums(val_grad),
        column_sums(out_grad),
        gain_two,
        shift_two,
        column_sums(down_grad),
        up_sums,
    ]
    factors = [
        [(joined_grad, hidden), (attended, out_grad)],
        [(up_grad, normed)],
        [(active, down_grad)],
    ]
    return (mid_grad + state_back, factors, small_grad)


def adam_step(weights, moment, square, grad, rate, decay, step):
    moment = BETA_ONE * moment + (1 - BETA_ONE) * grad
    square = BETA_TWO * square + (1 - BETA_TWO) * grad * grad
    moment_hat = moment / (1 - BETA_ONE**step)
    square_hat = square / (1 - BETA_TWO**step)
    weights = weights - rate * (moment_hat / (jnp.sqrt(square_hat) + ADAM_EPS) + decay * weights)
    return (weights, moment, square)


def pad_rows(x, rows):
    return jnp.pad(x, ((0, rows - x.shape[0]), (0, 0)))


def on_device(
    tokens,
    block_ids,
    completion,
    regroup,
    targets,
    step_count,
    layer_mats,
    mats_moment,
    mats_square,
    embed_table,
    table_moment,
    table_square,
):
    seqs, tok_count = tokens.shape
    seq_length = block_ids.shape[1]
    width = embed_table.shape[1]
    table_local = embed_table.shape[0]
    layers = layer_mats.shape[0]
    replicas, groups, shards = (lax.axis_size(axis) for axis in AXES)
    total = replicas * groups * shards
    seq_at = lax.axis_index("seq")
    shard_at = lax.axis_index("shard")
    device_at = lax.axis_index(AXES)
    seq_bits, dp_bits, shard_bits = bits_of("seq"), bits_of("dp"), bits_of("shard")
    first_row = device_at * table_local
    table_own = embed_table.astype(jnp.bfloat16)
    mats_low = layer_mats.astype(jnp.bfloat16)
    token_ids = tokens.reshape(-1)
    local_rows = token_ids.shape[0]
    small_count = 12 * layers + 2
    small_rows = -(-small_count // 16) * 16

    packed_ids = jnp.pad(token_ids, (0, -local_rows % 1024)).reshape(-1, 128)
    ids_all = run_jobs([spread_job(packed_ids, False)], "share_ids", 0, 16)[0][0]
    ids_all = ids_all.reshape(total, -1)[:, :local_rows]
    owner_all = ids_all // table_local
    loads = jnp.sum(
        (owner_all[:, :, None] == jnp.arange(total)[None, None, :]).astype(jnp.int32), 1
    )
    rounds = (jnp.max(loads) + SLOTS - 1) // SLOTS
    asked = owner_all == device_at
    asked_rank = counts_before(asked)
    asked_row = ids_all - first_row
    own_owner = token_ids // table_local
    same = own_owner[:, None] == own_owner[None, :]
    before = jnp.arange(local_rows)[None, :] < jnp.arange(local_rows)[:, None]
    own_rank = jnp.sum((same & before).astype(jnp.int32), 1)

    def asked_rows(at):
        chosen = asked[:, None, :] & (
            asked_rank[:, None, :] == at * SLOTS + jnp.arange(SLOTS)[None, :, None]
        )
        return (jnp.sum(jnp.where(chosen, asked_row[:, None, :] + 1, 0), 2) - 1).reshape(-1)

    def own_slots(at):
        slot = own_rank - at * SLOTS
        return jnp.where((slot >= 0) & (slot < SLOTS), own_owner * SLOTS + slot, -1)

    def fetch(at, given):
        return dot_plain(
            one_hot(own_slots(at), total * SLOTS, 1), given.reshape(total * SLOTS, width)
        )

    fixed = jnp.arange(seq_length + small_rows, dtype=jnp.int32)
    fixed_row = jnp.where(fixed < seq_length + small_count, VOCAB + fixed - first_row, -1)
    wanted = jnp.concatenate([asked_rows(0), fixed_row])
    rows_out = dot_plain(one_hot(wanted, table_local, 1), table_own).astype(jnp.bfloat16)
    exchanged = total * SLOTS
    piece = seq_length // total
    gathered = []
    for layer_at in range(layers):
        if layer_at == 0:
            whole = lax.all_gather(mats_low[0], AXES, axis=1, tiled=True)
            gathered.append([whole[k] for k in range(3)])
        else:
            rest = lax.all_gather(mats_low[layer_at, 1:], AXES, axis=1, tiled=True)
            gathered.append([rest[0], rest[1]])
    (upper_first,), (place_rows,), (small,), (given,) = run_jobs(
        [
            gather_job([mats_low[1, 0]]),
            sum_job(
                rows_out[exchanged : exchanged + seq_length].reshape(total, piece, width),
                sum_axes=("seq", "dp", "shard"),
                sum_orders=[seq_bits + dp_bits + shard_bits],
                join_axes=("dp", "shard"),
                join_orders=[shard_bits[::-1] + dp_bits[::-1]],
            ),
            combine_job(rows_out[exchanged + seq_length :], add_pair),
            swap_job(rows_out[:exchanged].reshape(total, SLOTS, width), late=7),
        ],
        "open_rows",
        2,
        32,
    )
    gathered[1].insert(0, upper_first.reshape(-1, width))
    place_rows = place_rows.reshape(tok_count, width)
    small = small[:small_count].astype(jnp.float32)
    place_state = jnp.broadcast_to(place_rows.astype(jnp.float32), (seqs, tok_count, width))
    state = fetch(0, given) + place_state.reshape(local_rows, width)

    def fetch_more(at, held):
        rows = dot_plain(one_hot(asked_rows(at), table_local, 1), table_own).astype(jnp.bfloat16)
        return held + fetch(at, swap(rows.reshape(total, SLOTS, width), "swap_rows", 1))

    state = lax.fori_loop(1, rounds, fetch_more, state)

    query_ids = lax.dynamic_slice_in_dim(block_ids[0], seq_at * tok_count, tok_count, 0)
    inputs, kept, saved = [], [], []
    for layer_at in range(layers):
        weights = gathered[layer_at]
        inputs.append(state)
        kept.append(weights)
        state, held = layer_forward(
            state,
            weights,
            small[12 * layer_at : 12 * layer_at + 12],
            query_ids,
            block_ids[0],
        )
        saved.append(held)
    final_gain = small[12 * layers : 12 * layers + 1]
    final_shift = small[12 * layers + 1 : 12 * layers + 2]
    final = layer_norm(state, final_gain, final_shift).astype(jnp.bfloat16)

    group_mask = completion[0]
    slot_of = regroup[0]
    slots = slot_of.shape[0]
    comp_rows = slots // shards
    rank_all = counts_before(group_mask[None])[0]
    mine = lax.dynamic_slice_in_dim(group_mask, shard_at * local_rows, local_rows)
    my_rank = lax.dynamic_slice_in_dim(rank_all, shard_at * local_rows, local_rows)
    my_slot = jnp.sum(
        jnp.where(my_rank[:, None] == jnp.arange(slots)[None, :], slot_of[None, :], 0), 1
    )
    to_slot = one_hot(jnp.where(mine == 1, my_slot, -1), slots, 0)
    outgoing = dot_plain(to_slot, final).astype(jnp.bfloat16).reshape(shards, comp_rows, width)
    two_ways = [seq_bits[1:] + dp_bits, dp_bits + seq_bits[1:]]
    head_in = exchange(
        outgoing,
        "share_final",
        5,
        sum_axes=("shard",),
        sum_orders=[shard_bits, shard_bits],
        join_axes=AXES,
        join_orders=[shard_bits[::-1] + way[::-1] + seq_bits[:1] for way in two_ways],
        chunks=2,
    ).reshape(-1, width)

    rows_all = targets.shape[0]
    columns = first_row + jnp.arange(table_local, dtype=jnp.int32)
    live = (columns < VOCAB)[None, :]
    logits = dot_rows(head_in, table_own)
    masked = jnp.where(live, logits, MASK_FILL)
    top_local = jnp.max(masked, 1)
    total_local = jnp.sum(jnp.where(live, jnp.exp(masked - top_local[:, None]), 0.0), 1)
    target_hit = columns[None, :] == targets[:, None]
    pick_local = jnp.sum(jnp.where(target_hit, logits, 0.0), 1)
    stats = combine_all(
        jnp.stack([top_local, total_local, pick_local]).reshape(3, -1, 128),
        merge_soft,
        "share_stats",
        6,
    ).reshape(3, rows_all)
    log_total = stats[0] + jnp.log(stats[1])
    loss_value = jnp.sum(log_total - stats[2]) / rows_all
    probs = jnp.where(live, jnp.exp(masked - log_total[:, None]), 0.0)
    logit_grad = ((probs - target_hit.astype(jnp.float32)) / rows_all).astype(jnp.bfloat16)
    head_grad = dot_cols(logit_grad, head_in)
    returned = exchange(
        dot_plain(logit_grad, table_own).reshape(total, comp_rows, width),
        "return_final",
        7,
        sum_axes=AXES,
        sum_orders=[seq_bits[:1] + way + shard_bits for way in two_ways],
        join_axes=("shard",),
        join_orders=[shard_bits[::-1], shard_bits[::-1]],
        chunks=2,
    ).reshape(slots, width)
    final_grad = rows_major(dot_cols(to_slot, returned))
    state_grad, gain_final, shift_final = norm_back(state, final_gain, final_shift, final_grad)

    late = []
    arrived = []
    small_grads = [None] * layers
    for layer_at in reversed(range(layers)):
        state_grad, factors, small_grads[layer_at] = layer_backward(
            inputs[layer_at],
            kept[layer_at],
            small[12 * layer_at : 12 * layer_at + 12],
            saved[layer_at],
            query_ids,
            block_ids[0],
            state_grad,
            arrived,
        )
        if layer_at > 0:
            arrived = [scatter_rows(factors[2:]), scatter_rows(factors[1:2])]
            late = factors[:1]
        else:
            late = factors + late

    low_grad = state_grad.astype(jnp.bfloat16)
    place_grad = jnp.sum(state_grad.reshape(seqs, tok_count, width), 0)
    small_grad = jnp.concatenate(
        [x.reshape(-1) for x in sum(small_grads, []) + [gain_final, shift_final]]
    )
    small_size = small_grad.shape[0]
    small_grad = jnp.pad(small_grad, (0, -small_size % 1024)).reshape(-1, 128)

    def leaving(at):
        rows = dot_cols(one_hot(own_slots(at), total * SLOTS, 1), low_grad).astype(jnp.bfloat16)
        return rows_major(rows).reshape(total, SLOTS, width)

    late = late_mats(late, 12)
    fits = mats_fit(late)
    (own_mats,), (place_grad,), (small_grad,), (came,) = run_jobs(
        [
            mats_job(late[:fits]),
            sum_job(
                place_grad.reshape(replicas * shards, piece, width),
                sum_axes=("dp", "shard"),
                sum_orders=[dp_bits + shard_bits],
                join_axes=("seq", "dp", "shard"),
                join_orders=[shard_bits[::-1] + dp_bits[::-1] + seq_bits[::-1]],
            ),
            combine_job(small_grad, add_pair),
            swap_job(leaving(0), late=5),
        ],
        "close_rows",
        10,
        61,
    )
    for k in range(fits, len(late), fits):
        more = run_jobs([mats_job(late[k : k + fits])], "sum_mats", 14 + k, 61)[0][0]
        own_mats = jnp.concatenate([own_mats, lax.optimization_barrier(more)], 0)
    place_grad = place_grad.reshape(seq_length, width)
    came, arrived[1] = lax.optimization_barrier((came, arrived[1]))
    upper = jnp.concatenate([arrived[1], arrived[0]], 0).astype(jnp.float32)
    small_grad = pad_rows(small_grad.reshape(-1)[:small_size].reshape(-1, width), small_rows)
    small_high = small_grad.astype(jnp.bfloat16)
    small_low = (small_grad - small_high.astype(jnp.float32)).astype(jnp.bfloat16)
    values = jnp.concatenate([came.reshape(-1, width), place_grad, small_high, small_low], 0)
    value_row = jnp.concatenate([wanted, fixed_row[seq_length:]])
    table_grad = dot_plain(one_hot(value_row, table_local, 0), values) + head_grad

    def return_more(at, held):
        rows = swap(leaving(at), "swap_rows", 1).reshape(-1, width)
        return held + dot_plain(one_hot(asked_rows(at), table_local, 0), rows)

    table_grad = lax.fori_loop(1, rounds, return_more, table_grad)
    mats_grad = jnp.concatenate([own_mats, upper], 0).reshape(layer_mats.shape)
    local_squares = jnp.sum(mats_grad * mats_grad) + jnp.sum(table_grad * table_grad)
    squares = jnp.full((8, 128), local_squares)
    squares = run_jobs([spread_job(squares, True)], "share_norm", 11, 16)[0][0]
    grad_norm = jnp.sqrt(squares[0, 0])
    factor = CLIP_NORM / grad_norm
    step = step_count[0].astype(jnp.float32)
    new_mats = adam_step(
        layer_mats, mats_moment, mats_square, factor * mats_grad, RATE_MATS, DECAY_RATE, step
    )
    plain_rows = (columns < VOCAB + seq_length)[:, None]
    rate = jnp.where(plain_rows, RATE_TABLE, RATE_SMALL)
    decay = jnp.where(plain_rows, DECAY_RATE, 0.0)
    new_table = adam_step(
        embed_table, table_moment, table_square, factor * table_grad, rate, decay, step
    )
    return (
        loss_value.reshape(1),
        grad_norm.reshape(1),
        new_mats[0],
        new_mats[1],
        new_mats[2],
        new_table[0],
        new_table[1],
        new_table[2],
    )


def solution(mesh):
    in_specs = (
        P(("dp", "shard"), "seq"),
        P(("dp", "shard"), None),
        P(("dp", "seq"), None),
        P(("dp", "seq"), None),
        P(),
        P(),
        P(None, None, ("dp", "seq", "shard"), None),
        P(None, None, ("dp", "seq", "shard"), None),
        P(None, None, ("dp", "seq", "shard"), None),
        P(("dp", "seq", "shard"), None),
        P(("dp", "seq", "shard"), None),
        P(("dp", "seq", "shard"), None),
    )
    out_specs = (
        P(),
        P(),
        P(None, None, ("dp", "seq", "shard"), None),
        P(None, None, ("dp", "seq", "shard"), None),
        P(None, None, ("dp", "seq", "shard"), None),
        P(("dp", "seq", "shard"), None),
        P(("dp", "seq", "shard"), None),
        P(("dp", "seq", "shard"), None),
    )
    return jax.shard_map(
        on_device, mesh=mesh, in_specs=in_specs, out_specs=out_specs, check_vma=False
    )
```
